32 devices in a mesh: batch: 2 (over x), seq: 16 (over z, y, core).
Axes of the slice: x: 2, y: 2, z: 4, core: 2. Of those that a mesh axis runs over, the one named last changes fastest.
Arguments:
- frames: bfloat16 [1024, 4, 1024], P('seq', 'batch'), may hold values from -6 to 6
- cotangent: bfloat16 [1024, 4, 1024], P('seq', 'batch'), may hold values from -6 to 6
- segment_lengths: int32 [4, 4], P('batch'), may hold values from 1 to 832, 1024 in all within a row
- position_offsets: int32 [4, 4], P('batch'), may hold values from 0 to 1023
- first_gain: bfloat16 [1024], P('seq'), may hold values from 0.5 to 1.5
- first_shift: bfloat16 [1024], P('seq'), may hold values from -3 to 3
- inward_weight: bfloat16 [1024, 3072], P('seq'), may hold values from -0.1875 to 0.1875
- query_bias: bfloat16 [1024], P('seq'), may hold values from -3 to 3
- value_bias: bfloat16 [1024], P('seq'), may hold values from -3 to 3
- outward_weight: bfloat16 [1024, 1024], P('seq'), may hold values from -1.5 to 1.5
- outward_bias: bfloat16 [1024], P('seq'), may hold values from -3 to 3
- second_gain: bfloat16 [1024], P('seq'), may hold values from 0.5 to 1.5
- second_shift: bfloat16 [1024], P('seq'), may hold values from -3 to 3
- expand_weight: bfloat16 [1024, 4096], P('seq'), may hold values from -0.1875 to 0.1875
- expand_bias: bfloat16 [4096], P('seq'), may hold values from -3 to 3
- shrink_weight: bfloat16 [4096, 1024], P('seq'), may hold values from -0.09375 to 0.09375
- shrink_bias: bfloat16 [1024], P('seq'), may hold values from -3 to 3
Outputs:
- layer_output: bfloat16 [1024, 4, 1024], P('seq', 'batch')
- frames_grad: float32 [1024, 4, 1024], P('seq', 'batch')
- first_gain_grad: float32 [1024], P('seq')
- first_shift_grad: float32 [1024], P('seq')
- inward_weight_grad: float32 [1024, 3072], P('seq')
- query_bias_grad: float32 [1024], P('seq')
- value_bias_grad: float32 [1024], P('seq')
- outward_weight_grad: float32 [1024, 1024], P('seq')
- outward_bias_grad: float32 [1024], P('seq')
- second_gain_grad: float32 [1024], P('seq')
- second_shift_grad: float32 [1024], P('seq')
- expand_weight_grad: float32 [1024, 4096], P('seq')
- expand_bias_grad: float32 [4096], P('seq')
- shrink_weight_grad: float32 [4096, 1024], P('seq')
- shrink_bias_grad: float32 [1024], P('seq')
The draws below stay inside these ranges and needn't reach their ends.
Inputs may be any that keep to these rules, and one draw needn't show every extreme that they name: `segment_lengths`: in each row the 4 lengths sum to 1024, and the largest is exactly 832.
All inputs are finite; a program needn't handle non-finite values.
Results may differ from the reference program's by a relative error of at most 0.011.
Values may be sent and summed in bfloat16 or wider, within the bound.
No kernel may reach another device: no remote copies, remote signals or barrier semaphores. Data moves between devices by JAX's collectives and lax.ppermute only.
A program may use at most 320 MiB of HBM per device.

```python
import math
import jax
import jax.numpy as jnp
import numpy as np
from jax import lax

D = 1024
HEADS = 16
HEAD_DIM = 64
FF = 4096
NSEG = 4
LEN_DEV = 64
LEN = 1024
ROWS = 4


def place_ends(values, rng, smallest, top_value):
    shape = values.shape
    spot = [jax.random.randint(jax.random.fold_in(rng, axis), (), 0, shape[axis]) for axis in range(len(shape))]
    values = values.at[tuple(spot)].set(smallest)
    longest = shape.index(max(shape))
    spot[longest] = (spot[longest] + 1) % shape[longest]
    return values.at[tuple(spot)].set(top_value)


def levels(own_key, extent, pieces, least, high):
    level = 1.0
    for dim, parts in pieces:
        steps = jax.random.uniform(jax.random.fold_in(jax.random.fold_in(own_key, 6), dim), (parts,), jnp.float32, least / len(pieces), high / len(pieces))
        level = level * jnp.repeat(jnp.exp(steps), extent[dim] // parts).reshape((-1,) + (1,) * (len(extent) - 1 - dim))
    return level


def split_up(count, total, most, skew):
    loads = [(1 << 20) // math.isqrt(rank ** skew) + 1 for rank in range(2, count + 1)]
    surplus, given = total - most - (count - 1), [1] * (count - 1)
    while surplus > 0:
        candidates = [i for i in range(count - 1) if given[i] < most]
        mass, budget = sum([loads[i] for i in candidates]), surplus
        for i in candidates:
            extra = min(most - given[i], max(1, budget * loads[i] // mass), surplus)
            given[i] = given[i] + extra
            surplus = surplus - extra
    return np.array([most] + given)


def uneven_parts(stream_key, count, total, reach, lean):
    if count == 2:
        one = jax.random.randint(stream_key, (), max(1, total - reach), min(reach, total - 1) + 1)
        return jnp.stack([one, total - one])
    sizes = jnp.asarray(split_up(count, total, reach, lean), jnp.int32)
    couples = (count - 1) // 2
    donor, receiver = sizes[1:1 + 2 * couples:2], sizes[2:2 + 2 * couples:2]
    room = jnp.minimum(donor - 1, reach - receiver)
    shifted = jax.random.randint(jax.random.fold_in(stream_key, 1), (couples,), 0, 1 << 20) % (room + 1)
    sizes = sizes.at[1:1 + 2 * couples:2].set(donor - shifted).at[2:2 + 2 * couples:2].set(receiver + shifted)
    return sizes[jax.random.permutation(jax.random.fold_in(stream_key, 2), count)]


def gaussian(own_key, shape, scale, bound, cuts=(), kind=jnp.bfloat16):
    entries = scale * jax.random.normal(own_key, shape, jnp.float32)
    if cuts:
        entries = entries * levels(own_key, shape, cuts, -0.22, 0.18)
    return jnp.clip(entries, -bound, bound).astype(kind)


def setup_inputs(seed: int = 0) -> dict:
    splits = jax.random.split(jax.random.key(seed), 18)
    return {
        "frames": gaussian(splits[0], (LEN, ROWS, D), 1.0, 6.0, ((0, 16), (1, 2))),
        "cotangent": gaussian(splits[1], (LEN, ROWS, D), 1.0, 6.0, ((0, 16), (1, 2))),
        "segment_lengths": jax.vmap(lambda own: uneven_parts(own, NSEG, LEN, LEN - 3 * LEN_DEV, 2))(jax.random.split(splits[2], ROWS)).reshape((ROWS, NSEG)).astype(jnp.int32),
        "position_offsets": place_ends(jax.random.randint(splits[3], (ROWS, NSEG), 0, 1024), jax.random.fold_in(splits[3], 1), 0, 1023).astype(jnp.int32),
        "first_gain": jnp.clip(1.0 + 0.1 * jax.random.normal(splits[4], (D,), jnp.float32), 0.5, 1.5).astype(jnp.bfloat16),
        "first_shift": gaussian(splits[5], (D,), 0.3, 3.0, ((0, 16),)),
        "inward_weight": gaussian(splits[6], (D, 3 * D), D ** -0.5, 0.1875, ((0, 16),)),
        "query_bias": gaussian(splits[7], (D,), 0.3, 3.0, ((0, 16),)),
        "value_bias": gaussian(splits[8], (D,), 0.3, 3.0, ((0, 16),)),
        "outward_weight": gaussian(splits[9], (D, D), (D // 64) ** -0.5, 1.5, ((0, 16),)),
        "outward_bias": gaussian(splits[10], (D,), 0.3, 3.0, ((0, 16),)),
        "second_gain": jnp.clip(1.0 + 0.1 * jax.random.normal(splits[11], (D,), jnp.float32), 0.5, 1.5).astype(jnp.bfloat16),
        "second_shift": gaussian(splits[12], (D,), 0.3, 3.0, ((0, 16),)),
        "expand_weight": gaussian(splits[13], (D, FF), D ** -0.5, 0.1875, ((0, 16),)),
        "expand_bias": gaussian(splits[14], (FF,), 0.5, 3.0, ((0, 16),)),
        "shrink_weight": gaussian(splits[15], (FF, D), FF ** -0.5, 0.09375, ((0, 16),)),
        "shrink_bias": gaussian(splits[16], (D,), 0.3, 3.0, ((0, 16),)),
    }


@jax.custom_vjp
def low(v):
    return lax.optimization_barrier(v.astype(jnp.bfloat16)).astype(jnp.float32)

@jax.custom_vjp
def low_back(v):
    return v

def low_keep(v):
    return (low(v), None)

def low_pass(kept, grad):
    return (grad,)

def back_keep(v):
    return (v, None)

def back_low(kept, grad):
    return (low(grad),)
low.defvjp(low_keep, low_pass)
low_back.defvjp(back_keep, back_low)
norm_eps = 1e-05
exact_mode = lax.Precision.HIGHEST

def layer_norm(values, gain, shift):
    center = values - lax.optimization_barrier(jnp.mean(values, axis=-1, keepdims=True))
    spread = lax.optimization_barrier(jnp.mean(center * center, axis=-1, keepdims=True))
    return center * lax.rsqrt(spread + norm_eps) * gain + shift

def frame_layout(frame_index, lengths, offsets):
    ends = jnp.cumsum(lengths, axis=1).astype(jnp.int32)
    starts = (ends - lengths).astype(jnp.int32)
    place = frame_index[:, None, None]
    inside = (place >= starts[None]) & (place < ends[None])
    labels = jnp.arange(lengths.shape[1], dtype=jnp.int32)
    segment = lax.optimization_barrier(jnp.sum(jnp.where(inside, labels, 0), axis=2)).astype(jnp.int32)
    position = lax.optimization_barrier(jnp.sum(jnp.where(inside, offsets[None] + place - starts[None], 0), axis=2)).astype(jnp.int32)
    return (segment, position)

def sinusoid(position, width):
    index = jnp.arange(width // 2, dtype=jnp.float32)
    rates = jnp.exp(index * (-2.0 * math.log(10000.0) / width))
    angles = position.astype(jnp.float32)[..., None] * rates
    return jnp.stack([jnp.sin(angles), jnp.cos(angles)], axis=-1).reshape(position.shape + (width,))

def rounded_both(values):
    return low_back(low(values))

def reference(frames, cotangent, segment_lengths, position_offsets, first_gain, first_shift, inward_weight, query_bias, value_bias, outward_weight, outward_bias, second_gain, second_shift, expand_weight, expand_bias, shrink_weight, shrink_bias):
    frame_index = jnp.arange(LEN, dtype=jnp.int32)
    segment, position = frame_layout(frame_index, segment_lengths, position_offsets)
    encoding = sinusoid(position, D)
    causal = frame_index[:, None] >= frame_index[None, :]
    scale_factor = 1.0 / math.sqrt(HEAD_DIM)
    params = tuple((item.astype(jnp.float32) for item in (first_gain, first_shift, inward_weight, query_bias, value_bias, outward_weight, outward_bias, second_gain, second_shift, expand_weight, expand_bias, shrink_weight, shrink_bias)))

    def one_row(row_input, row_segment, weights):
        gain_one, shift_one, inward, query_b, value_b, outward, outward_b, gain_two, shift_two, expand, expand_b, shrink, shrink_b = weights
        normed = low(layer_norm(row_input, gain_one, shift_one))
        mixed = jnp.dot(normed, inward, precision=exact_mode)
        queries = rounded_both(mixed[:, :D] + query_b).reshape(LEN, HEADS, HEAD_DIM)
        keys = rounded_both(mixed[:, D:2 * D]).reshape(LEN, HEADS, HEAD_DIM)
        values = rounded_both(mixed[:, 2 * D:] + value_b).reshape(LEN, HEADS, HEAD_DIM)
        scores = low_back(jnp.einsum('ihd,jhd->hij', queries, keys, precision=exact_mode) * scale_factor)
        allowed = causal & (row_segment[:, None] == row_segment[None, :])
        scores = jnp.where(allowed[None], scores, -1e+30)
        probs = low(jax.nn.softmax(scores, axis=-1))
        context = jnp.einsum('hij,jhd->ihd', probs, values, precision=exact_mode).reshape(LEN, D)
        context = rounded_both(context)
        attended = low_back(jnp.dot(context, outward, precision=exact_mode) + outward_b)
        middle = row_input + attended
        normed_two = low(layer_norm(middle, gain_two, shift_two))
        before = low_back(jnp.dot(normed_two, expand, precision=exact_mode) + expand_b)
        active = low(jax.nn.gelu(before, approximate=True))
        return middle + jnp.dot(active, shrink, precision=exact_mode) + shrink_b

    def layer(values, weights):
        rows_first = jnp.swapaxes(values + encoding, 0, 1)
        row_step = jax.checkpoint(lambda item: one_row(item[0], item[1], weights))
        outputs = lax.map(row_step, (rows_first, jnp.swapaxes(segment, 0, 1)))
        return jnp.swapaxes(outputs, 0, 1)
    result, backward = jax.vjp(layer, frames.astype(jnp.float32), params)
    frames_grad, grads = backward(cotangent.astype(jnp.float32))
    g_one, s_one, g_inward, g_query, g_value, g_outward, g_outward_b, g_two, s_two, g_expand, g_expand_b, g_shrink, g_shrink_b = grads
    return (result.astype(jnp.bfloat16), frames_grad, g_one, s_one, g_inward, g_query, g_value, g_outward, g_outward_b, g_two, s_two, g_expand, g_expand_b, g_shrink, g_shrink_b)
```

```python
import functools
import math

import jax
import jax.numpy as jnp
from jax import lax
from jax.experimental import pallas as pl
from jax.experimental.pallas import tpu as pltpu
from jax.sharding import Mesh, PartitionSpec as P


HEADS = 16
NZ = 4
NORM_EPS = 1e-05
NEG = -1e30
F32 = jnp.float32
BF16 = jnp.bfloat16
LAYER_OF_ROW = (1, 2, 0, 3)
SWAP = [(0, 1), (1, 0)]
LAYER = ("x", "y", "c")


def xor_perm(count, k):
    return [(i, i ^ k) for i in range(count)]


def hop(value, axis, count=2, k=1):
    return lax.ppermute(value, axis, xor_perm(count, k))


def pick(value, index, axis=0):
    return lax.dynamic_index_in_dim(value, index, axis, keepdims=False)


def stack_rows(parts):
    return jnp.concatenate(parts, axis=0)


def to_layer(block, ny):
    half = block.shape[0] // 2
    over_x = hop(block, "x")
    over_y = {k: hop(block, "y", ny, k) for k in range(1, ny)}
    mine_c = hop(block, "c")
    over_xy = {
        k: stack_rows([hop(over_x[:half], "y", ny, k), hop(over_y[k][half:], "x")]) for k in range(1, ny)
    }
    near = {(0, 0): block, (1, 0): over_x}
    for k in range(1, ny):
        near[0, k] = over_y[k]
        near[1, k] = over_xy[k]
    far = {key: hop(value, "c") for key, value in near.items() if key != (0, 0)}
    far[0, 0] = mine_c
    return stack_rows([v for dx in range(2) for k in range(ny) for v in (near[dx, k], far[dx, k])])


def from_layer(parts, ny):
    rows, width = parts.shape
    size = rows // (4 * ny)
    view = parts.reshape(2, ny, 2, size, width)
    half = size // 2
    total = {}
    for dx in (1, 0):
        for k in reversed(range(ny)):
            total[dx, k] = view[dx, k, 0].astype(F32) + hop(view[dx, k, 1], "c").astype(F32)
    top, bottom = {}, total[1, 0][half:]
    for k in range(1, ny):
        low = total[1, k].astype(BF16)
        top[k] = total[0, k][:half] + hop(low[:half], "x").astype(F32)
        bottom = bottom + hop(low[half:], "y", ny, k).astype(F32)
    result = total[0, 0]
    for k in range(1, ny):
        send = stack_rows([top[k].astype(BF16), total[0, k][half:].astype(BF16)])
        result = result + hop(send, "y", ny, k).astype(F32)
    send = stack_rows([total[1, 0][:half].astype(BF16), bottom.astype(BF16)])
    return result + hop(send, "x").astype(F32)


def rehome_flat(x, z, c):
    return (x * NZ + z) * 2 + c


def rehome_perm(k):
    return [
        (rehome_flat(x, z, c), rehome_flat(z >> 1, LAYER_OF_ROW[2 * x + (c ^ k)], z & 1))
        for x in range(2)
        for z in range(NZ)
        for c in range(2)
    ]


def to_home(block, place):
    got = [
        lax.ppermute(jnp.where(place.c == k, block[:, 0], block[:, 1]), ("x", "z", "c"), rehome_perm(k))
        for k in range(2)
    ]
    first = place.z < 2
    return stack_rows([jnp.where(first, got[0], got[1]), jnp.where(first, got[1], got[0])])


def to_origin(block, place):
    half = block.shape[0] // 2
    first = place.z < 2
    low, high = block[:half], block[half:]
    sent = [jnp.where(first, low, high), jnp.where(first, high, low)]
    got = [
        lax.ppermute(sent[k], ("x", "z", "c"), [(b, a) for a, b in rehome_perm(k)]) for k in range(2)
    ]
    return jnp.stack(
        [jnp.where(place.c == 0, got[0], got[1]), jnp.where(place.c == 0, got[1], got[0])], axis=1
    )


def over_z(value):
    return [value] + [hop(value, "z", NZ, k) for k in range(1, NZ)]


def sum_over_z(parts):
    total = parts[0].astype(F32)
    for k in range(1, NZ):
        total = total + hop(parts[k].astype(BF16), "z", NZ, k).astype(F32)
    return total


def z_order(value, z):
    quarter = value.shape[1] // NZ
    return jnp.concatenate(
        [lax.dynamic_slice_in_dim(value, (z ^ k) * quarter, quarter, 1) for k in range(NZ)], axis=1
    )


def by_half(x, mine, other, axis):
    return jnp.concatenate([jnp.where(x == 0, mine, other), jnp.where(x == 0, other, mine)], axis=axis)


def sin_cos(position, width):
    feature = jnp.arange(width, dtype=jnp.int32)
    rates = jnp.exp((feature // 2).astype(F32) * (-2.0 * math.log(10000.0) / width))
    angle = position.astype(F32)[:, None] * rates[None, :]
    turn = jnp.round(angle * (2.0 / math.pi))
    rest = angle - turn * 1.5703125
    rest = rest - turn * 0.00048375129699707031
    rest = rest - turn * 7.5497899548918861e-08
    quadrant = turn.astype(jnp.int32) + (feature % 2)[None, :]
    square = rest * rest
    sine = rest + rest * square * (
        -0.16666666641626524 + square * (0.008333329385889463 + square * (-0.00019839334836096632 + square * 2.718311493989822e-06))
    )
    cosine = 1.0 + square * (
        -0.49999999725103100 + square * (0.04166662332373906 + square * (-0.001388676377460993 + square * 2.439044879627741e-05))
    )
    value = jnp.where((quadrant & 1) == 0, sine, cosine)
    return jnp.where((quadrant & 2) == 0, value, -value)


def normalize(values):
    center = values - jnp.mean(values, axis=-1, keepdims=True)
    scale = lax.rsqrt(jnp.mean(center * center, axis=-1, keepdims=True) + NORM_EPS)
    return center * scale, scale


def normalize_back(normal, scale, gain, upstream):
    scaled = upstream * gain
    inner = scaled - jnp.mean(scaled, axis=-1, keepdims=True)
    inner = inner - normal * jnp.mean(scaled * normal, axis=-1, keepdims=True)
    return inner * scale, jnp.sum(upstream * normal, axis=0), jnp.sum(upstream, axis=0)


def dot_nt(a, b):
    return lax.dot_general(a, b, (((1,), (1,)), ((), ())), preferred_element_type=F32)


def dot_tn(a, b):
    return lax.dot_general(a, b, (((0,), (0,)), ((), ())), preferred_element_type=F32)


def dot_nn(a, b):
    return jnp.dot(a, b, preferred_element_type=F32)


BLOCK = 256


def chunk_owner(chunk, ny):
    outer, y = divmod(chunk, ny)
    return ((outer >> 1) * ny + y) * 2 + (outer & 1)


def lane_parts(heads, width):
    if heads == 1:
        return [None]
    lane = lax.broadcasted_iota(jnp.int32, (1, width), 1)
    return [(lane >= h * (width // heads)) & (lane < (h + 1) * (width // heads)) for h in range(heads)]


def only(value, lanes):
    return value if lanes is None else jnp.where(lanes, value, jnp.zeros_like(value))


def allowed_pairs(start_ref, first, total):
    key = lax.broadcasted_iota(jnp.int32, (total, BLOCK), 0)
    frame = first + lax.broadcasted_iota(jnp.int32, (total, BLOCK), 1)
    return (key >= start_ref[:, first : first + BLOCK]) & (key <= frame)


def attend(heads, ny, size, me_ref, qkv_ref, start_ref, near_ref, far_ref, log_ref, q_s, k_s, vt_s):
    count = 4 * ny
    width = q_s.shape[1]
    me = me_ref[0]
    for chunk in range(count):
        rel = me ^ chunk_owner(chunk, ny)
        rows = pl.ds(pl.multiple_of(rel * size, size), size)
        here = slice(chunk * size, (chunk + 1) * size)
        q_s[here, :] = qkv_ref[rows, 0:width] * 0.125
        k_s[here, :] = qkv_ref[rows, width : 2 * width]
        vt_s[:, here] = jnp.transpose(qkv_ref[rows, 2 * width : 3 * width].astype(F32)).astype(BF16)
    lanes = lane_parts(heads, width)
    each = width // heads
    for block in range(count * size // BLOCK):
        first = block * BLOCK
        total = first + BLOCK
        allowed = allowed_pairs(start_ref, first, total)
        q_block = q_s[first:total, :]
        contexts = []
        for h in range(heads):
            scores = dot_nt(k_s[0:total, :], only(q_block, lanes[h]))
            scores = jnp.where(allowed, scores, NEG)
            top = jnp.max(scores, axis=0, keepdims=True)
            weight = jnp.exp(scores - top)
            mass = jnp.sum(weight, axis=0, keepdims=True)
            part = dot_nn(vt_s[h * each : (h + 1) * each, 0:total], weight.astype(BF16))
            contexts.append(part / mass)
            log_ref[h : h + 1, first:total] = top + jnp.log(mass)
        context = contexts[0] if heads == 1 else jnp.concatenate(contexts, axis=0)
        context = jnp.transpose(context).astype(BF16)
        for sub in range(BLOCK // size):
            owner = chunk_owner(block * (BLOCK // size) + sub, ny)
            piece = context[sub * size : (sub + 1) * size]
            near_ref[owner] = piece
            far_ref[pl.ds(pl.multiple_of((me ^ owner) * size, size), size), :] = piece


def attend_back(
    heads, ny, size, me_ref, qkv_ref, grad_ref, start_ref, log_ref, out_ref, q_s, k_s, v_s, g_s, kt_s, dq_s, dk_s, dv_s
):
    count = 4 * ny
    width = q_s.shape[1]
    me = me_ref[0]
    for chunk in range(count):
        rel = me ^ chunk_owner(chunk, ny)
        rows = pl.ds(pl.multiple_of(rel * size, size), size)
        here = slice(chunk * size, (chunk + 1) * size)
        q_s[here, :] = qkv_ref[rows, 0:width] * 0.125
        key = qkv_ref[rows, width : 2 * width]
        k_s[here, :] = key
        kt_s[:, here] = jnp.transpose(key.astype(F32)).astype(BF16)
        v_s[here, :] = qkv_ref[rows, 2 * width : 3 * width]
        g_s[here, :] = grad_ref[rows, :]
    dk_s[...] = jnp.zeros_like(dk_s)
    dv_s[...] = jnp.zeros_like(dv_s)
    lanes = lane_parts(heads, width)
    each = width // heads
    for block in range(count * size // BLOCK):
        first = block * BLOCK
        total = first + BLOCK
        allowed = allowed_pairs(start_ref, first, total)
        q_block, g_block = q_s[first:total, :], g_s[first:total, :]
        queries = []
        for h in range(heads):
            q_one, g_one = only(q_block, lanes[h]), only(g_block, lanes[h])
            scores = dot_nt(k_s[0:total, :], q_one)
            probs = jnp.where(allowed, jnp.exp(scores - log_ref[h : h + 1, first:total]), 0.0)
            prob_grad = dot_nt(v_s[0:total, :], g_one)
            delta = jnp.sum(probs * prob_grad, axis=0, keepdims=True)
            score_grad = (probs * (prob_grad - delta)).astype(BF16)
            dv_s[0:total, :] += dot_nn(probs.astype(BF16), g_one)
            dk_s[0:total, :] += dot_nn(score_grad, q_one)
            queries.append(dot_nn(kt_s[h * each : (h + 1) * each, 0:total], score_grad))
        query_grad = queries[0] if heads == 1 else jnp.concatenate(queries, axis=0)
        dq_s[first:total, :] = jnp.transpose(query_grad) * 0.125
    for chunk in range(count):
        rel = me ^ chunk_owner(chunk, ny)
        rows = pl.ds(pl.multiple_of(rel * size, size), size)
        here = slice(chunk * size, (chunk + 1) * size)
        out_ref[rows, 0:width] = dq_s[here, :].astype(BF16)
        out_ref[rows, width : 2 * width] = dk_s[here, :].astype(BF16)
        out_ref[rows, 2 * width : 3 * width] = dv_s[here, :].astype(BF16)


def whole(count):
    return [pl.BlockSpec(memory_space=pltpu.VMEM)] * count


def attention(qkv, starts, me, heads, ny, size):
    frames, wide = qkv.shape
    width = wide // 3
    pairs = frames * frames * heads
    return pl.pallas_call(
        functools.partial(attend, heads, ny, size),
        out_shape=(
            jax.ShapeDtypeStruct((4 * ny, size, width), BF16),
            jax.ShapeDtypeStruct((frames, width), BF16),
            jax.ShapeDtypeStruct((heads, frames), F32),
        ),
        in_specs=[pl.BlockSpec(memory_space=pltpu.SMEM)] + whole(2),
        out_specs=tuple(whole(3)),
        scratch_shapes=[
            pltpu.VMEM((frames, width), BF16),
            pltpu.VMEM((frames, width), BF16),
            pltpu.VMEM((width, frames), BF16),
        ],
        compiler_params=pltpu.CompilerParams(vmem_limit_bytes=40 << 20),
        cost_estimate=pl.CostEstimate(flops=pairs * 256, bytes_accessed=frames * wide * 4, transcendentals=pairs // 2),
        name="attend",
    )(me, qkv, starts)


def attention_back(qkv, grad, starts, log_total, me, heads, ny, size):
    frames, wide = qkv.shape
    width = wide // 3
    pairs = frames * frames * heads
    return pl.pallas_call(
        functools.partial(attend_back, heads, ny, size),
        out_shape=jax.ShapeDtypeStruct((frames, wide), BF16),
        in_specs=[pl.BlockSpec(memory_space=pltpu.SMEM)] + whole(4),
        out_specs=whole(1)[0],
        scratch_shapes=[pltpu.VMEM((frames, width), BF16)] * 4
        + [pltpu.VMEM((width, frames), BF16)]
        + [pltpu.VMEM((frames, width), F32)] * 3,
        compiler_params=pltpu.CompilerParams(vmem_limit_bytes=40 << 20),
        cost_estimate=pl.CostEstimate(flops=pairs * 640, bytes_accessed=frames * wide * 6, transcendentals=pairs // 2),
        name="attend_back",
    )(me, qkv, grad, starts, log_total)


class Place:
    def __init__(self):
        self.x, self.z, self.y, self.c = (lax.axis_index(a) for a in ("x", "z", "y", "c"))


def on_device(
    groups,
    ny,
    frames,
    cotangent,
    segment_lengths,
    position_offsets,
    first_gain,
    first_shift,
    inward_weight,
    query_bias,
    value_bias,
    outward_weight,
    outward_bias,
    second_gain,
    second_shift,
    expand_weight,
    expand_bias,
    shrink_weight,
    shrink_bias,
):
    place = Place()
    x, z, y, c = place.x, place.z, place.y, place.c
    local_len, rows, width = frames.shape
    share = inward_weight.shape[0]
    layer = 4 * ny
    full_len = local_len * NZ * ny * 2
    size = 2 * local_len
    hd = HEADS // layer
    head_dim = width // HEADS
    hw = hd * head_dim
    hidden = expand_bias.shape[0]
    part = hidden // 2
    me = (x * ny + y) * 2 + c

    def sum_groups(value):
        return lax.psum(value, "g") if groups > 1 else value

    fr = to_home(frames, place)
    ct = to_home(cotangent, place)

    table = jnp.stack([segment_lengths, position_offsets], axis=1)
    other = hop(table, "x")
    row_x = jnp.where((z == 0) | (z == 3), 1, 0)
    table = pick(jnp.where(x == row_x, table, other), z >> 1)
    lengths, offsets = table[0], table[1]
    count = lengths.shape[0]
    starts = jnp.sum(
        jnp.where(jnp.arange(count)[None, :] < jnp.arange(count)[:, None], lengths[None, :], 0), axis=1
    )
    frame_ids = jnp.arange(full_len, dtype=jnp.int32)
    row_starts = jnp.max(jnp.where(starts[:, None] <= frame_ids[None, :], starts[:, None], 0), axis=0)[None, :]
    chunk = (2 * x + c) * ny + y
    mine = chunk * size + jnp.arange(size, dtype=jnp.int32)
    inside = (mine[:, None] >= starts[None, :]) & (mine[:, None] < (starts + lengths)[None, :])
    position = jnp.sum(jnp.where(inside, offsets[None, :] + mine[:, None] - starts[None, :], 0), axis=1)

    small = [first_gain, first_shift, query_bias, value_bias, outward_bias, second_gain, second_shift, shrink_bias]
    packed = jnp.stack(small + [jnp.zeros_like(first_gain)] * (16 - len(small)))
    lines = over_z(packed)
    grid = jnp.stack(lines, axis=0)
    grid = jnp.stack([grid] + [hop(grid, "y", ny, k) for k in range(1, ny)], axis=1)
    grid = jnp.stack([grid, hop(grid, "c")], axis=2)
    ids = jnp.arange(NZ * ny * 2)
    mine_id = (z * ny + y) * 2 + c
    select = (ids[:, None] == (ids[None, :] ^ mine_id)).astype(BF16)
    vectors = dot_nn(select, grid.reshape(NZ * ny * 2, 16 * share)).reshape(NZ * ny * 2, 16, share)
    vectors = jnp.swapaxes(vectors, 0, 1).reshape(16, width)
    gain_one, shift_one, query_b, value_b, outward_b, gain_two, shift_two, shrink_b = (
        vectors[i][None, :] for i in range(8)
    )
    expand_line = over_z(jnp.where(x == 0, expand_bias[:part], expand_bias[part:]))
    expand_b = jnp.concatenate(expand_line).astype(F32)[None, :]

    def my_heads(value):
        return pick(pick(pick(value.reshape(2, hd, ny, 2, head_dim), x), y, 1), c, 1).reshape(1, hw)

    qkv_bias = jnp.concatenate([my_heads(query_b), jnp.zeros((1, hw), F32), my_heads(value_b)], axis=1)

    in_cols = pick(inward_weight.reshape(share, 3, 2, hd, ny, 2, head_dim), x, 2)
    in_cols = jnp.transpose(in_cols, (3, 4, 0, 1, 2, 5)).reshape(ny * 2, share, 3 * hw)
    ex_cols = pick(expand_weight.reshape(share, NZ, ny, 2, 2, part), x, 4)
    ex_cols = jnp.stack([pick(ex_cols, z ^ m, 1) for m in range(NZ)], axis=3)
    ex_cols = jnp.transpose(ex_cols, (1, 2, 0, 3, 4)).reshape(ny * 2, share, NZ * part)
    quarter = lax.all_to_all(jnp.concatenate([in_cols, ex_cols], axis=2), ("y", "c"), 0, 0, tiled=True)
    quarter = quarter.reshape(ny * 2 * share, 3 * hw + NZ * part)
    w_in = stack_rows(over_z(quarter[:, : 3 * hw]))
    outward = lax.all_gather(outward_weight, ("z", "y", "c"), axis=0, tiled=True)
    ex_parts = over_z(quarter[:, 3 * hw :])
    w_expand = stack_rows(
        [
            jnp.concatenate([got[:, (q ^ k) * part : ((q ^ k) + 1) * part] for k in range(NZ)], axis=1)
            for q, got in enumerate(ex_parts)
        ]
    )
    w_shrink = stack_rows(over_z(lax.dynamic_slice_in_dim(shrink_weight, x * part, part, 0)))
    w_out = outward.reshape(2, hd, ny, 2, head_dim, width)
    w_out = pick(pick(pick(w_out, x), y, 1), c, 1).reshape(hw, width)

    inputs = fr.astype(F32) + sin_cos(position, width)
    normal_one, scale_one = normalize(inputs)
    first = (normal_one * gain_one + shift_one).astype(BF16)
    first_all = to_layer(z_order(first, z), ny)
    qkv = (dot_nn(first_all, w_in) + qkv_bias).astype(BF16)
    me_ref = jnp.reshape(me, (1,)).astype(jnp.int32)
    context_to, context_all, log_total = attention(qkv, row_starts, me_ref, hd, ny, size)
    context = lax.all_to_all(context_to, LAYER, 0, 0, tiled=True)
    context = jnp.transpose(context.reshape(2, ny, 2, size, hd, head_dim), (3, 0, 4, 1, 2, 5)).reshape(size, width)
    middle = inputs + dot_nn(context, outward) + outward_b

    upstream_all = to_layer(ct, ny)
    normal_two, scale_two = normalize(middle)
    second = (normal_two * gain_two + shift_two).astype(BF16)
    second_all = to_layer(z_order(second, z), ny)
    before = dot_nn(second_all, w_expand) + expand_b
    active_grad = dot_nt(upstream_all, w_shrink)
    rate = math.sqrt(2.0 / math.pi)
    inner = jnp.tanh(rate * (before + 0.044715 * before * before * before))
    active = (0.5 * before * (1.0 + inner)).astype(BF16)
    slope = 0.5 * (1.0 + inner) + 0.5 * before * (1.0 - inner * inner) * rate * (1.0 + 3 * 0.044715 * before * before)
    before_grad = (active_grad * slope).astype(BF16)
    second_grad = z_order(from_layer(dot_nt(before_grad, w_expand).astype(BF16), ny), z)
    out_part = from_layer(dot_nn(active, w_shrink).astype(BF16), ny)
    layer_output = to_origin((middle + out_part + shrink_b).astype(BF16), place)
    shrink_part = dot_tn(active, upstream_all).astype(BF16)
    expand_part = dot_tn(second_all, before_grad).astype(BF16)
    expand_b_sum = jnp.sum(before_grad.astype(F32), axis=0)

    upstream = ct.astype(F32)
    middle_part, gain_two_sum, shift_two_sum = normalize_back(normal_two, scale_two, gain_two, second_grad)
    middle_grad = upstream + middle_part
    low_middle = middle_grad.astype(BF16)
    low_all = to_layer(low_middle, ny)
    context_grad = dot_nt(low_all, w_out).astype(BF16)
    outward_part = dot_tn(context_all, low_all)
    mixed_grad = attention_back(qkv, context_grad, row_starts, log_total, me_ref, hd, ny, size)
    first_grad = z_order(from_layer(dot_nt(mixed_grad, w_in).astype(BF16), ny), z)
    inward_part = dot_tn(first_all, mixed_grad).astype(BF16)
    input_part, gain_one_sum, shift_one_sum = normalize_back(normal_one, scale_one, gain_one, first_grad)
    frames_grad = to_origin((middle_grad + input_part).astype(BF16), place).astype(F32)

    shrink_sum = sum_groups(sum_over_z([shrink_part[k * part : (k + 1) * part] for k in range(NZ)])).astype(BF16)
    g_shrink = by_half(x, shrink_sum, hop(shrink_sum, "x"), 0).astype(F32)
    rows_z = ny * 2 * share
    expand_sum = sum_over_z(
        [
            jnp.concatenate(
                [expand_part[q * rows_z : (q + 1) * rows_z, (q ^ m) * part : ((q ^ m) + 1) * part] for m in range(NZ)],
                axis=1,
            )
            for q in range(NZ)
        ]
    )
    inward_sum = sum_over_z([inward_part[q * rows_z : (q + 1) * rows_z] for q in range(NZ)])
    both = sum_groups(jnp.concatenate([inward_sum, expand_sum], axis=1)).astype(BF16)
    both = lax.all_to_all(both.reshape(ny * 2, share, -1), ("y", "c"), 0, 0, tiled=True)
    both_x = hop(both, "x")
    in_pair = [v[:, :, : 3 * hw].reshape(ny, 2, share, 3, hd, head_dim) for v in (both, both_x)]
    g_inward = by_half(x, in_pair[0][None], in_pair[1][None], 0)
    g_inward = jnp.transpose(g_inward, (3, 4, 0, 5, 1, 2, 6)).reshape(share, 3 * width).astype(F32)
    ex_pair = [v[:, :, 3 * hw :].reshape(ny, 2, share, NZ, part) for v in (both, both_x)]
    g_expand = by_half(x, ex_pair[0][None], ex_pair[1][None], 0)
    g_expand = jnp.stack([pick(g_expand, z ^ m, 4) for m in range(NZ)], axis=0)
    g_expand = jnp.transpose(g_expand, (4, 0, 2, 3, 1, 5)).reshape(share, -1).astype(F32)

    if share == head_dim and hd == 2:
        half = width // 2
        split = outward_part.astype(BF16).reshape(2, share, 2, half)
        keep, send = pick(split, x, 2), pick(split, 1 - x, 2)
        line = by_half(x, keep, hop(send, "x"), 0)
        out_sum = sum_groups(sum_over_z([pick(line, z ^ k) for k in range(NZ)])).astype(BF16)
        g_outward = by_half(x, out_sum, hop(out_sum, "x"), 1).astype(F32)
    else:
        spot = jnp.zeros((2, ny, 2, hd, head_dim, width), F32)
        spot = lax.dynamic_update_slice(spot, outward_part.reshape(1, 1, 1, hd, head_dim, width), (x, y, c, 0, 0, 0))
        spot = jnp.transpose(spot, (0, 3, 1, 2, 4, 5)).reshape(width, width).astype(BF16)
        g_outward = lax.psum_scatter(spot, ("z", "y", "c"), scatter_dimension=0, tiled=True)
        g_outward = lax.psum(g_outward.astype(F32), ("g", "x"))

    mixed_sum = jnp.sum(mixed_grad.astype(F32), axis=0)

    def from_heads(value):
        spot = jnp.zeros((2, hd, ny, 2, head_dim), F32)
        return lax.dynamic_update_slice(spot, value.reshape(1, hd, 1, 1, head_dim), (x, 0, y, c, 0)).reshape(width)

    flat = [
        gain_one_sum,
        shift_one_sum,
        from_heads(mixed_sum[:hw]),
        from_heads(mixed_sum[2 * hw :]),
        jnp.sum(low_middle.astype(F32), axis=0),
        gain_two_sum,
        shift_two_sum,
        jnp.sum(upstream, axis=0),
    ]
    line = jnp.stack([pick(expand_b_sum.reshape(NZ, part), z ^ m) for m in range(NZ)])
    spot = jnp.zeros((NZ, ny, 2, 2, part), F32)
    spot = lax.dynamic_update_slice(spot, line.reshape(NZ, 1, 1, 1, part), (0, y, c, x, 0))
    sums = jnp.stack(flat).reshape(8, NZ, ny, 2, share)
    sums = jnp.transpose(sums, (1, 2, 3, 0, 4)).reshape(NZ, ny, 2, 8 * share)
    sums = jnp.concatenate([sums, spot.reshape(NZ, ny, 2, hidden)], axis=3)
    sums = pick(sums, c, 2) + hop(pick(sums, 1 - c, 2), "c")
    over = pick(sums, y, 1)
    for k in range(1, ny):
        over = over + hop(pick(sums, y ^ k, 1), "y", ny, k)
    over = over + hop(over, "x")
    total = pick(over, z)
    for k in range(1, NZ):
        total = total + hop(pick(over, z ^ k), "z", NZ, k)
    total = sum_groups(total)
    g_small = total[: 8 * share].reshape(8, share)
    g_expand_b = total[8 * share :]
    return (
        layer_output,
        frames_grad,
        g_small[0],
        g_small[1],
        g_inward,
        g_small[2],
        g_small[3],
        g_outward,
        g_small[4],
        g_small[5],
        g_small[6],
        g_expand,
        g_expand_b,
        g_shrink,
        g_small[7],
    )


def solution(mesh):
    batch, seq = mesh.shape["batch"], mesh.shape["seq"]
    groups, ny = batch // 2, seq // (2 * NZ)
    fine = Mesh(mesh.devices.reshape(groups, 2, NZ, ny, 2), ("g", "x", "z", "y", "c"))
    b, s = ("g", "x"), ("z", "y", "c")
    in_specs = (
        P(s, b, None),
        P(s, b, None),
        P(b, None),
        P(b, None),
        P(s),
        P(s),
        P(s, None),
        P(s),
        P(s),
        P(s, None),
        P(s),
        P(s),
        P(s),
        P(s, None),
        P(s),
        P(s, None),
        P(s),
    )
    out_specs = (
        P(s, b, None),
        P(s, b, None),
        P(s),
        P(s),
        P(s, None),
        P(s),
        P(s),
        P(s, None),
        P(s),
        P(s),
        P(s),
        P(s, None),
        P(s),
        P(s, None),
        P(s),
    )
    return jax.shard_map(
        functools.partial(on_device, groups, ny), mesh=fine, in_specs=in_specs, out_specs=out_specs, check_vma=False
    )
```

```python
import functools
import math

import jax
import jax.numpy as jnp
from jax import lax
from jax.experimental import pallas as pl
from jax.experimental.pallas import tpu as pltpu
from jax.sharding import Mesh, PartitionSpec as P


HEADS = 16
NZ = 4
NORM_EPS = 1e-05
NEG = -1e30
F32 = jnp.float32
BF16 = jnp.bfloat16
LAYER_OF_ROW = (1, 2, 0, 3)
SWAP = [(0, 1), (1, 0)]
LAYER = ("c", "x", "y")
SEQ = ("z", "y", "c")


def xor_perm(count, k):
    return [(i, i ^ k) for i in range(count)]


def hop(value, axis, count=2, k=1):
    return lax.ppermute(value, axis, xor_perm(count, k))


def pick(value, index, axis=0):
    return lax.dynamic_index_in_dim(value, index, axis, keepdims=False)


def stack_rows(parts):
    return jnp.concatenate(parts, axis=0)


def assemble_body(pieces, size, place_ref, *refs):
    out_ref = refs[pieces]
    for r in range(pieces):
        spot = place_ref[0] ^ r
        out_ref[pl.ds(pl.multiple_of(spot * size, size), size), :] = refs[r][...]


def assemble(parts, me):
    size, width = parts[0].shape
    count = len(parts)
    return pl.pallas_call(
        functools.partial(assemble_body, count, size),
        out_shape=jax.ShapeDtypeStruct((count * size, width), parts[0].dtype),
        in_specs=[pl.BlockSpec(memory_space=pltpu.SMEM)] + whole(count),
        out_specs=whole(1)[0],
        compiler_params=pltpu.CompilerParams(vmem_limit_bytes=24 << 20),
        cost_estimate=pl.CostEstimate(flops=0, bytes_accessed=4 * count * size * width, transcendentals=0),
        name="assemble",
    )(me, *parts)


def to_layer(block, place, ny):
    count = 2 * ny
    parts = [block] + [lax.ppermute(block, ("x", "y"), xor_perm(count, r)) for r in range(1, count)]
    mine = assemble(parts, place.xy)
    return assemble([mine, hop(mine, "c")], place.core)


def fold_body(count, size, place_ref, keep_ref, got_ref, own_ref, *out_refs):
    for r in range(count):
        spot = place_ref[0] ^ r
        here = pl.ds(pl.multiple_of(spot * size, size), size)
        value = keep_ref[here, :].astype(F32) + got_ref[here, :].astype(F32)
        if r == 0:
            own_ref[...] = value
        else:
            out_refs[r - 1][...] = value.astype(BF16)


def from_layer(send, keep, place, ny):
    rows, width = keep.shape
    count = 2 * ny
    size = rows // count
    own, *away = pl.pallas_call(
        functools.partial(fold_body, count, size),
        out_shape=[jax.ShapeDtypeStruct((size, width), F32)] + [jax.ShapeDtypeStruct((size, width), BF16)] * (count - 1),
        in_specs=[pl.BlockSpec(memory_space=pltpu.SMEM)] + whole(2),
        out_specs=whole(count),
        compiler_params=pltpu.CompilerParams(vmem_limit_bytes=24 << 20),
        cost_estimate=pl.CostEstimate(flops=count * size * width, bytes_accessed=6 * count * size * width, transcendentals=0),
        name="fold",
    )(place.xy, keep, hop(send, "c"))
    for r in range(1, count):
        own = own + lax.ppermute(away[r - 1], ("x", "y"), xor_perm(count, r)).astype(F32)
    return own


def disperse_body(count, size, place_ref, value_ref, *out_refs):
    for r in range(count):
        out_refs[r][...] = value_ref[pl.ds(pl.multiple_of((place_ref[0] ^ r) * size, size), size), :]


def sum_over_z(value, place):
    size, width = value.shape[0] // NZ, value.shape[1]
    parts = pl.pallas_call(
        functools.partial(disperse_body, NZ, size),
        out_shape=[jax.ShapeDtypeStruct((size, width), BF16)] * NZ,
        in_specs=[pl.BlockSpec(memory_space=pltpu.SMEM)] + whole(1),
        out_specs=whole(NZ),
        compiler_params=pltpu.CompilerParams(vmem_limit_bytes=24 << 20),
        cost_estimate=pl.CostEstimate(flops=0, bytes_accessed=4 * NZ * size * width, transcendentals=0),
        name="disperse",
    )(place.layer, value)
    return [parts[0]] + [hop(parts[k], "z", NZ, k) for k in range(1, NZ)]


def total_of(parts):
    total = parts[0].astype(F32)
    for value in parts[1:]:
        total = total + value.astype(F32)
    return total


def rehome_flat(x, z, c):
    return (x * NZ + z) * 2 + c


def rehome_perm(k):
    return [
        (rehome_flat(x, z, c), rehome_flat(z >> 1, LAYER_OF_ROW[2 * x + (c ^ k)], z & 1))
        for x in range(2)
        for z in range(NZ)
        for c in range(2)
    ]


def to_home(block, place):
    got = [
        lax.ppermute(jnp.where(place.c == k, block[:, 0], block[:, 1]), ("x", "z", "c"), rehome_perm(k))
        for k in range(2)
    ]
    first = place.z < 2
    return stack_rows([jnp.where(first, got[0], got[1]), jnp.where(first, got[1], got[0])])


def to_origin(block, place):
    half = block.shape[0] // 2
    first = place.z < 2
    low, high = block[:half], block[half:]
    sent = [jnp.where(first, low, high), jnp.where(first, high, low)]
    got = [
        lax.ppermute(sent[k], ("x", "z", "c"), [(b, a) for a, b in rehome_perm(k)]) for k in range(2)
    ]
    return jnp.stack(
        [jnp.where(place.c == 0, got[0], got[1]), jnp.where(place.c == 0, got[1], got[0])], axis=1
    )


def after(first, *values):
    return lax.optimization_barrier((first, *values))


def sum_sources(value, count):
    return jnp.sum(value.reshape((count, -1) + value.shape[1:]).astype(F32), axis=0)


def by_half(x, mine, other, axis):
    return jnp.concatenate([jnp.where(x == 0, mine, other), jnp.where(x == 0, other, mine)], axis=axis)


def sin_cos(position, width):
    feature = jnp.arange(width, dtype=jnp.int32)
    rates = jnp.exp((feature // 2).astype(F32) * (-2.0 * math.log(10000.0) / width))
    angle = position.astype(F32)[:, None] * rates[None, :]
    turn = jnp.round(angle * (2.0 / math.pi))
    rest = angle - turn * 1.5703125
    rest = rest - turn * 0.00048375129699707031
    rest = rest - turn * 7.5497899548918861e-08
    quadrant = turn.astype(jnp.int32) + (feature % 2)[None, :]
    square = rest * rest
    sine = rest + rest * square * (
        -0.16666666641626524 + square * (0.008333329385889463 + square * (-0.00019839334836096632 + square * 2.718311493989822e-06))
    )
    cosine = 1.0 + square * (
        -0.49999999725103100 + square * (0.04166662332373906 + square * (-0.001388676377460993 + square * 2.439044879627741e-05))
    )
    value = jnp.where((quadrant & 1) == 0, sine, cosine)
    return jnp.where((quadrant & 2) == 0, value, -value)


def normalize(values):
    center = values - jnp.mean(values, axis=-1, keepdims=True)
    scale = lax.rsqrt(jnp.mean(center * center, axis=-1, keepdims=True) + NORM_EPS)
    return center * scale, scale


def normalize_back(normal, scale, gain, upstream):
    scaled = upstream * gain
    inner = scaled - jnp.mean(scaled, axis=-1, keepdims=True)
    inner = inner - normal * jnp.mean(scaled * normal, axis=-1, keepdims=True)
    return inner * scale, jnp.sum(upstream * normal, axis=0), jnp.sum(upstream, axis=0)


def dot_nt(a, b):
    return lax.dot_general(a, b, (((1,), (1,)), ((), ())), preferred_element_type=F32)


def dot_tn(a, b):
    return lax.dot_general(a, b, (((0,), (0,)), ((), ())), preferred_element_type=F32)


def dot_nn(a, b):
    return jnp.dot(a, b, preferred_element_type=F32)


BLOCK = 256


def chunk_owner(chunk, ny):
    outer, y = divmod(chunk, ny)
    return ((outer & 1) * 2 + (outer >> 1)) * ny + y


def lane_parts(heads, width):
    if heads == 1:
        return [None]
    lane = lax.broadcasted_iota(jnp.int32, (1, width), 1)
    return [(lane >= h * (width // heads)) & (lane < (h + 1) * (width // heads)) for h in range(heads)]


def only(value, lanes):
    return value if lanes is None else jnp.where(lanes, value, jnp.zeros_like(value))


def allowed_pairs(start_ref, first, total):
    key = lax.broadcasted_iota(jnp.int32, (total, BLOCK), 0)
    frame = first + lax.broadcasted_iota(jnp.int32, (total, BLOCK), 1)
    return (key >= start_ref[:, first : first + BLOCK]) & (key <= frame)


def attend(heads, ny, size, first_ref, weight_ref, bias_ref, start_ref, qkv_ref, out_ref, log_ref, q_s, k_s, vt_s):
    count = 4 * ny
    width = q_s.shape[1]
    step = 2 * size
    for owner in range(0, count, 2):
        rows = slice(owner * size, owner * size + step)
        mixed = dot_nn(first_ref[rows, :], weight_ref[...]) + bias_ref[...]
        qkv_ref[rows, :] = mixed.astype(BF16)
    for chunk in range(count):
        owner = chunk_owner(chunk, ny)
        rows = slice(owner * size, (owner + 1) * size)
        here = slice(chunk * size, (chunk + 1) * size)
        q_s[here, :] = qkv_ref[rows, 0:width] * 0.125
        k_s[here, :] = qkv_ref[rows, width : 2 * width]
        vt_s[:, here] = jnp.transpose(qkv_ref[rows, 2 * width : 3 * width].astype(F32)).astype(BF16)
    lanes = lane_parts(heads, width)
    each = width // heads
    for block in range(count * size // BLOCK):
        first = block * BLOCK
        total = first + BLOCK
        allowed = allowed_pairs(start_ref, first, total)
        q_block = q_s[first:total, :]
        contexts = []
        for h in range(heads):
            scores = dot_nt(k_s[0:total, :], only(q_block, lanes[h]))
            scores = jnp.where(allowed, scores, NEG)
            top = jnp.max(scores, axis=0, keepdims=True)
            weight = jnp.exp(scores - top)
            mass = jnp.sum(weight, axis=0, keepdims=True)
            part = dot_nn(vt_s[h * each : (h + 1) * each, 0:total], weight.astype(BF16))
            contexts.append(part / mass)
            log_ref[h : h + 1, first:total] = top + jnp.log(mass)
        context = contexts[0] if heads == 1 else jnp.concatenate(contexts, axis=0)
        context = jnp.transpose(context).astype(BF16)
        for sub in range(BLOCK // size):
            owner = chunk_owner(block * (BLOCK // size) + sub, ny)
            out_ref[owner * size : (owner + 1) * size, :] = context[sub * size : (sub + 1) * size]


def attend_back(
    heads,
    ny,
    size,
    core_ref,
    qkv_ref,
    low_ref,
    outward_ref,
    weight_ref,
    start_ref,
    log_ref,
    out_ref,
    send_ref,
    keep_ref,
    q_s,
    k_s,
    v_s,
    g_s,
    kt_s,
    dq_s,
    dk_s,
    dv_s,
):
    count = 4 * ny
    width = q_s.shape[1]
    for chunk in range(count):
        owner = chunk_owner(chunk, ny)
        rows = slice(owner * size, (owner + 1) * size)
        here = slice(chunk * size, (chunk + 1) * size)
        q_s[here, :] = qkv_ref[rows, 0:width] * 0.125
        key = qkv_ref[rows, width : 2 * width]
        k_s[here, :] = key
        kt_s[:, here] = jnp.transpose(key.astype(F32)).astype(BF16)
        v_s[here, :] = qkv_ref[rows, 2 * width : 3 * width]
        g_s[here, :] = dot_nt(low_ref[rows, :], outward_ref[...]).astype(BF16)
    dk_s[...] = jnp.zeros_like(dk_s)
    dv_s[...] = jnp.zeros_like(dv_s)
    lanes = lane_parts(heads, width)
    each = width // heads
    for block in range(count * size // BLOCK):
        first = block * BLOCK
        total = first + BLOCK
        allowed = allowed_pairs(start_ref, first, total)
        q_block, g_block = q_s[first:total, :], g_s[first:total, :]
        queries = []
        for h in range(heads):
            q_one, g_one = only(q_block, lanes[h]), only(g_block, lanes[h])
            scores = dot_nt(k_s[0:total, :], q_one)
            probs = jnp.where(allowed, jnp.exp(scores - log_ref[h : h + 1, first:total]), 0.0)
            prob_grad = dot_nt(v_s[0:total, :], g_one)
            delta = jnp.sum(probs * prob_grad, axis=0, keepdims=True)
            score_grad = (probs * (prob_grad - delta)).astype(BF16)
            dv_s[0:total, :] += dot_nn(probs.astype(BF16), g_one)
            dk_s[0:total, :] += dot_nn(score_grad, q_one)
            queries.append(dot_nn(kt_s[h * each : (h + 1) * each, 0:total], score_grad))
        query_grad = queries[0] if heads == 1 else jnp.concatenate(queries, axis=0)
        dq_s[first:total, :] = jnp.transpose(query_grad) * 0.125
    for chunk in range(count):
        owner = chunk_owner(chunk, ny)
        rows = slice(owner * size, (owner + 1) * size)
        here = slice(chunk * size, (chunk + 1) * size)
        out_ref[rows, 0:width] = dq_s[here, :].astype(BF16)
        out_ref[rows, width : 2 * width] = dk_s[here, :].astype(BF16)
        out_ref[rows, 2 * width : 3 * width] = dv_s[here, :].astype(BF16)
    half = count // 2 * size
    for ref, core in ((send_ref, 1 - core_ref[0]), (keep_ref, core_ref[0])):
        for start in range(0, half, 2 * size):
            rows = pl.ds(pl.multiple_of(core * half + start, 2 * size), 2 * size)
            ref[start : start + 2 * size, :] = dot_nt(out_ref[rows, :], weight_ref[...]).astype(BF16)


def feed_forward(
    size, core_ref, second_ref, up_ref, expand_ref, shrink_ref, bias_ref, active_ref, grad_ref, send_ref, keep_ref
):
    half = keep_ref.shape[0]
    step = 2 * size
    rate = math.sqrt(2.0 / math.pi)
    for ref, core in ((send_ref, 1 - core_ref[0]), (keep_ref, core_ref[0])):
        for start in range(0, half, step):
            rows = pl.ds(pl.multiple_of(core * half + start, step), step)
            before = dot_nn(second_ref[rows, :], expand_ref[...]) + bias_ref[...]
            upper = dot_nt(up_ref[rows, :], shrink_ref[...])
            square = before * before
            inner = jnp.tanh(rate * (before + 0.044715 * before * square))
            plus = 0.5 * (1.0 + inner)
            active_ref[rows, :] = (before * plus).astype(BF16)
            slope = plus + 0.5 * before * (1.0 - inner * inner) * (rate + rate * 3 * 0.044715 * square)
            lower = (upper * slope).astype(BF16)
            grad_ref[rows, :] = lower
            ref[start : start + step, :] = dot_nt(lower, expand_ref[...]).astype(BF16)


def whole(count):
    return [pl.BlockSpec(memory_space=pltpu.VMEM)] * count


def attention(first_all, w_in, bias, starts, heads, ny, size):
    frames, wide = first_all.shape[0], w_in.shape[1]
    width = wide // 3
    pairs = frames * frames * heads
    return pl.pallas_call(
        functools.partial(attend, heads, ny, size),
        out_shape=(
            jax.ShapeDtypeStruct((frames, wide), BF16),
            jax.ShapeDtypeStruct((frames, width), BF16),
            jax.ShapeDtypeStruct((heads, frames), F32),
        ),
        in_specs=whole(4),
        out_specs=tuple(whole(3)),
        scratch_shapes=[
            pltpu.VMEM((frames, width), BF16),
            pltpu.VMEM((frames, width), BF16),
            pltpu.VMEM((width, frames), BF16),
        ],
        compiler_params=pltpu.CompilerParams(vmem_limit_bytes=32 << 20),
        cost_estimate=pl.CostEstimate(
            flops=pairs * 256 + 2 * first_all.size * wide, bytes_accessed=4 * first_all.size, transcendentals=pairs // 2
        ),
        name="attend",
    )(first_all, w_in, bias, starts)


def attention_back(core, qkv, low_all, w_out, w_in, starts, log_total, heads, ny, size):
    frames, wide = qkv.shape
    width = wide // 3
    pairs = frames * frames * heads
    half = jax.ShapeDtypeStruct((frames // 2, low_all.shape[1]), BF16)
    return pl.pallas_call(
        functools.partial(attend_back, heads, ny, size),
        out_shape=(jax.ShapeDtypeStruct((frames, wide), BF16), half, half),
        in_specs=[pl.BlockSpec(memory_space=pltpu.SMEM)] + whole(6),
        out_specs=tuple(whole(3)),
        scratch_shapes=[pltpu.VMEM((frames, width), BF16)] * 4
        + [pltpu.VMEM((width, frames), BF16)]
        + [pltpu.VMEM((frames, width), F32)] * 3,
        compiler_params=pltpu.CompilerParams(vmem_limit_bytes=32 << 20),
        cost_estimate=pl.CostEstimate(
            flops=pairs * 640 + 2 * low_all.size * (wide + width), bytes_accessed=6 * low_all.size, transcendentals=pairs // 2
        ),
        name="attend_back",
    )(core, qkv, low_all, w_out, w_in, starts, log_total)


def feed_forward_front(core, second_all, upstream_all, w_expand, w_shrink, bias, size):
    frames, width = second_all.shape
    units = w_expand.shape[1]
    half = jax.ShapeDtypeStruct((frames // 2, width), BF16)
    inner = jax.ShapeDtypeStruct((frames, units), BF16)
    return pl.pallas_call(
        functools.partial(feed_forward, size),
        out_shape=(inner, inner, half, half),
        in_specs=[pl.BlockSpec(memory_space=pltpu.SMEM)] + whole(5),
        out_specs=tuple(whole(4)),
        compiler_params=pltpu.CompilerParams(vmem_limit_bytes=32 << 20),
        cost_estimate=pl.CostEstimate(
            flops=6 * frames * width * units, bytes_accessed=8 * frames * width, transcendentals=frames * units
        ),
        name="feed_forward",
    )(core, second_all, upstream_all, w_expand, w_shrink, bias)


class Place:
    def __init__(self, ny):
        self.x, self.z, self.y, self.c = (lax.axis_index(a) for a in ("x", "z", "y", "c"))
        self.xy = jnp.reshape(self.x * ny + self.y, (1,)).astype(jnp.int32)
        self.core = jnp.reshape(self.c, (1,)).astype(jnp.int32)
        self.layer = jnp.reshape(self.z, (1,)).astype(jnp.int32)


def on_device(
    groups,
    ny,
    frames,
    cotangent,
    segment_lengths,
    position_offsets,
    first_gain,
    first_shift,
    inward_weight,
    query_bias,
    value_bias,
    outward_weight,
    outward_bias,
    second_gain,
    second_shift,
    expand_weight,
    expand_bias,
    shrink_weight,
    shrink_bias,
):
    place = Place(ny)
    x, z, y, c = place.x, place.z, place.y, place.c
    local_len, rows, width = frames.shape
    share = inward_weight.shape[0]
    layer = 4 * ny
    spread = NZ * ny * 2
    full_len = local_len * spread
    size = 2 * local_len
    hd = HEADS // layer
    hw = hd * (width // HEADS)
    hidden = expand_bias.shape[0]
    part = hidden // 2
    me = (c * 2 + x) * ny + y

    def sum_groups(value):
        return lax.psum(value, "g") if groups > 1 else value

    def exchange(value, axes):
        return lax.all_to_all(value, axes, 0, 0, tiled=True)

    fr = to_home(frames, place)

    small = [first_gain, first_shift, query_bias, value_bias, outward_bias, second_gain, second_shift, shrink_bias]
    table = jnp.stack([segment_lengths, position_offsets], axis=1)
    table = jnp.stack([table >> 6, table & 63]).astype(BF16).reshape(1, -1)
    table = jnp.pad(table, ((0, 0), (0, share - table.shape[1])))
    bias_rows = expand_bias.reshape(-1, share)
    packed = jnp.concatenate([v[None] for v in small] + [bias_rows, table], axis=0)
    packed = jnp.pad(packed, ((0, -packed.shape[0] % 16), (0, 0)))
    kinds = packed.shape[0]
    other_table = hop(packed, "x")
    grid = jnp.stack([packed] + [hop(packed, "z", NZ, k) for k in range(1, NZ)])
    grid = jnp.stack([grid] + [hop(grid, "y", ny, k) for k in range(1, ny)], axis=1)
    grid = jnp.stack([grid, hop(grid, "c")], axis=2).reshape(spread, kinds, share)

    in_cols = jnp.transpose(inward_weight.reshape(share, 3, 2, 2, ny, hw), (3, 4, 2, 0, 1, 5))
    in_cols = pick(in_cols, x).reshape(1, ny * 2, share, 3 * hw)
    in_cols = jnp.broadcast_to(in_cols, (NZ, ny * 2, share, 3 * hw)).reshape(spread, share, 3 * hw)
    w_in = exchange(in_cols, SEQ).reshape(width, 3 * hw)
    outward = lax.all_gather(outward_weight, SEQ, axis=0, tiled=True)

    ids = jnp.arange(spread)
    select = (ids[:, None] == (ids[None, :] ^ ((z * ny + y) * 2 + c))).astype(BF16)
    vectors = lax.dot_general(grid, select, (((0,), (1,)), ((), ())), preferred_element_type=F32)
    vectors = jnp.swapaxes(vectors, 1, 2)
    expand_b = jnp.swapaxes(vectors[len(small) : len(small) + 4], 0, 1).reshape(NZ, ny, 2, 2, part)
    vectors = vectors[: len(small)].reshape(len(small), width)
    gain_one, shift_one, query_b, value_b, outward_b, gain_two, shift_two, shrink_b = (
        vectors[i : i + 1] for i in range(len(small))
    )
    expand_b = pick(pick(pick(expand_b, y, 1), c, 1), x, 1).reshape(1, NZ * part)
    qkv_bias = jnp.concatenate(
        [
            lax.dynamic_slice_in_dim(query_b, me * hw, hw, 1),
            jnp.zeros((1, hw), F32),
            lax.dynamic_slice_in_dim(value_b, me * hw, hw, 1),
        ],
        axis=1,
    )

    row_x = jnp.where((z == 0) | (z == 3), 1, 0)
    spot = len(small) + bias_rows.shape[0]
    table = jnp.where(x == row_x, packed[spot], other_table[spot]).astype(jnp.int32)
    table = table[: 4 * segment_lengths.size].reshape(2, rows, 2, -1)
    table = pick(table[0] * 64 + table[1], z >> 1)
    lengths, offsets = table[0], table[1]
    count = lengths.shape[0]
    starts = jnp.sum(
        jnp.where(jnp.arange(count)[None, :] < jnp.arange(count)[:, None], lengths[None, :], 0), axis=1
    )
    frame_ids = jnp.arange(full_len, dtype=jnp.int32)
    row_starts = jnp.max(jnp.where(starts[:, None] <= frame_ids[None, :], starts[:, None], 0), axis=0)[None, :]
    chunk = (2 * x + c) * ny + y
    mine = chunk * size + jnp.arange(size, dtype=jnp.int32)
    inside = (mine[:, None] >= starts[None, :]) & (mine[:, None] < (starts + lengths)[None, :])
    position = jnp.sum(jnp.where(inside, offsets[None, :] + mine[:, None] - starts[None, :], 0), axis=1)

    inputs = fr.astype(F32) + sin_cos(position, width)
    normal_one, scale_one = normalize(inputs)
    first = (normal_one * gain_one + shift_one).astype(BF16)
    _, later_cotangent = after(fr, cotangent)
    first_all = to_layer(first, place, ny)
    w_in, later_shrink = after(w_in, shrink_weight)
    sh_rows = lax.dynamic_slice_in_dim(later_shrink, x * part, part, 0)
    sh_rows = [sh_rows] + [hop(sh_rows, "z", NZ, k) for k in range(1, NZ)]
    qkv, context_all, log_total = attention(first_all, w_in, qkv_bias, row_starts, hd, ny, size)
    context = exchange(context_all.reshape(layer, size, hw), LAYER)

    context, later_expand, *sh_rows = after(context, expand_weight, *sh_rows)
    ct = to_home(later_cotangent, place)
    upstream_all = lax.all_gather(ct, LAYER, axis=0, tiled=True)
    ex_cols = pick(later_expand.reshape(share, NZ, ny, 2, 2, part), x, 4)
    ex_cols = jnp.transpose(ex_cols, (2, 3, 0, 1, 4)).reshape(1, ny * 2, share, NZ * part)
    ex_cols = jnp.broadcast_to(ex_cols, (NZ, ny * 2, share, NZ * part)).reshape(spread, share, NZ * part)
    w_expand = exchange(ex_cols, SEQ).reshape(width, NZ * part)
    w_shrink = assemble(sh_rows, place.layer)

    context = jnp.swapaxes(context, 0, 1).reshape(size, width)
    middle = inputs + dot_nn(context, outward) + outward_b

    normal_two, scale_two = normalize(middle)
    second = (normal_two * gain_two + shift_two).astype(BF16)
    second_all = to_layer(second, place, ny)
    active, before_grad, send, keep = feed_forward_front(
        place.core, second_all, upstream_all, w_expand, w_shrink, expand_b, size
    )
    second_grad = from_layer(send, keep, place, ny)
    out_part = dot_nn(active, w_shrink).astype(BF16)
    out_part = lax.psum_scatter(out_part, LAYER, scatter_dimension=0, tiled=True)
    shrink_got = sum_over_z(dot_tn(active, upstream_all).astype(BF16), place)
    expand_part = dot_tn(second_all, before_grad).astype(BF16)
    expand_got = exchange(expand_part.reshape(spread, share, NZ * part), SEQ)
    expand_b_sum = jnp.sum(before_grad.astype(F32), axis=0)

    upstream = ct.astype(F32)
    middle_part, gain_two_sum, shift_two_sum = normalize_back(normal_two, scale_two, gain_two, second_grad)
    middle_grad = upstream + middle_part
    low_middle = middle_grad.astype(BF16)
    low_all = to_layer(low_middle, place, ny)
    low_all, expand_got, *shrink_got = after(low_all, expand_got, *shrink_got)
    w_out = lax.dynamic_slice_in_dim(outward, me * hw, hw, 0)
    mixed_grad, send, keep = attention_back(
        place.core, qkv, low_all, w_out, w_in, row_starts, log_total, hd, ny, size
    )
    first_grad = from_layer(send, keep, place, ny)
    inward_part = dot_tn(first_all, mixed_grad).astype(BF16)
    inward_got = exchange(inward_part.reshape(spread, share, 3 * hw), SEQ)
    input_part, gain_one_sum, shift_one_sum = normalize_back(normal_one, scale_one, gain_one, first_grad)
    frames_grad = to_origin((middle_grad + input_part).astype(BF16), place).astype(F32)
    layer_output = to_origin((middle + out_part.astype(F32) + shrink_b).astype(BF16), place)

    shrink_sum = sum_groups(total_of(shrink_got)).astype(BF16)
    g_shrink = by_half(x, shrink_sum, hop(shrink_sum, "x"), 0).astype(F32)

    expand_sum = sum_groups(sum_sources(expand_got, NZ)).astype(BF16)
    g_expand = [v.reshape(ny, 2, 1, share, NZ, part) for v in (expand_sum, hop(expand_sum, "x"))]
    g_expand = jnp.transpose(by_half(x, *g_expand, 2), (3, 4, 0, 1, 2, 5)).reshape(share, -1).astype(F32)

    inward_sum = sum_groups(sum_sources(inward_got, NZ)).astype(BF16)
    g_inward = [v.reshape(ny, 2, 1, share, 3, hw) for v in (inward_sum, hop(inward_sum, "x"))]
    g_inward = jnp.transpose(by_half(x, *g_inward, 2), (3, 4, 1, 2, 0, 5)).reshape(share, -1).astype(F32)

    outward_part = dot_tn(context_all, low_all).astype(BF16)
    if hd == 2 and ny == 2:
        half = width // 2
        split = outward_part.reshape(2, share, width)
        pair = by_half(c, pick(split, c)[None], hop(pick(split, 1 - c), "c")[None], 0)
        pair = pair.reshape(2, 1, share, 2, half)
        pair = by_half(x, pick(pair, x, 3), hop(pick(pair, 1 - x, 3), "x"), 1)
        out_sum = sum_sources(exchange(pair.reshape(NZ, share, half), ("z",)), NZ).reshape(share, half)
        out_sum = sum_groups(out_sum).astype(BF16)
        g_outward = by_half(x, out_sum, hop(out_sum, "x"), 1).astype(F32)
    else:
        spot = lax.dynamic_update_slice(jnp.zeros((width, width), BF16), outward_part, (me * hw, 0))
        g_outward = lax.psum_scatter(spot, SEQ, scatter_dimension=0, tiled=True)
        g_outward = lax.psum(g_outward.astype(F32), ("g", "x"))

    mixed_sum = jnp.sum(mixed_grad.astype(F32), axis=0)

    def from_heads(value):
        return lax.dynamic_update_slice(jnp.zeros((width,), F32), value, (me * hw,))

    flat = jnp.stack(
        [
            gain_one_sum,
            shift_one_sum,
            from_heads(mixed_sum[:hw]),
            from_heads(mixed_sum[2 * hw :]),
            jnp.sum(low_middle.astype(F32), axis=0),
            gain_two_sum,
            shift_two_sum,
            jnp.sum(upstream, axis=0),
        ]
    )
    small_len = len(small) * share
    sums = jnp.swapaxes(flat.reshape(len(small), spread, share), 0, 1).reshape(spread, small_len)
    spot = jnp.zeros((NZ, ny, 2, 2, part), F32)
    spot = lax.dynamic_update_slice(spot, expand_b_sum.reshape(NZ, 1, 1, 1, part), (0, y, c, x, 0))
    sums = jnp.concatenate([sums, spot.reshape(spread, hidden)], axis=1)
    sums = jnp.broadcast_to(sums[None], (2,) + sums.shape).reshape(2 * spread, -1, 128)
    total = sum_groups(jnp.sum(exchange(sums, ("x",) + SEQ), axis=0)).reshape(-1)
    g_small = total[:small_len].reshape(len(small), share)
    g_expand_b = total[small_len:]
    return (
        layer_output,
        frames_grad,
        g_small[0],
        g_small[1],
        g_inward,
        g_small[2],
        g_small[3],
        g_outward,
        g_small[4],
        g_small[5],
        g_small[6],
        g_expand,
        g_expand_b,
        g_shrink,
        g_small[7],
    )


def solution(mesh):
    batch, seq = mesh.shape["batch"], mesh.shape["seq"]
    groups, ny = batch // 2, seq // (2 * NZ)
    fine = Mesh(mesh.devices.reshape(groups, 2, NZ, ny, 2), ("g", "x", "z", "y", "c"))
    b, s = ("g", "x"), ("z", "y", "c")
    in_specs = (
        P(s, b, None),
        P(s, b, None),
        P(b, None),
        P(b, None),
        P(s),
        P(s),
        P(s, None),
        P(s),
        P(s),
        P(s, None),
        P(s),
        P(s),
        P(s),
        P(s, None),
        P(s),
        P(s, None),
        P(s),
    )
    out_specs = (
        P(s, b, None),
        P(s, b, None),
        P(s),
        P(s),
        P(s, None),
        P(s),
        P(s),
        P(s, None),
        P(s),
        P(s),
        P(s),
        P(s, None),
        P(s),
        P(s, None),
        P(s),
    )
    return jax.shard_map(
        functools.partial(on_device, groups, ny), mesh=fine, in_specs=in_specs, out_specs=out_specs, check_vma=False
    )
```

```python
import functools
import math

import jax
import jax.numpy as jnp
from jax import lax
from jax.experimental import pallas as pl
from jax.experimental.pallas import tpu as pltpu
from jax.sharding import Mesh, PartitionSpec as P


HEADS = 16
NZ = 4
NORM_EPS = 1e-05
NEG = -1e30
F32 = jnp.float32
BF16 = jnp.bfloat16
LAYER_OF_ROW = (1, 2, 0, 3)
SWAP = [(0, 1), (1, 0)]
LAYER = ("c", "x", "y")
SEQ = ("z", "y", "c")


def xor_perm(count, k):
    return [(i, i ^ k) for i in range(count)]


def hop(value, axis, count=2, k=1):
    return lax.ppermute(value, axis, xor_perm(count, k))


def pick(value, index, axis=0):
    return lax.dynamic_index_in_dim(value, index, axis, keepdims=False)


def stack_rows(parts):
    return jnp.concatenate(parts, axis=0)


def assemble_body(pieces, size, place_ref, *refs):
    out_ref = refs[pieces]
    for r in range(pieces):
        spot = place_ref[0] ^ r
        out_ref[pl.ds(pl.multiple_of(spot * size, size), size), :] = refs[r][...]


def assemble(parts, me):
    size, width = parts[0].shape
    count = len(parts)
    return pl.pallas_call(
        functools.partial(assemble_body, count, size),
        out_shape=jax.ShapeDtypeStruct((count * size, width), parts[0].dtype),
        in_specs=[pl.BlockSpec(memory_space=pltpu.SMEM)] + whole(count),
        out_specs=whole(1)[0],
        compiler_params=pltpu.CompilerParams(vmem_limit_bytes=4 << 20),
        cost_estimate=pl.CostEstimate(flops=0, bytes_accessed=4 * count * size * width, transcendentals=0),
        name="assemble",
    )(me, *parts)


def near_parts(block, ny):
    return [block] + [lax.ppermute(block, ("x", "y"), xor_perm(2 * ny, r)) for r in range(1, 2 * ny)]


def both_cores(parts, place):
    mine = assemble(parts, place.xy)
    return assemble([mine, hop(mine, "c")], place.core)


def fold_body(count, size, place_ref, keep_ref, got_ref, own_ref, *out_refs):
    for r in range(count):
        spot = place_ref[0] ^ r
        here = pl.ds(pl.multiple_of(spot * size, size), size)
        value = keep_ref[here, :].astype(F32) + got_ref[here, :].astype(F32)
        if r == 0:
            own_ref[...] = value
        else:
            out_refs[r - 1][...] = value.astype(BF16)


def fold(keep, got, place, ny):
    rows, width = keep.shape
    count = 2 * ny
    size = rows // count
    return pl.pallas_call(
        functools.partial(fold_body, count, size),
        out_shape=[jax.ShapeDtypeStruct((size, width), F32)] + [jax.ShapeDtypeStruct((size, width), BF16)] * (count - 1),
        in_specs=[pl.BlockSpec(memory_space=pltpu.SMEM)] + whole(2),
        out_specs=whole(count),
        compiler_params=pltpu.CompilerParams(vmem_limit_bytes=4 << 20),
        cost_estimate=pl.CostEstimate(flops=count * size * width, bytes_accessed=6 * count * size * width, transcendentals=0),
        name="fold",
    )(place.xy, keep, got)


def finish(parts, ny):
    own = parts[0]
    for r in range(1, 2 * ny):
        own = own + lax.ppermute(parts[r], ("x", "y"), xor_perm(2 * ny, r)).astype(F32)
    return own


def total_of(parts):
    total = parts[0].astype(F32)
    for value in parts[1:]:
        total = total + value.astype(F32)
    return total


def rehome_flat(x, z, c):
    return (x * NZ + z) * 2 + c


def rehome_perm(k):
    return [
        (rehome_flat(x, z, c), rehome_flat(z >> 1, LAYER_OF_ROW[2 * x + (c ^ k)], z & 1))
        for x in range(2)
        for z in range(NZ)
        for c in range(2)
    ]


def to_home(block, place):
    got = [
        lax.ppermute(jnp.where(place.c == k, block[:, 0], block[:, 1]), ("x", "z", "c"), rehome_perm(k))
        for k in range(2)
    ]
    first = place.z < 2
    return stack_rows([jnp.where(first, got[0], got[1]), jnp.where(first, got[1], got[0])])


def to_origin(block, place):
    half = block.shape[0] // 2
    first = place.z < 2
    low, high = block[:half], block[half:]
    sent = [jnp.where(first, low, high), jnp.where(first, high, low)]
    got = [
        lax.ppermute(sent[k], ("x", "z", "c"), [(b, a) for a, b in rehome_perm(k)]) for k in range(2)
    ]
    return jnp.stack(
        [jnp.where(place.c == 0, got[0], got[1]), jnp.where(place.c == 0, got[1], got[0])], axis=1
    )


def after(first, *values):
    return lax.optimization_barrier((first, *values))


def sum_sources(value, count):
    return jnp.sum(value.reshape((count, -1) + value.shape[1:]).astype(F32), axis=0)


def by_half(x, mine, other, axis):
    return jnp.concatenate([jnp.where(x == 0, mine, other), jnp.where(x == 0, other, mine)], axis=axis)


def sin_cos(position, width):
    feature = jnp.arange(width, dtype=jnp.int32)
    rates = jnp.exp((feature // 2).astype(F32) * (-2.0 * math.log(10000.0) / width))
    angle = position.astype(F32)[:, None] * rates[None, :]
    turn = jnp.round(angle * (2.0 / math.pi))
    rest = angle - turn * 1.5703125
    rest = rest - turn * 0.00048375129699707031
    rest = rest - turn * 7.5497899548918861e-08
    quadrant = turn.astype(jnp.int32) + (feature % 2)[None, :]
    square = rest * rest
    sine = rest + rest * square * (
        -0.16666666641626524 + square * (0.008333329385889463 + square * (-0.00019839334836096632 + square * 2.718311493989822e-06))
    )
    cosine = 1.0 + square * (
        -0.49999999725103100 + square * (0.04166662332373906 + square * (-0.001388676377460993 + square * 2.439044879627741e-05))
    )
    value = jnp.where((quadrant & 1) == 0, sine, cosine)
    return jnp.where((quadrant & 2) == 0, value, -value)


def normalize(values):
    center = values - jnp.mean(values, axis=-1, keepdims=True)
    scale = lax.rsqrt(jnp.mean(center * center, axis=-1, keepdims=True) + NORM_EPS)
    return center * scale, scale


def normalize_back(normal, scale, gain, upstream):
    scaled = upstream * gain
    inner = scaled - jnp.mean(scaled, axis=-1, keepdims=True)
    inner = inner - normal * jnp.mean(scaled * normal, axis=-1, keepdims=True)
    return inner * scale, jnp.sum(upstream * normal, axis=0), jnp.sum(upstream, axis=0)


def dot_nt(a, b):
    return lax.dot_general(a, b, (((1,), (1,)), ((), ())), preferred_element_type=F32)


def dot_tn(a, b):
    return lax.dot_general(a, b, (((0,), (0,)), ((), ())), preferred_element_type=F32)


def dot_nn(a, b):
    return jnp.dot(a, b, preferred_element_type=F32)


BLOCK = 256


def chunk_owner(chunk, ny):
    outer, y = divmod(chunk, ny)
    return ((outer & 1) * 2 + (outer >> 1)) * ny + y


def lane_parts(heads, width):
    if heads == 1:
        return [None]
    lane = lax.broadcasted_iota(jnp.int32, (1, width), 1)
    return [(lane >= h * (width // heads)) & (lane < (h + 1) * (width // heads)) for h in range(heads)]


def only(value, lanes):
    return value if lanes is None else jnp.where(lanes, value, jnp.zeros_like(value))


def allowed_pairs(start_ref, first, total):
    key = lax.broadcasted_iota(jnp.int32, (total, BLOCK), 0)
    frame = first + lax.broadcasted_iota(jnp.int32, (total, BLOCK), 1)
    return (key >= start_ref[:, first : first + BLOCK]) & (key <= frame)


def attend(heads, ny, size, first_ref, weight_ref, bias_ref, start_ref, qkv_ref, out_ref, log_ref, q_s, k_s, vt_s):
    count = 4 * ny
    width = q_s.shape[1]
    step = 2 * size
    for owner in range(0, count, 2):
        rows = slice(owner * size, owner * size + step)
        mixed = dot_nn(first_ref[rows, :], weight_ref[...]) + bias_ref[...]
        qkv_ref[rows, :] = mixed.astype(BF16)
    for chunk in range(count):
        owner = chunk_owner(chunk, ny)
        rows = slice(owner * size, (owner + 1) * size)
        here = slice(chunk * size, (chunk + 1) * size)
        q_s[here, :] = qkv_ref[rows, 0:width] * 0.125
        k_s[here, :] = qkv_ref[rows, width : 2 * width]
        vt_s[:, here] = jnp.transpose(qkv_ref[rows, 2 * width : 3 * width].astype(F32)).astype(BF16)
    lanes = lane_parts(heads, width)
    each = width // heads
    for block in range(count * size // BLOCK):
        first = block * BLOCK
        total = first + BLOCK
        allowed = allowed_pairs(start_ref, first, total)
        q_block = q_s[first:total, :]
        contexts = []
        for h in range(heads):
            scores = dot_nt(k_s[0:total, :], only(q_block, lanes[h]))
            scores = jnp.where(allowed, scores, NEG)
            top = jnp.max(scores, axis=0, keepdims=True)
            weight = jnp.exp(scores - top)
            mass = jnp.sum(weight, axis=0, keepdims=True)
            part = dot_nn(vt_s[h * each : (h + 1) * each, 0:total], weight.astype(BF16))
            contexts.append(part / mass)
            log_ref[h : h + 1, first:total] = top + jnp.log(mass)
        context = contexts[0] if heads == 1 else jnp.concatenate(contexts, axis=0)
        context = jnp.transpose(context).astype(BF16)
        for sub in range(BLOCK // size):
            owner = chunk_owner(block * (BLOCK // size) + sub, ny)
            out_ref[owner * size : (owner + 1) * size, :] = context[sub * size : (sub + 1) * size]


def attend_back(
    heads,
    ny,
    size,
    core_ref,
    qkv_ref,
    low_ref,
    outward_ref,
    weight_ref,
    start_ref,
    log_ref,
    out_ref,
    send_ref,
    keep_ref,
    q_s,
    k_s,
    v_s,
    g_s,
    kt_s,
    dq_s,
    dk_s,
    dv_s,
):
    count = 4 * ny
    width = q_s.shape[1]
    for chunk in range(count):
        owner = chunk_owner(chunk, ny)
        rows = slice(owner * size, (owner + 1) * size)
        here = slice(chunk * size, (chunk + 1) * size)
        q_s[here, :] = qkv_ref[rows, 0:width] * 0.125
        key = qkv_ref[rows, width : 2 * width]
        k_s[here, :] = key
        kt_s[:, here] = jnp.transpose(key.astype(F32)).astype(BF16)
        v_s[here, :] = qkv_ref[rows, 2 * width : 3 * width]
        g_s[here, :] = dot_nt(low_ref[rows, :], outward_ref[...]).astype(BF16)
    dk_s[...] = jnp.zeros_like(dk_s)
    dv_s[...] = jnp.zeros_like(dv_s)
    lanes = lane_parts(heads, width)
    each = width // heads
    for block in range(count * size // BLOCK):
        first = block * BLOCK
        total = first + BLOCK
        allowed = allowed_pairs(start_ref, first, total)
        q_block, g_block = q_s[first:total, :], g_s[first:total, :]
        queries = []
        for h in range(heads):
            q_one, g_one = only(q_block, lanes[h]), only(g_block, lanes[h])
            scores = dot_nt(k_s[0:total, :], q_one)
            probs = jnp.where(allowed, jnp.exp(scores - log_ref[h : h + 1, first:total]), 0.0)
            prob_grad = dot_nt(v_s[0:total, :], g_one)
            delta = jnp.sum(probs * prob_grad, axis=0, keepdims=True)
            score_grad = (probs * (prob_grad - delta)).astype(BF16)
            dv_s[0:total, :] += dot_nn(probs.astype(BF16), g_one)
            dk_s[0:total, :] += dot_nn(score_grad, q_one)
            queries.append(dot_nn(kt_s[h * each : (h + 1) * each, 0:total], score_grad))
        query_grad = queries[0] if heads == 1 else jnp.concatenate(queries, axis=0)
        dq_s[first:total, :] = jnp.transpose(query_grad) * 0.125
    for chunk in range(count):
        owner = chunk_owner(chunk, ny)
        rows = slice(owner * size, (owner + 1) * size)
        here = slice(chunk * size, (chunk + 1) * size)
        out_ref[rows, 0:width] = dq_s[here, :].astype(BF16)
        out_ref[rows, width : 2 * width] = dk_s[here, :].astype(BF16)
        out_ref[rows, 2 * width : 3 * width] = dv_s[here, :].astype(BF16)
    half = count // 2 * size
    for ref, core in ((send_ref, 1 - core_ref[0]), (keep_ref, core_ref[0])):
        for start in range(0, half, 2 * size):
            rows = pl.ds(pl.multiple_of(core * half + start, 2 * size), 2 * size)
            ref[start : start + 2 * size, :] = dot_nt(out_ref[rows, :], weight_ref[...]).astype(BF16)


def feed_forward(
    size, core_ref, second_ref, up_ref, expand_ref, shrink_ref, bias_ref, active_ref, grad_ref, send_ref, keep_ref
):
    half = keep_ref.shape[0]
    step = 2 * size
    rate = math.sqrt(2.0 / math.pi)
    for ref, core in ((send_ref, 1 - core_ref[0]), (keep_ref, core_ref[0])):
        for start in range(0, half, step):
            rows = pl.ds(pl.multiple_of(core * half + start, step), step)
            before = dot_nn(second_ref[rows, :], expand_ref[...]) + bias_ref[...]
            upper = dot_nt(up_ref[rows, :], shrink_ref[...])
            square = before * before
            inner = jnp.tanh(rate * (before + 0.044715 * before * square))
            plus = 0.5 * (1.0 + inner)
            active_ref[rows, :] = (before * plus).astype(BF16)
            slope = plus + 0.5 * before * (1.0 - inner * inner) * (rate + rate * 3 * 0.044715 * square)
            lower = (upper * slope).astype(BF16)
            grad_ref[rows, :] = lower
            ref[start : start + step, :] = dot_nt(lower, expand_ref[...]).astype(BF16)


def shrink_parts(size, place_ref, active_ref, up_ref, *out_refs):
    for r in range(NZ):
        units = pl.ds(pl.multiple_of((place_ref[0] ^ r) * size, size), size)
        out_refs[r][...] = dot_tn(active_ref[:, units], up_ref[...]).astype(BF16)


def shrink_gradient(active, upstream_all, place):
    frames, units = active.shape
    width, size = upstream_all.shape[1], units // NZ
    if size % 128:
        value = dot_tn(active, upstream_all).astype(BF16).reshape(NZ, size, width)
        return [pick(value, place.z ^ k) for k in range(NZ)]
    return pl.pallas_call(
        functools.partial(shrink_parts, size),
        out_shape=[jax.ShapeDtypeStruct((size, width), BF16)] * NZ,
        in_specs=[pl.BlockSpec(memory_space=pltpu.SMEM)] + whole(2),
        out_specs=whole(NZ),
        compiler_params=pltpu.CompilerParams(vmem_limit_bytes=16 << 20),
        cost_estimate=pl.CostEstimate(
            flops=2 * frames * width * units, bytes_accessed=4 * frames * width, transcendentals=0
        ),
        name="shrink_gradient",
    )(place.layer, active, upstream_all)


def whole(count):
    return [pl.BlockSpec(memory_space=pltpu.VMEM)] * count


def attention(first_all, w_in, bias, starts, heads, ny, size):
    frames, wide = first_all.shape[0], w_in.shape[1]
    width = wide // 3
    pairs = frames * frames * heads
    return pl.pallas_call(
        functools.partial(attend, heads, ny, size),
        out_shape=(
            jax.ShapeDtypeStruct((frames, wide), BF16),
            jax.ShapeDtypeStruct((frames, width), BF16),
            jax.ShapeDtypeStruct((heads, frames), F32),
        ),
        in_specs=whole(4),
        out_specs=tuple(whole(3)),
        scratch_shapes=[
            pltpu.VMEM((frames, width), BF16),
            pltpu.VMEM((frames, width), BF16),
            pltpu.VMEM((width, frames), BF16),
        ],
        compiler_params=pltpu.CompilerParams(vmem_limit_bytes=20 << 20),
        cost_estimate=pl.CostEstimate(
            flops=pairs * 256 + 2 * first_all.size * wide, bytes_accessed=4 * first_all.size, transcendentals=pairs // 2
        ),
        name="attend",
    )(first_all, w_in, bias, starts)


def attention_back(core, qkv, low_all, w_out, w_in, starts, log_total, heads, ny, size):
    frames, wide = qkv.shape
    width = wide // 3
    pairs = frames * frames * heads
    half = jax.ShapeDtypeStruct((frames // 2, low_all.shape[1]), BF16)
    return pl.pallas_call(
        functools.partial(attend_back, heads, ny, size),
        out_shape=(jax.ShapeDtypeStruct((frames, wide), BF16), half, half),
        in_specs=[pl.BlockSpec(memory_space=pltpu.SMEM)] + whole(6),
        out_specs=tuple(whole(3)),
        scratch_shapes=[pltpu.VMEM((frames, width), BF16)] * 4
        + [pltpu.VMEM((width, frames), BF16)]
        + [pltpu.VMEM((frames, width), F32)] * 3,
        compiler_params=pltpu.CompilerParams(vmem_limit_bytes=20 << 20),
        cost_estimate=pl.CostEstimate(
            flops=pairs * 640 + 2 * low_all.size * (wide + width), bytes_accessed=6 * low_all.size, transcendentals=pairs // 2
        ),
        name="attend_back",
    )(core, qkv, low_all, w_out, w_in, starts, log_total)


def feed_forward_front(core, second_all, upstream_all, w_expand, w_shrink, bias, size):
    frames, width = second_all.shape
    units = w_expand.shape[1]
    half = jax.ShapeDtypeStruct((frames // 2, width), BF16)
    inner = jax.ShapeDtypeStruct((frames, units), BF16)
    return pl.pallas_call(
        functools.partial(feed_forward, size),
        out_shape=(inner, inner, half, half),
        in_specs=[pl.BlockSpec(memory_space=pltpu.SMEM)] + whole(5),
        out_specs=tuple(whole(4)),
        compiler_params=pltpu.CompilerParams(vmem_limit_bytes=20 << 20),
        cost_estimate=pl.CostEstimate(
            flops=6 * frames * width * units, bytes_accessed=8 * frames * width, transcendentals=frames * units
        ),
        name="feed_forward",
    )(core, second_all, upstream_all, w_expand, w_shrink, bias)


class Place:
    def __init__(self, ny):
        self.x, self.z, self.y, self.c = (lax.axis_index(a) for a in ("x", "z", "y", "c"))
        self.xy = jnp.reshape(self.x * ny + self.y, (1,)).astype(jnp.int32)
        self.core = jnp.reshape(self.c, (1,)).astype(jnp.int32)
        self.layer = jnp.reshape(self.z, (1,)).astype(jnp.int32)


def on_device(
    groups,
    ny,
    frames,
    cotangent,
    segment_lengths,
    position_offsets,
    first_gain,
    first_shift,
    inward_weight,
    query_bias,
    value_bias,
    outward_weight,
    outward_bias,
    second_gain,
    second_shift,
    expand_weight,
    expand_bias,
    shrink_weight,
    shrink_bias,
):
    place = Place(ny)
    x, z, y, c = place.x, place.z, place.y, place.c
    local_len, rows, width = frames.shape
    share = inward_weight.shape[0]
    layer = 4 * ny
    spread = NZ * ny * 2
    full_len = local_len * spread
    size = 2 * local_len
    hd = HEADS // layer
    hw = hd * (width // HEADS)
    hidden = expand_bias.shape[0]
    part = hidden // 2
    me = (c * 2 + x) * ny + y

    def sum_groups(value):
        return lax.psum(value, "g") if groups > 1 else value

    def exchange(value, axes):
        return lax.all_to_all(value, axes, 0, 0, tiled=True)

    fr = to_home(frames, place)

    small = [first_gain, first_shift, query_bias, value_bias, outward_bias, second_gain, second_shift, shrink_bias]
    table = jnp.stack([segment_lengths, position_offsets], axis=1)
    table = jnp.stack([table >> 6, table & 63]).astype(BF16).reshape(1, -1)
    table = jnp.pad(table, ((0, 0), (0, share - table.shape[1])))
    bias_rows = expand_bias.reshape(-1, share)
    packed = jnp.concatenate([v[None] for v in small] + [bias_rows, table], axis=0)
    packed = jnp.pad(packed, ((0, -packed.shape[0] % 16), (0, 0)))
    kinds = packed.shape[0]
    other_table = hop(packed, "x")
    grid = jnp.stack([packed] + [hop(packed, "z", NZ, k) for k in range(1, NZ)])
    grid, later_inward = after(grid, inward_weight)
    in_cols = jnp.transpose(later_inward.reshape(share, 3, 2, 2, ny, hw), (3, 4, 2, 0, 1, 5))
    in_cols = pick(in_cols, x).reshape(1, ny * 2, share, 3 * hw)
    in_cols = jnp.broadcast_to(in_cols, (NZ, ny * 2, share, 3 * hw)).reshape(spread, share, 3 * hw)
    w_in = exchange(in_cols, SEQ).reshape(width, 3 * hw)
    grid = jnp.stack([grid] + [hop(grid, "y", ny, k) for k in range(1, ny)], axis=1)
    grid = jnp.stack([grid, hop(grid, "c")], axis=2).reshape(spread, kinds, share)
    outward = lax.all_gather(outward_weight, SEQ, axis=0, tiled=True)

    ids = jnp.arange(spread)
    select = (ids[:, None] == (ids[None, :] ^ ((z * ny + y) * 2 + c))).astype(BF16)
    vectors = lax.dot_general(grid, select, (((0,), (1,)), ((), ())), preferred_element_type=F32)
    vectors = jnp.swapaxes(vectors, 1, 2)
    expand_b = jnp.swapaxes(vectors[len(small) : len(small) + 4], 0, 1).reshape(NZ, ny, 2, 2, part)
    vectors = vectors[: len(small)].reshape(len(small), width)
    gain_one, shift_one, query_b, value_b, outward_b, gain_two, shift_two, shrink_b = (
        vectors[i : i + 1] for i in range(len(small))
    )
    expand_b = pick(pick(pick(expand_b, y, 1), c, 1), x, 1).reshape(1, NZ * part)
    qkv_bias = jnp.concatenate(
        [
            lax.dynamic_slice_in_dim(query_b, me * hw, hw, 1),
            jnp.zeros((1, hw), F32),
            lax.dynamic_slice_in_dim(value_b, me * hw, hw, 1),
        ],
        axis=1,
    )

    row_x = jnp.where((z == 0) | (z == 3), 1, 0)
    spot = len(small) + bias_rows.shape[0]
    table = jnp.where(x == row_x, packed[spot], other_table[spot]).astype(jnp.int32)
    table = table[: 4 * segment_lengths.size].reshape(2, rows, 2, -1)
    table = pick(table[0] * 64 + table[1], z >> 1)
    lengths, offsets = table[0], table[1]
    count = lengths.shape[0]
    starts = jnp.sum(
        jnp.where(jnp.arange(count)[None, :] < jnp.arange(count)[:, None], lengths[None, :], 0), axis=1
    )
    frame_ids = jnp.arange(full_len, dtype=jnp.int32)
    row_starts = jnp.max(jnp.where(starts[:, None] <= frame_ids[None, :], starts[:, None], 0), axis=0)[None, :]
    chunk = (2 * x + c) * ny + y
    mine = chunk * size + jnp.arange(size, dtype=jnp.int32)
    inside = (mine[:, None] >= starts[None, :]) & (mine[:, None] < (starts + lengths)[None, :])
    position = jnp.sum(jnp.where(inside, offsets[None, :] + mine[:, None] - starts[None, :], 0), axis=1)

    fr, later_cotangent = after(fr, cotangent)
    inputs = fr.astype(F32) + sin_cos(position, width)
    normal_one, scale_one = normalize(inputs)
    first = (normal_one * gain_one + shift_one).astype(BF16)
    first_near = near_parts(first, ny)
    ct = to_home(later_cotangent, place)
    ct, *first_near = after(ct, *first_near)
    first_all = both_cores(first_near, place)
    upstream_all = lax.all_gather(ct, LAYER, axis=0, tiled=True)
    first_all, w_in, later_shrink = after(first_all, w_in, shrink_weight)
    sh_rows = [lax.dynamic_slice_in_dim(later_shrink, x * part, part, 0)]
    sh_rows.append(hop(sh_rows[0], "z", NZ, 1))
    qkv, context_all, log_total = attention(first_all, w_in, qkv_bias, row_starts, hd, ny, size)
    context_all, *sh_rows = after(context_all, *sh_rows)
    context = exchange(context_all.reshape(layer, size, hw), LAYER)
    sh_rows.append(hop(sh_rows[0], "z", NZ, 2))
    context, later_expand, *sh_rows = after(context, expand_weight, *sh_rows)
    sh_rows.append(hop(sh_rows[0], "z", NZ, 3))
    ex_cols = pick(later_expand.reshape(share, NZ, ny, 2, 2, part), x, 4)
    ex_cols = jnp.transpose(ex_cols, (2, 3, 0, 1, 4)).reshape(1, ny * 2, share, NZ * part)
    ex_cols = jnp.broadcast_to(ex_cols, (NZ, ny * 2, share, NZ * part)).reshape(spread, share, NZ * part)
    w_expand = exchange(ex_cols, SEQ).reshape(width, NZ * part)

    context = jnp.swapaxes(context, 0, 1).reshape(size, width)
    middle = inputs + dot_nn(context, outward) + outward_b

    normal_two, scale_two = normalize(middle)
    second = (normal_two * gain_two + shift_two).astype(BF16)
    second_near = near_parts(second, ny)
    both = after(sh_rows[3], *second_near)
    sh_rows[3], second_near = both[0], both[1:]
    w_shrink = assemble(sh_rows, place.layer)
    second_all = both_cores(second_near, place)
    active, before_grad, send, keep = feed_forward_front(
        place.core, second_all, upstream_all, w_expand, w_shrink, expand_b, size
    )
    got = hop(send, "c")
    got, *shrink_part = after(got, *shrink_gradient(active, upstream_all, place))
    second_parts = list(fold(keep, got, place, ny))
    second_parts[0], active, before_grad, *shrink_part = after(second_parts[0], active, before_grad, *shrink_part)
    second_grad = finish(second_parts, ny)
    shrink_got = [shrink_part[0], hop(shrink_part[1], "z", NZ, 1)]
    second_grad, before_grad, *shrink_got = after(second_grad, before_grad, *shrink_got)
    shrink_got.append(hop(shrink_part[2], "z", NZ, 2))
    expand_part = dot_tn(second_all, before_grad).astype(BF16)
    expand_got = exchange(expand_part.reshape(spread, share, NZ * part), SEQ)
    out_part = dot_nn(active, w_shrink).astype(BF16)
    out_part = lax.psum_scatter(out_part, LAYER, scatter_dimension=0, tiled=True)
    expand_b_sum = jnp.sum(before_grad.astype(F32), axis=0)

    upstream = ct.astype(F32)
    middle_part, gain_two_sum, shift_two_sum = normalize_back(normal_two, scale_two, gain_two, second_grad)
    middle_grad = upstream + middle_part
    low_middle = middle_grad.astype(BF16)
    low_near = near_parts(low_middle, ny)
    both = after(*shrink_got, *low_near)
    shrink_got, low_near = list(both[:3]), both[3:]
    shrink_got.append(hop(shrink_part[3], "z", NZ, 3))
    low_all = both_cores(low_near, place)
    w_out = lax.dynamic_slice_in_dim(outward, me * hw, hw, 0)
    mixed_grad, send, keep = attention_back(
        place.core, qkv, low_all, w_out, w_in, row_starts, log_total, hd, ny, size
    )
    got = hop(send, "c")
    inward_part = dot_tn(first_all, mixed_grad).astype(BF16)
    got, inward_part = after(got, inward_part)
    first_parts = list(fold(keep, got, place, ny))
    first_parts[0], inward_part, low_late, out_part, expand_got, *shrink_got = after(
        first_parts[0], inward_part, low_all, out_part, expand_got, *shrink_got
    )
    outward_part = dot_tn(context_all, low_late).astype(BF16)
    first_grad = finish(first_parts, ny)
    inward_got = exchange(inward_part.reshape(spread, share, 3 * hw), SEQ)
    layer_output = to_origin((middle + out_part.astype(F32) + shrink_b).astype(BF16), place)
    input_part, gain_one_sum, shift_one_sum = normalize_back(normal_one, scale_one, gain_one, first_grad)
    frames_grad = to_origin((middle_grad + input_part).astype(BF16), place).astype(F32)

    shrink_sum = sum_groups(total_of(shrink_got)).astype(BF16)
    g_shrink = by_half(x, shrink_sum, hop(shrink_sum, "x"), 0).astype(F32)

    expand_sum = sum_groups(sum_sources(expand_got, NZ)).astype(BF16)
    g_expand = [v.reshape(ny, 2, 1, share, NZ, part) for v in (expand_sum, hop(expand_sum, "x"))]
    g_expand = jnp.transpose(by_half(x, *g_expand, 2), (3, 4, 0, 1, 2, 5)).reshape(share, -1).astype(F32)

    if hd == 2 and ny == 2:
        half = width // 2
        split = outward_part.reshape(2, share, width)
        pair = by_half(c, pick(split, c)[None], hop(pick(split, 1 - c), "c")[None], 0)
        pair = pair.reshape(2, 1, share, 2, half)
        pair = by_half(x, pick(pair, x, 3), hop(pick(pair, 1 - x, 3), "x"), 1)
        pair = pair.reshape(NZ, share, half)
        pair = [pick(pair, z ^ k) for k in range(NZ)]
        out_sum = total_of([pair[0]] + [hop(pair[k], "z", NZ, k) for k in range(1, NZ)])
        out_sum = sum_groups(out_sum).astype(BF16)
        g_outward = by_half(x, out_sum, hop(out_sum, "x"), 1).astype(F32)
    else:
        spot = lax.dynamic_update_slice(jnp.zeros((width, width), BF16), outward_part, (me * hw, 0))
        g_outward = lax.psum_scatter(spot, SEQ, scatter_dimension=0, tiled=True)
        g_outward = lax.psum(g_outward.astype(F32), ("g", "x"))

    mixed_sum = jnp.sum(mixed_grad.astype(F32), axis=0)

    def from_heads(value):
        return lax.dynamic_update_slice(jnp.zeros((width,), F32), value, (me * hw,))

    flat = jnp.stack(
        [
            gain_one_sum,
            shift_one_sum,
            from_heads(mixed_sum[:hw]),
            from_heads(mixed_sum[2 * hw :]),
            jnp.sum(low_middle.astype(F32), axis=0),
            gain_two_sum,
            shift_two_sum,
            jnp.sum(upstream, axis=0),
        ]
    )
    small_len = len(small) * share
    sums = jnp.swapaxes(flat.reshape(len(small), spread, share), 0, 1).reshape(spread, small_len)
    spot = jnp.zeros((NZ, ny, 2, 2, part), F32)
    spot = lax.dynamic_update_slice(spot, expand_b_sum.reshape(NZ, 1, 1, 1, part), (0, y, c, x, 0))
    sums = jnp.concatenate([sums, spot.reshape(spread, hidden)], axis=1)
    inward_got, sums = after(inward_got, sums)
    sums = jnp.broadcast_to(sums[None], (2,) + sums.shape).reshape(2 * spread, -1, 128)
    total = sum_groups(jnp.sum(exchange(sums, ("x",) + SEQ), axis=0)).reshape(-1)
    g_small = total[:small_len].reshape(len(small), share)
    g_expand_b = total[small_len:]
    inward_sum = sum_groups(sum_sources(inward_got, NZ)).astype(BF16)
    g_inward = [v.reshape(ny, 2, 1, share, 3, hw) for v in (inward_sum, hop(inward_sum, "x"))]
    g_inward = jnp.transpose(by_half(x, *g_inward, 2), (3, 4, 1, 2, 0, 5)).reshape(share, -1).astype(F32)

    return (
        layer_output,
        frames_grad,
        g_small[0],
        g_small[1],
        g_inward,
        g_small[2],
        g_small[3],
        g_outward,
        g_small[4],
        g_small[5],
        g_small[6],
        g_expand,
        g_expand_b,
        g_shrink,
        g_small[7],
    )


def solution(mesh):
    batch, seq = mesh.shape["batch"], mesh.shape["seq"]
    groups, ny = batch // 2, seq // (2 * NZ)
    fine = Mesh(mesh.devices.reshape(groups, 2, NZ, ny, 2), ("g", "x", "z", "y", "c"))
    b, s = ("g", "x"), ("z", "y", "c")
    in_specs = (
        P(s, b, None),
        P(s, b, None),
        P(b, None),
        P(b, None),
        P(s),
        P(s),
        P(s, None),
        P(s),
        P(s),
        P(s, None),
        P(s),
        P(s),
        P(s),
        P(s, None),
        P(s),
        P(s, None),
        P(s),
    )
    out_specs = (
        P(s, b, None),
        P(s, b, None),
        P(s),
        P(s),
        P(s, None),
        P(s),
        P(s),
        P(s, None),
        P(s),
        P(s),
        P(s),
        P(s, None),
        P(s),
        P(s, None),
        P(s),
    )
    return jax.shard_map(
        functools.partial(on_device, groups, ny), mesh=fine, in_specs=in_specs, out_specs=out_specs, check_vma=False
    )
```

```python
import functools
import math

import jax
import jax.numpy as jnp
from jax import lax
from jax.experimental import pallas as pl
from jax.experimental.pallas import tpu as pltpu
from jax.sharding import Mesh, PartitionSpec as P


HEADS = 16
NZ = 4
NORM_EPS = 1e-05
NEG = -1e30
F32 = jnp.float32
BF16 = jnp.bfloat16
LAYER_OF_ROW = (1, 2, 0, 3)
SWAP = [(0, 1), (1, 0)]
LAYER = ("c", "x", "y")
SEQ = ("z", "y", "c")


def xor_perm(count, k):
    return [(i, i ^ k) for i in range(count)]


def hop(value, axis, count=2, k=1):
    return lax.ppermute(value, axis, xor_perm(count, k))


def pick(value, index, axis=0):
    return lax.dynamic_index_in_dim(value, index, axis, keepdims=False)


def stack_rows(parts):
    return jnp.concatenate(parts, axis=0)


def assemble_body(pieces, size, place_ref, *refs):
    out_ref = refs[pieces]
    for r in range(pieces):
        spot = place_ref[0] ^ r
        out_ref[pl.ds(pl.multiple_of(spot * size, size), size), :] = refs[r][...]


def assemble(parts, me):
    size, width = parts[0].shape
    count = len(parts)
    return pl.pallas_call(
        functools.partial(assemble_body, count, size),
        out_shape=jax.ShapeDtypeStruct((count * size, width), parts[0].dtype),
        in_specs=[pl.BlockSpec(memory_space=pltpu.SMEM)] + whole(count),
        out_specs=whole(1)[0],
        compiler_params=pltpu.CompilerParams(vmem_limit_bytes=4 << 20),
        cost_estimate=pl.CostEstimate(flops=0, bytes_accessed=4 * count * size * width, transcendentals=0),
        name="assemble",
    )(me, *parts)


def near_parts(block, ny):
    return [block] + [lax.ppermute(block, ("x", "y"), xor_perm(2 * ny, r)) for r in range(1, 2 * ny)]


def both_cores(parts, place):
    mine = assemble(parts, place.xy)
    return mine, hop(mine, "c")


def fold_body(count, size, place_ref, keep_ref, got_ref, own_ref, *out_refs):
    for r in range(count):
        spot = place_ref[0] ^ r
        here = pl.ds(pl.multiple_of(spot * size, size), size)
        value = keep_ref[here, :].astype(F32) + got_ref[here, :].astype(F32)
        if r == 0:
            own_ref[...] = value
        else:
            out_refs[r - 1][...] = value.astype(BF16)


def fold(keep, got, place, ny):
    rows, width = keep.shape
    count = 2 * ny
    size = rows // count
    return pl.pallas_call(
        functools.partial(fold_body, count, size),
        out_shape=[jax.ShapeDtypeStruct((size, width), F32)] + [jax.ShapeDtypeStruct((size, width), BF16)] * (count - 1),
        in_specs=[pl.BlockSpec(memory_space=pltpu.SMEM)] + whole(2),
        out_specs=whole(count),
        compiler_params=pltpu.CompilerParams(vmem_limit_bytes=4 << 20),
        cost_estimate=pl.CostEstimate(flops=count * size * width, bytes_accessed=6 * count * size * width, transcendentals=0),
        name="fold",
    )(place.xy, keep, got)


def finish(parts, ny):
    own = parts[0]
    for r in range(1, 2 * ny):
        own = own + lax.ppermute(parts[r], ("x", "y"), xor_perm(2 * ny, r)).astype(F32)
    return own


def total_of(parts):
    total = parts[0].astype(F32)
    for value in parts[1:]:
        total = total + value.astype(F32)
    return total


def rehome_flat(x, z, c):
    return (x * NZ + z) * 2 + c


def rehome_perm(k):
    return [
        (rehome_flat(x, z, c), rehome_flat(z >> 1, LAYER_OF_ROW[2 * x + (c ^ k)], z & 1))
        for x in range(2)
        for z in range(NZ)
        for c in range(2)
    ]


def to_home(block, place):
    got = [
        lax.ppermute(jnp.where(place.c == k, block[:, 0], block[:, 1]), ("x", "z", "c"), rehome_perm(k))
        for k in range(2)
    ]
    first = place.z < 2
    return stack_rows([jnp.where(first, got[0], got[1]), jnp.where(first, got[1], got[0])])


def to_origin(block, place):
    half = block.shape[0] // 2
    first = place.z < 2
    low, high = block[:half], block[half:]
    sent = [jnp.where(first, low, high), jnp.where(first, high, low)]
    got = [
        lax.ppermute(sent[k], ("x", "z", "c"), [(b, a) for a, b in rehome_perm(k)]) for k in range(2)
    ]
    return jnp.stack(
        [jnp.where(place.c == 0, got[0], got[1]), jnp.where(place.c == 0, got[1], got[0])], axis=1
    )


def after(first, *values):
    return lax.optimization_barrier((first, *values))


def sum_sources(value, count):
    return jnp.sum(value.reshape((count, -1) + value.shape[1:]).astype(F32), axis=0)


def by_half(x, mine, other, axis):
    return jnp.concatenate([jnp.where(x == 0, mine, other), jnp.where(x == 0, other, mine)], axis=axis)


def sin_cos(position, width):
    feature = jnp.arange(width, dtype=jnp.int32)
    rates = jnp.exp((feature // 2).astype(F32) * (-2.0 * math.log(10000.0) / width))
    angle = position.astype(F32)[:, None] * rates[None, :]
    turn = jnp.round(angle * (2.0 / math.pi))
    rest = angle - turn * 1.5703125
    rest = rest - turn * 0.00048375129699707031
    rest = rest - turn * 7.5497899548918861e-08
    quadrant = turn.astype(jnp.int32) + (feature % 2)[None, :]
    square = rest * rest
    sine = rest + rest * square * (
        -0.16666666641626524 + square * (0.008333329385889463 + square * (-0.00019839334836096632 + square * 2.718311493989822e-06))
    )
    cosine = 1.0 + square * (
        -0.49999999725103100 + square * (0.04166662332373906 + square * (-0.001388676377460993 + square * 2.439044879627741e-05))
    )
    value = jnp.where((quadrant & 1) == 0, sine, cosine)
    return jnp.where((quadrant & 2) == 0, value, -value)


def normalize(values):
    center = values - jnp.mean(values, axis=-1, keepdims=True)
    scale = lax.rsqrt(jnp.mean(center * center, axis=-1, keepdims=True) + NORM_EPS)
    return center * scale, scale


def normalize_back(normal, scale, gain, upstream):
    scaled = upstream * gain
    inner = scaled - jnp.mean(scaled, axis=-1, keepdims=True)
    inner = inner - normal * jnp.mean(scaled * normal, axis=-1, keepdims=True)
    return inner * scale, jnp.sum(upstream * normal, axis=0), jnp.sum(upstream, axis=0)


def dot_nt(a, b):
    return lax.dot_general(a, b, (((1,), (1,)), ((), ())), preferred_element_type=F32)


def dot_tn(a, b):
    return lax.dot_general(a, b, (((0,), (0,)), ((), ())), preferred_element_type=F32)


def dot_nn(a, b):
    return jnp.dot(a, b, preferred_element_type=F32)


BLOCK = 256


def chunk_owner(chunk, ny):
    outer, y = divmod(chunk, ny)
    return ((outer & 1) * 2 + (outer >> 1)) * ny + y


def lane_parts(heads, width):
    if heads == 1:
        return [None]
    lane = lax.broadcasted_iota(jnp.int32, (1, width), 1)
    return [(lane >= h * (width // heads)) & (lane < (h + 1) * (width // heads)) for h in range(heads)]


def only(value, lanes):
    return value if lanes is None else jnp.where(lanes, value, jnp.zeros_like(value))


def allowed_pairs(start_ref, first, total):
    key = lax.broadcasted_iota(jnp.int32, (total, BLOCK), 0)
    frame = first + lax.broadcasted_iota(jnp.int32, (total, BLOCK), 1)
    return (key >= start_ref[:, first : first + BLOCK]) & (key <= frame)


def chunk_rows(chunk, ny, size, core):
    half, spot = divmod(chunk_owner(chunk, ny), 2 * ny)
    return pl.ds(pl.multiple_of(((half ^ core) * (2 * ny) + spot) * size, size), size)


def attend(
    heads,
    ny,
    size,
    core_ref,
    mine_ref,
    other_ref,
    affine_ref,
    weight_ref,
    bias_ref,
    start_ref,
    first_ref,
    qkv_ref,
    out_ref,
    log_ref,
    q_s,
    k_s,
    vt_s,
):
    count = 4 * ny
    width = q_s.shape[1]
    core = core_ref[0]
    step = 2 * size
    half = mine_ref.shape[0]
    for base, ref in ((0, mine_ref), (half, other_ref)):
        for start in range(0, half, step):
            normal = ref[start : start + step, :].astype(F32)
            value = (normal * affine_ref[0:1, :] + affine_ref[1:2, :]).astype(BF16)
            rows = slice(base + start, base + start + step)
            first_ref[rows, :] = value
            qkv_ref[rows, :] = (dot_nn(value, weight_ref[...]) + bias_ref[...]).astype(BF16)
    for chunk in range(count):
        rows = chunk_rows(chunk, ny, size, core)
        here = slice(chunk * size, (chunk + 1) * size)
        q_s[here, :] = qkv_ref[rows, 0:width] * 0.125
        k_s[here, :] = qkv_ref[rows, width : 2 * width]
        vt_s[:, here] = jnp.transpose(qkv_ref[rows, 2 * width : 3 * width].astype(F32)).astype(BF16)
    lanes = lane_parts(heads, width)
    each = width // heads
    for block in range(count * size // BLOCK):
        first = block * BLOCK
        total = first + BLOCK
        allowed = allowed_pairs(start_ref, first, total)
        q_block = q_s[first:total, :]
        contexts = []
        for h in range(heads):
            scores = dot_nt(k_s[0:total, :], only(q_block, lanes[h]))
            scores = jnp.where(allowed, scores, NEG)
            top = jnp.max(scores, axis=0, keepdims=True)
            weight = jnp.exp(scores - top)
            mass = jnp.sum(weight, axis=0, keepdims=True)
            part = dot_nn(vt_s[h * each : (h + 1) * each, 0:total], weight.astype(BF16))
            contexts.append(part / mass)
            log_ref[h : h + 1, first:total] = top + jnp.log(mass)
        context = contexts[0] if heads == 1 else jnp.concatenate(contexts, axis=0)
        context = jnp.transpose(context).astype(BF16)
        for sub in range(BLOCK // size):
            owner = chunk_owner(block * (BLOCK // size) + sub, ny)
            out_ref[owner * size : (owner + 1) * size, :] = context[sub * size : (sub + 1) * size]


def attend_back(
    heads,
    ny,
    size,
    place_ref,
    qkv_ref,
    mine_ref,
    other_ref,
    context_ref,
    outward_ref,
    weight_ref,
    start_ref,
    log_ref,
    out_ref,
    send_ref,
    keep_ref,
    outward_grad_ref,
    q_s,
    k_s,
    v_s,
    g_s,
    kt_s,
    dq_s,
    dk_s,
    dv_s,
):
    count = 4 * ny
    width = q_s.shape[1]
    core = place_ref[0]
    half = mine_ref.shape[0]
    step = 2 * size
    for base, ref in ((0, mine_ref), (half, other_ref)):
        for start in range(0, half, step):
            rows = slice(start, start + step)
            out_ref[base + start : base + start + step, 0:width] = dot_nt(ref[rows, :], outward_ref[...]).astype(BF16)
    for chunk in range(count):
        rows = chunk_rows(chunk, ny, size, core)
        here = slice(chunk * size, (chunk + 1) * size)
        q_s[here, :] = qkv_ref[rows, 0:width] * 0.125
        key = qkv_ref[rows, width : 2 * width]
        k_s[here, :] = key
        kt_s[:, here] = jnp.transpose(key.astype(F32)).astype(BF16)
        v_s[here, :] = qkv_ref[rows, 2 * width : 3 * width]
        g_s[here, :] = out_ref[rows, 0:width]
    dk_s[...] = jnp.zeros_like(dk_s)
    dv_s[...] = jnp.zeros_like(dv_s)
    lanes = lane_parts(heads, width)
    each = width // heads
    for block in range(count * size // BLOCK):
        first = block * BLOCK
        total = first + BLOCK
        allowed = allowed_pairs(start_ref, first, total)
        q_block, g_block = q_s[first:total, :], g_s[first:total, :]
        queries = []
        for h in range(heads):
            q_one, g_one = only(q_block, lanes[h]), only(g_block, lanes[h])
            scores = dot_nt(k_s[0:total, :], q_one)
            probs = jnp.where(allowed, jnp.exp(scores - log_ref[h : h + 1, first:total]), 0.0)
            prob_grad = dot_nt(v_s[0:total, :], g_one)
            delta = jnp.sum(probs * prob_grad, axis=0, keepdims=True)
            score_grad = (probs * (prob_grad - delta)).astype(BF16)
            dv_s[0:total, :] += dot_nn(probs.astype(BF16), g_one)
            dk_s[0:total, :] += dot_nn(score_grad, q_one)
            queries.append(dot_nn(kt_s[h * each : (h + 1) * each, 0:total], score_grad))
        query_grad = queries[0] if heads == 1 else jnp.concatenate(queries, axis=0)
        dq_s[first:total, :] = jnp.transpose(query_grad) * 0.125
    for chunk in range(count):
        rows = chunk_rows(chunk, ny, size, core)
        here = slice(chunk * size, (chunk + 1) * size)
        out_ref[rows, 0:width] = dq_s[here, :].astype(BF16)
        out_ref[rows, width : 2 * width] = dk_s[here, :].astype(BF16)
        out_ref[rows, 2 * width : 3 * width] = dv_s[here, :].astype(BF16)
    for ref, base in ((send_ref, half), (keep_ref, 0)):
        for start in range(0, half, step):
            rows = slice(base + start, base + start + step)
            ref[start : start + step, :] = dot_nt(out_ref[rows, :], weight_ref[...]).astype(BF16)
    outward_grad_ref[...] = jnp.zeros_like(outward_grad_ref)
    near = context_ref[pl.ds(pl.multiple_of(core * half, half), half), :]
    far = context_ref[pl.ds(pl.multiple_of((1 - core) * half, half), half), :]
    total = dot_tn(near, mine_ref[...]) + dot_tn(far, other_ref[...])
    outward_grad_ref[pl.ds(pl.multiple_of(place_ref[1] * width, width), width), :] = total.astype(BF16)


def feed_forward(
    size,
    core_ref,
    mine_ref,
    other_ref,
    up_ref,
    expand_ref,
    shrink_ref,
    bias_ref,
    active_ref,
    grad_ref,
    send_ref,
    keep_ref,
    result_ref,
):
    half = keep_ref.shape[0]
    step = 2 * size
    rate = math.sqrt(2.0 / math.pi)
    core = core_ref[0]
    for ref, source_ref, base, side in ((send_ref, other_ref, half, 1 - core), (keep_ref, mine_ref, 0, core)):
        for start in range(0, half, step):
            rows = slice(start, start + step)
            pair = slice(base + start, base + start + step)
            place = pl.ds(pl.multiple_of(side * half + start, step), step)
            before = dot_nn(source_ref[rows, :], expand_ref[...]) + bias_ref[...]
            upper = dot_nt(up_ref[place, :], shrink_ref[...])
            square = before * before
            inner = jnp.tanh(rate * (before + 0.044715 * before * square))
            plus = 0.5 * (1.0 + inner)
            active = (before * plus).astype(BF16)
            active_ref[pair, :] = active
            slope = plus + 0.5 * before * (1.0 - inner * inner) * (rate + rate * 3 * 0.044715 * square)
            lower = (upper * slope).astype(BF16)
            grad_ref[pair, :] = lower
            ref[rows, :] = dot_nt(lower, expand_ref[...]).astype(BF16)
            result_ref[place, :] = dot_nn(active, shrink_ref[...]).astype(BF16)


def weight_parts(
    part, place_ref, mine_ref, other_ref, up_ref, active_ref, grad_ref, expand_ref, bias_ref, *out_refs
):
    half = mine_ref.shape[0]
    core = place_ref[0]
    near = pl.ds(pl.multiple_of(core * half, half), half)
    far = pl.ds(pl.multiple_of((1 - core) * half, half), half)
    for r in range(NZ):
        units = pl.ds(pl.multiple_of((place_ref[1] ^ r) * part, part), part)
        total = dot_tn(active_ref[0:half, units], up_ref[near, :])
        total = total + dot_tn(active_ref[half : 2 * half, units], up_ref[far, :])
        out_refs[r][...] = total.astype(BF16)
    width = mine_ref.shape[1]
    for start in range(0, width, width // 4):
        here = slice(start, start + width // 4)
        total = dot_tn(mine_ref[:, here], grad_ref[0:half, :]) + dot_tn(other_ref[:, here], grad_ref[half : 2 * half, :])
        expand_ref[here, :] = total.astype(BF16)
    bias_ref[...] = jnp.sum(grad_ref[...].astype(F32), axis=0, keepdims=True)


def feed_forward_weights(place, second, upstream_all, active, before_grad):
    frames, units = active.shape
    width, part = upstream_all.shape[1], units // NZ
    if part % 128:
        half = frames // 2
        up = stack_rows([lax.dynamic_slice_in_dim(upstream_all, i * half, half, 0) for i in (place.c, 1 - place.c)])
        value = dot_tn(active, up).astype(BF16).reshape(NZ, part, width)
        expand = dot_tn(stack_rows(second), before_grad).astype(BF16)
        bias = jnp.sum(before_grad.astype(F32), axis=0, keepdims=True)
        return [expand, bias] + [pick(value, place.z ^ k) for k in range(NZ)]
    return pl.pallas_call(
        functools.partial(weight_parts, part),
        out_shape=[jax.ShapeDtypeStruct((width, units), BF16), jax.ShapeDtypeStruct((1, units), F32)]
        + [jax.ShapeDtypeStruct((part, width), BF16)] * NZ,
        in_specs=[pl.BlockSpec(memory_space=pltpu.SMEM)] + whole(5),
        out_specs=whole(2 + NZ),
        compiler_params=pltpu.CompilerParams(vmem_limit_bytes=16 << 20),
        cost_estimate=pl.CostEstimate(
            flops=4 * frames * width * units, bytes_accessed=8 * frames * width, transcendentals=0
        ),
        name="feed_forward_weights",
    )(jnp.concatenate([place.core, place.layer]), *second, upstream_all, active, before_grad)


def whole(count):
    return [pl.BlockSpec(memory_space=pltpu.VMEM)] * count


def attention(core, pair, affine, w_in, bias, starts, heads, ny, size):
    half, wide = pair[0].shape[0], w_in.shape[1]
    frames, depth, width = 2 * half, pair[0].shape[1], wide // 3
    pairs = frames * frames * heads
    return pl.pallas_call(
        functools.partial(attend, heads, ny, size),
        out_shape=(
            jax.ShapeDtypeStruct((frames, depth), BF16),
            jax.ShapeDtypeStruct((frames, wide), BF16),
            jax.ShapeDtypeStruct((frames, width), BF16),
            jax.ShapeDtypeStruct((heads, frames), F32),
        ),
        in_specs=[pl.BlockSpec(memory_space=pltpu.SMEM)] + whole(6),
        out_specs=tuple(whole(4)),
        scratch_shapes=[
            pltpu.VMEM((frames, width), BF16),
            pltpu.VMEM((frames, width), BF16),
            pltpu.VMEM((width, frames), BF16),
        ],
        compiler_params=pltpu.CompilerParams(vmem_limit_bytes=16 << 20),
        cost_estimate=pl.CostEstimate(
            flops=pairs * 256 + 2 * frames * depth * wide, bytes_accessed=8 * frames * depth, transcendentals=pairs // 2
        ),
        name="attend",
    )(core, *pair, affine, w_in, bias, starts)


def attention_back(place, qkv, pair, context, w_out, w_in, starts, log_total, heads, ny, size):
    frames, wide = qkv.shape
    width = wide // 3
    depth = pair[0].shape[1]
    pairs = frames * frames * heads
    half = jax.ShapeDtypeStruct(pair[0].shape, BF16)
    return pl.pallas_call(
        functools.partial(attend_back, heads, ny, size),
        out_shape=(
            jax.ShapeDtypeStruct((frames, wide), BF16),
            half,
            half,
            jax.ShapeDtypeStruct((HEADS * width // heads, depth), BF16),
        ),
        in_specs=[pl.BlockSpec(memory_space=pltpu.SMEM)] + whole(8),
        out_specs=tuple(whole(4)),
        scratch_shapes=[pltpu.VMEM((frames, width), BF16)] * 4
        + [pltpu.VMEM((width, frames), BF16)]
        + [pltpu.VMEM((frames, width), F32)] * 3,
        compiler_params=pltpu.CompilerParams(vmem_limit_bytes=20 << 20),
        cost_estimate=pl.CostEstimate(
            flops=pairs * 640 + 2 * frames * depth * (wide + 2 * width),
            bytes_accessed=8 * frames * depth,
            transcendentals=pairs // 2,
        ),
        name="attend_back",
    )(jnp.concatenate([place.core, place.me]), qkv, *pair, context, w_out, w_in, starts, log_total)


def feed_forward_front(core, pair, upstream_all, w_expand, w_shrink, bias, size):
    frames, width = upstream_all.shape
    units = w_expand.shape[1]
    half = jax.ShapeDtypeStruct((frames // 2, width), BF16)
    inner = jax.ShapeDtypeStruct((frames, units), BF16)
    return pl.pallas_call(
        functools.partial(feed_forward, size),
        out_shape=(inner, inner, half, half, jax.ShapeDtypeStruct((frames, width), BF16)),
        in_specs=[pl.BlockSpec(memory_space=pltpu.SMEM)] + whole(6),
        out_specs=tuple(whole(5)),
        compiler_params=pltpu.CompilerParams(vmem_limit_bytes=16 << 20),
        cost_estimate=pl.CostEstimate(
            flops=8 * frames * width * units, bytes_accessed=10 * frames * width, transcendentals=frames * units
        ),
        name="feed_forward",
    )(core, *pair, upstream_all, w_expand, w_shrink, bias)


class Place:
    def __init__(self, ny):
        self.x, self.z, self.y, self.c = (lax.axis_index(a) for a in ("x", "z", "y", "c"))
        self.xy = jnp.reshape(self.x * ny + self.y, (1,)).astype(jnp.int32)
        self.core = jnp.reshape(self.c, (1,)).astype(jnp.int32)
        self.layer = jnp.reshape(self.z, (1,)).astype(jnp.int32)
        self.me = (self.core * 2) * ny + self.xy


def on_device(
    groups,
    ny,
    frames,
    cotangent,
    segment_lengths,
    position_offsets,
    first_gain,
    first_shift,
    inward_weight,
    query_bias,
    value_bias,
    outward_weight,
    outward_bias,
    second_gain,
    second_shift,
    expand_weight,
    expand_bias,
    shrink_weight,
    shrink_bias,
):
    place = Place(ny)
    x, z, y, c = place.x, place.z, place.y, place.c
    local_len, rows, width = frames.shape
    share = inward_weight.shape[0]
    layer = 4 * ny
    spread = NZ * ny * 2
    full_len = local_len * spread
    size = 2 * local_len
    hd = HEADS // layer
    hw = hd * (width // HEADS)
    hidden = expand_bias.shape[0]
    part = hidden // 2
    me = (c * 2 + x) * ny + y

    def sum_groups(value):
        return lax.psum(value, "g") if groups > 1 else value

    def exchange(value, axes):
        return lax.all_to_all(value, axes, 0, 0, tiled=True)

    fr = to_home(frames, place)
    table = jnp.stack([segment_lengths, position_offsets], axis=1)
    other_table = hop(table, "x")
    other_table, later_cotangent = after(other_table, cotangent)
    ct = to_home(later_cotangent, place)

    small = [first_gain, first_shift, query_bias, value_bias, outward_bias, second_gain, second_shift, shrink_bias]
    kinds = len(small) + hidden // share
    packed = jnp.concatenate([v[None] for v in small] + [expand_bias.reshape(-1, share)], axis=0)
    packed = packed.reshape(-1, 3 * hw)
    extra = packed.shape[0]
    packed = jnp.pad(packed, ((0, -extra % 8), (0, 0)))[None]
    in_cols = jnp.transpose(inward_weight.reshape(share, 3, 2, 2, ny, hw), (3, 4, 2, 0, 1, 5))
    in_cols = pick(in_cols, x).reshape(ny * 2, share, 3 * hw)
    in_cols = jnp.concatenate([in_cols, jnp.broadcast_to(packed, (ny * 2,) + packed.shape[1:])], axis=1)
    in_cols = jnp.broadcast_to(in_cols[None], (NZ,) + in_cols.shape).reshape((spread,) + in_cols.shape[1:])
    in_got = exchange(in_cols, SEQ)
    outward = lax.all_gather(outward_weight, SEQ, axis=0, tiled=True)

    row_x = jnp.where((z == 0) | (z == 3), 1, 0)
    table = pick(jnp.where(x == row_x, table, other_table), z >> 1)
    lengths, offsets = table[0], table[1]
    count = lengths.shape[0]
    starts = jnp.sum(
        jnp.where(jnp.arange(count)[None, :] < jnp.arange(count)[:, None], lengths[None, :], 0), axis=1
    )
    frame_ids = jnp.arange(full_len, dtype=jnp.int32)
    row_starts = jnp.max(jnp.where(starts[:, None] <= frame_ids[None, :], starts[:, None], 0), axis=0)[None, :]
    chunk = (2 * x + c) * ny + y
    mine = chunk * size + jnp.arange(size, dtype=jnp.int32)
    inside = (mine[:, None] >= starts[None, :]) & (mine[:, None] < (starts + lengths)[None, :])
    position = jnp.sum(jnp.where(inside, offsets[None, :] + mine[:, None] - starts[None, :], 0), axis=1)

    inputs = fr.astype(F32) + sin_cos(position, width)
    normal_one, scale_one = normalize(inputs)
    first_near = near_parts(normal_one.astype(BF16), ny)
    first_pair = both_cores(first_near, place)
    ct, *first_pair = after(ct, *first_pair)
    upstream_all = lax.all_gather(ct, LAYER, axis=0, tiled=True)

    *first_pair, in_got, later_shrink = after(*first_pair, in_got, shrink_weight)
    w_in = in_got[:, :share].reshape(width, 3 * hw)
    vectors = in_got[:, share : share + extra].reshape(spread, kinds, share).astype(F32)
    expand_b = vectors[:, len(small) :].reshape(NZ, ny, 2, 2, part)
    expand_b = pick(pick(pick(expand_b, y, 1), c, 1), x, 1).reshape(1, NZ * part)
    vectors = jnp.swapaxes(vectors[:, : len(small)], 0, 1).reshape(len(small), width)
    gain_one, shift_one, query_b, value_b, outward_b, gain_two, shift_two, shrink_b = (
        vectors[i : i + 1] for i in range(len(small))
    )
    qkv_bias = jnp.concatenate(
        [
            lax.dynamic_slice_in_dim(query_b, me * hw, hw, 1),
            jnp.zeros((1, hw), F32),
            lax.dynamic_slice_in_dim(value_b, me * hw, hw, 1),
        ],
        axis=1,
    )

    sh_rows = [lax.dynamic_slice_in_dim(later_shrink, x * part, part, 0)]
    sh_rows.append(hop(sh_rows[0], "z", NZ, 1))
    first_all, qkv, context_all, log_total = attention(
        place.core, first_pair, vectors[:2], w_in, qkv_bias, row_starts, hd, ny, size
    )
    context_all, *sh_rows = after(context_all, *sh_rows)
    context = exchange(context_all.reshape(layer, size, hw), LAYER)
    sh_rows.append(hop(sh_rows[0], "z", NZ, 2))
    context, later_expand, *sh_rows = after(context, expand_weight, *sh_rows)
    sh_rows.append(hop(sh_rows[0], "z", NZ, 3))
    ex_cols = pick(later_expand.reshape(share, NZ, ny, 2, 2, part), x, 4)
    ex_cols = jnp.transpose(ex_cols, (2, 3, 0, 1, 4)).reshape(1, ny * 2, share, NZ * part)
    ex_cols = jnp.broadcast_to(ex_cols, (NZ, ny * 2, share, NZ * part)).reshape(spread, share, NZ * part)
    w_expand = exchange(ex_cols, SEQ).reshape(width, NZ * part)

    context = jnp.swapaxes(context, 0, 1).reshape(size, width)
    middle = inputs + dot_nn(context, outward) + outward_b

    normal_two, scale_two = normalize(middle)
    second = (normal_two * gain_two + shift_two).astype(BF16)
    second_near = near_parts(second, ny)
    both = after(sh_rows[3], *second_near)
    sh_rows[3], second_near = both[0], both[1:]
    w_shrink = assemble(sh_rows, place.layer)
    second_pair = both_cores(second_near, place)
    active, before_grad, send, keep, out_part = feed_forward_front(
        place.core, second_pair, upstream_all, w_expand, w_shrink, expand_b, size
    )
    second_parts = list(fold(keep, hop(send, "c"), place, ny))
    second_parts[0], active, before_grad = after(second_parts[0], active, before_grad)
    second_grad = finish(second_parts, ny)
    expand_part, expand_b_sum, *shrink_part = feed_forward_weights(place, second_pair, upstream_all, active, before_grad)
    out_part = lax.psum_scatter(out_part, LAYER, scatter_dimension=0, tiled=True)
    shrink_got = [shrink_part[0], hop(shrink_part[1], "z", NZ, 1)]
    shrink_two = hop(shrink_part[2], "z", NZ, 2)
    second_grad, expand_part, *shrink_got = after(second_grad, expand_part, *shrink_got)
    expand_got = exchange(expand_part.reshape(spread, share, NZ * part), SEQ)

    upstream = ct.astype(F32)
    middle_part, gain_two_sum, shift_two_sum = normalize_back(normal_two, scale_two, gain_two, second_grad)
    middle_grad = upstream + middle_part
    low_middle = middle_grad.astype(BF16)
    both = after(shrink_two, *near_parts(low_middle, ny))
    low_near = both[1:]
    shrink_got += [both[0], hop(shrink_part[3], "z", NZ, 3)]
    low_pair = both_cores(low_near, place)
    expand_got, *low_pair = after(expand_got, *low_pair)
    w_out = lax.dynamic_slice_in_dim(outward, me * hw, hw, 0)
    mixed_grad, send, keep, outward_part = attention_back(
        place, qkv, low_pair, context_all, w_out, w_in, row_starts, log_total, hd, ny, size
    )
    got = hop(send, "c")
    inward_part = dot_tn(first_all, mixed_grad).astype(BF16)
    got, inward_part = after(got, inward_part)
    first_parts = list(fold(keep, got, place, ny))
    first_parts[0], inward_part = after(first_parts[0], inward_part)
    first_grad = finish(first_parts, ny)
    outward_part, out_part = after(outward_part, out_part)
    first_grad, expand_got, *shrink_got = after(first_grad, expand_got, *shrink_got)
    inward_got = exchange(inward_part.reshape(spread, share, 3 * hw), SEQ)
    input_part, gain_one_sum, shift_one_sum = normalize_back(normal_one, scale_one, vectors[:1], first_grad)
    both = [middle + out_part.astype(F32) + shrink_b, middle_grad + input_part]
    both = to_origin(jnp.concatenate(both, axis=1).astype(BF16), place)
    layer_output, frames_grad = both[:, :, :width], both[:, :, width:].astype(F32)

    split = width // 2
    shrink_sum = sum_groups(total_of(shrink_got))
    expand_sum = sum_groups(sum_sources(expand_got, NZ)).reshape(-1, NZ * part)
    if NZ * part == split:
        mine = stack_rows([expand_sum, shrink_sum[:, :split], shrink_sum[:, split:]]).astype(BF16)
        other = hop(mine, "x")
        deep = expand_sum.shape[0]
        shrink_pair = [jnp.concatenate([v[deep : deep + part], v[deep + part :]], axis=1) for v in (mine, other)]
        expand_pair = [v[:deep] for v in (mine, other)]
    else:
        shrink_pair = [shrink_sum.astype(BF16), hop(shrink_sum.astype(BF16), "x")]
        expand_pair = [expand_sum.astype(BF16), hop(expand_sum.astype(BF16), "x")]
    g_shrink = by_half(x, *shrink_pair, 0).astype(F32)
    g_expand = [v.reshape(ny, 2, 1, share, NZ, part) for v in expand_pair]
    g_expand = jnp.transpose(by_half(x, *g_expand, 2), (3, 4, 0, 1, 2, 5)).reshape(share, -1).astype(F32)

    g_outward = lax.psum_scatter(outward_part, SEQ, scatter_dimension=0, tiled=True)
    g_outward = sum_groups(g_outward.astype(F32) + hop(g_outward, "x").astype(F32))

    mixed_sum = jnp.sum(mixed_grad.astype(F32), axis=0)

    def from_heads(value):
        return lax.dynamic_update_slice(jnp.zeros((width,), F32), value, (me * hw,))

    flat = jnp.stack(
        [
            gain_one_sum,
            shift_one_sum,
            from_heads(mixed_sum[:hw]),
            from_heads(mixed_sum[2 * hw :]),
            jnp.sum(low_middle.astype(F32), axis=0),
            gain_two_sum,
            shift_two_sum,
            jnp.sum(upstream, axis=0),
        ]
    )
    small_len = len(small) * share
    sums = jnp.swapaxes(flat.reshape(len(small), spread, share), 0, 1).reshape(spread, small_len)
    spot = jnp.zeros((NZ, ny, 2, 2, part), F32)
    spot = lax.dynamic_update_slice(spot, expand_b_sum.reshape(NZ, 1, 1, 1, part), (0, y, c, x, 0))
    sums = jnp.concatenate([sums, spot.reshape(spread, hidden)], axis=1)
    inward_got, sums = after(inward_got, sums)
    sums = jnp.broadcast_to(sums[None], (2,) + sums.shape).reshape(2 * spread, -1, 128)
    total = sum_groups(jnp.sum(exchange(sums, ("x",) + SEQ), axis=0)).reshape(-1)
    g_small = total[:small_len].reshape(len(small), share)
    g_expand_b = total[small_len:]
    inward_sum = sum_groups(sum_sources(inward_got, NZ)).astype(BF16)
    g_inward = [v.reshape(ny, 2, 1, share, 3, hw) for v in (inward_sum, hop(inward_sum, "x"))]
    g_inward = jnp.transpose(by_half(x, *g_inward, 2), (3, 4, 1, 2, 0, 5)).reshape(share, -1).astype(F32)

    return (
        layer_output,
        frames_grad,
        g_small[0],
        g_small[1],
        g_inward,
        g_small[2],
        g_small[3],
        g_outward,
        g_small[4],
        g_small[5],
        g_small[6],
        g_expand,
        g_expand_b,
        g_shrink,
        g_small[7],
    )


def solution(mesh):
    batch, seq = mesh.shape["batch"], mesh.shape["seq"]
    groups, ny = batch // 2, seq // (2 * NZ)
    fine = Mesh(mesh.devices.reshape(groups, 2, NZ, ny, 2), ("g", "x", "z", "y", "c"))
    b, s = ("g", "x"), ("z", "y", "c")
    in_specs = (
        P(s, b, None),
        P(s, b, None),
        P(b, None),
        P(b, None),
        P(s),
        P(s),
        P(s, None),
        P(s),
        P(s),
        P(s, None),
        P(s),
        P(s),
        P(s),
        P(s, None),
        P(s),
        P(s, None),
        P(s),
    )
    out_specs = (
        P(s, b, None),
        P(s, b, None),
        P(s),
        P(s),
        P(s, None),
        P(s),
        P(s),
        P(s, None),
        P(s),
        P(s),
        P(s),
        P(s, None),
        P(s),
        P(s, None),
        P(s),
    )
    return jax.shard_map(
        functools.partial(on_device, groups, ny), mesh=fine, in_specs=in_specs, out_specs=out_specs, check_vma=False
    )
```

```python
import functools
import math

import jax
import jax.numpy as jnp
from jax import lax
from jax.experimental import pallas as pl
from jax.experimental.pallas import tpu as pltpu
from jax.sharding import Mesh, PartitionSpec as P


HEADS = 16
NZ = 4
NORM_EPS = 1e-05
NEG = -1e30
F32 = jnp.float32
BF16 = jnp.bfloat16
LAYER_OF_ROW = (1, 2, 0, 3)
SWAP = [(0, 1), (1, 0)]
LAYER = ("c", "x", "y")
SEQ = ("z", "y", "c")


def xor_perm(count, k):
    return [(i, i ^ k) for i in range(count)]


def hop(value, axis, count=2, k=1):
    return lax.ppermute(value, axis, xor_perm(count, k))


def pick(value, index, axis=0):
    return lax.dynamic_index_in_dim(value, index, axis, keepdims=False)


def stack_rows(parts):
    return jnp.concatenate(parts, axis=0)


def assemble_body(pieces, size, place_ref, *refs):
    out_ref = refs[pieces]
    for r in range(pieces):
        spot = place_ref[0] ^ r
        out_ref[pl.ds(pl.multiple_of(spot * size, size), size), :] = refs[r][...]


def assemble(parts, me):
    size, width = parts[0].shape
    count = len(parts)
    return pl.pallas_call(
        functools.partial(assemble_body, count, size),
        out_shape=jax.ShapeDtypeStruct((count * size, width), parts[0].dtype),
        in_specs=[pl.BlockSpec(memory_space=pltpu.SMEM)] + whole(count),
        out_specs=whole(1)[0],
        compiler_params=pltpu.CompilerParams(vmem_limit_bytes=4 << 20),
        cost_estimate=pl.CostEstimate(flops=0, bytes_accessed=4 * count * size * width, transcendentals=0),
        name="assemble",
    )(me, *parts)


def near_parts(block, ny):
    return [block] + [lax.ppermute(block, ("x", "y"), xor_perm(2 * ny, r)) for r in range(1, 2 * ny)]


def both_cores(parts, place):
    mine = assemble(parts, place.xy)
    return mine, hop(mine, "c")


def fold_body(count, size, place_ref, keep_ref, got_ref, own_ref, *out_refs):
    for r in range(count):
        spot = place_ref[0] ^ r
        here = pl.ds(pl.multiple_of(spot * size, size), size)
        value = keep_ref[here, :].astype(F32) + got_ref[here, :].astype(F32)
        if r == 0:
            own_ref[...] = value
        else:
            out_refs[r - 1][...] = value.astype(BF16)


def fold(keep, got, place, ny):
    rows, width = keep.shape
    count = 2 * ny
    size = rows // count
    return pl.pallas_call(
        functools.partial(fold_body, count, size),
        out_shape=[jax.ShapeDtypeStruct((size, width), F32)] + [jax.ShapeDtypeStruct((size, width), BF16)] * (count - 1),
        in_specs=[pl.BlockSpec(memory_space=pltpu.SMEM)] + whole(2),
        out_specs=whole(count),
        compiler_params=pltpu.CompilerParams(vmem_limit_bytes=4 << 20),
        cost_estimate=pl.CostEstimate(flops=count * size * width, bytes_accessed=6 * count * size * width, transcendentals=0),
        name="fold",
    )(place.xy, keep, got)


def finish(parts, ny):
    own = parts[0]
    for r in range(1, 2 * ny):
        own = own + lax.ppermute(parts[r], ("x", "y"), xor_perm(2 * ny, r)).astype(F32)
    return own


def total_of(parts):
    total = parts[0].astype(F32)
    for value in parts[1:]:
        total = total + value.astype(F32)
    return total


def rehome_flat(x, z, c):
    return (x * NZ + z) * 2 + c


def rehome_perm(k):
    return [
        (rehome_flat(x, z, c), rehome_flat(z >> 1, LAYER_OF_ROW[2 * x + (c ^ k)], z & 1))
        for x in range(2)
        for z in range(NZ)
        for c in range(2)
    ]


def to_home(block, place):
    got = [
        lax.ppermute(jnp.where(place.c == k, block[:, 0], block[:, 1]), ("x", "z", "c"), rehome_perm(k))
        for k in range(2)
    ]
    first = place.z < 2
    return stack_rows([jnp.where(first, got[0], got[1]), jnp.where(first, got[1], got[0])])


def to_origin(block, place):
    half = block.shape[0] // 2
    first = place.z < 2
    low, high = block[:half], block[half:]
    sent = [jnp.where(first, low, high), jnp.where(first, high, low)]
    got = [
        lax.ppermute(sent[k], ("x", "z", "c"), [(b, a) for a, b in rehome_perm(k)]) for k in range(2)
    ]
    return jnp.stack(
        [jnp.where(place.c == 0, got[0], got[1]), jnp.where(place.c == 0, got[1], got[0])], axis=1
    )


def after(first, *values):
    return lax.optimization_barrier((first, *values))


def sum_sources(value, count):
    return jnp.sum(value.reshape((count, -1) + value.shape[1:]).astype(F32), axis=0)


def by_half(x, mine, other, axis):
    return jnp.concatenate([jnp.where(x == 0, mine, other), jnp.where(x == 0, other, mine)], axis=axis)


def sin_cos(position, width):
    feature = jnp.arange(width, dtype=jnp.int32)
    rates = jnp.exp((feature // 2).astype(F32) * (-2.0 * math.log(10000.0) / width))
    angle = position.astype(F32)[:, None] * rates[None, :]
    turn = jnp.round(angle * (2.0 / math.pi))
    rest = angle - turn * 1.5703125
    rest = rest - turn * 0.00048375129699707031
    rest = rest - turn * 7.5497899548918861e-08
    quadrant = turn.astype(jnp.int32) + (feature % 2)[None, :]
    square = rest * rest
    sine = rest + rest * square * (
        -0.16666666641626524 + square * (0.008333329385889463 + square * (-0.00019839334836096632 + square * 2.718311493989822e-06))
    )
    cosine = 1.0 + square * (
        -0.49999999725103100 + square * (0.04166662332373906 + square * (-0.001388676377460993 + square * 2.439044879627741e-05))
    )
    value = jnp.where((quadrant & 1) == 0, sine, cosine)
    return jnp.where((quadrant & 2) == 0, value, -value)


def normalize(values):
    center = values - jnp.mean(values, axis=-1, keepdims=True)
    scale = lax.rsqrt(jnp.mean(center * center, axis=-1, keepdims=True) + NORM_EPS)
    return center * scale, scale


def normalize_back(normal, scale, gain, upstream):
    scaled = upstream * gain
    inner = scaled - jnp.mean(scaled, axis=-1, keepdims=True)
    inner = inner - normal * jnp.mean(scaled * normal, axis=-1, keepdims=True)
    return inner * scale, jnp.sum(upstream * normal, axis=0), jnp.sum(upstream, axis=0)


def dot_nt(a, b):
    return lax.dot_general(a, b, (((1,), (1,)), ((), ())), preferred_element_type=F32)


def dot_tn(a, b):
    return lax.dot_general(a, b, (((0,), (0,)), ((), ())), preferred_element_type=F32)


def dot_nn(a, b):
    return jnp.dot(a, b, preferred_element_type=F32)


BLOCK = 256


def chunk_owner(chunk, ny):
    outer, y = divmod(chunk, ny)
    return ((outer & 1) * 2 + (outer >> 1)) * ny + y


def lane_parts(heads, width):
    if heads == 1:
        return [None]
    lane = lax.broadcasted_iota(jnp.int32, (1, width), 1)
    return [(lane >= h * (width // heads)) & (lane < (h + 1) * (width // heads)) for h in range(heads)]


def only(value, lanes):
    return value if lanes is None else jnp.where(lanes, value, jnp.zeros_like(value))


def allowed_pairs(start_ref, first, total):
    key = lax.broadcasted_iota(jnp.int32, (total, BLOCK), 0)
    frame = first + lax.broadcasted_iota(jnp.int32, (total, BLOCK), 1)
    return (key >= start_ref[:, first : first + BLOCK]) & (key <= frame)


def chunk_rows(chunk, ny, size, core):
    half, spot = divmod(chunk_owner(chunk, ny), 2 * ny)
    return pl.ds(pl.multiple_of(((half ^ core) * (2 * ny) + spot) * size, size), size)


def attend(
    heads,
    ny,
    size,
    core_ref,
    mine_ref,
    other_ref,
    encoding_ref,
    affine_ref,
    weight_ref,
    bias_ref,
    start_ref,
    first_ref,
    qkv_ref,
    out_ref,
    log_ref,
    q_s,
    k_s,
    vt_s,
):
    count = 4 * ny
    width = q_s.shape[1]
    core = core_ref[0]
    step = 2 * size
    half = mine_ref.shape[0]
    for base, ref in ((0, mine_ref), (half, other_ref)):
        for start in range(0, half, step):
            rows = slice(base + start, base + start + step)
            normal, _ = normalize(ref[start : start + step, :].astype(F32) + encoding_ref[rows, :])
            value = (normal * affine_ref[0:1, :] + affine_ref[1:2, :]).astype(BF16)
            first_ref[rows, :] = value
            qkv_ref[rows, :] = (dot_nn(value, weight_ref[...]) + bias_ref[...]).astype(BF16)
    for chunk in range(count):
        rows = chunk_rows(chunk, ny, size, core)
        here = slice(chunk * size, (chunk + 1) * size)
        q_s[here, :] = qkv_ref[rows, 0:width] * 0.125
        k_s[here, :] = qkv_ref[rows, width : 2 * width]
        vt_s[:, here] = jnp.transpose(qkv_ref[rows, 2 * width : 3 * width].astype(F32)).astype(BF16)
    lanes = lane_parts(heads, width)
    each = width // heads
    for block in range(count * size // BLOCK):
        first = block * BLOCK
        total = first + BLOCK
        allowed = allowed_pairs(start_ref, first, total)
        q_block = q_s[first:total, :]
        contexts = []
        for h in range(heads):
            scores = dot_nt(k_s[0:total, :], only(q_block, lanes[h]))
            scores = jnp.where(allowed, scores, NEG)
            top = jnp.max(scores, axis=0, keepdims=True)
            weight = jnp.exp(scores - top)
            mass = jnp.sum(weight, axis=0, keepdims=True)
            part = dot_nn(vt_s[h * each : (h + 1) * each, 0:total], weight.astype(BF16))
            contexts.append(part / mass)
            log_ref[h : h + 1, first:total] = top + jnp.log(mass)
        context = contexts[0] if heads == 1 else jnp.concatenate(contexts, axis=0)
        context = jnp.transpose(context).astype(BF16)
        for sub in range(BLOCK // size):
            owner = chunk_owner(block * (BLOCK // size) + sub, ny)
            out_ref[owner * size : (owner + 1) * size, :] = context[sub * size : (sub + 1) * size]


def attend_back(
    heads,
    ny,
    size,
    core_ref,
    qkv_ref,
    mine_ref,
    other_ref,
    context_ref,
    outward_ref,
    weight_ref,
    start_ref,
    log_ref,
    out_ref,
    send_ref,
    keep_ref,
    outward_grad_ref,
    q_s,
    k_s,
    v_s,
    g_s,
    kt_s,
    dq_s,
    dk_s,
    dv_s,
):
    count = 4 * ny
    width = q_s.shape[1]
    core = core_ref[0]
    half = mine_ref.shape[0]
    step = 2 * size
    for base, ref in ((0, mine_ref), (half, other_ref)):
        for start in range(0, half, step):
            rows = slice(start, start + step)
            out_ref[base + start : base + start + step, 0:width] = dot_nt(ref[rows, :], outward_ref[...]).astype(BF16)
    for chunk in range(count):
        rows = chunk_rows(chunk, ny, size, core)
        here = slice(chunk * size, (chunk + 1) * size)
        q_s[here, :] = qkv_ref[rows, 0:width] * 0.125
        key = qkv_ref[rows, width : 2 * width]
        k_s[here, :] = key
        kt_s[:, here] = jnp.transpose(key.astype(F32)).astype(BF16)
        v_s[here, :] = qkv_ref[rows, 2 * width : 3 * width]
        g_s[here, :] = out_ref[rows, 0:width]
    dk_s[...] = jnp.zeros_like(dk_s)
    dv_s[...] = jnp.zeros_like(dv_s)
    lanes = lane_parts(heads, width)
    each = width // heads
    for block in range(count * size // BLOCK):
        first = block * BLOCK
        total = first + BLOCK
        allowed = allowed_pairs(start_ref, first, total)
        q_block, g_block = q_s[first:total, :], g_s[first:total, :]
        queries = []
        for h in range(heads):
            q_one, g_one = only(q_block, lanes[h]), only(g_block, lanes[h])
            scores = dot_nt(k_s[0:total, :], q_one)
            probs = jnp.where(allowed, jnp.exp(scores - log_ref[h : h + 1, first:total]), 0.0)
            prob_grad = dot_nt(v_s[0:total, :], g_one)
            delta = jnp.sum(probs * prob_grad, axis=0, keepdims=True)
            score_grad = (probs * (prob_grad - delta)).astype(BF16)
            dv_s[0:total, :] += dot_nn(probs.astype(BF16), g_one)
            dk_s[0:total, :] += dot_nn(score_grad, q_one)
            queries.append(dot_nn(kt_s[h * each : (h + 1) * each, 0:total], score_grad))
        query_grad = queries[0] if heads == 1 else jnp.concatenate(queries, axis=0)
        dq_s[first:total, :] = jnp.transpose(query_grad) * 0.125
    for chunk in range(count):
        rows = chunk_rows(chunk, ny, size, core)
        here = slice(chunk * size, (chunk + 1) * size)
        out_ref[rows, 0:width] = dq_s[here, :].astype(BF16)
        out_ref[rows, width : 2 * width] = dk_s[here, :].astype(BF16)
        out_ref[rows, 2 * width : 3 * width] = dv_s[here, :].astype(BF16)
    for ref, base in ((send_ref, half), (keep_ref, 0)):
        for start in range(0, half, step):
            rows = slice(base + start, base + start + step)
            ref[start : start + step, :] = dot_nt(out_ref[rows, :], weight_ref[...]).astype(BF16)
    near = context_ref[pl.ds(pl.multiple_of(core * half, half), half), :]
    far = context_ref[pl.ds(pl.multiple_of((1 - core) * half, half), half), :]
    total = dot_tn(near, mine_ref[...]) + dot_tn(far, other_ref[...])
    outward_grad_ref[...] = total.astype(BF16)


def feed_forward(
    size,
    core_ref,
    mine_ref,
    other_ref,
    up_ref,
    expand_ref,
    shrink_ref,
    bias_ref,
    active_ref,
    grad_ref,
    send_ref,
    keep_ref,
    result_ref,
):
    half = keep_ref.shape[0]
    step = 2 * size
    rate = math.sqrt(2.0 / math.pi)
    core = core_ref[0]
    for ref, source_ref, base, side in ((send_ref, other_ref, half, 1 - core), (keep_ref, mine_ref, 0, core)):
        for start in range(0, half, step):
            rows = slice(start, start + step)
            pair = slice(base + start, base + start + step)
            place = pl.ds(pl.multiple_of(side * half + start, step), step)
            before = dot_nn(source_ref[rows, :], expand_ref[...]) + bias_ref[...]
            upper = dot_nt(up_ref[place, :], shrink_ref[...])
            square = before * before
            inner = jnp.tanh(rate * (before + 0.044715 * before * square))
            plus = 0.5 * (1.0 + inner)
            active = (before * plus).astype(BF16)
            active_ref[pair, :] = active
            slope = plus + 0.5 * before * (1.0 - inner * inner) * (rate + rate * 3 * 0.044715 * square)
            lower = (upper * slope).astype(BF16)
            grad_ref[pair, :] = lower
            ref[rows, :] = dot_nt(lower, expand_ref[...]).astype(BF16)
            result_ref[place, :] = dot_nn(active, shrink_ref[...]).astype(BF16)


def weight_parts(
    part, place_ref, mine_ref, other_ref, up_ref, active_ref, grad_ref, expand_ref, bias_ref, *out_refs
):
    half = mine_ref.shape[0]
    core = place_ref[0]
    near = pl.ds(pl.multiple_of(core * half, half), half)
    far = pl.ds(pl.multiple_of((1 - core) * half, half), half)
    for r in range(NZ):
        units = pl.ds(pl.multiple_of((place_ref[1] ^ r) * part, part), part)
        total = dot_tn(active_ref[0:half, units], up_ref[near, :])
        total = total + dot_tn(active_ref[half : 2 * half, units], up_ref[far, :])
        if r < 2:
            out_refs[r][...] = total.astype(BF16)
        else:
            out_refs[2][(r - 2) * part : (r - 1) * part, :] = total.astype(BF16)
    width = mine_ref.shape[1]
    for start in range(0, width, width // 4):
        here = slice(start, start + width // 4)
        total = dot_tn(mine_ref[:, here], grad_ref[0:half, :]) + dot_tn(other_ref[:, here], grad_ref[half : 2 * half, :])
        expand_ref[here, :] = total.astype(BF16)
    bias_ref[...] = jnp.sum(grad_ref[...].astype(F32), axis=0, keepdims=True)


def feed_forward_weights(place, second, upstream_all, active, before_grad):
    frames, units = active.shape
    width, part = upstream_all.shape[1], units // NZ
    if part % 128:
        half = frames // 2
        up = stack_rows([lax.dynamic_slice_in_dim(upstream_all, i * half, half, 0) for i in (place.c, 1 - place.c)])
        value = dot_tn(active, up).astype(BF16).reshape(NZ, part, width)
        expand = dot_tn(stack_rows(second), before_grad).astype(BF16)
        bias = jnp.sum(before_grad.astype(F32), axis=0, keepdims=True)
        blocks = [pick(value, place.z ^ k) for k in range(NZ)]
        return [expand, bias, blocks[0], blocks[1], stack_rows(blocks[2:])]
    return pl.pallas_call(
        functools.partial(weight_parts, part),
        out_shape=[jax.ShapeDtypeStruct((width, units), BF16), jax.ShapeDtypeStruct((1, units), F32)]
        + [jax.ShapeDtypeStruct((n * part, width), BF16) for n in (1, 1, 2)],
        in_specs=[pl.BlockSpec(memory_space=pltpu.SMEM)] + whole(5),
        out_specs=whole(5),
        compiler_params=pltpu.CompilerParams(vmem_limit_bytes=16 << 20),
        cost_estimate=pl.CostEstimate(
            flops=4 * frames * width * units, bytes_accessed=8 * frames * width, transcendentals=0
        ),
        name="feed_forward_weights",
    )(jnp.concatenate([place.core, place.layer]), *second, upstream_all, active, before_grad)


def whole(count):
    return [pl.BlockSpec(memory_space=pltpu.VMEM)] * count


def attention(core, pair, encoding, affine, w_in, bias, starts, heads, ny, size):
    half, wide = pair[0].shape[0], w_in.shape[1]
    frames, depth, width = 2 * half, pair[0].shape[1], wide // 3
    pairs = frames * frames * heads
    return pl.pallas_call(
        functools.partial(attend, heads, ny, size),
        out_shape=(
            jax.ShapeDtypeStruct((frames, depth), BF16),
            jax.ShapeDtypeStruct((frames, wide), BF16),
            jax.ShapeDtypeStruct((frames, width), BF16),
            jax.ShapeDtypeStruct((heads, frames), F32),
        ),
        in_specs=[pl.BlockSpec(memory_space=pltpu.SMEM)] + whole(7),
        out_specs=tuple(whole(4)),
        scratch_shapes=[
            pltpu.VMEM((frames, width), BF16),
            pltpu.VMEM((frames, width), BF16),
            pltpu.VMEM((width, frames), BF16),
        ],
        compiler_params=pltpu.CompilerParams(vmem_limit_bytes=16 << 20),
        cost_estimate=pl.CostEstimate(
            flops=pairs * 256 + 2 * frames * depth * wide, bytes_accessed=8 * frames * depth, transcendentals=pairs // 2
        ),
        name="attend",
    )(core, *pair, encoding, affine, w_in, bias, starts)


def attention_back(place, qkv, pair, context, w_out, w_in, starts, log_total, heads, ny, size):
    frames, wide = qkv.shape
    width = wide // 3
    depth = pair[0].shape[1]
    pairs = frames * frames * heads
    half = jax.ShapeDtypeStruct(pair[0].shape, BF16)
    return pl.pallas_call(
        functools.partial(attend_back, heads, ny, size),
        out_shape=(
            jax.ShapeDtypeStruct((frames, wide), BF16),
            half,
            half,
            jax.ShapeDtypeStruct((width, depth), BF16),
        ),
        in_specs=[pl.BlockSpec(memory_space=pltpu.SMEM)] + whole(8),
        out_specs=tuple(whole(4)),
        scratch_shapes=[pltpu.VMEM((frames, width), BF16)] * 4
        + [pltpu.VMEM((width, frames), BF16)]
        + [pltpu.VMEM((frames, width), F32)] * 3,
        compiler_params=pltpu.CompilerParams(vmem_limit_bytes=20 << 20),
        cost_estimate=pl.CostEstimate(
            flops=pairs * 640 + 2 * frames * depth * (wide + 2 * width),
            bytes_accessed=8 * frames * depth,
            transcendentals=pairs // 2,
        ),
        name="attend_back",
    )(place.core, qkv, *pair, context, w_out, w_in, starts, log_total)


def feed_forward_front(core, pair, upstream_all, w_expand, w_shrink, bias, size):
    frames, width = upstream_all.shape
    units = w_expand.shape[1]
    half = jax.ShapeDtypeStruct((frames // 2, width), BF16)
    inner = jax.ShapeDtypeStruct((frames, units), BF16)
    return pl.pallas_call(
        functools.partial(feed_forward, size),
        out_shape=(inner, inner, half, half, jax.ShapeDtypeStruct((frames, width), BF16)),
        in_specs=[pl.BlockSpec(memory_space=pltpu.SMEM)] + whole(6),
        out_specs=tuple(whole(5)),
        compiler_params=pltpu.CompilerParams(vmem_limit_bytes=16 << 20),
        cost_estimate=pl.CostEstimate(
            flops=8 * frames * width * units, bytes_accessed=10 * frames * width, transcendentals=frames * units
        ),
        name="feed_forward",
    )(core, *pair, upstream_all, w_expand, w_shrink, bias)


class Place:
    def __init__(self, ny):
        self.x, self.z, self.y, self.c = (lax.axis_index(a) for a in ("x", "z", "y", "c"))
        self.xy = jnp.reshape(self.x * ny + self.y, (1,)).astype(jnp.int32)
        self.core = jnp.reshape(self.c, (1,)).astype(jnp.int32)
        self.layer = jnp.reshape(self.z, (1,)).astype(jnp.int32)


def on_device(
    groups,
    ny,
    frames,
    cotangent,
    segment_lengths,
    position_offsets,
    first_gain,
    first_shift,
    inward_weight,
    query_bias,
    value_bias,
    outward_weight,
    outward_bias,
    second_gain,
    second_shift,
    expand_weight,
    expand_bias,
    shrink_weight,
    shrink_bias,
):
    place = Place(ny)
    x, z, y, c = place.x, place.z, place.y, place.c
    local_len, rows, width = frames.shape
    share = inward_weight.shape[0]
    layer = 4 * ny
    spread = NZ * ny * 2
    full_len = local_len * spread
    size = 2 * local_len
    hd = HEADS // layer
    hw = hd * (width // HEADS)
    hidden = expand_bias.shape[0]
    part = hidden // 2
    me = (c * 2 + x) * ny + y

    def sum_groups(value):
        return lax.psum(value, "g") if groups > 1 else value

    def exchange(value, axes):
        return lax.all_to_all(value, axes, 0, 0, tiled=True)

    both = to_home(jnp.concatenate([frames, cotangent], axis=2), place)
    table = jnp.stack([segment_lengths, position_offsets], axis=1)
    other_table = hop(table, "x")
    other_table, later_inward = after(other_table, inward_weight)

    small = [first_gain, first_shift, query_bias, value_bias, outward_bias, second_gain, second_shift, shrink_bias]
    kinds = len(small) + hidden // share
    packed = jnp.concatenate([v[None] for v in small] + [expand_bias.reshape(-1, share)], axis=0)
    packed = packed.reshape(-1, 3 * hw)
    extra = packed.shape[0]
    packed = jnp.pad(packed, ((0, -extra % 8), (0, 0)))[None]
    in_cols = jnp.transpose(later_inward.reshape(share, 3, 2, 2, ny, hw), (3, 4, 2, 0, 1, 5))
    in_cols = pick(in_cols, x).reshape(ny * 2, share, 3 * hw)
    in_cols = jnp.concatenate([in_cols, jnp.broadcast_to(packed, (ny * 2,) + packed.shape[1:])], axis=1)
    in_cols = jnp.broadcast_to(in_cols[None], (NZ,) + in_cols.shape).reshape((spread,) + in_cols.shape[1:])
    in_got = exchange(in_cols, SEQ)

    row_x = jnp.where((z == 0) | (z == 3), 1, 0)
    table = pick(jnp.where(x == row_x, table, other_table), z >> 1)
    lengths, offsets = table[0], table[1]
    count = lengths.shape[0]
    starts = jnp.sum(
        jnp.where(jnp.arange(count)[None, :] < jnp.arange(count)[:, None], lengths[None, :], 0), axis=1
    )
    frame_ids = jnp.arange(full_len, dtype=jnp.int32)
    row_starts = jnp.max(jnp.where(starts[:, None] <= frame_ids[None, :], starts[:, None], 0), axis=0)[None, :]
    spot = jnp.arange(2 * ny)
    chunk = jnp.concatenate([(2 * (spot // ny) + i) * ny + spot % ny for i in (c, 1 - c)])
    mine = (chunk[:, None] * size + jnp.arange(size, dtype=jnp.int32)).reshape(-1)
    inside = (mine[:, None] >= starts[None, :]) & (mine[:, None] < (starts + lengths)[None, :])
    position = jnp.sum(jnp.where(inside, offsets[None, :] + mine[:, None] - starts[None, :], 0), axis=1)
    encoding = sin_cos(position, width)

    both, encoding, later_outward = after(both, encoding, outward_weight)
    fr, ct = both[:, :width], both[:, width:]
    outward = lax.all_gather(later_outward, SEQ, axis=0, tiled=True)
    mine = assemble(near_parts(fr, ny), place.xy)
    mine, in_got = after(mine, in_got)
    first_pair = [mine, hop(mine, "c")]
    upstream_all = lax.all_gather(ct, LAYER, axis=0, tiled=True)

    *first_pair, in_got, later_shrink = after(*first_pair, in_got, shrink_weight)
    w_in = in_got[:, :share].reshape(width, 3 * hw)
    vectors = in_got[:, share : share + extra].reshape(spread, kinds, share).astype(F32)
    expand_b = vectors[:, len(small) :].reshape(NZ, ny, 2, 2, part)
    expand_b = pick(pick(pick(expand_b, y, 1), c, 1), x, 1).reshape(1, NZ * part)
    vectors = jnp.swapaxes(vectors[:, : len(small)], 0, 1).reshape(len(small), width)
    gain_one, shift_one, query_b, value_b, outward_b, gain_two, shift_two, shrink_b = (
        vectors[i : i + 1] for i in range(len(small))
    )
    qkv_bias = jnp.concatenate(
        [
            lax.dynamic_slice_in_dim(query_b, me * hw, hw, 1),
            jnp.zeros((1, hw), F32),
            lax.dynamic_slice_in_dim(value_b, me * hw, hw, 1),
        ],
        axis=1,
    )

    sh_rows = [lax.dynamic_slice_in_dim(later_shrink, x * part, part, 0)]
    sh_rows.append(hop(sh_rows[0], "z", NZ, 1))
    first_all, qkv, context_all, log_total = attention(
        place.core, first_pair, encoding, vectors[:2], w_in, qkv_bias, row_starts, hd, ny, size
    )
    context_all, *sh_rows = after(context_all, *sh_rows)
    context = exchange(context_all.reshape(layer, size, hw), LAYER)
    sh_rows.append(hop(sh_rows[0], "z", NZ, 2))
    context, later_expand, *sh_rows = after(context, expand_weight, *sh_rows)
    sh_rows.append(hop(sh_rows[0], "z", NZ, 3))
    ex_cols = pick(later_expand.reshape(share, NZ, ny, 2, 2, part), x, 4)
    ex_cols = jnp.transpose(ex_cols, (2, 3, 0, 1, 4)).reshape(1, ny * 2, share, NZ * part)
    ex_cols = jnp.broadcast_to(ex_cols, (NZ, ny * 2, share, NZ * part)).reshape(spread, share, NZ * part)
    w_expand = exchange(ex_cols, SEQ).reshape(width, NZ * part)

    inputs = fr.astype(F32) + lax.dynamic_slice_in_dim(encoding, (x * ny + y) * size, size, 0)
    normal_one, scale_one = normalize(inputs)
    context = jnp.swapaxes(context, 0, 1).reshape(size, width)
    middle = inputs + dot_nn(context, outward) + outward_b

    normal_two, scale_two = normalize(middle)
    second = (normal_two * gain_two + shift_two).astype(BF16)
    second_near = near_parts(second, ny)
    both = after(sh_rows[3], *second_near)
    sh_rows[3], second_near = both[0], both[1:]
    w_shrink = assemble(sh_rows, place.layer)
    second_pair = both_cores(second_near, place)
    active, before_grad, send, keep, out_part = feed_forward_front(
        place.core, second_pair, upstream_all, w_expand, w_shrink, expand_b, size
    )
    second_parts = list(fold(keep, hop(send, "c"), place, ny))
    second_parts[0], active, before_grad = after(second_parts[0], active, before_grad)
    second_grad = finish(second_parts, ny)
    expand_part, expand_b_sum, *shrink_part = feed_forward_weights(place, second_pair, upstream_all, active, before_grad)
    out_part = lax.psum_scatter(out_part, LAYER, scatter_dimension=0, tiled=True)
    shrink_got = hop(shrink_part[2], "z", NZ, 2)

    upstream = ct.astype(F32)
    middle_part, gain_two_sum, shift_two_sum = normalize_back(normal_two, scale_two, gain_two, second_grad)
    middle_grad = upstream + middle_part
    low_middle = middle_grad.astype(BF16)
    both = after(shrink_got, expand_part, *near_parts(low_middle, ny))
    shrink_got, expand_part, low_near = both[0].reshape(2, part, width), both[1], both[2:]
    expand_got = exchange(expand_part.reshape(spread, share, NZ * part), SEQ)
    shrink_sum = [v.astype(F32) + got.astype(F32) for v, got in zip(shrink_part, shrink_got)]
    shrink_got = hop(shrink_sum[1].astype(BF16), "z", NZ, 1)
    low_pair = both_cores(low_near, place)
    w_out = lax.dynamic_slice_in_dim(outward, me * hw, hw, 0)
    mixed_grad, send, keep, outward_part = attention_back(
        place, qkv, low_pair, context_all, w_out, w_in, row_starts, log_total, hd, ny, size
    )
    got = hop(send, "c")
    inward_part = dot_tn(first_all, mixed_grad).astype(BF16)
    cut = outward_part.reshape(2, -1, width)
    far_cut = hop(pick(cut, 1 - c), "c")
    got, inward_part, expand_got, far_cut, out_part = after(got, inward_part, expand_got, far_cut, out_part)
    first_parts = list(fold(keep, got, place, ny))
    first_parts[0], inward_part = after(first_parts[0], inward_part)
    first_grad = finish(first_parts, ny)
    first_grad, expand_got, shrink_got = after(first_grad, expand_got, shrink_got)
    inward_got = exchange(inward_part.reshape(spread, share, 3 * hw), SEQ)
    input_part, gain_one_sum, shift_one_sum = normalize_back(normal_one, scale_one, vectors[:1], first_grad)
    late = (middle_grad + input_part).astype(BF16)
    late, out_part = after(late, out_part)
    frames_grad = to_origin(late, place).astype(F32)
    layer_output = to_origin((middle + out_part.astype(F32) + shrink_b).astype(BF16), place)

    split = width // 2
    shrink_sum = sum_groups(shrink_sum[0] + shrink_got.astype(F32))
    expand_sum = sum_groups(sum_sources(expand_got, NZ)).reshape(-1, NZ * part)
    if NZ * part == split:
        mine = stack_rows([expand_sum, shrink_sum[:, :split], shrink_sum[:, split:]]).astype(BF16)
        other = hop(mine, "x")
        deep = expand_sum.shape[0]
        shrink_pair = [jnp.concatenate([v[deep : deep + part], v[deep + part :]], axis=1) for v in (mine, other)]
        expand_pair = [v[:deep] for v in (mine, other)]
    else:
        shrink_pair = [shrink_sum.astype(BF16), hop(shrink_sum.astype(BF16), "x")]
        expand_pair = [expand_sum.astype(BF16), hop(expand_sum.astype(BF16), "x")]
    g_shrink = by_half(x, *shrink_pair, 0).astype(F32)
    g_expand = [v.reshape(ny, 2, 1, share, NZ, part) for v in expand_pair]
    g_expand = jnp.transpose(by_half(x, *g_expand, 2), (3, 4, 0, 1, 2, 5)).reshape(share, -1).astype(F32)

    if hd == 2 and ny == 2:
        line = by_half(c, pick(cut, c)[None], far_cut[None], 0)
        line = line.reshape(2, 1, share, 2, split)
        line = by_half(x, pick(line, x, 3), hop(pick(line, 1 - x, 3), "x"), 1)
        out_sum = lax.psum_scatter(line.reshape(NZ * share, split), "z", scatter_dimension=0, tiled=True)
        out_sum = sum_groups(out_sum.astype(F32)).astype(BF16)
        g_outward = by_half(x, out_sum, hop(out_sum, "x"), 1).astype(F32)
    else:
        cut = lax.dynamic_update_slice(jnp.zeros((width, width), BF16), outward_part, (me * hw, 0))
        g_outward = lax.psum_scatter(cut, SEQ, scatter_dimension=0, tiled=True)
        g_outward = lax.psum(g_outward.astype(F32), ("g", "x"))

    mixed_sum = jnp.sum(mixed_grad.astype(F32), axis=0)

    def from_heads(value):
        return lax.dynamic_update_slice(jnp.zeros((width,), F32), value, (me * hw,))

    flat = jnp.stack(
        [
            gain_one_sum,
            shift_one_sum,
            from_heads(mixed_sum[:hw]),
            from_heads(mixed_sum[2 * hw :]),
            jnp.sum(low_middle.astype(F32), axis=0),
            gain_two_sum,
            shift_two_sum,
            jnp.sum(upstream, axis=0),
        ]
    )
    small_len = len(small) * share
    sums = jnp.swapaxes(flat.reshape(len(small), spread, share), 0, 1).reshape(spread, small_len)
    spot = jnp.zeros((NZ, ny, 2, 2, part), F32)
    spot = lax.dynamic_update_slice(spot, expand_b_sum.reshape(NZ, 1, 1, 1, part), (0, y, c, x, 0))
    sums = jnp.concatenate([sums, spot.reshape(spread, hidden)], axis=1)
    inward_got, sums = after(inward_got, sums)
    sums = jnp.broadcast_to(sums[None], (2,) + sums.shape).reshape(2 * spread, -1, 128)
    total = sum_groups(jnp.sum(exchange(sums, ("x",) + SEQ), axis=0)).reshape(-1)
    g_small = total[:small_len].reshape(len(small), share)
    g_expand_b = total[small_len:]
    inward_sum = sum_groups(sum_sources(inward_got, NZ)).astype(BF16)
    g_inward = [v.reshape(ny, 2, 1, share, 3, hw) for v in (inward_sum, hop(inward_sum, "x"))]
    g_inward = jnp.transpose(by_half(x, *g_inward, 2), (3, 4, 1, 2, 0, 5)).reshape(share, -1).astype(F32)

    return (
        layer_output,
        frames_grad,
        g_small[0],
        g_small[1],
        g_inward,
        g_small[2],
        g_small[3],
        g_outward,
        g_small[4],
        g_small[5],
        g_small[6],
        g_expand,
        g_expand_b,
        g_shrink,
        g_small[7],
    )


def solution(mesh):
    batch, seq = mesh.shape["batch"], mesh.shape["seq"]
    groups, ny = batch // 2, seq // (2 * NZ)
    fine = Mesh(mesh.devices.reshape(groups, 2, NZ, ny, 2), ("g", "x", "z", "y", "c"))
    b, s = ("g", "x"), ("z", "y", "c")
    in_specs = (
        P(s, b, None),
        P(s, b, None),
        P(b, None),
        P(b, None),
        P(s),
        P(s),
        P(s, None),
        P(s),
        P(s),
        P(s, None),
        P(s),
        P(s),
        P(s),
        P(s, None),
        P(s),
        P(s, None),
        P(s),
    )
    out_specs = (
        P(s, b, None),
        P(s, b, None),
        P(s),
        P(s),
        P(s, None),
        P(s),
        P(s),
        P(s, None),
        P(s),
        P(s),
        P(s),
        P(s, None),
        P(s),
        P(s, None),
        P(s),
    )
    return jax.shard_map(
        functools.partial(on_device, groups, ny), mesh=fine, in_specs=in_specs, out_specs=out_specs, check_vma=False
    )
```

```python
import functools
import math

import jax
import jax.numpy as jnp
from jax import lax
from jax.experimental import pallas as pl
from jax.experimental.pallas import tpu as pltpu
from jax.sharding import Mesh, PartitionSpec as P


HEADS = 16
NZ = 4
SMALL_ROWS = 16
NORM_EPS = 1e-05
NEG = -1e30
F32 = jnp.float32
BF16 = jnp.bfloat16
LAYER_OF_ROW = (1, 2, 0, 3)
SWAP = [(0, 1), (1, 0)]
LAYER = ("c", "x", "y")
SEQ = ("z", "y", "c")


def xor_perm(count, k):
    return [(i, i ^ k) for i in range(count)]


def hop(value, axis, count=2, k=1):
    return lax.ppermute(value, axis, xor_perm(count, k))


def pick(value, index, axis=0):
    return lax.dynamic_index_in_dim(value, index, axis, keepdims=False)


def stack_rows(parts):
    return jnp.concatenate(parts, axis=0)


def assemble_body(pieces, size, place_ref, *refs):
    out_ref = refs[pieces]
    for r in range(pieces):
        spot = place_ref[0] ^ r
        out_ref[pl.ds(pl.multiple_of(spot * size, size), size), :] = refs[r][...]


def assemble(parts, me):
    size, width = parts[0].shape
    count = len(parts)
    return pl.pallas_call(
        functools.partial(assemble_body, count, size),
        out_shape=jax.ShapeDtypeStruct((count * size, width), parts[0].dtype),
        in_specs=[pl.BlockSpec(memory_space=pltpu.SMEM)] + whole(count),
        out_specs=whole(1)[0],
        compiler_params=pltpu.CompilerParams(vmem_limit_bytes=4 << 20),
        cost_estimate=pl.CostEstimate(flops=0, bytes_accessed=4 * count * size * width, transcendentals=0),
        name="assemble",
    )(me, *parts)


def near_parts(block, ny):
    return [block] + [lax.ppermute(block, ("x", "y"), xor_perm(2 * ny, r)) for r in range(1, 2 * ny)]


def both_cores(parts, place):
    mine = assemble(parts, place.xy)
    return mine, hop(mine, "c")


def fold_body(count, size, place_ref, keep_ref, got_ref, own_ref, *out_refs):
    for r in range(count):
        spot = place_ref[0] ^ r
        here = pl.ds(pl.multiple_of(spot * size, size), size)
        value = keep_ref[here, :].astype(F32) + got_ref[here, :].astype(F32)
        if r == 0:
            own_ref[...] = value
        else:
            out_refs[r - 1][...] = value.astype(BF16)


def fold(keep, got, place, ny):
    rows, width = keep.shape
    count = 2 * ny
    size = rows // count
    return pl.pallas_call(
        functools.partial(fold_body, count, size),
        out_shape=[jax.ShapeDtypeStruct((size, width), F32)] + [jax.ShapeDtypeStruct((size, width), BF16)] * (count - 1),
        in_specs=[pl.BlockSpec(memory_space=pltpu.SMEM)] + whole(2),
        out_specs=whole(count),
        compiler_params=pltpu.CompilerParams(vmem_limit_bytes=4 << 20),
        cost_estimate=pl.CostEstimate(flops=count * size * width, bytes_accessed=6 * count * size * width, transcendentals=0),
        name="fold",
    )(place.xy, keep, got)


def finish(parts, ny):
    own = parts[0]
    for r in range(1, 2 * ny):
        own = own + lax.ppermute(parts[r], ("x", "y"), xor_perm(2 * ny, r)).astype(F32)
    return own


def fold_columns(value, units):
    return stack_rows([value[:, i : i + units] for i in range(0, value.shape[1], units)])


def unfold_columns(value, count):
    size = value.shape[0] // count
    return jnp.concatenate([value[i * size : (i + 1) * size] for i in range(count)], axis=1)


def collect_inward_body(share, place_ref, *refs):
    weight_ref, small_ref = refs[NZ:]
    deep = share + SMALL_ROWS
    lines = refs[0].shape[0] // deep
    for r in range(NZ):
        base = (place_ref[0] ^ r) * lines
        for i in range(lines):
            start = i * deep
            rows = pl.ds(pl.multiple_of((base + i) * share, share), share)
            weight_ref[rows, :] = refs[r][start : start + share, :]
            rows = pl.ds(pl.multiple_of((base + i) * SMALL_ROWS, SMALL_ROWS), SMALL_ROWS)
            small_ref[rows, :] = refs[r][start + share : start + deep, :]


def collect_inward(parts, place, share):
    rows, width = parts[0].shape
    lines = NZ * rows // (share + SMALL_ROWS)
    return pl.pallas_call(
        functools.partial(collect_inward_body, share),
        out_shape=[jax.ShapeDtypeStruct((lines * n, width), BF16) for n in (share, SMALL_ROWS)],
        in_specs=[pl.BlockSpec(memory_space=pltpu.SMEM)] + whole(NZ),
        out_specs=whole(2),
        compiler_params=pltpu.CompilerParams(vmem_limit_bytes=4 << 20),
        cost_estimate=pl.CostEstimate(flops=0, bytes_accessed=16 * rows * width, transcendentals=0),
        name="collect_inward",
    )(place.layer, *parts)


def collect_hidden_body(place_ref, *refs):
    expand_ref, shrink_ref = refs[NZ:]
    quarter = expand_ref.shape[0] // NZ
    part, units = shrink_ref.shape[0] // NZ, expand_ref.shape[1]
    for r in range(NZ):
        spot = place_ref[0] ^ r
        expand_ref[pl.ds(pl.multiple_of(spot * quarter, quarter), quarter), :] = refs[r][0:quarter, :]
        for i in range(shrink_ref.shape[1] // units):
            rows = pl.ds(pl.multiple_of(spot * part, part), part)
            start = quarter + i * part
            shrink_ref[rows, i * units : (i + 1) * units] = refs[r][start : start + part, :]


def collect_hidden(parts, place, width):
    rows, units = parts[0].shape
    return pl.pallas_call(
        collect_hidden_body,
        out_shape=[jax.ShapeDtypeStruct((width, units), BF16), jax.ShapeDtypeStruct((units, width), BF16)],
        in_specs=[pl.BlockSpec(memory_space=pltpu.SMEM)] + whole(NZ),
        out_specs=whole(2),
        compiler_params=pltpu.CompilerParams(vmem_limit_bytes=4 << 20),
        cost_estimate=pl.CostEstimate(flops=0, bytes_accessed=16 * rows * units, transcendentals=0),
        name="collect_hidden",
    )(place.layer, *parts)


def rehome_flat(x, z, c):
    return (x * NZ + z) * 2 + c


def rehome_perm(k):
    return [
        (rehome_flat(x, z, c), rehome_flat(z >> 1, LAYER_OF_ROW[2 * x + (c ^ k)], z & 1))
        for x in range(2)
        for z in range(NZ)
        for c in range(2)
    ]


def to_home(block, place):
    got = [
        lax.ppermute(jnp.where(place.c == k, block[:, 0], block[:, 1]), ("x", "z", "c"), rehome_perm(k))
        for k in range(2)
    ]
    first = place.z < 2
    return stack_rows([jnp.where(first, got[0], got[1]), jnp.where(first, got[1], got[0])])


def to_origin(block, place):
    half = block.shape[0] // 2
    first = place.z < 2
    low, high = block[:half], block[half:]
    sent = [jnp.where(first, low, high), jnp.where(first, high, low)]
    got = [
        lax.ppermute(sent[k], ("x", "z", "c"), [(b, a) for a, b in rehome_perm(k)]) for k in range(2)
    ]
    return jnp.stack(
        [jnp.where(place.c == 0, got[0], got[1]), jnp.where(place.c == 0, got[1], got[0])], axis=1
    )


def after(first, *values):
    return lax.optimization_barrier((first, *values))


def sum_sources(value, count):
    return jnp.sum(value.reshape((count, -1) + value.shape[1:]).astype(F32), axis=0)


def by_half(x, mine, other, axis):
    return jnp.concatenate([jnp.where(x == 0, mine, other), jnp.where(x == 0, other, mine)], axis=axis)


def sin_cos(position, width):
    feature = jnp.arange(width, dtype=jnp.int32)
    rates = jnp.exp((feature // 2).astype(F32) * (-2.0 * math.log(10000.0) / width))
    angle = position.astype(F32)[:, None] * rates[None, :]
    turn = jnp.round(angle * (2.0 / math.pi))
    rest = angle - turn * 1.5703125
    rest = rest - turn * 0.00048375129699707031
    rest = rest - turn * 7.5497899548918861e-08
    quadrant = turn.astype(jnp.int32) + (feature % 2)[None, :]
    square = rest * rest
    sine = rest + rest * square * (
        -0.16666666641626524 + square * (0.008333329385889463 + square * (-0.00019839334836096632 + square * 2.718311493989822e-06))
    )
    cosine = 1.0 + square * (
        -0.49999999725103100 + square * (0.04166662332373906 + square * (-0.001388676377460993 + square * 2.439044879627741e-05))
    )
    value = jnp.where((quadrant & 1) == 0, sine, cosine)
    return jnp.where((quadrant & 2) == 0, value, -value)


def normalize(values):
    center = values - jnp.mean(values, axis=-1, keepdims=True)
    scale = lax.rsqrt(jnp.mean(center * center, axis=-1, keepdims=True) + NORM_EPS)
    return center * scale, scale


def normalize_back(normal, scale, gain, upstream):
    scaled = upstream * gain
    inner = scaled - jnp.mean(scaled, axis=-1, keepdims=True)
    inner = inner - normal * jnp.mean(scaled * normal, axis=-1, keepdims=True)
    return inner * scale, jnp.sum(upstream * normal, axis=0), jnp.sum(upstream, axis=0)


def dot_nt(a, b):
    return lax.dot_general(a, b, (((1,), (1,)), ((), ())), preferred_element_type=F32)


def dot_tn(a, b):
    return lax.dot_general(a, b, (((0,), (0,)), ((), ())), preferred_element_type=F32)


def dot_nn(a, b):
    return jnp.dot(a, b, preferred_element_type=F32)


BLOCK = 256


def chunk_owner(chunk, ny):
    outer, y = divmod(chunk, ny)
    return ((outer & 1) * 2 + (outer >> 1)) * ny + y


def lane_parts(heads, width):
    if heads == 1:
        return [None]
    lane = lax.broadcasted_iota(jnp.int32, (1, width), 1)
    return [(lane >= h * (width // heads)) & (lane < (h + 1) * (width // heads)) for h in range(heads)]


def only(value, lanes):
    return value if lanes is None else jnp.where(lanes, value, jnp.zeros_like(value))


def allowed_pairs(start_ref, first, total):
    key = lax.broadcasted_iota(jnp.int32, (total, BLOCK), 0)
    frame = first + lax.broadcasted_iota(jnp.int32, (total, BLOCK), 1)
    return (key >= start_ref[:, first : first + BLOCK]) & (key <= frame)


def chunk_rows(chunk, ny, size, core):
    half, spot = divmod(chunk_owner(chunk, ny), 2 * ny)
    return pl.ds(pl.multiple_of(((half ^ core) * (2 * ny) + spot) * size, size), size)


def attend(
    heads,
    ny,
    size,
    core_ref,
    mine_ref,
    other_ref,
    encoding_ref,
    affine_ref,
    weight_ref,
    bias_ref,
    start_ref,
    first_ref,
    qkv_ref,
    out_ref,
    log_ref,
    q_s,
    k_s,
    vt_s,
):
    count = 4 * ny
    width = q_s.shape[1]
    core = core_ref[0]
    step = 2 * size
    half = mine_ref.shape[0]
    for base, ref in ((0, mine_ref), (half, other_ref)):
        for start in range(0, half, step):
            rows = slice(base + start, base + start + step)
            normal, _ = normalize(ref[start : start + step, :].astype(F32) + encoding_ref[rows, :])
            value = (normal * affine_ref[0:1, :] + affine_ref[1:2, :]).astype(BF16)
            first_ref[rows, :] = value
            qkv_ref[rows, :] = (dot_nn(value, weight_ref[...]) + bias_ref[...]).astype(BF16)
    for chunk in range(count):
        rows = chunk_rows(chunk, ny, size, core)
        here = slice(chunk * size, (chunk + 1) * size)
        q_s[here, :] = qkv_ref[rows, 0:width] * 0.125
        k_s[here, :] = qkv_ref[rows, width : 2 * width]
        vt_s[:, here] = jnp.transpose(qkv_ref[rows, 2 * width : 3 * width].astype(F32)).astype(BF16)
    lanes = lane_parts(heads, width)
    each = width // heads
    for block in range(count * size // BLOCK):
        first = block * BLOCK
        total = first + BLOCK
        allowed = allowed_pairs(start_ref, first, total)
        q_block = q_s[first:total, :]
        contexts = []
        for h in range(heads):
            scores = dot_nt(k_s[0:total, :], only(q_block, lanes[h]))
            scores = jnp.where(allowed, scores, NEG)
            top = jnp.max(scores, axis=0, keepdims=True)
            weight = jnp.exp(scores - top)
            mass = jnp.sum(weight, axis=0, keepdims=True)
            part = dot_nn(vt_s[h * each : (h + 1) * each, 0:total], weight.astype(BF16))
            contexts.append(part / mass)
            log_ref[h : h + 1, first:total] = top + jnp.log(mass)
        context = contexts[0] if heads == 1 else jnp.concatenate(contexts, axis=0)
        context = jnp.transpose(context).astype(BF16)
        for sub in range(BLOCK // size):
            owner = chunk_owner(block * (BLOCK // size) + sub, ny)
            out_ref[owner * size : (owner + 1) * size, :] = context[sub * size : (sub + 1) * size]


def attend_back(
    heads,
    ny,
    size,
    core_ref,
    qkv_ref,
    mine_ref,
    other_ref,
    context_ref,
    outward_ref,
    weight_ref,
    start_ref,
    log_ref,
    out_ref,
    send_ref,
    keep_ref,
    outward_grad_ref,
    q_s,
    k_s,
    v_s,
    g_s,
    kt_s,
    dq_s,
    dk_s,
    dv_s,
):
    count = 4 * ny
    width = q_s.shape[1]
    core = core_ref[0]
    half = mine_ref.shape[0]
    step = 2 * size
    for base, ref in ((0, mine_ref), (half, other_ref)):
        for start in range(0, half, step):
            rows = slice(start, start + step)
            out_ref[base + start : base + start + step, 0:width] = dot_nt(ref[rows, :], outward_ref[...]).astype(BF16)
    for chunk in range(count):
        rows = chunk_rows(chunk, ny, size, core)
        here = slice(chunk * size, (chunk + 1) * size)
        q_s[here, :] = qkv_ref[rows, 0:width] * 0.125
        key = qkv_ref[rows, width : 2 * width]
        k_s[here, :] = key
        kt_s[:, here] = jnp.transpose(key.astype(F32)).astype(BF16)
        v_s[here, :] = qkv_ref[rows, 2 * width : 3 * width]
        g_s[here, :] = out_ref[rows, 0:width]
    dk_s[...] = jnp.zeros_like(dk_s)
    dv_s[...] = jnp.zeros_like(dv_s)
    lanes = lane_parts(heads, width)
    each = width // heads
    for block in range(count * size // BLOCK):
        first = block * BLOCK
        total = first + BLOCK
        allowed = allowed_pairs(start_ref, first, total)
        q_block, g_block = q_s[first:total, :], g_s[first:total, :]
        queries = []
        for h in range(heads):
            q_one, g_one = only(q_block, lanes[h]), only(g_block, lanes[h])
            scores = dot_nt(k_s[0:total, :], q_one)
            probs = jnp.where(allowed, jnp.exp(scores - log_ref[h : h + 1, first:total]), 0.0)
            prob_grad = dot_nt(v_s[0:total, :], g_one)
            delta = jnp.sum(probs * prob_grad, axis=0, keepdims=True)
            score_grad = (probs * (prob_grad - delta)).astype(BF16)
            dv_s[0:total, :] += dot_nn(probs.astype(BF16), g_one)
            dk_s[0:total, :] += dot_nn(score_grad, q_one)
            queries.append(dot_nn(kt_s[h * each : (h + 1) * each, 0:total], score_grad))
        query_grad = queries[0] if heads == 1 else jnp.concatenate(queries, axis=0)
        dq_s[first:total, :] = jnp.transpose(query_grad) * 0.125
    for chunk in range(count):
        rows = chunk_rows(chunk, ny, size, core)
        here = slice(chunk * size, (chunk + 1) * size)
        out_ref[rows, 0:width] = dq_s[here, :].astype(BF16)
        out_ref[rows, width : 2 * width] = dk_s[here, :].astype(BF16)
        out_ref[rows, 2 * width : 3 * width] = dv_s[here, :].astype(BF16)
    for ref, base in ((send_ref, half), (keep_ref, 0)):
        for start in range(0, half, step):
            rows = slice(base + start, base + start + step)
            ref[start : start + step, :] = dot_nt(out_ref[rows, :], weight_ref[...]).astype(BF16)
    near = context_ref[pl.ds(pl.multiple_of(core * half, half), half), :]
    far = context_ref[pl.ds(pl.multiple_of((1 - core) * half, half), half), :]
    total = dot_tn(near, mine_ref[...]) + dot_tn(far, other_ref[...])
    outward_grad_ref[...] = total.astype(BF16)


def feed_forward(
    size,
    core_ref,
    mine_ref,
    other_ref,
    up_ref,
    expand_ref,
    shrink_ref,
    bias_ref,
    active_ref,
    grad_ref,
    send_ref,
    keep_ref,
    result_ref,
):
    half = keep_ref.shape[0]
    step = 2 * size
    rate = math.sqrt(2.0 / math.pi)
    core = core_ref[0]
    for ref, source_ref, base, side in ((send_ref, other_ref, half, 1 - core), (keep_ref, mine_ref, 0, core)):
        for start in range(0, half, step):
            rows = slice(start, start + step)
            pair = slice(base + start, base + start + step)
            place = pl.ds(pl.multiple_of(side * half + start, step), step)
            before = dot_nn(source_ref[rows, :], expand_ref[...]) + bias_ref[...]
            upper = dot_nt(up_ref[place, :], shrink_ref[...])
            square = before * before
            inner = jnp.tanh(rate * (before + 0.044715 * before * square))
            plus = 0.5 * (1.0 + inner)
            active = (before * plus).astype(BF16)
            active_ref[pair, :] = active
            slope = plus + 0.5 * before * (1.0 - inner * inner) * (rate + rate * 3 * 0.044715 * square)
            lower = (upper * slope).astype(BF16)
            grad_ref[pair, :] = lower
            ref[rows, :] = dot_nt(lower, expand_ref[...]).astype(BF16)
            result_ref[place, :] = dot_nn(active, shrink_ref[...]).astype(BF16)


def weight_parts(part, place_ref, mine_ref, other_ref, up_ref, active_ref, grad_ref, bias_ref, *out_refs):
    half, width = mine_ref.shape
    core = place_ref[0]
    near = pl.ds(pl.multiple_of(core * half, half), half)
    far = pl.ds(pl.multiple_of((1 - core) * half, half), half)
    quarter, all_units = width // NZ, NZ * part
    for r in range(NZ):
        spot = place_ref[1] ^ r
        ref = out_refs[r]
        here = pl.ds(pl.multiple_of(spot * quarter, quarter), quarter)
        total = dot_tn(mine_ref[:, here], grad_ref[0:half, :]) + dot_tn(other_ref[:, here], grad_ref[half : 2 * half, :])
        ref[0:quarter, :] = total.astype(BF16)
        units = pl.ds(pl.multiple_of(spot * part, part), part)
        total = dot_tn(active_ref[0:half, units], up_ref[near, :])
        total = (total + dot_tn(active_ref[half : 2 * half, units], up_ref[far, :])).astype(BF16)
        for i in range(width // all_units):
            start = quarter + i * part
            ref[start : start + part, :] = total[:, i * all_units : (i + 1) * all_units]
    bias_ref[...] = jnp.sum(grad_ref[...].astype(F32), axis=0, keepdims=True)


def feed_forward_weights(place, second, upstream_all, active, before_grad):
    frames, units = active.shape
    width, part = upstream_all.shape[1], units // NZ
    quarter = width // NZ
    if part % 128:
        half = frames // 2
        up = stack_rows([lax.dynamic_slice_in_dim(upstream_all, i * half, half, 0) for i in (place.c, 1 - place.c)])
        shrink = dot_tn(active, up).astype(BF16).reshape(NZ, part, width)
        expand = dot_tn(stack_rows(second), before_grad).astype(BF16).reshape(NZ, quarter, units)
        bias = jnp.sum(before_grad.astype(F32), axis=0, keepdims=True)
        blocks = [
            stack_rows([pick(expand, place.z ^ k), fold_columns(pick(shrink, place.z ^ k), units)]) for k in range(NZ)
        ]
        return [bias] + blocks
    return pl.pallas_call(
        functools.partial(weight_parts, part),
        out_shape=[jax.ShapeDtypeStruct((1, units), F32)]
        + [jax.ShapeDtypeStruct((2 * quarter, units), BF16)] * NZ,
        in_specs=[pl.BlockSpec(memory_space=pltpu.SMEM)] + whole(5),
        out_specs=whole(1 + NZ),
        compiler_params=pltpu.CompilerParams(vmem_limit_bytes=16 << 20),
        cost_estimate=pl.CostEstimate(
            flops=4 * frames * width * units, bytes_accessed=8 * frames * width, transcendentals=0
        ),
        name="feed_forward_weights",
    )(jnp.concatenate([place.core, place.layer]), *second, upstream_all, active, before_grad)


def whole(count):
    return [pl.BlockSpec(memory_space=pltpu.VMEM)] * count


def attention(core, pair, encoding, affine, w_in, bias, starts, heads, ny, size):
    half, wide = pair[0].shape[0], w_in.shape[1]
    frames, depth, width = 2 * half, pair[0].shape[1], wide // 3
    pairs = frames * frames * heads
    return pl.pallas_call(
        functools.partial(attend, heads, ny, size),
        out_shape=(
            jax.ShapeDtypeStruct((frames, depth), BF16),
            jax.ShapeDtypeStruct((frames, wide), BF16),
            jax.ShapeDtypeStruct((frames, width), BF16),
            jax.ShapeDtypeStruct((heads, frames), F32),
        ),
        in_specs=[pl.BlockSpec(memory_space=pltpu.SMEM)] + whole(7),
        out_specs=tuple(whole(4)),
        scratch_shapes=[
            pltpu.VMEM((frames, width), BF16),
            pltpu.VMEM((frames, width), BF16),
            pltpu.VMEM((width, frames), BF16),
        ],
        compiler_params=pltpu.CompilerParams(vmem_limit_bytes=16 << 20),
        cost_estimate=pl.CostEstimate(
            flops=pairs * 256 + 2 * frames * depth * wide, bytes_accessed=8 * frames * depth, transcendentals=pairs // 2
        ),
        name="attend",
    )(core, *pair, encoding, affine, w_in, bias, starts)


def attention_back(place, qkv, pair, context, w_out, w_in, starts, log_total, heads, ny, size):
    frames, wide = qkv.shape
    width = wide // 3
    depth = pair[0].shape[1]
    pairs = frames * frames * heads
    half = jax.ShapeDtypeStruct(pair[0].shape, BF16)
    return pl.pallas_call(
        functools.partial(attend_back, heads, ny, size),
        out_shape=(
            jax.ShapeDtypeStruct((frames, wide), BF16),
            half,
            half,
            jax.ShapeDtypeStruct((width, depth), BF16),
        ),
        in_specs=[pl.BlockSpec(memory_space=pltpu.SMEM)] + whole(8),
        out_specs=tuple(whole(4)),
        scratch_shapes=[pltpu.VMEM((frames, width), BF16)] * 4
        + [pltpu.VMEM((width, frames), BF16)]
        + [pltpu.VMEM((frames, width), F32)] * 3,
        compiler_params=pltpu.CompilerParams(vmem_limit_bytes=20 << 20),
        cost_estimate=pl.CostEstimate(
            flops=pairs * 640 + 2 * frames * depth * (wide + 2 * width),
            bytes_accessed=8 * frames * depth,
            transcendentals=pairs // 2,
        ),
        name="attend_back",
    )(place.core, qkv, *pair, context, w_out, w_in, starts, log_total)


def feed_forward_front(core, pair, upstream_all, w_expand, w_shrink, bias, size):
    frames, width = upstream_all.shape
    units = w_expand.shape[1]
    half = jax.ShapeDtypeStruct((frames // 2, width), BF16)
    inner = jax.ShapeDtypeStruct((frames, units), BF16)
    return pl.pallas_call(
        functools.partial(feed_forward, size),
        out_shape=(inner, inner, half, half, jax.ShapeDtypeStruct((frames, width), BF16)),
        in_specs=[pl.BlockSpec(memory_space=pltpu.SMEM)] + whole(6),
        out_specs=tuple(whole(5)),
        compiler_params=pltpu.CompilerParams(vmem_limit_bytes=16 << 20),
        cost_estimate=pl.CostEstimate(
            flops=8 * frames * width * units, bytes_accessed=10 * frames * width, transcendentals=frames * units
        ),
        name="feed_forward",
    )(core, *pair, upstream_all, w_expand, w_shrink, bias)


class Place:
    def __init__(self, ny):
        self.x, self.z, self.y, self.c = (lax.axis_index(a) for a in ("x", "z", "y", "c"))
        self.xy = jnp.reshape(self.x * ny + self.y, (1,)).astype(jnp.int32)
        self.core = jnp.reshape(self.c, (1,)).astype(jnp.int32)
        self.layer = jnp.reshape(self.z, (1,)).astype(jnp.int32)


def on_device(
    groups,
    ny,
    frames,
    cotangent,
    segment_lengths,
    position_offsets,
    first_gain,
    first_shift,
    inward_weight,
    query_bias,
    value_bias,
    outward_weight,
    outward_bias,
    second_gain,
    second_shift,
    expand_weight,
    expand_bias,
    shrink_weight,
    shrink_bias,
):
    place = Place(ny)
    x, z, y, c = place.x, place.z, place.y, place.c
    local_len, rows, width = frames.shape
    share = inward_weight.shape[0]
    layer = 4 * ny
    spread = NZ * ny * 2
    full_len = local_len * spread
    size = 2 * local_len
    hd = HEADS // layer
    hw = hd * (width // HEADS)
    hidden = expand_bias.shape[0]
    part = hidden // 2
    me = (c * 2 + x) * ny + y

    def sum_groups(value):
        return lax.psum(value, "g") if groups > 1 else value

    def exchange(value, axes):
        return lax.all_to_all(value, axes, 0, 0, tiled=True)

    both = to_home(jnp.concatenate([frames, cotangent], axis=2), place)
    table = jnp.stack([segment_lengths, position_offsets], axis=1)
    other_table = hop(table, "x")
    other_table, later_inward = after(other_table, inward_weight)

    small = [first_gain, first_shift, query_bias, value_bias, outward_bias, second_gain, second_shift, shrink_bias]
    kinds = len(small) + hidden // share
    units = NZ * part
    packed = jnp.concatenate([v[None] for v in small] + [expand_bias.reshape(-1, share)], axis=0)
    packed = packed.reshape(-1, 3 * hw)
    extra = packed.shape[0]
    packed = jnp.pad(packed, ((0, SMALL_ROWS - extra), (0, units)))[None]
    in_cols = jnp.transpose(later_inward.reshape(share, 3, 2, 2, ny, hw), (3, 4, 2, 0, 1, 5))
    in_cols = pick(in_cols, x).reshape(ny * 2, share, 3 * hw)
    ex_cols = pick(expand_weight.reshape(share, NZ, ny, 2, 2, part), x, 4)
    ex_cols = jnp.transpose(ex_cols, (2, 3, 0, 1, 4)).reshape(ny * 2, share, units)
    columns = jnp.concatenate([in_cols, ex_cols], axis=2)
    columns = jnp.concatenate([columns, jnp.broadcast_to(packed, (ny * 2,) + packed.shape[1:])], axis=1)
    columns = exchange(columns, ("y", "c"))

    row_x = jnp.where((z == 0) | (z == 3), 1, 0)
    table = pick(jnp.where(x == row_x, table, other_table), z >> 1)
    lengths, offsets = table[0], table[1]
    count = lengths.shape[0]
    starts = jnp.sum(
        jnp.where(jnp.arange(count)[None, :] < jnp.arange(count)[:, None], lengths[None, :], 0), axis=1
    )
    frame_ids = jnp.arange(full_len, dtype=jnp.int32)
    row_starts = jnp.max(jnp.where(starts[:, None] <= frame_ids[None, :], starts[:, None], 0), axis=0)[None, :]
    spot = jnp.arange(2 * ny)
    chunk = jnp.concatenate([(2 * (spot // ny) + i) * ny + spot % ny for i in (c, 1 - c)])
    mine = (chunk[:, None] * size + jnp.arange(size, dtype=jnp.int32)).reshape(-1)
    inside = (mine[:, None] >= starts[None, :]) & (mine[:, None] < (starts + lengths)[None, :])
    position = jnp.sum(jnp.where(inside, offsets[None, :] + mine[:, None] - starts[None, :], 0), axis=1)
    encoding = sin_cos(position, width)

    both, encoding, later_outward, columns = after(both, encoding, outward_weight, columns)
    fr, ct = both[:, :width], both[:, width:]
    outward = lax.all_gather(later_outward, SEQ, axis=0, tiled=True)
    in_part = columns[:, :, : 3 * hw].reshape(-1, 3 * hw)
    in_parts = [in_part] + [hop(in_part, "z", NZ, k) for k in range(1, NZ)]
    sh_rows = lax.dynamic_slice_in_dim(shrink_weight, x * part, part, 0)
    ff_part = stack_rows([columns[:, :share, 3 * hw :].reshape(-1, units), fold_columns(sh_rows, units)])
    mine = assemble(near_parts(fr, ny), place.xy)
    mine, *in_parts = after(mine, *in_parts)
    first_pair = [mine, hop(mine, "c")]
    w_in, small_rows = collect_inward(in_parts, place, share)
    upstream_all = lax.all_gather(ct, LAYER, axis=0, tiled=True)

    *first_pair, ff_part = after(*first_pair, ff_part)
    ff_parts = [ff_part, hop(ff_part, "z", NZ, 1)]
    vectors = small_rows.reshape(spread, SMALL_ROWS, 3 * hw)[:, :extra].reshape(spread, kinds, share).astype(F32)
    expand_b = vectors[:, len(small) :].reshape(NZ, ny, 2, 2, part)
    expand_b = pick(pick(pick(expand_b, y, 1), c, 1), x, 1).reshape(1, NZ * part)
    vectors = jnp.swapaxes(vectors[:, : len(small)], 0, 1).reshape(len(small), width)
    gain_one, shift_one, query_b, value_b, outward_b, gain_two, shift_two, shrink_b = (
        vectors[i : i + 1] for i in range(len(small))
    )
    qkv_bias = jnp.concatenate(
        [
            lax.dynamic_slice_in_dim(query_b, me * hw, hw, 1),
            jnp.zeros((1, hw), F32),
            lax.dynamic_slice_in_dim(value_b, me * hw, hw, 1),
        ],
        axis=1,
    )

    first_all, qkv, context_all, log_total = attention(
        place.core, first_pair, encoding, vectors[:2], w_in, qkv_bias, row_starts, hd, ny, size
    )
    context_all, *ff_parts = after(context_all, *ff_parts)
    context = exchange(context_all.reshape(layer, size, hw), LAYER)
    ff_parts.append(hop(ff_parts[0], "z", NZ, 2))
    context, ff_part = after(context, ff_parts[0])
    ff_parts.append(hop(ff_part, "z", NZ, 3))

    inputs = fr.astype(F32) + lax.dynamic_slice_in_dim(encoding, (x * ny + y) * size, size, 0)
    normal_one, scale_one = normalize(inputs)
    context = jnp.swapaxes(context, 0, 1).reshape(size, width)
    middle = inputs + dot_nn(context, outward) + outward_b

    normal_two, scale_two = normalize(middle)
    second = (normal_two * gain_two + shift_two).astype(BF16)
    second, ff_parts[2] = after(second, ff_parts[2])
    ff_parts[3], *second_near = after(ff_parts[3], *near_parts(second, ny))
    second_pair = both_cores(second_near, place)
    w_expand, w_shrink = collect_hidden(ff_parts, place, width)
    active, before_grad, send, keep, out_part = feed_forward_front(
        place.core, second_pair, upstream_all, w_expand, w_shrink, expand_b, size
    )
    second_parts = list(fold(keep, hop(send, "c"), place, ny))
    second_parts[0], active, before_grad = after(second_parts[0], active, before_grad)
    second_grad = finish(second_parts, ny)
    expand_b_sum, *hidden_part = feed_forward_weights(place, second_pair, upstream_all, active, before_grad)
    out_part = lax.psum_scatter(out_part, LAYER, scatter_dimension=0, tiled=True)
    hidden_got = hop(hidden_part[2], "z", NZ, 2)
    second_grad, *hidden_part = after(second_grad, *hidden_part)

    upstream = ct.astype(F32)
    middle_part, gain_two_sum, shift_two_sum = normalize_back(normal_two, scale_two, gain_two, second_grad)
    middle_grad = upstream + middle_part
    low_middle = middle_grad.astype(BF16)
    hidden_got, hidden_far, *low_near = after(hidden_got, hidden_part[3], *near_parts(low_middle, ny))
    hidden_far = hop(hidden_far, "z", NZ, 2)
    low_pair = both_cores(low_near, place)
    w_out = lax.dynamic_slice_in_dim(outward, me * hw, hw, 0)
    mixed_grad, send, keep, outward_part = attention_back(
        place, qkv, low_pair, context_all, w_out, w_in, row_starts, log_total, hd, ny, size
    )
    got = hop(send, "c")
    cut = outward_part.reshape(2, -1, width)
    far_cut = hop(pick(cut, 1 - c), "c")
    got, far_cut, out_part = after(got, far_cut, out_part)
    first_parts = list(fold(keep, got, place, ny))
    first_parts[0], mixed_late = after(first_parts[0], mixed_grad)
    inward_part = dot_tn(first_all, mixed_late).astype(BF16)
    first_grad = finish(first_parts, ny)
    first_grad, hidden_far, far_cut = after(first_grad, hidden_far, far_cut)
    hidden_send = (hidden_part[1].astype(F32) + hidden_far.astype(F32)).astype(BF16)
    hidden_sum = hidden_part[0].astype(F32) + hidden_got.astype(F32)
    hidden_got = hop(hidden_send, "z", NZ, 1)
    inward_got = exchange(inward_part.reshape(spread, share, 3 * hw), SEQ)
    input_part, gain_one_sum, shift_one_sum = normalize_back(normal_one, scale_one, vectors[:1], first_grad)
    late = (middle_grad + input_part).astype(BF16)
    late, out_part = after(late, out_part)
    frames_grad = to_origin(late, place).astype(F32)
    layer_output = to_origin((middle + out_part.astype(F32) + shrink_b).astype(BF16), place)

    split = width // 2
    hidden_sum = sum_groups(hidden_sum + hidden_got.astype(F32)).astype(BF16)
    line = hidden_sum[: width // NZ].reshape(ny, 2, share, units)
    if ny == 2:
        line = by_half(c, pick(line, c, 1)[:, None], hop(pick(line, 1 - c, 1), "c")[:, None], 1)
        line = by_half(y, pick(line, y)[None], hop(pick(line, 1 - y), "y")[None], 0)
    else:
        line = exchange(line.reshape(ny * 2, share, units), ("y", "c"))
    mine = stack_rows([line.reshape(-1, units), hidden_sum[width // NZ :]])
    other = hop(mine, "x")

    def full_hidden(other):
        pair = [unfold_columns(v[width // NZ :], width // units) for v in (mine, other)]
        g_shrink = by_half(x, *pair, 0).astype(F32)
        pair = [v[: width // NZ].reshape(ny, 2, 1, share, NZ, part) for v in (mine, other)]
        return g_shrink, jnp.transpose(by_half(x, *pair, 2), (3, 4, 0, 1, 2, 5)).reshape(share, -1).astype(F32)

    if hd == 2 and ny == 2:
        line = by_half(c, pick(cut, c)[None], far_cut[None], 0)
        line = line.reshape(2, 1, share, 2, split)
        line = by_half(x, pick(line, x, 3), hop(pick(line, 1 - x, 3), "x"), 1)
        out_sum = lax.psum_scatter(line.reshape(NZ * share, split), "z", scatter_dimension=0, tiled=True)
        out_sum = sum_groups(out_sum.astype(F32)).astype(BF16)
        g_outward = by_half(x, out_sum, hop(out_sum, "x"), 1).astype(F32)
    else:
        cut = lax.dynamic_update_slice(jnp.zeros((width, width), BF16), outward_part, (me * hw, 0))
        g_outward = lax.psum_scatter(cut, SEQ, scatter_dimension=0, tiled=True)
        g_outward = lax.psum(g_outward.astype(F32), ("g", "x"))

    mixed_sum = jnp.sum(mixed_grad.astype(F32), axis=0)

    def from_heads(value):
        return lax.dynamic_update_slice(jnp.zeros((width,), F32), value, (me * hw,))

    flat = jnp.stack(
        [
            gain_one_sum,
            shift_one_sum,
            from_heads(mixed_sum[:hw]),
            from_heads(mixed_sum[2 * hw :]),
            jnp.sum(low_middle.astype(F32), axis=0),
            gain_two_sum,
            shift_two_sum,
            jnp.sum(upstream, axis=0),
        ]
    )
    small_len = len(small) * share
    sums = jnp.swapaxes(flat.reshape(len(small), spread, share), 0, 1).reshape(spread, small_len)
    spot = jnp.zeros((NZ, ny, 2, 2, part), F32)
    spot = lax.dynamic_update_slice(spot, expand_b_sum.reshape(NZ, 1, 1, 1, part), (0, y, c, x, 0))
    sums = jnp.concatenate([sums, spot.reshape(spread, hidden)], axis=1)
    inward_got, sums = after(inward_got, sums)
    sums = jnp.broadcast_to(sums[None], (2,) + sums.shape).reshape(2 * spread, -1, 128)
    total = sum_groups(jnp.sum(exchange(sums, ("x",) + SEQ), axis=0)).reshape(-1)
    total, other = after(total, other)
    g_shrink, g_expand = full_hidden(other)
    g_small = total[:small_len].reshape(len(small), share)
    g_expand_b = total[small_len:]
    inward_sum = sum_groups(sum_sources(inward_got, NZ)).astype(BF16)
    g_inward = [v.reshape(ny, 2, 1, share, 3, hw) for v in (inward_sum, hop(inward_sum, "x"))]
    g_inward = jnp.transpose(by_half(x, *g_inward, 2), (3, 4, 1, 2, 0, 5)).reshape(share, -1).astype(F32)

    return (
        layer_output,
        frames_grad,
        g_small[0],
        g_small[1],
        g_inward,
        g_small[2],
        g_small[3],
        g_outward,
        g_small[4],
        g_small[5],
        g_small[6],
        g_expand,
        g_expand_b,
        g_shrink,
        g_small[7],
    )


def solution(mesh):
    batch, seq = mesh.shape["batch"], mesh.shape["seq"]
    groups, ny = batch // 2, seq // (2 * NZ)
    fine = Mesh(mesh.devices.reshape(groups, 2, NZ, ny, 2), ("g", "x", "z", "y", "c"))
    b, s = ("g", "x"), ("z", "y", "c")
    in_specs = (
        P(s, b, None),
        P(s, b, None),
        P(b, None),
        P(b, None),
        P(s),
        P(s),
        P(s, None),
        P(s),
        P(s),
        P(s, None),
        P(s),
        P(s),
        P(s),
        P(s, None),
        P(s),
        P(s, None),
        P(s),
    )
    out_specs = (
        P(s, b, None),
        P(s, b, None),
        P(s),
        P(s),
        P(s, None),
        P(s),
        P(s),
        P(s, None),
        P(s),
        P(s),
        P(s),
        P(s, None),
        P(s),
        P(s, None),
        P(s),
    )
    return jax.shard_map(
        functools.partial(on_device, groups, ny), mesh=fine, in_specs=in_specs, out_specs=out_specs, check_vma=False
    )
```

```python
import functools
import math

import jax
import jax.numpy as jnp
from jax import lax
from jax.experimental import pallas as pl
from jax.experimental.pallas import tpu as pltpu
from jax.sharding import Mesh, PartitionSpec as P


HEADS = 16
NZ = 4
SMALL_ROWS = 16
NORM_EPS = 1e-05
NEG = -1e30
F32 = jnp.float32
BF16 = jnp.bfloat16
LAYER_OF_ROW = (1, 2, 0, 3)
SWAP = [(0, 1), (1, 0)]
LAYER = ("c", "x", "y")
SEQ = ("z", "y", "c")


def xor_perm(count, k):
    return [(i, i ^ k) for i in range(count)]


def hop(value, axis, count=2, k=1):
    return lax.ppermute(value, axis, xor_perm(count, k))


def pick(value, index, axis=0):
    return lax.dynamic_index_in_dim(value, index, axis, keepdims=False)


def stack_rows(parts):
    return jnp.concatenate(parts, axis=0)


def assemble_body(pieces, size, place_ref, *refs):
    out_ref = refs[pieces]
    for r in range(pieces):
        spot = place_ref[0] ^ r
        out_ref[pl.ds(pl.multiple_of(spot * size, size), size), :] = refs[r][...]


def assemble(parts, me):
    size, width = parts[0].shape
    count = len(parts)
    return pl.pallas_call(
        functools.partial(assemble_body, count, size),
        out_shape=jax.ShapeDtypeStruct((count * size, width), parts[0].dtype),
        in_specs=[pl.BlockSpec(memory_space=pltpu.SMEM)] + whole(count),
        out_specs=whole(1)[0],
        compiler_params=pltpu.CompilerParams(vmem_limit_bytes=4 << 20),
        cost_estimate=pl.CostEstimate(flops=0, bytes_accessed=4 * count * size * width, transcendentals=0),
        name="assemble",
    )(me, *parts)


def assemble_pair_body(pieces, size, place_ref, *refs):
    left_ref, right_ref = refs[pieces:]
    width = left_ref.shape[1]
    for r in range(pieces):
        rows = pl.ds(pl.multiple_of((place_ref[0] ^ r) * size, size), size)
        left_ref[rows, :] = refs[r][:, 0:width]
        right_ref[rows, :] = refs[r][:, width : 2 * width]


def assemble_pair(parts, me):
    size, width = parts[0].shape
    count = len(parts)
    return pl.pallas_call(
        functools.partial(assemble_pair_body, count, size),
        out_shape=[jax.ShapeDtypeStruct((count * size, width // 2), parts[0].dtype)] * 2,
        in_specs=[pl.BlockSpec(memory_space=pltpu.SMEM)] + whole(count),
        out_specs=whole(2),
        compiler_params=pltpu.CompilerParams(vmem_limit_bytes=4 << 20),
        cost_estimate=pl.CostEstimate(flops=0, bytes_accessed=4 * count * size * width, transcendentals=0),
        name="assemble_pair",
    )(me, *parts)


def near_parts(block, ny):
    return [block] + [lax.ppermute(block, ("x", "y"), xor_perm(2 * ny, r)) for r in range(1, 2 * ny)]


def both_cores(parts, place):
    mine = assemble(parts, place.xy)
    return mine, hop(mine, "c")


def fold_body(count, size, place_ref, keep_ref, got_ref, own_ref, *out_refs):
    for r in range(count):
        spot = place_ref[0] ^ r
        here = pl.ds(pl.multiple_of(spot * size, size), size)
        value = keep_ref[here, :].astype(F32) + got_ref[here, :].astype(F32)
        if r == 0:
            own_ref[...] = value
        else:
            out_refs[r - 1][...] = value.astype(BF16)


def fold(keep, got, place, ny):
    rows, width = keep.shape
    count = 2 * ny
    size = rows // count
    return pl.pallas_call(
        functools.partial(fold_body, count, size),
        out_shape=[jax.ShapeDtypeStruct((size, width), F32)] + [jax.ShapeDtypeStruct((size, width), BF16)] * (count - 1),
        in_specs=[pl.BlockSpec(memory_space=pltpu.SMEM)] + whole(2),
        out_specs=whole(count),
        compiler_params=pltpu.CompilerParams(vmem_limit_bytes=4 << 20),
        cost_estimate=pl.CostEstimate(flops=count * size * width, bytes_accessed=6 * count * size * width, transcendentals=0),
        name="fold",
    )(place.xy, keep, got)


def finish(parts, ny):
    own = parts[0]
    for r in range(1, 2 * ny):
        own = own + lax.ppermute(parts[r], ("x", "y"), xor_perm(2 * ny, r)).astype(F32)
    return own


def fold_columns(value, units):
    return stack_rows([value[:, i : i + units] for i in range(0, value.shape[1], units)])


def unfold_columns(value, count):
    size = value.shape[0] // count
    return jnp.concatenate([value[i * size : (i + 1) * size] for i in range(count)], axis=1)


def collect_inward_body(share, place_ref, *refs):
    weight_ref, small_ref = refs[NZ:]
    deep = share + SMALL_ROWS
    lines = refs[0].shape[0] // deep
    for r in range(NZ):
        base = (place_ref[0] ^ r) * lines
        for i in range(lines):
            start = i * deep
            rows = pl.ds(pl.multiple_of((base + i) * share, share), share)
            weight_ref[rows, :] = refs[r][start : start + share, :]
            rows = pl.ds(pl.multiple_of((base + i) * SMALL_ROWS, SMALL_ROWS), SMALL_ROWS)
            small_ref[rows, :] = refs[r][start + share : start + deep, :]


def collect_inward(parts, place, share):
    rows, width = parts[0].shape
    lines = NZ * rows // (share + SMALL_ROWS)
    return pl.pallas_call(
        functools.partial(collect_inward_body, share),
        out_shape=[jax.ShapeDtypeStruct((lines * n, width), BF16) for n in (share, SMALL_ROWS)],
        in_specs=[pl.BlockSpec(memory_space=pltpu.SMEM)] + whole(NZ),
        out_specs=whole(2),
        compiler_params=pltpu.CompilerParams(vmem_limit_bytes=4 << 20),
        cost_estimate=pl.CostEstimate(flops=0, bytes_accessed=16 * rows * width, transcendentals=0),
        name="collect_inward",
    )(place.layer, *parts)


def collect_hidden_body(parts_ref, expand_ref, shrink_ref):
    quarter = expand_ref.shape[0] // NZ
    part, units = shrink_ref.shape[0] // NZ, expand_ref.shape[1]
    for r in range(NZ):
        expand_ref[r * quarter : (r + 1) * quarter, :] = parts_ref[r, 0:quarter, :]
        for i in range(shrink_ref.shape[1] // units):
            start = quarter + i * part
            here = slice(r * part, (r + 1) * part)
            shrink_ref[here, i * units : (i + 1) * units] = parts_ref[r, start : start + part, :]


def collect_hidden(parts, width):
    units = parts.shape[2]
    return pl.pallas_call(
        collect_hidden_body,
        out_shape=[jax.ShapeDtypeStruct((width, units), BF16), jax.ShapeDtypeStruct((units, width), BF16)],
        in_specs=whole(1),
        out_specs=whole(2),
        compiler_params=pltpu.CompilerParams(vmem_limit_bytes=4 << 20),
        cost_estimate=pl.CostEstimate(flops=0, bytes_accessed=4 * parts.size, transcendentals=0),
        name="collect_hidden",
    )(parts)


def rehome_flat(x, z, c):
    return (x * NZ + z) * 2 + c


def rehome_perm(k):
    return [
        (rehome_flat(x, z, c), rehome_flat(z >> 1, LAYER_OF_ROW[2 * x + (c ^ k)], z & 1))
        for x in range(2)
        for z in range(NZ)
        for c in range(2)
    ]


def to_home(block, place):
    got = [
        lax.ppermute(jnp.where(place.c == k, block[:, 0], block[:, 1]), ("x", "z", "c"), rehome_perm(k))
        for k in range(2)
    ]
    first = place.z < 2
    return stack_rows([jnp.where(first, got[0], got[1]), jnp.where(first, got[1], got[0])])


def to_origin(block, place):
    half = block.shape[0] // 2
    first = place.z < 2
    low, high = block[:half], block[half:]
    sent = [jnp.where(first, low, high), jnp.where(first, high, low)]
    got = [
        lax.ppermute(sent[k], ("x", "z", "c"), [(b, a) for a, b in rehome_perm(k)]) for k in range(2)
    ]
    return jnp.stack(
        [jnp.where(place.c == 0, got[0], got[1]), jnp.where(place.c == 0, got[1], got[0])], axis=1
    )


def after(first, *values):
    return lax.optimization_barrier((first, *values))


def sum_sources(value, count):
    return jnp.sum(value.reshape((count, -1) + value.shape[1:]).astype(F32), axis=0)


def by_half(x, mine, other, axis):
    return jnp.concatenate([jnp.where(x == 0, mine, other), jnp.where(x == 0, other, mine)], axis=axis)


def sin_cos(position, width):
    feature = jnp.arange(width, dtype=jnp.int32)
    rates = jnp.exp((feature // 2).astype(F32) * (-2.0 * math.log(10000.0) / width))
    angle = position.astype(F32)[:, None] * rates[None, :]
    turn = jnp.round(angle * (2.0 / math.pi))
    rest = angle - turn * 1.5703125
    rest = rest - turn * 0.00048375129699707031
    rest = rest - turn * 7.5497899548918861e-08
    quadrant = turn.astype(jnp.int32) + (feature % 2)[None, :]
    square = rest * rest
    sine = rest + rest * square * (
        -0.16666666641626524 + square * (0.008333329385889463 + square * (-0.00019839334836096632 + square * 2.718311493989822e-06))
    )
    cosine = 1.0 + square * (
        -0.49999999725103100 + square * (0.04166662332373906 + square * (-0.001388676377460993 + square * 2.439044879627741e-05))
    )
    value = jnp.where((quadrant & 1) == 0, sine, cosine)
    return jnp.where((quadrant & 2) == 0, value, -value)


def normalize(values):
    center = values - jnp.mean(values, axis=-1, keepdims=True)
    scale = lax.rsqrt(jnp.mean(center * center, axis=-1, keepdims=True) + NORM_EPS)
    return center * scale, scale


def normalize_back(normal, scale, gain, upstream):
    scaled = upstream * gain
    inner = scaled - jnp.mean(scaled, axis=-1, keepdims=True)
    inner = inner - normal * jnp.mean(scaled * normal, axis=-1, keepdims=True)
    return inner * scale, jnp.sum(upstream * normal, axis=0), jnp.sum(upstream, axis=0)


def dot_nt(a, b):
    return lax.dot_general(a, b, (((1,), (1,)), ((), ())), preferred_element_type=F32)


def dot_tn(a, b):
    return lax.dot_general(a, b, (((0,), (0,)), ((), ())), preferred_element_type=F32)


def dot_nn(a, b):
    return jnp.dot(a, b, preferred_element_type=F32)


BLOCK = 256


def chunk_owner(chunk, ny):
    outer, y = divmod(chunk, ny)
    return ((outer & 1) * 2 + (outer >> 1)) * ny + y


def lane_parts(heads, width):
    if heads == 1:
        return [None]
    lane = lax.broadcasted_iota(jnp.int32, (1, width), 1)
    return [(lane >= h * (width // heads)) & (lane < (h + 1) * (width // heads)) for h in range(heads)]


def only(value, lanes):
    return value if lanes is None else jnp.where(lanes, value, jnp.zeros_like(value))


def allowed_pairs(start_ref, first, total):
    key = lax.broadcasted_iota(jnp.int32, (total, BLOCK), 0)
    frame = first + lax.broadcasted_iota(jnp.int32, (total, BLOCK), 1)
    return (key >= start_ref[:, first : first + BLOCK]) & (key <= frame)


def chunk_rows(chunk, ny, size, core):
    half, spot = divmod(chunk_owner(chunk, ny), 2 * ny)
    return pl.ds(pl.multiple_of(((half ^ core) * (2 * ny) + spot) * size, size), size)


def attend(
    heads,
    ny,
    size,
    core_ref,
    mine_ref,
    other_ref,
    encoding_ref,
    affine_ref,
    weight_ref,
    bias_ref,
    start_ref,
    first_ref,
    qkv_ref,
    near_ref,
    far_ref,
    log_ref,
    q_s,
    k_s,
    vt_s,
):
    count = 4 * ny
    width = q_s.shape[1]
    core = core_ref[0]
    step = 2 * size
    half = mine_ref.shape[0]
    for base, ref in ((0, mine_ref), (half, other_ref)):
        for start in range(0, half, step):
            rows = slice(base + start, base + start + step)
            normal, _ = normalize(ref[start : start + step, :].astype(F32) + encoding_ref[rows, :])
            value = (normal * affine_ref[0:1, :] + affine_ref[1:2, :]).astype(BF16)
            first_ref[rows, :] = value
            qkv_ref[rows, :] = (dot_nn(value, weight_ref[...]) + bias_ref[...]).astype(BF16)
    for chunk in range(count):
        rows = chunk_rows(chunk, ny, size, core)
        here = slice(chunk * size, (chunk + 1) * size)
        q_s[here, :] = qkv_ref[rows, 0:width] * 0.125
        k_s[here, :] = qkv_ref[rows, width : 2 * width]
        vt_s[:, here] = jnp.transpose(qkv_ref[rows, 2 * width : 3 * width].astype(F32)).astype(BF16)
    lanes = lane_parts(heads, width)
    each = width // heads
    for block in range(count * size // BLOCK):
        first = block * BLOCK
        total = first + BLOCK
        allowed = allowed_pairs(start_ref, first, total)
        q_block = q_s[first:total, :]
        contexts = []
        for h in range(heads):
            scores = dot_nt(k_s[0:total, :], only(q_block, lanes[h]))
            scores = jnp.where(allowed, scores, NEG)
            top = jnp.max(scores, axis=0, keepdims=True)
            weight = jnp.exp(scores - top)
            mass = jnp.sum(weight, axis=0, keepdims=True)
            part = dot_nn(vt_s[h * each : (h + 1) * each, 0:total], weight.astype(BF16))
            contexts.append(part / mass)
            log_ref[h : h + 1, first:total] = top + jnp.log(mass)
        context = contexts[0] if heads == 1 else jnp.concatenate(contexts, axis=0)
        context = jnp.transpose(context).astype(BF16)
        for sub in range(BLOCK // size):
            owner = chunk_owner(block * (BLOCK // size) + sub, ny)
            side, spot = divmod(owner, 2 * ny)
            rows, piece = slice(spot * size, (spot + 1) * size), context[sub * size : (sub + 1) * size]

            @pl.when(core == side)
            def _(rows=rows, piece=piece):
                near_ref[rows, :] = piece

            @pl.when(core != side)
            def _(rows=rows, piece=piece):
                far_ref[rows, :] = piece


def attend_back(
    heads,
    ny,
    size,
    core_ref,
    qkv_ref,
    mine_ref,
    other_ref,
    near_ref,
    far_ref,
    outward_ref,
    weight_ref,
    start_ref,
    log_ref,
    out_ref,
    send_ref,
    keep_ref,
    outward_grad_ref,
    q_s,
    k_s,
    v_s,
    g_s,
    kt_s,
    dq_s,
    dk_s,
    dv_s,
):
    count = 4 * ny
    width = q_s.shape[1]
    core = core_ref[0]
    half = mine_ref.shape[0]
    step = 2 * size
    for base, ref in ((0, mine_ref), (half, other_ref)):
        for start in range(0, half, step):
            rows = slice(start, start + step)
            out_ref[base + start : base + start + step, 0:width] = dot_nt(ref[rows, :], outward_ref[...]).astype(BF16)
    for chunk in range(count):
        rows = chunk_rows(chunk, ny, size, core)
        here = slice(chunk * size, (chunk + 1) * size)
        q_s[here, :] = qkv_ref[rows, 0:width] * 0.125
        key = qkv_ref[rows, width : 2 * width]
        k_s[here, :] = key
        kt_s[:, here] = jnp.transpose(key.astype(F32)).astype(BF16)
        v_s[here, :] = qkv_ref[rows, 2 * width : 3 * width]
        g_s[here, :] = out_ref[rows, 0:width]
    dk_s[...] = jnp.zeros_like(dk_s)
    dv_s[...] = jnp.zeros_like(dv_s)
    lanes = lane_parts(heads, width)
    each = width // heads
    for block in range(count * size // BLOCK):
        first = block * BLOCK
        total = first + BLOCK
        allowed = allowed_pairs(start_ref, first, total)
        q_block, g_block = q_s[first:total, :], g_s[first:total, :]
        queries = []
        for h in range(heads):
            q_one, g_one = only(q_block, lanes[h]), only(g_block, lanes[h])
            scores = dot_nt(k_s[0:total, :], q_one)
            probs = jnp.where(allowed, jnp.exp(scores - log_ref[h : h + 1, first:total]), 0.0)
            prob_grad = dot_nt(v_s[0:total, :], g_one)
            delta = jnp.sum(probs * prob_grad, axis=0, keepdims=True)
            score_grad = (probs * (prob_grad - delta)).astype(BF16)
            dv_s[0:total, :] += dot_nn(probs.astype(BF16), g_one)
            dk_s[0:total, :] += dot_nn(score_grad, q_one)
            queries.append(dot_nn(kt_s[h * each : (h + 1) * each, 0:total], score_grad))
        query_grad = queries[0] if heads == 1 else jnp.concatenate(queries, axis=0)
        dq_s[first:total, :] = jnp.transpose(query_grad) * 0.125
    for chunk in range(count):
        rows = chunk_rows(chunk, ny, size, core)
        here = slice(chunk * size, (chunk + 1) * size)
        out_ref[rows, 0:width] = dq_s[here, :].astype(BF16)
        out_ref[rows, width : 2 * width] = dk_s[here, :].astype(BF16)
        out_ref[rows, 2 * width : 3 * width] = dv_s[here, :].astype(BF16)
    for ref, base in ((send_ref, half), (keep_ref, 0)):
        for start in range(0, half, step):
            rows = slice(base + start, base + start + step)
            ref[start : start + step, :] = dot_nt(out_ref[rows, :], weight_ref[...]).astype(BF16)
    total = dot_tn(near_ref[...], mine_ref[...]) + dot_tn(far_ref[...], other_ref[...])
    outward_grad_ref[...] = total.astype(BF16)


def feed_forward(
    size,
    core_ref,
    mine_ref,
    other_ref,
    up_mine_ref,
    up_other_ref,
    expand_ref,
    shrink_ref,
    bias_ref,
    active_ref,
    grad_ref,
    send_ref,
    keep_ref,
    result_ref,
):
    half = keep_ref.shape[0]
    step = 2 * size
    rate = math.sqrt(2.0 / math.pi)
    core = core_ref[0]
    sides = ((send_ref, other_ref, up_other_ref, half, 1 - core), (keep_ref, mine_ref, up_mine_ref, 0, core))
    for ref, source_ref, up_ref, base, side in sides:
        for start in range(0, half, step):
            rows = slice(start, start + step)
            pair = slice(base + start, base + start + step)
            place = pl.ds(pl.multiple_of(side * half + start, step), step)
            before = dot_nn(source_ref[rows, :], expand_ref[...]) + bias_ref[...]
            upper = dot_nt(up_ref[rows, :], shrink_ref[...])
            square = before * before
            inner = jnp.tanh(rate * (before + 0.044715 * before * square))
            plus = 0.5 * (1.0 + inner)
            active = (before * plus).astype(BF16)
            active_ref[pair, :] = active
            slope = plus + 0.5 * before * (1.0 - inner * inner) * (rate + rate * 3 * 0.044715 * square)
            lower = (upper * slope).astype(BF16)
            grad_ref[pair, :] = lower
            ref[rows, :] = dot_nt(lower, expand_ref[...]).astype(BF16)
            result_ref[place, :] = dot_nn(active, shrink_ref[...]).astype(BF16)


def weight_parts(part, mine_ref, other_ref, up_mine_ref, up_other_ref, active_ref, grad_ref, bias_ref, out_ref):
    half, width = mine_ref.shape
    quarter, all_units = width // NZ, NZ * part
    for r in range(NZ):
        spot, ref = r, out_ref.at[r]
        here = slice(spot * quarter, (spot + 1) * quarter)
        total = dot_tn(mine_ref[:, here], grad_ref[0:half, :]) + dot_tn(other_ref[:, here], grad_ref[half : 2 * half, :])
        ref[0:quarter, :] = total.astype(BF16)
        units = slice(spot * part, (spot + 1) * part)
        total = dot_tn(active_ref[0:half, units], up_mine_ref[...])
        total = (total + dot_tn(active_ref[half : 2 * half, units], up_other_ref[...])).astype(BF16)
        for i in range(width // all_units):
            start = quarter + i * part
            ref[start : start + part, :] = total[:, i * all_units : (i + 1) * all_units]
    bias_ref[...] = jnp.sum(grad_ref[...].astype(F32), axis=0, keepdims=True)


def feed_forward_weights(second, up, active, before_grad):
    frames, units = active.shape
    width, part = up[0].shape[1], units // NZ
    quarter = width // NZ
    if part % 128:
        shrink = dot_tn(active, stack_rows(up)).astype(BF16).reshape(NZ, part, width)
        expand = dot_tn(stack_rows(second), before_grad).astype(BF16).reshape(NZ, quarter, units)
        bias = jnp.sum(before_grad.astype(F32), axis=0, keepdims=True)
        return bias, jnp.stack([stack_rows([expand[k], fold_columns(shrink[k], units)]) for k in range(NZ)])
    return pl.pallas_call(
        functools.partial(weight_parts, part),
        out_shape=(jax.ShapeDtypeStruct((1, units), F32), jax.ShapeDtypeStruct((NZ, 2 * quarter, units), BF16)),
        in_specs=whole(6),
        out_specs=tuple(whole(2)),
        compiler_params=pltpu.CompilerParams(vmem_limit_bytes=16 << 20),
        cost_estimate=pl.CostEstimate(
            flops=4 * frames * width * units, bytes_accessed=8 * frames * width, transcendentals=0
        ),
        name="feed_forward_weights",
    )(*second, *up, active, before_grad)


def whole(count):
    return [pl.BlockSpec(memory_space=pltpu.VMEM)] * count


def attention(core, pair, encoding, affine, w_in, bias, starts, heads, ny, size):
    half, wide = pair[0].shape[0], w_in.shape[1]
    frames, depth, width = 2 * half, pair[0].shape[1], wide // 3
    pairs = frames * frames * heads
    return pl.pallas_call(
        functools.partial(attend, heads, ny, size),
        out_shape=(
            jax.ShapeDtypeStruct((frames, depth), BF16),
            jax.ShapeDtypeStruct((frames, wide), BF16),
            jax.ShapeDtypeStruct((half, width), BF16),
            jax.ShapeDtypeStruct((half, width), BF16),
            jax.ShapeDtypeStruct((heads, frames), F32),
        ),
        in_specs=[pl.BlockSpec(memory_space=pltpu.SMEM)] + whole(7),
        out_specs=tuple(whole(5)),
        scratch_shapes=[
            pltpu.VMEM((frames, width), BF16),
            pltpu.VMEM((frames, width), BF16),
            pltpu.VMEM((width, frames), BF16),
        ],
        compiler_params=pltpu.CompilerParams(vmem_limit_bytes=16 << 20),
        cost_estimate=pl.CostEstimate(
            flops=pairs * 256 + 2 * frames * depth * wide, bytes_accessed=8 * frames * depth, transcendentals=pairs // 2
        ),
        name="attend",
    )(core, *pair, encoding, affine, w_in, bias, starts)


def attention_back(place, qkv, pair, context, w_out, w_in, starts, log_total, heads, ny, size):
    frames, wide = qkv.shape
    width = wide // 3
    depth = pair[0].shape[1]
    pairs = frames * frames * heads
    half = jax.ShapeDtypeStruct(pair[0].shape, BF16)
    return pl.pallas_call(
        functools.partial(attend_back, heads, ny, size),
        out_shape=(
            jax.ShapeDtypeStruct((frames, wide), BF16),
            half,
            half,
            jax.ShapeDtypeStruct((width, depth), BF16),
        ),
        in_specs=[pl.BlockSpec(memory_space=pltpu.SMEM)] + whole(9),
        out_specs=tuple(whole(4)),
        scratch_shapes=[pltpu.VMEM((frames, width), BF16)] * 4
        + [pltpu.VMEM((width, frames), BF16)]
        + [pltpu.VMEM((frames, width), F32)] * 3,
        compiler_params=pltpu.CompilerParams(vmem_limit_bytes=20 << 20),
        cost_estimate=pl.CostEstimate(
            flops=pairs * 640 + 2 * frames * depth * (wide + 2 * width),
            bytes_accessed=8 * frames * depth,
            transcendentals=pairs // 2,
        ),
        name="attend_back",
    )(place.core, qkv, *pair, *context, w_out, w_in, starts, log_total)


def feed_forward_front(core, pair, up_pair, w_expand, w_shrink, bias, size):
    frames, width = 2 * pair[0].shape[0], pair[0].shape[1]
    units = w_expand.shape[1]
    half = jax.ShapeDtypeStruct((frames // 2, width), BF16)
    inner = jax.ShapeDtypeStruct((frames, units), BF16)
    return pl.pallas_call(
        functools.partial(feed_forward, size),
        out_shape=(inner, inner, half, half, jax.ShapeDtypeStruct((frames, width), BF16)),
        in_specs=[pl.BlockSpec(memory_space=pltpu.SMEM)] + whole(7),
        out_specs=tuple(whole(5)),
        compiler_params=pltpu.CompilerParams(vmem_limit_bytes=16 << 20),
        cost_estimate=pl.CostEstimate(
            flops=8 * frames * width * units, bytes_accessed=10 * frames * width, transcendentals=frames * units
        ),
        name="feed_forward",
    )(core, *pair, *up_pair, w_expand, w_shrink, bias)


class Place:
    def __init__(self, ny):
        self.x, self.z, self.y, self.c = (lax.axis_index(a) for a in ("x", "z", "y", "c"))
        self.xy = jnp.reshape(self.x * ny + self.y, (1,)).astype(jnp.int32)
        self.core = jnp.reshape(self.c, (1,)).astype(jnp.int32)
        self.layer = jnp.reshape(self.z, (1,)).astype(jnp.int32)


def on_device(
    groups,
    ny,
    frames,
    cotangent,
    segment_lengths,
    position_offsets,
    first_gain,
    first_shift,
    inward_weight,
    query_bias,
    value_bias,
    outward_weight,
    outward_bias,
    second_gain,
    second_shift,
    expand_weight,
    expand_bias,
    shrink_weight,
    shrink_bias,
):
    place = Place(ny)
    x, z, y, c = place.x, place.z, place.y, place.c
    local_len, rows, width = frames.shape
    share = inward_weight.shape[0]
    layer = 4 * ny
    spread = NZ * ny * 2
    full_len = local_len * spread
    size = 2 * local_len
    hd = HEADS // layer
    hw = hd * (width // HEADS)
    hidden = expand_bias.shape[0]
    part = hidden // 2
    me = (c * 2 + x) * ny + y

    def sum_groups(value):
        return lax.psum(value, "g") if groups > 1 else value

    def exchange(value, axes):
        return lax.all_to_all(value, axes, 0, 0, tiled=True)

    both = to_home(jnp.concatenate([frames, cotangent], axis=2), place)
    table = jnp.stack([segment_lengths, position_offsets], axis=1)
    other_table = hop(table, "x")
    other_table, later_inward = after(other_table, inward_weight)

    small = [first_gain, first_shift, query_bias, value_bias, outward_bias, second_gain, second_shift, shrink_bias]
    kinds = len(small) + hidden // share
    units = NZ * part
    packed = jnp.concatenate([v[None] for v in small] + [expand_bias.reshape(-1, share)], axis=0)
    packed = packed.reshape(-1, 3 * hw)
    extra = packed.shape[0]
    packed = jnp.pad(packed, ((0, SMALL_ROWS - extra), (0, units)))[None]
    in_cols = jnp.transpose(later_inward.reshape(share, 3, 2, 2, ny, hw), (3, 4, 2, 0, 1, 5))
    in_cols = pick(in_cols, x).reshape(ny * 2, share, 3 * hw)
    ex_cols = pick(expand_weight.reshape(share, NZ, ny, 2, 2, part), x, 4)
    ex_cols = jnp.transpose(ex_cols, (2, 3, 0, 1, 4)).reshape(ny * 2, share, units)
    columns = jnp.concatenate([in_cols, ex_cols], axis=2)
    columns = jnp.concatenate([columns, jnp.broadcast_to(packed, (ny * 2,) + packed.shape[1:])], axis=1)
    columns = exchange(columns, ("y", "c"))

    row_x = jnp.where((z == 0) | (z == 3), 1, 0)
    table = pick(jnp.where(x == row_x, table, other_table), z >> 1)
    lengths, offsets = table[0], table[1]
    count = lengths.shape[0]
    starts = jnp.sum(
        jnp.where(jnp.arange(count)[None, :] < jnp.arange(count)[:, None], lengths[None, :], 0), axis=1
    )
    frame_ids = jnp.arange(full_len, dtype=jnp.int32)
    row_starts = jnp.max(jnp.where(starts[:, None] <= frame_ids[None, :], starts[:, None], 0), axis=0)[None, :]
    spot = jnp.arange(2 * ny)
    chunk = jnp.concatenate([(2 * (spot // ny) + i) * ny + spot % ny for i in (c, 1 - c)])
    mine = (chunk[:, None] * size + jnp.arange(size, dtype=jnp.int32)).reshape(-1)
    inside = (mine[:, None] >= starts[None, :]) & (mine[:, None] < (starts + lengths)[None, :])
    position = jnp.sum(jnp.where(inside, offsets[None, :] + mine[:, None] - starts[None, :], 0), axis=1)
    encoding = sin_cos(position, width)

    both, encoding, later_outward, columns = after(both, encoding, outward_weight, columns)
    fr, ct = both[:, :width], both[:, width:]
    outward = lax.all_gather(later_outward, SEQ, axis=0, tiled=True)
    in_part = columns[:, :, : 3 * hw].reshape(-1, 3 * hw)
    in_parts = [in_part] + [hop(in_part, "z", NZ, k) for k in range(1, NZ)]
    sh_rows = lax.dynamic_slice_in_dim(shrink_weight, x * part, part, 0)
    ff_part = stack_rows([columns[:, :share, 3 * hw :].reshape(-1, units), fold_columns(sh_rows, units)])
    mine, up_mine = assemble_pair(near_parts(both, ny), place.xy)
    mine, ff_part, *in_parts = after(mine, ff_part, *in_parts)
    first_pair = [mine, hop(mine, "c")]
    w_in, small_rows = collect_inward(in_parts, place, share)
    ff_got = exchange(jnp.broadcast_to(ff_part[None], (NZ,) + ff_part.shape), ("z",))

    vectors = small_rows.reshape(spread, SMALL_ROWS, 3 * hw)[:, :extra].reshape(spread, kinds, share).astype(F32)
    expand_b = vectors[:, len(small) :].reshape(NZ, ny, 2, 2, part)
    expand_b = pick(pick(pick(expand_b, y, 1), c, 1), x, 1).reshape(1, NZ * part)
    vectors = jnp.swapaxes(vectors[:, : len(small)], 0, 1).reshape(len(small), width)
    gain_one, shift_one, query_b, value_b, outward_b, gain_two, shift_two, shrink_b = (
        vectors[i : i + 1] for i in range(len(small))
    )
    qkv_bias = jnp.concatenate(
        [
            lax.dynamic_slice_in_dim(query_b, me * hw, hw, 1),
            jnp.zeros((1, hw), F32),
            lax.dynamic_slice_in_dim(value_b, me * hw, hw, 1),
        ],
        axis=1,
    )

    first_all, qkv, *context_pair, log_total = attention(
        place.core, first_pair, encoding, vectors[:2], w_in, qkv_bias, row_starts, hd, ny, size
    )
    *context_pair, up_mine = after(*context_pair, up_mine)
    if ny == 2:
        context = by_half(c, context_pair[0][None], hop(context_pair[1], "c")[None], 0)
        context = context.reshape(2, 2, ny, size, hw)
        context = by_half(x, pick(context, x, 1)[:, None], hop(pick(context, 1 - x, 1), "x")[:, None], 1)
        context = by_half(y, pick(context, y, 2)[:, :, None], hop(pick(context, 1 - y, 2), "y")[:, :, None], 2)
    else:
        context = exchange(by_half(c, *context_pair, 0).reshape(layer, size, hw), LAYER)
    context = context.reshape(layer, size, hw)
    up_pair = [up_mine, hop(up_mine, "c")]

    inputs = fr.astype(F32) + lax.dynamic_slice_in_dim(encoding, (x * ny + y) * size, size, 0)
    normal_one, scale_one = normalize(inputs)
    context = jnp.swapaxes(context, 0, 1).reshape(size, width)
    middle = inputs + dot_nn(context, outward) + outward_b

    normal_two, scale_two = normalize(middle)
    second = (normal_two * gain_two + shift_two).astype(BF16)
    ff_got, *second_near = after(ff_got, *near_parts(second, ny))
    second_pair = both_cores(second_near, place)
    w_expand, w_shrink = collect_hidden(ff_got, width)
    active, before_grad, send, keep, out_part = feed_forward_front(
        place.core, second_pair, up_pair, w_expand, w_shrink, expand_b, size
    )
    second_parts = list(fold(keep, hop(send, "c"), place, ny))
    second_parts[0], active, before_grad = after(second_parts[0], active, before_grad)
    second_grad = finish(second_parts, ny)
    expand_b_sum, hidden_part = feed_forward_weights(second_pair, up_pair, active, before_grad)
    out_part = lax.psum_scatter(out_part, LAYER, scatter_dimension=0, tiled=True)
    hidden_got = exchange(hidden_part, ("z",))

    upstream = ct.astype(F32)
    middle_part, gain_two_sum, shift_two_sum = normalize_back(normal_two, scale_two, gain_two, second_grad)
    middle_grad = upstream + middle_part
    low_middle = middle_grad.astype(BF16)
    low_pair = both_cores(near_parts(low_middle, ny), place)
    w_out = lax.dynamic_slice_in_dim(outward, me * hw, hw, 0)
    mixed_grad, send, keep, outward_part = attention_back(
        place, qkv, low_pair, context_pair, w_out, w_in, row_starts, log_total, hd, ny, size
    )
    got = hop(send, "c")
    cut = outward_part.reshape(2, -1, width)
    far_cut = hop(pick(cut, 1 - c), "c")
    got, far_cut, out_part, hidden_got = after(got, far_cut, out_part, hidden_got)
    first_parts = list(fold(keep, got, place, ny))
    first_parts[0], mixed_late = after(first_parts[0], mixed_grad)
    inward_part = dot_tn(first_all, mixed_late).astype(BF16)
    first_grad = finish(first_parts, ny)
    first_grad, hidden_got = after(first_grad, hidden_got)
    hidden_sum = sum_sources(hidden_got, NZ)
    inward_got = exchange(inward_part.reshape(spread, share, 3 * hw), SEQ)
    input_part, gain_one_sum, shift_one_sum = normalize_back(normal_one, scale_one, vectors[:1], first_grad)
    late = (middle_grad + input_part).astype(BF16)
    late, out_part = after(late, out_part)
    frames_grad = to_origin(late, place).astype(F32)
    layer_output = to_origin((middle + out_part.astype(F32) + shrink_b).astype(BF16), place)

    split = width // 2
    hidden_sum = sum_groups(hidden_sum.reshape(-1, units)).astype(BF16)
    line = hidden_sum[: width // NZ].reshape(ny, 2, share, units)
    if ny == 2:
        line = by_half(c, pick(line, c, 1)[:, None], hop(pick(line, 1 - c, 1), "c")[:, None], 1)
        line = by_half(y, pick(line, y)[None], hop(pick(line, 1 - y), "y")[None], 0)
    else:
        line = exchange(line.reshape(ny * 2, share, units), ("y", "c"))
    mine = stack_rows([line.reshape(-1, units), hidden_sum[width // NZ :]])
    other = hop(mine, "x")

    def full_hidden(other):
        pair = [unfold_columns(v[width // NZ :], width // units) for v in (mine, other)]
        g_shrink = by_half(x, *pair, 0).astype(F32)
        pair = [v[: width // NZ].reshape(ny, 2, 1, share, NZ, part) for v in (mine, other)]
        return g_shrink, jnp.transpose(by_half(x, *pair, 2), (3, 4, 0, 1, 2, 5)).reshape(share, -1).astype(F32)

    if hd == 2 and ny == 2:
        line = by_half(c, pick(cut, c)[None], far_cut[None], 0)
        line = line.reshape(2, 1, share, 2, split)
        line = by_half(x, pick(line, x, 3), hop(pick(line, 1 - x, 3), "x"), 1)
        out_sum = lax.psum_scatter(line.reshape(NZ * share, split), "z", scatter_dimension=0, tiled=True)
        out_sum = sum_groups(out_sum.astype(F32)).astype(BF16)
        g_outward = by_half(x, out_sum, hop(out_sum, "x"), 1).astype(F32)
    else:
        cut = lax.dynamic_update_slice(jnp.zeros((width, width), BF16), outward_part, (me * hw, 0))
        g_outward = lax.psum_scatter(cut, SEQ, scatter_dimension=0, tiled=True)
        g_outward = lax.psum(g_outward.astype(F32), ("g", "x"))

    mixed_sum = jnp.sum(mixed_grad.astype(F32), axis=0)

    def from_heads(value):
        return lax.dynamic_update_slice(jnp.zeros((width,), F32), value, (me * hw,))

    flat = jnp.stack(
        [
            gain_one_sum,
            shift_one_sum,
            from_heads(mixed_sum[:hw]),
            from_heads(mixed_sum[2 * hw :]),
            jnp.sum(low_middle.astype(F32), axis=0),
            gain_two_sum,
            shift_two_sum,
            jnp.sum(upstream, axis=0),
        ]
    )
    small_len = len(small) * share
    sums = jnp.swapaxes(flat.reshape(len(small), spread, share), 0, 1).reshape(spread, small_len)
    spot = jnp.zeros((NZ, ny, 2, 2, part), F32)
    spot = lax.dynamic_update_slice(spot, expand_b_sum.reshape(NZ, 1, 1, 1, part), (0, y, c, x, 0))
    sums = jnp.concatenate([sums, spot.reshape(spread, hidden)], axis=1)
    inward_got, sums = after(inward_got, sums)
    sums = jnp.broadcast_to(sums[None], (2,) + sums.shape).reshape(2 * spread, -1, 128)
    total = sum_groups(jnp.sum(exchange(sums, ("x",) + SEQ), axis=0)).reshape(-1)
    total, other = after(total, other)
    g_shrink, g_expand = full_hidden(other)
    g_small = total[:small_len].reshape(len(small), share)
    g_expand_b = total[small_len:]
    inward_sum = sum_groups(sum_sources(inward_got, NZ)).astype(BF16)
    g_inward = [v.reshape(ny, 2, 1, share, 3, hw) for v in (inward_sum, hop(inward_sum, "x"))]
    g_inward = jnp.transpose(by_half(x, *g_inward, 2), (3, 4, 1, 2, 0, 5)).reshape(share, -1).astype(F32)

    return (
        layer_output,
        frames_grad,
        g_small[0],
        g_small[1],
        g_inward,
        g_small[2],
        g_small[3],
        g_outward,
        g_small[4],
        g_small[5],
        g_small[6],
        g_expand,
        g_expand_b,
        g_shrink,
        g_small[7],
    )


def solution(mesh):
    batch, seq = mesh.shape["batch"], mesh.shape["seq"]
    groups, ny = batch // 2, seq // (2 * NZ)
    fine = Mesh(mesh.devices.reshape(groups, 2, NZ, ny, 2), ("g", "x", "z", "y", "c"))
    b, s = ("g", "x"), ("z", "y", "c")
    in_specs = (
        P(s, b, None),
        P(s, b, None),
        P(b, None),
        P(b, None),
        P(s),
        P(s),
        P(s, None),
        P(s),
        P(s),
        P(s, None),
        P(s),
        P(s),
        P(s),
        P(s, None),
        P(s),
        P(s, None),
        P(s),
    )
    out_specs = (
        P(s, b, None),
        P(s, b, None),
        P(s),
        P(s),
        P(s, None),
        P(s),
        P(s),
        P(s, None),
        P(s),
        P(s),
        P(s),
        P(s, None),
        P(s),
        P(s, None),
        P(s),
    )
    return jax.shard_map(
        functools.partial(on_device, groups, ny), mesh=fine, in_specs=in_specs, out_specs=out_specs, check_vma=False
    )
```

```python
import functools
import math

import jax
import jax.numpy as jnp
from jax import lax
from jax.experimental import pallas as pl
from jax.experimental.pallas import tpu as pltpu
from jax.sharding import Mesh, PartitionSpec as P


HEADS = 16
NZ = 4
SMALL_ROWS = 16
NORM_EPS = 1e-05
NEG = -1e30
F32 = jnp.float32
BF16 = jnp.bfloat16
LAYER_OF_ROW = (1, 2, 0, 3)
SWAP = [(0, 1), (1, 0)]
LAYER = ("c", "x", "y")
SEQ = ("z", "y", "c")


def xor_perm(count, k):
    return [(i, i ^ k) for i in range(count)]


def hop(value, axis, count=2, k=1):
    return lax.ppermute(value, axis, xor_perm(count, k))


def pick(value, index, axis=0):
    return lax.dynamic_index_in_dim(value, index, axis, keepdims=False)


def stack_rows(parts):
    return jnp.concatenate(parts, axis=0)


def assemble_body(pieces, size, place_ref, *refs):
    out_ref = refs[pieces]
    for r in range(pieces):
        spot = place_ref[0] ^ r
        out_ref[pl.ds(pl.multiple_of(spot * size, size), size), :] = refs[r][...]


def assemble(parts, me):
    size, width = parts[0].shape
    count = len(parts)
    return pl.pallas_call(
        functools.partial(assemble_body, count, size),
        out_shape=jax.ShapeDtypeStruct((count * size, width), parts[0].dtype),
        in_specs=[pl.BlockSpec(memory_space=pltpu.SMEM)] + whole(count),
        out_specs=whole(1)[0],
        compiler_params=pltpu.CompilerParams(vmem_limit_bytes=4 << 20),
        cost_estimate=pl.CostEstimate(flops=0, bytes_accessed=4 * count * size * width, transcendentals=0),
        name="assemble",
    )(me, *parts)


def assemble_pair_body(pieces, size, place_ref, *refs):
    left_ref, right_ref = refs[pieces:]
    width = left_ref.shape[1]
    for r in range(pieces):
        rows = pl.ds(pl.multiple_of((place_ref[0] ^ r) * size, size), size)
        left_ref[rows, :] = refs[r][:, 0:width]
        right_ref[rows, :] = refs[r][:, width : 2 * width]


def assemble_pair(parts, me):
    size, width = parts[0].shape
    count = len(parts)
    return pl.pallas_call(
        functools.partial(assemble_pair_body, count, size),
        out_shape=[jax.ShapeDtypeStruct((count * size, width // 2), parts[0].dtype)] * 2,
        in_specs=[pl.BlockSpec(memory_space=pltpu.SMEM)] + whole(count),
        out_specs=whole(2),
        compiler_params=pltpu.CompilerParams(vmem_limit_bytes=4 << 20),
        cost_estimate=pl.CostEstimate(flops=0, bytes_accessed=4 * count * size * width, transcendentals=0),
        name="assemble_pair",
    )(me, *parts)


def near_parts(block, ny):
    return [block] + [lax.ppermute(block, ("x", "y"), xor_perm(2 * ny, r)) for r in range(1, 2 * ny)]


def both_cores(parts, place):
    mine = assemble(parts, place.xy)
    return mine, hop(mine, "c")


def fold_body(count, size, place_ref, keep_ref, got_ref, own_ref, *out_refs):
    for r in range(count):
        spot = place_ref[0] ^ r
        here = pl.ds(pl.multiple_of(spot * size, size), size)
        value = keep_ref[here, :].astype(F32) + got_ref[here, :].astype(F32)
        if r == 0:
            own_ref[...] = value
        else:
            out_refs[r - 1][...] = value.astype(BF16)


def fold(keep, got, place, ny):
    rows, width = keep.shape
    count = 2 * ny
    size = rows // count
    return pl.pallas_call(
        functools.partial(fold_body, count, size),
        out_shape=[jax.ShapeDtypeStruct((size, width), F32)] + [jax.ShapeDtypeStruct((size, width), BF16)] * (count - 1),
        in_specs=[pl.BlockSpec(memory_space=pltpu.SMEM)] + whole(2),
        out_specs=whole(count),
        compiler_params=pltpu.CompilerParams(vmem_limit_bytes=4 << 20),
        cost_estimate=pl.CostEstimate(flops=count * size * width, bytes_accessed=6 * count * size * width, transcendentals=0),
        name="fold",
    )(place.xy, keep, got)


def finish(parts, ny):
    own = parts[0]
    for r in range(1, 2 * ny):
        own = own + lax.ppermute(parts[r], ("x", "y"), xor_perm(2 * ny, r)).astype(F32)
    return own


def fold_columns(value, units):
    return stack_rows([value[:, i : i + units] for i in range(0, value.shape[1], units)])


def unfold_columns(value, count):
    size = value.shape[0] // count
    return jnp.concatenate([value[i * size : (i + 1) * size] for i in range(count)], axis=1)


def collect_inward_body(share, place_ref, *refs):
    weight_ref, small_ref = refs[NZ:]
    deep = share + SMALL_ROWS
    lines = refs[0].shape[0] // deep
    for r in range(NZ):
        base = (place_ref[0] ^ r) * lines
        for i in range(lines):
            start = i * deep
            rows = pl.ds(pl.multiple_of((base + i) * share, share), share)
            weight_ref[rows, :] = refs[r][start : start + share, :]
            rows = pl.ds(pl.multiple_of((base + i) * SMALL_ROWS, SMALL_ROWS), SMALL_ROWS)
            small_ref[rows, :] = refs[r][start + share : start + deep, :]


def collect_inward(parts, place, share):
    rows, width = parts[0].shape
    lines = NZ * rows // (share + SMALL_ROWS)
    return pl.pallas_call(
        functools.partial(collect_inward_body, share),
        out_shape=[jax.ShapeDtypeStruct((lines * n, width), BF16) for n in (share, SMALL_ROWS)],
        in_specs=[pl.BlockSpec(memory_space=pltpu.SMEM)] + whole(NZ),
        out_specs=whole(2),
        compiler_params=pltpu.CompilerParams(vmem_limit_bytes=4 << 20),
        cost_estimate=pl.CostEstimate(flops=0, bytes_accessed=16 * rows * width, transcendentals=0),
        name="collect_inward",
    )(place.layer, *parts)


def collect_hidden_body(parts_ref, expand_ref, shrink_ref):
    quarter = expand_ref.shape[0] // NZ
    part, units = shrink_ref.shape[0] // NZ, expand_ref.shape[1]
    for r in range(NZ):
        expand_ref[r * quarter : (r + 1) * quarter, :] = parts_ref[r, 0:quarter, :]
        for i in range(shrink_ref.shape[1] // units):
            start = quarter + i * part
            here = slice(r * part, (r + 1) * part)
            shrink_ref[here, i * units : (i + 1) * units] = parts_ref[r, start : start + part, :]


def collect_hidden(parts, width):
    units = parts.shape[2]
    return pl.pallas_call(
        collect_hidden_body,
        out_shape=[jax.ShapeDtypeStruct((width, units), BF16), jax.ShapeDtypeStruct((units, width), BF16)],
        in_specs=whole(1),
        out_specs=whole(2),
        compiler_params=pltpu.CompilerParams(vmem_limit_bytes=4 << 20),
        cost_estimate=pl.CostEstimate(flops=0, bytes_accessed=4 * parts.size, transcendentals=0),
        name="collect_hidden",
    )(parts)


def rehome_flat(x, z, c):
    return (x * NZ + z) * 2 + c


def rehome_perm(k):
    return [
        (rehome_flat(x, z, c), rehome_flat(z >> 1, LAYER_OF_ROW[2 * x + (c ^ k)], z & 1))
        for x in range(2)
        for z in range(NZ)
        for c in range(2)
    ]


def to_home(block, place):
    got = [
        lax.ppermute(jnp.where(place.c == k, block[:, 0], block[:, 1]), ("x", "z", "c"), rehome_perm(k))
        for k in range(2)
    ]
    first = place.z < 2
    return stack_rows([jnp.where(first, got[0], got[1]), jnp.where(first, got[1], got[0])])


def to_origin(block, place):
    half = block.shape[0] // 2
    first = place.z < 2
    low, high = block[:half], block[half:]
    sent = [jnp.where(first, low, high), jnp.where(first, high, low)]
    got = [
        lax.ppermute(sent[k], ("x", "z", "c"), [(b, a) for a, b in rehome_perm(k)]) for k in range(2)
    ]
    return jnp.stack(
        [jnp.where(place.c == 0, got[0], got[1]), jnp.where(place.c == 0, got[1], got[0])], axis=1
    )


def after(first, *values):
    return lax.optimization_barrier((first, *values))


def sum_sources(value, count):
    return jnp.sum(value.reshape((count, -1) + value.shape[1:]).astype(F32), axis=0)


def by_half(x, mine, other, axis):
    return jnp.concatenate([jnp.where(x == 0, mine, other), jnp.where(x == 0, other, mine)], axis=axis)


def sin_cos(position, width):
    feature = jnp.arange(width, dtype=jnp.int32)
    rates = jnp.exp((feature // 2).astype(F32) * (-2.0 * math.log(10000.0) / width))
    angle = position.astype(F32)[:, None] * rates[None, :]
    turn = jnp.round(angle * (2.0 / math.pi))
    rest = angle - turn * 1.5703125
    rest = rest - turn * 0.00048375129699707031
    rest = rest - turn * 7.5497899548918861e-08
    quadrant = turn.astype(jnp.int32) + (feature % 2)[None, :]
    square = rest * rest
    sine = rest + rest * square * (
        -0.16666666641626524 + square * (0.008333329385889463 + square * (-0.00019839334836096632 + square * 2.718311493989822e-06))
    )
    cosine = 1.0 + square * (
        -0.49999999725103100 + square * (0.04166662332373906 + square * (-0.001388676377460993 + square * 2.439044879627741e-05))
    )
    value = jnp.where((quadrant & 1) == 0, sine, cosine)
    return jnp.where((quadrant & 2) == 0, value, -value)


def normalize(values):
    center = values - jnp.mean(values, axis=-1, keepdims=True)
    scale = lax.rsqrt(jnp.mean(center * center, axis=-1, keepdims=True) + NORM_EPS)
    return center * scale, scale


def normalize_back(normal, scale, gain, upstream):
    scaled = upstream * gain
    inner = scaled - jnp.mean(scaled, axis=-1, keepdims=True)
    inner = inner - normal * jnp.mean(scaled * normal, axis=-1, keepdims=True)
    return inner * scale, jnp.sum(upstream * normal, axis=0), jnp.sum(upstream, axis=0)


def dot_nt(a, b):
    return lax.dot_general(a, b, (((1,), (1,)), ((), ())), preferred_element_type=F32)


def dot_tn(a, b):
    return lax.dot_general(a, b, (((0,), (0,)), ((), ())), preferred_element_type=F32)


def dot_nn(a, b):
    return jnp.dot(a, b, preferred_element_type=F32)


BLOCK = 256


def chunk_owner(chunk, ny):
    outer, y = divmod(chunk, ny)
    return ((outer & 1) * 2 + (outer >> 1)) * ny + y


def lane_parts(heads, width):
    if heads == 1:
        return [None]
    lane = lax.broadcasted_iota(jnp.int32, (1, width), 1)
    return [(lane >= h * (width // heads)) & (lane < (h + 1) * (width // heads)) for h in range(heads)]


def only(value, lanes):
    return value if lanes is None else jnp.where(lanes, value, jnp.zeros_like(value))


def allowed_pairs(start_ref, first, total):
    key = lax.broadcasted_iota(jnp.int32, (total, BLOCK), 0)
    frame = first + lax.broadcasted_iota(jnp.int32, (total, BLOCK), 1)
    return (key >= start_ref[:, first : first + BLOCK]) & (key <= frame)


def chunk_rows(chunk, ny, size, core):
    half, spot = divmod(chunk_owner(chunk, ny), 2 * ny)
    return pl.ds(pl.multiple_of(((half ^ core) * (2 * ny) + spot) * size, size), size)


def attend(
    heads,
    ny,
    size,
    core_ref,
    mine_ref,
    other_ref,
    encoding_ref,
    affine_ref,
    weight_ref,
    bias_ref,
    start_ref,
    first_ref,
    qkv_ref,
    near_ref,
    far_ref,
    log_ref,
    q_s,
    k_s,
    vt_s,
):
    count = 4 * ny
    width = q_s.shape[1]
    core = core_ref[0]
    step = 2 * size
    half = mine_ref.shape[0]
    for base, ref in ((0, mine_ref), (half, other_ref)):
        for start in range(0, half, step):
            rows = slice(base + start, base + start + step)
            normal, _ = normalize(ref[start : start + step, :].astype(F32) + encoding_ref[rows, :])
            value = (normal * affine_ref[0:1, :] + affine_ref[1:2, :]).astype(BF16)
            first_ref[rows, :] = value
            qkv_ref[rows, :] = (dot_nn(value, weight_ref[...]) + bias_ref[...]).astype(BF16)
    for chunk in range(count):
        rows = chunk_rows(chunk, ny, size, core)
        here = slice(chunk * size, (chunk + 1) * size)
        q_s[here, :] = qkv_ref[rows, 0:width] * 0.125
        k_s[here, :] = qkv_ref[rows, width : 2 * width]
        vt_s[:, here] = jnp.transpose(qkv_ref[rows, 2 * width : 3 * width].astype(F32)).astype(BF16)
    lanes = lane_parts(heads, width)
    each = width // heads
    for block in range(count * size // BLOCK):
        first = block * BLOCK
        total = first + BLOCK
        allowed = allowed_pairs(start_ref, first, total)
        q_block = q_s[first:total, :]
        contexts = []
        for h in range(heads):
            scores = dot_nt(k_s[0:total, :], only(q_block, lanes[h]))
            scores = jnp.where(allowed, scores, NEG)
            top = jnp.max(scores, axis=0, keepdims=True)
            weight = jnp.exp(scores - top)
            mass = jnp.sum(weight, axis=0, keepdims=True)
            part = dot_nn(vt_s[h * each : (h + 1) * each, 0:total], weight.astype(BF16))
            contexts.append(part / mass)
            log_ref[h : h + 1, first:total] = top + jnp.log(mass)
        context = contexts[0] if heads == 1 else jnp.concatenate(contexts, axis=0)
        context = jnp.transpose(context).astype(BF16)
        for sub in range(BLOCK // size):
            owner = chunk_owner(block * (BLOCK // size) + sub, ny)
            side, spot = divmod(owner, 2 * ny)
            rows, piece = slice(spot * size, (spot + 1) * size), context[sub * size : (sub + 1) * size]

            @pl.when(core == side)
            def _(rows=rows, piece=piece):
                near_ref[rows, :] = piece

            @pl.when(core != side)
            def _(rows=rows, piece=piece):
                far_ref[rows, :] = piece


def attend_back(
    heads,
    ny,
    size,
    core_ref,
    qkv_ref,
    mine_ref,
    other_ref,
    near_ref,
    far_ref,
    outward_ref,
    weight_ref,
    start_ref,
    log_ref,
    out_ref,
    send_ref,
    keep_ref,
    outward_grad_ref,
    q_s,
    k_s,
    v_s,
    g_s,
    kt_s,
    dq_s,
    dk_s,
    dv_s,
):
    count = 4 * ny
    width = q_s.shape[1]
    core = core_ref[0]
    half = mine_ref.shape[0]
    step = 2 * size
    for base, ref in ((0, mine_ref), (half, other_ref)):
        for start in range(0, half, step):
            rows = slice(start, start + step)
            out_ref[base + start : base + start + step, 0:width] = dot_nt(ref[rows, :], outward_ref[...]).astype(BF16)
    for chunk in range(count):
        rows = chunk_rows(chunk, ny, size, core)
        here = slice(chunk * size, (chunk + 1) * size)
        q_s[here, :] = qkv_ref[rows, 0:width] * 0.125
        key = qkv_ref[rows, width : 2 * width]
        k_s[here, :] = key
        kt_s[:, here] = jnp.transpose(key.astype(F32)).astype(BF16)
        v_s[here, :] = qkv_ref[rows, 2 * width : 3 * width]
        g_s[here, :] = out_ref[rows, 0:width]
    dk_s[...] = jnp.zeros_like(dk_s)
    dv_s[...] = jnp.zeros_like(dv_s)
    lanes = lane_parts(heads, width)
    each = width // heads
    for block in range(count * size // BLOCK):
        first = block * BLOCK
        total = first + BLOCK
        allowed = allowed_pairs(start_ref, first, total)
        q_block, g_block = q_s[first:total, :], g_s[first:total, :]
        queries = []
        for h in range(heads):
            q_one, g_one = only(q_block, lanes[h]), only(g_block, lanes[h])
            scores = dot_nt(k_s[0:total, :], q_one)
            probs = jnp.where(allowed, jnp.exp(scores - log_ref[h : h + 1, first:total]), 0.0)
            prob_grad = dot_nt(v_s[0:total, :], g_one)
            delta = jnp.sum(probs * prob_grad, axis=0, keepdims=True)
            score_grad = (probs * (prob_grad - delta)).astype(BF16)
            dv_s[0:total, :] += dot_nn(probs.astype(BF16), g_one)
            dk_s[0:total, :] += dot_nn(score_grad, q_one)
            queries.append(dot_nn(kt_s[h * each : (h + 1) * each, 0:total], score_grad))
        query_grad = queries[0] if heads == 1 else jnp.concatenate(queries, axis=0)
        dq_s[first:total, :] = jnp.transpose(query_grad) * 0.125
    for chunk in range(count):
        rows = chunk_rows(chunk, ny, size, core)
        here = slice(chunk * size, (chunk + 1) * size)
        out_ref[rows, 0:width] = dq_s[here, :].astype(BF16)
        out_ref[rows, width : 2 * width] = dk_s[here, :].astype(BF16)
        out_ref[rows, 2 * width : 3 * width] = dv_s[here, :].astype(BF16)
    for ref, base in ((send_ref, half), (keep_ref, 0)):
        for start in range(0, half, step):
            rows = slice(base + start, base + start + step)
            ref[start : start + step, :] = dot_nt(out_ref[rows, :], weight_ref[...]).astype(BF16)
    total = dot_tn(near_ref[...], mine_ref[...]) + dot_tn(far_ref[...], other_ref[...])
    outward_grad_ref[...] = total.astype(BF16)


def feed_forward(
    size,
    core_ref,
    mine_ref,
    other_ref,
    up_mine_ref,
    up_other_ref,
    expand_ref,
    shrink_ref,
    bias_ref,
    active_ref,
    grad_ref,
    send_ref,
    keep_ref,
    result_ref,
):
    half = keep_ref.shape[0]
    step = 2 * size
    rate = math.sqrt(2.0 / math.pi)
    core = core_ref[0]
    sides = ((send_ref, other_ref, up_other_ref, half, 1 - core), (keep_ref, mine_ref, up_mine_ref, 0, core))
    for ref, source_ref, up_ref, base, side in sides:
        for start in range(0, half, step):
            rows = slice(start, start + step)
            pair = slice(base + start, base + start + step)
            place = pl.ds(pl.multiple_of(side * half + start, step), step)
            before = dot_nn(source_ref[rows, :], expand_ref[...]) + bias_ref[...]
            upper = dot_nt(up_ref[rows, :], shrink_ref[...])
            square = before * before
            inner = jnp.tanh(rate * (before + 0.044715 * before * square))
            plus = 0.5 * (1.0 + inner)
            active = (before * plus).astype(BF16)
            active_ref[pair, :] = active
            slope = plus + 0.5 * before * (1.0 - inner * inner) * (rate + rate * 3 * 0.044715 * square)
            lower = (upper * slope).astype(BF16)
            grad_ref[pair, :] = lower
            ref[rows, :] = dot_nt(lower, expand_ref[...]).astype(BF16)
            result_ref[place, :] = dot_nn(active, shrink_ref[...]).astype(BF16)


def weight_parts(part, mine_ref, other_ref, up_mine_ref, up_other_ref, active_ref, grad_ref, bias_ref, out_ref):
    half, width = mine_ref.shape
    quarter, all_units = width // NZ, NZ * part
    for r in range(NZ):
        spot, ref = r, out_ref.at[r]
        here = slice(spot * quarter, (spot + 1) * quarter)
        total = dot_tn(mine_ref[:, here], grad_ref[0:half, :]) + dot_tn(other_ref[:, here], grad_ref[half : 2 * half, :])
        ref[0:quarter, :] = total.astype(BF16)
        units = slice(spot * part, (spot + 1) * part)
        total = dot_tn(active_ref[0:half, units], up_mine_ref[...])
        total = (total + dot_tn(active_ref[half : 2 * half, units], up_other_ref[...])).astype(BF16)
        for i in range(width // all_units):
            start = quarter + i * part
            ref[start : start + part, :] = total[:, i * all_units : (i + 1) * all_units]
    bias_ref[...] = jnp.sum(grad_ref[...].astype(F32), axis=0, keepdims=True)


def feed_forward_weights(second, up, active, before_grad):
    frames, units = active.shape
    width, part = up[0].shape[1], units // NZ
    quarter = width // NZ
    if part % 128:
        shrink = dot_tn(active, stack_rows(up)).astype(BF16).reshape(NZ, part, width)
        expand = dot_tn(stack_rows(second), before_grad).astype(BF16).reshape(NZ, quarter, units)
        bias = jnp.sum(before_grad.astype(F32), axis=0, keepdims=True)
        return bias, jnp.stack([stack_rows([expand[k], fold_columns(shrink[k], units)]) for k in range(NZ)])
    return pl.pallas_call(
        functools.partial(weight_parts, part),
        out_shape=(jax.ShapeDtypeStruct((1, units), F32), jax.ShapeDtypeStruct((NZ, 2 * quarter, units), BF16)),
        in_specs=whole(6),
        out_specs=tuple(whole(2)),
        compiler_params=pltpu.CompilerParams(vmem_limit_bytes=16 << 20),
        cost_estimate=pl.CostEstimate(
            flops=4 * frames * width * units, bytes_accessed=8 * frames * width, transcendentals=0
        ),
        name="feed_forward_weights",
    )(*second, *up, active, before_grad)


def whole(count):
    return [pl.BlockSpec(memory_space=pltpu.VMEM)] * count


def attention(core, pair, encoding, affine, w_in, bias, starts, heads, ny, size):
    half, wide = pair[0].shape[0], w_in.shape[1]
    frames, depth, width = 2 * half, pair[0].shape[1], wide // 3
    pairs = frames * frames * heads
    return pl.pallas_call(
        functools.partial(attend, heads, ny, size),
        out_shape=(
            jax.ShapeDtypeStruct((frames, depth), BF16),
            jax.ShapeDtypeStruct((frames, wide), BF16),
            jax.ShapeDtypeStruct((half, width), BF16),
            jax.ShapeDtypeStruct((half, width), BF16),
            jax.ShapeDtypeStruct((heads, frames), F32),
        ),
        in_specs=[pl.BlockSpec(memory_space=pltpu.SMEM)] + whole(7),
        out_specs=tuple(whole(5)),
        scratch_shapes=[
            pltpu.VMEM((frames, width), BF16),
            pltpu.VMEM((frames, width), BF16),
            pltpu.VMEM((width, frames), BF16),
        ],
        compiler_params=pltpu.CompilerParams(vmem_limit_bytes=16 << 20),
        cost_estimate=pl.CostEstimate(
            flops=pairs * 256 + 2 * frames * depth * wide, bytes_accessed=8 * frames * depth, transcendentals=pairs // 2
        ),
        name="attend",
    )(core, *pair, encoding, affine, w_in, bias, starts)


def attention_back(place, qkv, pair, context, w_out, w_in, starts, log_total, heads, ny, size):
    frames, wide = qkv.shape
    width = wide // 3
    depth = pair[0].shape[1]
    pairs = frames * frames * heads
    half = jax.ShapeDtypeStruct(pair[0].shape, BF16)
    return pl.pallas_call(
        functools.partial(attend_back, heads, ny, size),
        out_shape=(
            jax.ShapeDtypeStruct((frames, wide), BF16),
            half,
            half,
            jax.ShapeDtypeStruct((width, depth), BF16),
        ),
        in_specs=[pl.BlockSpec(memory_space=pltpu.SMEM)] + whole(9),
        out_specs=tuple(whole(4)),
        scratch_shapes=[pltpu.VMEM((frames, width), BF16)] * 4
        + [pltpu.VMEM((width, frames), BF16)]
        + [pltpu.VMEM((frames, width), F32)] * 3,
        compiler_params=pltpu.CompilerParams(vmem_limit_bytes=20 << 20),
        cost_estimate=pl.CostEstimate(
            flops=pairs * 640 + 2 * frames * depth * (wide + 2 * width),
            bytes_accessed=8 * frames * depth,
            transcendentals=pairs // 2,
        ),
        name="attend_back",
    )(place.core, qkv, *pair, *context, w_out, w_in, starts, log_total)


def feed_forward_front(core, pair, up_pair, w_expand, w_shrink, bias, size):
    frames, width = 2 * pair[0].shape[0], pair[0].shape[1]
    units = w_expand.shape[1]
    half = jax.ShapeDtypeStruct((frames // 2, width), BF16)
    inner = jax.ShapeDtypeStruct((frames, units), BF16)
    return pl.pallas_call(
        functools.partial(feed_forward, size),
        out_shape=(inner, inner, half, half, jax.ShapeDtypeStruct((frames, width), BF16)),
        in_specs=[pl.BlockSpec(memory_space=pltpu.SMEM)] + whole(7),
        out_specs=tuple(whole(5)),
        compiler_params=pltpu.CompilerParams(vmem_limit_bytes=16 << 20),
        cost_estimate=pl.CostEstimate(
            flops=8 * frames * width * units, bytes_accessed=10 * frames * width, transcendentals=frames * units
        ),
        name="feed_forward",
    )(core, *pair, *up_pair, w_expand, w_shrink, bias)


class Place:
    def __init__(self, ny):
        self.x, self.z, self.y, self.c = (lax.axis_index(a) for a in ("x", "z", "y", "c"))
        self.xy = jnp.reshape(self.x * ny + self.y, (1,)).astype(jnp.int32)
        self.core = jnp.reshape(self.c, (1,)).astype(jnp.int32)
        self.layer = jnp.reshape(self.z, (1,)).astype(jnp.int32)


def on_device(
    groups,
    ny,
    frames,
    cotangent,
    segment_lengths,
    position_offsets,
    first_gain,
    first_shift,
    inward_weight,
    query_bias,
    value_bias,
    outward_weight,
    outward_bias,
    second_gain,
    second_shift,
    expand_weight,
    expand_bias,
    shrink_weight,
    shrink_bias,
):
    place = Place(ny)
    x, z, y, c = place.x, place.z, place.y, place.c
    local_len, rows, width = frames.shape
    share = inward_weight.shape[0]
    layer = 4 * ny
    spread = NZ * ny * 2
    full_len = local_len * spread
    size = 2 * local_len
    hd = HEADS // layer
    hw = hd * (width // HEADS)
    hidden = expand_bias.shape[0]
    part = hidden // 2
    me = (c * 2 + x) * ny + y

    def sum_groups(value):
        return lax.psum(value, "g") if groups > 1 else value

    def exchange(value, axes):
        return lax.all_to_all(value, axes, 0, 0, tiled=True)

    both = to_home(jnp.concatenate([frames, cotangent], axis=2), place)
    table = jnp.stack([segment_lengths, position_offsets], axis=1)
    other_table = hop(table, "x")
    other_table, later_inward = after(other_table, inward_weight)

    small = [first_gain, first_shift, query_bias, value_bias, outward_bias, second_gain, second_shift, shrink_bias]
    kinds = len(small) + hidden // share
    units = NZ * part
    packed = jnp.concatenate([v[None] for v in small] + [expand_bias.reshape(-1, share)], axis=0)
    packed = packed.reshape(-1, 3 * hw)
    extra = packed.shape[0]
    packed = jnp.pad(packed, ((0, SMALL_ROWS - extra), (0, units)))[None]
    in_cols = jnp.transpose(later_inward.reshape(share, 3, 2, 2, ny, hw), (3, 4, 2, 0, 1, 5))
    in_cols = pick(in_cols, x).reshape(ny * 2, share, 3 * hw)
    ex_cols = pick(expand_weight.reshape(share, NZ, ny, 2, 2, part), x, 4)
    ex_cols = jnp.transpose(ex_cols, (2, 3, 0, 1, 4)).reshape(ny * 2, share, units)
    columns = jnp.concatenate([in_cols, ex_cols], axis=2)
    columns = jnp.concatenate([columns, jnp.broadcast_to(packed, (ny * 2,) + packed.shape[1:])], axis=1)
    columns = exchange(columns, ("y", "c"))

    row_x = jnp.where((z == 0) | (z == 3), 1, 0)
    table = pick(jnp.where(x == row_x, table, other_table), z >> 1)
    lengths, offsets = table[0], table[1]
    count = lengths.shape[0]
    starts = jnp.sum(
        jnp.where(jnp.arange(count)[None, :] < jnp.arange(count)[:, None], lengths[None, :], 0), axis=1
    )
    frame_ids = jnp.arange(full_len, dtype=jnp.int32)
    row_starts = jnp.max(jnp.where(starts[:, None] <= frame_ids[None, :], starts[:, None], 0), axis=0)[None, :]
    spot = jnp.arange(2 * ny)
    chunk = jnp.concatenate([(2 * (spot // ny) + i) * ny + spot % ny for i in (c, 1 - c)])
    mine = (chunk[:, None] * size + jnp.arange(size, dtype=jnp.int32)).reshape(-1)
    inside = (mine[:, None] >= starts[None, :]) & (mine[:, None] < (starts + lengths)[None, :])
    position = jnp.sum(jnp.where(inside, offsets[None, :] + mine[:, None] - starts[None, :], 0), axis=1)
    encoding = sin_cos(position, width)

    both, later_outward, columns = after(both, outward_weight, columns)
    fr, ct = both[:, :width], both[:, width:]
    outward = lax.all_gather(later_outward, SEQ, axis=0, tiled=True)
    in_part = columns[:, :, : 3 * hw].reshape(-1, 3 * hw)
    in_parts = [in_part] + [hop(in_part, "z", NZ, k) for k in range(1, NZ)]
    sh_rows = lax.dynamic_slice_in_dim(shrink_weight, x * part, part, 0)
    ff_part = stack_rows([columns[:, :share, 3 * hw :].reshape(-1, units), fold_columns(sh_rows, units)])
    mine, up_mine = assemble_pair(near_parts(both, ny), place.xy)
    ff_part = jnp.broadcast_to(ff_part[None], (NZ,) + ff_part.shape)
    mine, encoding, ff_part, *in_parts = after(mine, encoding, ff_part, *in_parts)
    first_pair = [mine, hop(mine, "c")]
    w_in, small_rows = collect_inward(in_parts, place, share)
    ff_got = exchange(ff_part, ("z",))

    vectors = small_rows.reshape(spread, SMALL_ROWS, 3 * hw)[:, :extra].reshape(spread, kinds, share).astype(F32)
    expand_b = vectors[:, len(small) :].reshape(NZ, ny, 2, 2, part)
    expand_b = pick(pick(pick(expand_b, y, 1), c, 1), x, 1).reshape(1, NZ * part)
    vectors = jnp.swapaxes(vectors[:, : len(small)], 0, 1).reshape(len(small), width)
    gain_one, shift_one, query_b, value_b, outward_b, gain_two, shift_two, shrink_b = (
        vectors[i : i + 1] for i in range(len(small))
    )
    qkv_bias = jnp.concatenate(
        [
            lax.dynamic_slice_in_dim(query_b, me * hw, hw, 1),
            jnp.zeros((1, hw), F32),
            lax.dynamic_slice_in_dim(value_b, me * hw, hw, 1),
        ],
        axis=1,
    )

    first_all, qkv, *context_pair, log_total = attention(
        place.core, first_pair, encoding, vectors[:2], w_in, qkv_bias, row_starts, hd, ny, size
    )
    *context_pair, up_mine = after(*context_pair, up_mine)
    if ny == 2:
        context = by_half(c, context_pair[0][None], hop(context_pair[1], "c")[None], 0)
        context = context.reshape(2, 2, ny, size, hw)
        context = by_half(x, pick(context, x, 1)[:, None], hop(pick(context, 1 - x, 1), "x")[:, None], 1)
        context = by_half(y, pick(context, y, 2)[:, :, None], hop(pick(context, 1 - y, 2), "y")[:, :, None], 2)
    else:
        context = exchange(by_half(c, *context_pair, 0).reshape(layer, size, hw), LAYER)
    context = context.reshape(layer, size, hw)
    up_pair = [up_mine, hop(up_mine, "c")]

    inputs = fr.astype(F32) + lax.dynamic_slice_in_dim(encoding, (x * ny + y) * size, size, 0)
    normal_one, scale_one = normalize(inputs)
    context = jnp.swapaxes(context, 0, 1).reshape(size, width)
    middle = inputs + dot_nn(context, outward) + outward_b

    normal_two, scale_two = normalize(middle)
    second = (normal_two * gain_two + shift_two).astype(BF16)
    ff_got, *second_near = after(ff_got, *near_parts(second, ny))
    second_pair = both_cores(second_near, place)
    w_expand, w_shrink = collect_hidden(ff_got, width)
    active, before_grad, send, keep, out_part = feed_forward_front(
        place.core, second_pair, up_pair, w_expand, w_shrink, expand_b, size
    )
    second_parts = list(fold(keep, hop(send, "c"), place, ny))
    second_parts[0], active, before_grad = after(second_parts[0], active, before_grad)
    second_grad = finish(second_parts, ny)
    expand_b_sum, hidden_part = feed_forward_weights(second_pair, up_pair, active, before_grad)
    out_part = lax.psum_scatter(out_part, LAYER, scatter_dimension=0, tiled=True)
    second_grad, hidden_part = after(second_grad, hidden_part)
    hidden_got = exchange(hidden_part, ("z",))

    upstream = ct.astype(F32)
    middle_part, gain_two_sum, shift_two_sum = normalize_back(normal_two, scale_two, gain_two, second_grad)
    middle_grad = upstream + middle_part
    low_middle = middle_grad.astype(BF16)
    low_pair = both_cores(near_parts(low_middle, ny), place)
    w_out = lax.dynamic_slice_in_dim(outward, me * hw, hw, 0)
    mixed_grad, send, keep, outward_part = attention_back(
        place, qkv, low_pair, context_pair, w_out, w_in, row_starts, log_total, hd, ny, size
    )
    got = hop(send, "c")
    cut = outward_part.reshape(2, -1, width)
    far_cut = hop(pick(cut, 1 - c), "c")
    got, far_cut, out_part = after(got, far_cut, out_part)
    first_parts = list(fold(keep, got, place, ny))
    first_parts[0], mixed_late, far_cut, hidden_got = after(first_parts[0], mixed_grad, far_cut, hidden_got)
    inward_part = dot_tn(first_all, mixed_late).astype(BF16)
    first_grad = finish(first_parts, ny)
    inward_got = exchange(inward_part.reshape(spread, share, 3 * hw), SEQ)
    input_part, gain_one_sum, shift_one_sum = normalize_back(normal_one, scale_one, vectors[:1], first_grad)
    late = (middle_grad + input_part).astype(BF16)
    late, out_part, hidden_got = after(late, out_part, hidden_got)
    hidden_sum = sum_sources(hidden_got, NZ)
    frames_grad = to_origin(late, place)
    inward_got, out_part = after(inward_got, out_part)
    layer_output = to_origin((middle + out_part.astype(F32) + shrink_b).astype(BF16), place)

    split = width // 2
    hidden_sum = sum_groups(hidden_sum.reshape(-1, units)).astype(BF16)
    line = hidden_sum[: width // NZ].reshape(ny, 2, share, units)
    if ny == 2:
        line = by_half(c, pick(line, c, 1)[:, None], hop(pick(line, 1 - c, 1), "c")[:, None], 1)
        line = by_half(y, pick(line, y)[None], hop(pick(line, 1 - y), "y")[None], 0)
    else:
        line = exchange(line.reshape(ny * 2, share, units), ("y", "c"))
    mine = stack_rows([line.reshape(-1, units), hidden_sum[width // NZ :]])
    other = hop(mine, "x")

    def full_hidden(other):
        pair = [unfold_columns(v[width // NZ :], width // units) for v in (mine, other)]
        g_shrink = by_half(x, *pair, 0).astype(F32)
        pair = [v[: width // NZ].reshape(ny, 2, 1, share, NZ, part) for v in (mine, other)]
        return g_shrink, jnp.transpose(by_half(x, *pair, 2), (3, 4, 0, 1, 2, 5)).reshape(share, -1).astype(F32)

    if hd == 2 and ny == 2:
        line = by_half(c, pick(cut, c)[None], far_cut[None], 0)
        line = line.reshape(2, 1, share, 2, split)
        line = by_half(x, pick(line, x, 3), hop(pick(line, 1 - x, 3), "x"), 1)
        out_got = lax.psum_scatter(line.reshape(NZ * share, split), "z", scatter_dimension=0, tiled=True)
        inward_got, out_got = after(inward_got, out_got)
        out_sum = sum_groups(out_got.astype(F32)).astype(BF16)
        g_outward = by_half(x, out_sum, hop(out_sum, "x"), 1).astype(F32)
    else:
        cut = lax.dynamic_update_slice(jnp.zeros((width, width), BF16), outward_part, (me * hw, 0))
        g_outward = lax.psum_scatter(cut, SEQ, scatter_dimension=0, tiled=True)
        g_outward = lax.psum(g_outward.astype(F32), ("g", "x"))

    mixed_sum = jnp.sum(mixed_grad.astype(F32), axis=0)

    def from_heads(value):
        return lax.dynamic_update_slice(jnp.zeros((width,), F32), value, (me * hw,))

    flat = lax.optimization_barrier(jnp.stack(
        [
            gain_one_sum,
            shift_one_sum,
            from_heads(mixed_sum[:hw]),
            from_heads(mixed_sum[2 * hw :]),
            jnp.sum(low_middle.astype(F32), axis=0),
            gain_two_sum,
            shift_two_sum,
            jnp.sum(upstream, axis=0),
        ]
    ))
    small_len = len(small) * share
    sums = jnp.swapaxes(flat.reshape(len(small), spread, share), 0, 1).reshape(spread, small_len)
    spot = jnp.zeros((NZ, ny, 2, 2, part), F32)
    spot = lax.dynamic_update_slice(spot, expand_b_sum.reshape(NZ, 1, 1, 1, part), (0, y, c, x, 0))
    sums = jnp.concatenate([sums, spot.reshape(spread, hidden)], axis=1)
    inward_got, sums = after(inward_got, sums)
    sums = jnp.broadcast_to(sums[None], (2,) + sums.shape).reshape(2 * spread, -1, 128)
    total = sum_groups(jnp.sum(exchange(sums, ("x",) + SEQ), axis=0)).reshape(-1)
    frames_grad, total, other = after(frames_grad, total, other)
    g_shrink, g_expand = full_hidden(other)
    g_small = total[:small_len].reshape(len(small), share)
    g_expand_b = total[small_len:]
    inward_sum = sum_groups(sum_sources(inward_got, NZ)).astype(BF16)
    g_inward = [v.reshape(ny, 2, 1, share, 3, hw) for v in (inward_sum, hop(inward_sum, "x"))]
    g_inward = jnp.transpose(by_half(x, *g_inward, 2), (3, 4, 1, 2, 0, 5)).reshape(share, -1).astype(F32)

    return (
        layer_output,
        frames_grad.astype(F32),
        g_small[0],
        g_small[1],
        g_inward,
        g_small[2],
        g_small[3],
        g_outward,
        g_small[4],
        g_small[5],
        g_small[6],
        g_expand,
        g_expand_b,
        g_shrink,
        g_small[7],
    )


def solution(mesh):
    batch, seq = mesh.shape["batch"], mesh.shape["seq"]
    groups, ny = batch // 2, seq // (2 * NZ)
    fine = Mesh(mesh.devices.reshape(groups, 2, NZ, ny, 2), ("g", "x", "z", "y", "c"))
    b, s = ("g", "x"), ("z", "y", "c")
    in_specs = (
        P(s, b, None),
        P(s, b, None),
        P(b, None),
        P(b, None),
        P(s),
        P(s),
        P(s, None),
        P(s),
        P(s),
        P(s, None),
        P(s),
        P(s),
        P(s),
        P(s, None),
        P(s),
        P(s, None),
        P(s),
    )
    out_specs = (
        P(s, b, None),
        P(s, b, None),
        P(s),
        P(s),
        P(s, None),
        P(s),
        P(s),
        P(s, None),
        P(s),
        P(s),
        P(s),
        P(s, None),
        P(s),
        P(s, None),
        P(s),
    )
    return jax.shard_map(
        functools.partial(on_device, groups, ny), mesh=fine, in_specs=in_specs, out_specs=out_specs, check_vma=False
    )
```

```python
import functools
import math

import jax
import jax.numpy as jnp
from jax import lax
from jax.experimental import pallas as pl
from jax.experimental.pallas import tpu as pltpu
from jax.sharding import Mesh, PartitionSpec as P


HEADS = 16
NZ = 4
SMALL_ROWS = 16
NORM_EPS = 1e-05
NEG = -1e30
F32 = jnp.float32
BF16 = jnp.bfloat16
LAYER_OF_ROW = (1, 2, 0, 3)
SWAP = [(0, 1), (1, 0)]
LAYER = ("c", "x", "y")
SEQ = ("z", "y", "c")


def xor_perm(count, k):
    return [(i, i ^ k) for i in range(count)]


def hop(value, axis, count=2, k=1):
    return lax.ppermute(value, axis, xor_perm(count, k))


def pick(value, index, axis=0):
    return lax.dynamic_index_in_dim(value, index, axis, keepdims=False)


def stack_rows(parts):
    return jnp.concatenate(parts, axis=0)


def assemble_body(pieces, size, place_ref, *refs):
    out_ref = refs[pieces]
    for r in range(pieces):
        spot = place_ref[0] ^ r
        out_ref[pl.ds(pl.multiple_of(spot * size, size), size), :] = refs[r][...]


def assemble(parts, me):
    size, width = parts[0].shape
    count = len(parts)
    return pl.pallas_call(
        functools.partial(assemble_body, count, size),
        out_shape=jax.ShapeDtypeStruct((count * size, width), parts[0].dtype),
        in_specs=[pl.BlockSpec(memory_space=pltpu.SMEM)] + whole(count),
        out_specs=whole(1)[0],
        compiler_params=pltpu.CompilerParams(vmem_limit_bytes=4 << 20),
        cost_estimate=pl.CostEstimate(flops=0, bytes_accessed=4 * count * size * width, transcendentals=0),
        name="assemble",
    )(me, *parts)


def assemble_pair_body(pieces, size, place_ref, *refs):
    left_ref, right_ref = refs[pieces:]
    width = left_ref.shape[1]
    for r in range(pieces):
        rows = pl.ds(pl.multiple_of((place_ref[0] ^ r) * size, size), size)
        left_ref[rows, :] = refs[r][:, 0:width]
        right_ref[rows, :] = refs[r][:, width : 2 * width]


def assemble_pair(parts, me):
    size, width = parts[0].shape
    count = len(parts)
    return pl.pallas_call(
        functools.partial(assemble_pair_body, count, size),
        out_shape=[jax.ShapeDtypeStruct((count * size, width // 2), parts[0].dtype)] * 2,
        in_specs=[pl.BlockSpec(memory_space=pltpu.SMEM)] + whole(count),
        out_specs=whole(2),
        compiler_params=pltpu.CompilerParams(vmem_limit_bytes=4 << 20),
        cost_estimate=pl.CostEstimate(flops=0, bytes_accessed=4 * count * size * width, transcendentals=0),
        name="assemble_pair",
    )(me, *parts)


def near_parts(block, ny):
    return [block] + [lax.ppermute(block, ("x", "y"), xor_perm(2 * ny, r)) for r in range(1, 2 * ny)]


def both_cores(parts, place):
    mine = assemble(parts, place.xy)
    return mine, hop(mine, "c")


def fold_body(count, size, place_ref, keep_ref, got_ref, own_ref, *out_refs):
    for r in range(count):
        spot = place_ref[0] ^ r
        here = pl.ds(pl.multiple_of(spot * size, size), size)
        value = keep_ref[here, :].astype(F32) + got_ref[here, :].astype(F32)
        if r == 0:
            own_ref[...] = value
        else:
            out_refs[r - 1][...] = value.astype(BF16)


def fold(keep, got, place, ny):
    rows, width = keep.shape
    count = 2 * ny
    size = rows // count
    return pl.pallas_call(
        functools.partial(fold_body, count, size),
        out_shape=[jax.ShapeDtypeStruct((size, width), F32)] + [jax.ShapeDtypeStruct((size, width), BF16)] * (count - 1),
        in_specs=[pl.BlockSpec(memory_space=pltpu.SMEM)] + whole(2),
        out_specs=whole(count),
        compiler_params=pltpu.CompilerParams(vmem_limit_bytes=4 << 20),
        cost_estimate=pl.CostEstimate(flops=count * size * width, bytes_accessed=6 * count * size * width, transcendentals=0),
        name="fold",
    )(place.xy, keep, got)


def finish(parts, ny):
    own = parts[0]
    for r in range(1, 2 * ny):
        own = own + lax.ppermute(parts[r], ("x", "y"), xor_perm(2 * ny, r)).astype(F32)
    return own


def fold_columns(value, units):
    return stack_rows([value[:, i : i + units] for i in range(0, value.shape[1], units)])


def unfold_columns(value, count):
    size = value.shape[0] // count
    return jnp.concatenate([value[i * size : (i + 1) * size] for i in range(count)], axis=1)


def collect_inward_body(share, place_ref, *refs):
    weight_ref, small_ref = refs[NZ:]
    deep = share + SMALL_ROWS
    lines = refs[0].shape[0] // deep
    for r in range(NZ):
        base = (place_ref[0] ^ r) * lines
        for i in range(lines):
            start = i * deep
            rows = pl.ds(pl.multiple_of((base + i) * share, share), share)
            weight_ref[rows, :] = refs[r][start : start + share, :]
            rows = pl.ds(pl.multiple_of((base + i) * SMALL_ROWS, SMALL_ROWS), SMALL_ROWS)
            small_ref[rows, :] = refs[r][start + share : start + deep, :]


def collect_inward(parts, place, share):
    rows, width = parts[0].shape
    lines = NZ * rows // (share + SMALL_ROWS)
    return pl.pallas_call(
        functools.partial(collect_inward_body, share),
        out_shape=[jax.ShapeDtypeStruct((lines * n, width), BF16) for n in (share, SMALL_ROWS)],
        in_specs=[pl.BlockSpec(memory_space=pltpu.SMEM)] + whole(NZ),
        out_specs=whole(2),
        compiler_params=pltpu.CompilerParams(vmem_limit_bytes=4 << 20),
        cost_estimate=pl.CostEstimate(flops=0, bytes_accessed=16 * rows * width, transcendentals=0),
        name="collect_inward",
    )(place.layer, *parts)


def collect_hidden_body(parts_ref, expand_ref, shrink_ref):
    quarter = expand_ref.shape[0] // NZ
    part, units = shrink_ref.shape[0] // NZ, expand_ref.shape[1]
    for r in range(NZ):
        expand_ref[r * quarter : (r + 1) * quarter, :] = parts_ref[r, 0:quarter, :]
        for i in range(shrink_ref.shape[1] // units):
            start = quarter + i * part
            here = slice(r * part, (r + 1) * part)
            shrink_ref[here, i * units : (i + 1) * units] = parts_ref[r, start : start + part, :]


def collect_hidden(parts, width):
    units = parts.shape[2]
    return pl.pallas_call(
        collect_hidden_body,
        out_shape=[jax.ShapeDtypeStruct((width, units), BF16), jax.ShapeDtypeStruct((units, width), BF16)],
        in_specs=whole(1),
        out_specs=whole(2),
        compiler_params=pltpu.CompilerParams(vmem_limit_bytes=4 << 20),
        cost_estimate=pl.CostEstimate(flops=0, bytes_accessed=4 * parts.size, transcendentals=0),
        name="collect_hidden",
    )(parts)


def rehome_flat(x, z, c):
    return (x * NZ + z) * 2 + c


def rehome_perm(k):
    return [
        (rehome_flat(x, z, c), rehome_flat(z >> 1, LAYER_OF_ROW[2 * x + (c ^ k)], z & 1))
        for x in range(2)
        for z in range(NZ)
        for c in range(2)
    ]


def to_home(block, place):
    got = [
        lax.ppermute(jnp.where(place.c == k, block[:, 0], block[:, 1]), ("x", "z", "c"), rehome_perm(k))
        for k in range(2)
    ]
    first = place.z < 2
    return stack_rows([jnp.where(first, got[0], got[1]), jnp.where(first, got[1], got[0])])


def to_origin(block, place):
    half = block.shape[0] // 2
    first = place.z < 2
    low, high = block[:half], block[half:]
    sent = [jnp.where(first, low, high), jnp.where(first, high, low)]
    got = [
        lax.ppermute(sent[k], ("x", "z", "c"), [(b, a) for a, b in rehome_perm(k)]) for k in range(2)
    ]
    return jnp.stack(
        [jnp.where(place.c == 0, got[0], got[1]), jnp.where(place.c == 0, got[1], got[0])], axis=1
    )


def after(first, *values):
    return lax.optimization_barrier((first, *values))


def sum_sources(value, count):
    return jnp.sum(value.reshape((count, -1) + value.shape[1:]).astype(F32), axis=0)


def by_half(x, mine, other, axis):
    return jnp.concatenate([jnp.where(x == 0, mine, other), jnp.where(x == 0, other, mine)], axis=axis)


def sin_cos(position, width):
    feature = jnp.arange(width, dtype=jnp.int32)
    rates = jnp.exp((feature // 2).astype(F32) * (-2.0 * math.log(10000.0) / width))
    angle = position.astype(F32)[:, None] * rates[None, :]
    turn = jnp.round(angle * (2.0 / math.pi))
    rest = angle - turn * 1.5703125
    rest = rest - turn * 0.00048375129699707031
    rest = rest - turn * 7.5497899548918861e-08
    quadrant = turn.astype(jnp.int32) + (feature % 2)[None, :]
    square = rest * rest
    sine = rest + rest * square * (
        -0.16666666641626524 + square * (0.008333329385889463 + square * (-0.00019839334836096632 + square * 2.718311493989822e-06))
    )
    cosine = 1.0 + square * (
        -0.49999999725103100 + square * (0.04166662332373906 + square * (-0.001388676377460993 + square * 2.439044879627741e-05))
    )
    value = jnp.where((quadrant & 1) == 0, sine, cosine)
    return jnp.where((quadrant & 2) == 0, value, -value)


def normalize(values):
    center = values - jnp.mean(values, axis=-1, keepdims=True)
    scale = lax.rsqrt(jnp.mean(center * center, axis=-1, keepdims=True) + NORM_EPS)
    return center * scale, scale


def normalize_back(normal, scale, gain, upstream):
    scaled = upstream * gain
    inner = scaled - jnp.mean(scaled, axis=-1, keepdims=True)
    inner = inner - normal * jnp.mean(scaled * normal, axis=-1, keepdims=True)
    return inner * scale, jnp.sum(upstream * normal, axis=0), jnp.sum(upstream, axis=0)


def dot_nt(a, b):
    return lax.dot_general(a, b, (((1,), (1,)), ((), ())), preferred_element_type=F32)


def dot_tn(a, b):
    return lax.dot_general(a, b, (((0,), (0,)), ((), ())), preferred_element_type=F32)


def dot_nn(a, b):
    return jnp.dot(a, b, preferred_element_type=F32)


BLOCK = 256


def chunk_owner(chunk, ny):
    outer, y = divmod(chunk, ny)
    return ((outer & 1) * 2 + (outer >> 1)) * ny + y


def lane_parts(heads, width):
    if heads == 1:
        return [None]
    lane = lax.broadcasted_iota(jnp.int32, (1, width), 1)
    return [(lane >= h * (width // heads)) & (lane < (h + 1) * (width // heads)) for h in range(heads)]


def only(value, lanes):
    return value if lanes is None else jnp.where(lanes, value, jnp.zeros_like(value))


def allowed_pairs(start_ref, first, total):
    key = lax.broadcasted_iota(jnp.int32, (total, BLOCK), 0)
    frame = first + lax.broadcasted_iota(jnp.int32, (total, BLOCK), 1)
    return (key >= start_ref[:, first : first + BLOCK]) & (key <= frame)


def chunk_rows(chunk, ny, size, core):
    half, spot = divmod(chunk_owner(chunk, ny), 2 * ny)
    return pl.ds(pl.multiple_of(((half ^ core) * (2 * ny) + spot) * size, size), size)


def attend(
    heads,
    ny,
    size,
    core_ref,
    mine_ref,
    other_ref,
    encoding_ref,
    affine_ref,
    weight_ref,
    bias_ref,
    start_ref,
    first_ref,
    qkv_ref,
    near_ref,
    far_ref,
    log_ref,
    q_s,
    k_s,
    vt_s,
    encoding_s,
    first_s,
    qkv_s,
    in_sem,
    out_sem,
):
    count = 4 * ny
    width = q_s.shape[1]
    core = core_ref[0]
    step = 2 * size
    half = mine_ref.shape[0]
    blocks = 2 * half // step

    def encoding_copy(i):
        rows = pl.ds(i * step, step)
        return pltpu.make_async_copy(encoding_ref.at[rows], encoding_s.at[rows], in_sem.at[i])

    def first_copy(i):
        rows = pl.ds(i * step, step)
        return pltpu.make_async_copy(first_s.at[rows], first_ref.at[rows], out_sem.at[i])

    for i in range(blocks):
        encoding_copy(i).start()
    for i in range(blocks):
        ref, start = (mine_ref, i * step) if i * step < half else (other_ref, i * step - half)
        rows = slice(i * step, (i + 1) * step)
        encoding_copy(i).wait()
        normal, _ = normalize(ref[start : start + step, :].astype(F32) + encoding_s[rows, :])
        value = (normal * affine_ref[0:1, :] + affine_ref[1:2, :]).astype(BF16)
        first_s[rows, :] = value
        first_copy(i).start()
        qkv_s[rows, :] = (dot_nn(value, weight_ref[...]) + bias_ref[...]).astype(BF16)
    qkv_copy = pltpu.make_async_copy(qkv_s, qkv_ref, out_sem.at[blocks])
    qkv_copy.start()
    for chunk in range(count):
        rows = chunk_rows(chunk, ny, size, core)
        here = slice(chunk * size, (chunk + 1) * size)
        q_s[here, :] = qkv_s[rows, 0:width] * 0.125
        k_s[here, :] = qkv_s[rows, width : 2 * width]
        vt_s[:, here] = jnp.transpose(qkv_s[rows, 2 * width : 3 * width].astype(F32)).astype(BF16)
    lanes = lane_parts(heads, width)
    each = width // heads
    for block in range(count * size // BLOCK):
        first = block * BLOCK
        total = first + BLOCK
        allowed = allowed_pairs(start_ref, first, total)
        q_block = q_s[first:total, :]
        contexts = []
        for h in range(heads):
            scores = dot_nt(k_s[0:total, :], only(q_block, lanes[h]))
            scores = jnp.where(allowed, scores, NEG)
            top = jnp.max(scores, axis=0, keepdims=True)
            weight = jnp.exp(scores - top)
            mass = jnp.sum(weight, axis=0, keepdims=True)
            part = dot_nn(vt_s[h * each : (h + 1) * each, 0:total], weight.astype(BF16))
            contexts.append(part / mass)
            log_ref[h : h + 1, first:total] = top + jnp.log(mass)
        context = contexts[0] if heads == 1 else jnp.concatenate(contexts, axis=0)
        context = jnp.transpose(context).astype(BF16)
        for sub in range(BLOCK // size):
            owner = chunk_owner(block * (BLOCK // size) + sub, ny)
            side, spot = divmod(owner, 2 * ny)
            rows, piece = slice(spot * size, (spot + 1) * size), context[sub * size : (sub + 1) * size]

            @pl.when(core == side)
            def _(rows=rows, piece=piece):
                near_ref[rows, :] = piece

            @pl.when(core != side)
            def _(rows=rows, piece=piece):
                far_ref[rows, :] = piece
    for i in range(blocks):
        first_copy(i).wait()
    qkv_copy.wait()


def attend_back(
    heads,
    ny,
    size,
    place_ref,
    qkv_any,
    mine_ref,
    other_any,
    near_any,
    far_any,
    outward_any,
    weight_any,
    start_ref,
    log_ref,
    out_ref,
    send_ref,
    keep_ref,
    outward_grad_ref,
    q_s,
    k_s,
    v_s,
    g_s,
    kt_s,
    dq_s,
    dk_s,
    dv_s,
    qkv_ref,
    other_ref,
    near_ref,
    far_ref,
    outward_ref,
    weight_ref,
    in_sem,
):
    count = 4 * ny
    width = q_s.shape[1]
    core = place_ref[0]
    half = mine_ref.shape[0]
    step = 2 * size
    rows = pl.ds(pl.multiple_of(place_ref[1] * width, width), width)
    pairs = (
        (outward_any.at[rows], outward_ref),
        (other_any, other_ref),
        (qkv_any, qkv_ref),
        (weight_any, weight_ref),
        (near_any, near_ref),
        (far_any, far_ref),
    )
    copies = [pltpu.make_async_copy(source, target, in_sem.at[i]) for i, (source, target) in enumerate(pairs)]
    for copy in copies:
        copy.start()
    copies[0].wait()
    for base, ref in ((0, mine_ref), (half, other_ref)):
        if base:
            copies[1].wait()
        for start in range(0, half, step):
            rows = slice(start, start + step)
            out_ref[base + start : base + start + step, 0:width] = dot_nt(ref[rows, :], outward_ref[...]).astype(BF16)
    copies[2].wait()
    for chunk in range(count):
        rows = chunk_rows(chunk, ny, size, core)
        here = slice(chunk * size, (chunk + 1) * size)
        q_s[here, :] = qkv_ref[rows, 0:width] * 0.125
        key = qkv_ref[rows, width : 2 * width]
        k_s[here, :] = key
        kt_s[:, here] = jnp.transpose(key.astype(F32)).astype(BF16)
        v_s[here, :] = qkv_ref[rows, 2 * width : 3 * width]
        g_s[here, :] = out_ref[rows, 0:width]
    dk_s[...] = jnp.zeros_like(dk_s)
    dv_s[...] = jnp.zeros_like(dv_s)
    lanes = lane_parts(heads, width)
    each = width // heads
    for block in range(count * size // BLOCK):
        first = block * BLOCK
        total = first + BLOCK
        allowed = allowed_pairs(start_ref, first, total)
        q_block, g_block = q_s[first:total, :], g_s[first:total, :]
        queries = []
        for h in range(heads):
            q_one, g_one = only(q_block, lanes[h]), only(g_block, lanes[h])
            scores = dot_nt(k_s[0:total, :], q_one)
            probs = jnp.where(allowed, jnp.exp(scores - log_ref[h : h + 1, first:total]), 0.0)
            prob_grad = dot_nt(v_s[0:total, :], g_one)
            delta = jnp.sum(probs * prob_grad, axis=0, keepdims=True)
            score_grad = (probs * (prob_grad - delta)).astype(BF16)
            dv_s[0:total, :] += dot_nn(probs.astype(BF16), g_one)
            dk_s[0:total, :] += dot_nn(score_grad, q_one)
            queries.append(dot_nn(kt_s[h * each : (h + 1) * each, 0:total], score_grad))
        query_grad = queries[0] if heads == 1 else jnp.concatenate(queries, axis=0)
        dq_s[first:total, :] = jnp.transpose(query_grad) * 0.125
    for chunk in range(count):
        rows = chunk_rows(chunk, ny, size, core)
        here = slice(chunk * size, (chunk + 1) * size)
        out_ref[rows, 0:width] = dq_s[here, :].astype(BF16)
        out_ref[rows, width : 2 * width] = dk_s[here, :].astype(BF16)
        out_ref[rows, 2 * width : 3 * width] = dv_s[here, :].astype(BF16)
    for copy in copies[3:]:
        copy.wait()
    for ref, base in ((send_ref, half), (keep_ref, 0)):
        for start in range(0, half, step):
            rows = slice(base + start, base + start + step)
            ref[start : start + step, :] = dot_nt(out_ref[rows, :], weight_ref[...]).astype(BF16)
    total = dot_tn(near_ref[...], mine_ref[...]) + dot_tn(far_ref[...], other_ref[...])
    outward_grad_ref[...] = total.astype(BF16)


def feed_forward(
    size,
    core_ref,
    mine_ref,
    other_ref,
    up_mine_ref,
    up_other_ref,
    expand_ref,
    shrink_ref,
    bias_ref,
    active_ref,
    grad_ref,
    send_ref,
    keep_ref,
    result_ref,
):
    half = keep_ref.shape[0]
    step = 2 * size
    rate = math.sqrt(2.0 / math.pi)
    core = core_ref[0]
    sides = ((send_ref, other_ref, up_other_ref, half, 1 - core), (keep_ref, mine_ref, up_mine_ref, 0, core))
    for ref, source_ref, up_ref, base, side in sides:
        for start in range(0, half, step):
            rows = slice(start, start + step)
            pair = slice(base + start, base + start + step)
            place = pl.ds(pl.multiple_of(side * half + start, step), step)
            before = dot_nn(source_ref[rows, :], expand_ref[...]) + bias_ref[...]
            upper = dot_nt(up_ref[rows, :], shrink_ref[...])
            square = before * before
            inner = jnp.tanh(rate * (before + 0.044715 * before * square))
            plus = 0.5 * (1.0 + inner)
            active = (before * plus).astype(BF16)
            active_ref[pair, :] = active
            slope = plus + 0.5 * before * (1.0 - inner * inner) * (rate + rate * 3 * 0.044715 * square)
            lower = (upper * slope).astype(BF16)
            grad_ref[pair, :] = lower
            ref[rows, :] = dot_nt(lower, expand_ref[...]).astype(BF16)
            result_ref[place, :] = dot_nn(active, shrink_ref[...]).astype(BF16)


def weight_parts(part, mine_ref, other_ref, up_mine_ref, up_other_ref, active_ref, grad_ref, bias_ref, out_ref):
    half, width = mine_ref.shape
    quarter, all_units = width // NZ, NZ * part
    for r in range(NZ):
        spot, ref = r, out_ref.at[r]
        here = slice(spot * quarter, (spot + 1) * quarter)
        total = dot_tn(mine_ref[:, here], grad_ref[0:half, :]) + dot_tn(other_ref[:, here], grad_ref[half : 2 * half, :])
        ref[0:quarter, :] = total.astype(BF16)
        units = slice(spot * part, (spot + 1) * part)
        total = dot_tn(active_ref[0:half, units], up_mine_ref[...])
        total = (total + dot_tn(active_ref[half : 2 * half, units], up_other_ref[...])).astype(BF16)
        for i in range(width // all_units):
            start = quarter + i * part
            ref[start : start + part, :] = total[:, i * all_units : (i + 1) * all_units]
    bias_ref[...] = jnp.sum(grad_ref[...].astype(F32), axis=0, keepdims=True)


def feed_forward_weights(second, up, active, before_grad):
    frames, units = active.shape
    width, part = up[0].shape[1], units // NZ
    quarter = width // NZ
    if part % 128:
        shrink = dot_tn(active, stack_rows(up)).astype(BF16).reshape(NZ, part, width)
        expand = dot_tn(stack_rows(second), before_grad).astype(BF16).reshape(NZ, quarter, units)
        bias = jnp.sum(before_grad.astype(F32), axis=0, keepdims=True)
        return bias, jnp.stack([stack_rows([expand[k], fold_columns(shrink[k], units)]) for k in range(NZ)])
    return pl.pallas_call(
        functools.partial(weight_parts, part),
        out_shape=(jax.ShapeDtypeStruct((1, units), F32), jax.ShapeDtypeStruct((NZ, 2 * quarter, units), BF16)),
        in_specs=whole(6),
        out_specs=tuple(whole(2)),
        compiler_params=pltpu.CompilerParams(vmem_limit_bytes=16 << 20),
        cost_estimate=pl.CostEstimate(
            flops=4 * frames * width * units, bytes_accessed=8 * frames * width, transcendentals=0
        ),
        name="feed_forward_weights",
    )(*second, *up, active, before_grad)


def whole(count):
    return [pl.BlockSpec(memory_space=pltpu.VMEM)] * count


def anywhere(count):
    return [pl.BlockSpec(memory_space=pl.ANY)] * count


def attention(core, pair, encoding, affine, w_in, bias, starts, heads, ny, size):
    half, wide = pair[0].shape[0], w_in.shape[1]
    frames, depth, width = 2 * half, pair[0].shape[1], wide // 3
    pairs = frames * frames * heads
    return pl.pallas_call(
        functools.partial(attend, heads, ny, size),
        out_shape=(
            jax.ShapeDtypeStruct((frames, depth), BF16),
            jax.ShapeDtypeStruct((frames, wide), BF16),
            jax.ShapeDtypeStruct((half, width), BF16),
            jax.ShapeDtypeStruct((half, width), BF16),
            jax.ShapeDtypeStruct((heads, frames), F32),
        ),
        in_specs=[pl.BlockSpec(memory_space=pltpu.SMEM)] + whole(2) + anywhere(1) + whole(4),
        out_specs=tuple(anywhere(2) + whole(3)),
        scratch_shapes=[
            pltpu.VMEM((frames, width), BF16),
            pltpu.VMEM((frames, width), BF16),
            pltpu.VMEM((width, frames), BF16),
            pltpu.VMEM((frames, depth), F32),
            pltpu.VMEM((frames, depth), BF16),
            pltpu.VMEM((frames, wide), BF16),
            pltpu.SemaphoreType.DMA((2 * half // (2 * size),)),
            pltpu.SemaphoreType.DMA((2 * half // (2 * size) + 1,)),
        ],
        compiler_params=pltpu.CompilerParams(vmem_limit_bytes=(frames >> 6) << 20),
        cost_estimate=pl.CostEstimate(
            flops=pairs * 256 + 2 * frames * depth * wide, bytes_accessed=8 * frames * depth, transcendentals=pairs // 2
        ),
        name="attend",
    )(core, *pair, encoding, affine, w_in, bias, starts)


def attention_back(place, qkv, pair, context, outward, w_in, starts, log_total, heads, ny, size):
    frames, wide = qkv.shape
    width = wide // 3
    depth = pair[0].shape[1]
    pairs = frames * frames * heads
    half = jax.ShapeDtypeStruct(pair[0].shape, BF16)
    return pl.pallas_call(
        functools.partial(attend_back, heads, ny, size),
        out_shape=(
            jax.ShapeDtypeStruct((frames, wide), BF16),
            half,
            half,
            jax.ShapeDtypeStruct((width, depth), BF16),
        ),
        in_specs=[pl.BlockSpec(memory_space=pltpu.SMEM)] + anywhere(1) + whole(1) + anywhere(5) + whole(2),
        out_specs=tuple(whole(4)),
        scratch_shapes=[pltpu.VMEM((frames, width), BF16)] * 4
        + [pltpu.VMEM((width, frames), BF16)]
        + [pltpu.VMEM((frames, width), F32)] * 3
        + [pltpu.VMEM((frames, wide), BF16), pltpu.VMEM((frames // 2, depth), BF16)]
        + [pltpu.VMEM((frames // 2, width), BF16)] * 2
        + [pltpu.VMEM((width, depth), BF16), pltpu.VMEM((depth, wide), BF16), pltpu.SemaphoreType.DMA((6,))],
        compiler_params=pltpu.CompilerParams(vmem_limit_bytes=(frames >> 6) * 5 << 18),
        cost_estimate=pl.CostEstimate(
            flops=pairs * 640 + 2 * frames * depth * (wide + 2 * width),
            bytes_accessed=8 * frames * depth,
            transcendentals=pairs // 2,
        ),
        name="attend_back",
    )(jnp.concatenate([place.core, place.me]), qkv, *pair, *context, outward, w_in, starts, log_total)


def feed_forward_front(core, pair, up_pair, w_expand, w_shrink, bias, size):
    frames, width = 2 * pair[0].shape[0], pair[0].shape[1]
    units = w_expand.shape[1]
    half = jax.ShapeDtypeStruct((frames // 2, width), BF16)
    inner = jax.ShapeDtypeStruct((frames, units), BF16)
    return pl.pallas_call(
        functools.partial(feed_forward, size),
        out_shape=(inner, inner, half, half, jax.ShapeDtypeStruct((frames, width), BF16)),
        in_specs=[pl.BlockSpec(memory_space=pltpu.SMEM)] + whole(7),
        out_specs=tuple(whole(5)),
        compiler_params=pltpu.CompilerParams(vmem_limit_bytes=16 << 20),
        cost_estimate=pl.CostEstimate(
            flops=8 * frames * width * units, bytes_accessed=10 * frames * width, transcendentals=frames * units
        ),
        name="feed_forward",
    )(core, *pair, *up_pair, w_expand, w_shrink, bias)


class Place:
    def __init__(self, ny):
        self.x, self.z, self.y, self.c = (lax.axis_index(a) for a in ("x", "z", "y", "c"))
        self.xy = jnp.reshape(self.x * ny + self.y, (1,)).astype(jnp.int32)
        self.core = jnp.reshape(self.c, (1,)).astype(jnp.int32)
        self.layer = jnp.reshape(self.z, (1,)).astype(jnp.int32)
        self.me = (self.core * 2) * ny + self.xy


def on_device(
    groups,
    ny,
    frames,
    cotangent,
    segment_lengths,
    position_offsets,
    first_gain,
    first_shift,
    inward_weight,
    query_bias,
    value_bias,
    outward_weight,
    outward_bias,
    second_gain,
    second_shift,
    expand_weight,
    expand_bias,
    shrink_weight,
    shrink_bias,
):
    place = Place(ny)
    x, z, y, c = place.x, place.z, place.y, place.c
    local_len, rows, width = frames.shape
    share = inward_weight.shape[0]
    layer = 4 * ny
    spread = NZ * ny * 2
    full_len = local_len * spread
    size = 2 * local_len
    hd = HEADS // layer
    hw = hd * (width // HEADS)
    hidden = expand_bias.shape[0]
    part = hidden // 2
    me = (c * 2 + x) * ny + y

    def sum_groups(value):
        return lax.psum(value, "g") if groups > 1 else value

    def exchange(value, axes):
        return lax.all_to_all(value, axes, 0, 0, tiled=True)

    both = to_home(jnp.concatenate([frames, cotangent], axis=2), place)
    table = jnp.stack([segment_lengths, position_offsets], axis=1)
    other_table = hop(table, "x")
    other_table, later_inward = after(other_table, inward_weight)

    small = [first_gain, first_shift, query_bias, value_bias, outward_bias, second_gain, second_shift, shrink_bias]
    kinds = len(small) + hidden // share
    units = NZ * part
    packed = jnp.concatenate([v[None] for v in small] + [expand_bias.reshape(-1, share)], axis=0)
    packed = packed.reshape(-1, 3 * hw)
    extra = packed.shape[0]
    packed = jnp.pad(packed, ((0, SMALL_ROWS - extra), (0, units)))[None]
    in_cols = jnp.transpose(later_inward.reshape(share, 3, 2, 2, ny, hw), (3, 4, 2, 0, 1, 5))
    in_cols = pick(in_cols, x).reshape(ny * 2, share, 3 * hw)
    ex_cols = pick(expand_weight.reshape(share, NZ, ny, 2, 2, part), x, 4)
    ex_cols = jnp.transpose(ex_cols, (2, 3, 0, 1, 4)).reshape(ny * 2, share, units)
    columns = jnp.concatenate([in_cols, ex_cols], axis=2)
    columns = jnp.concatenate([columns, jnp.broadcast_to(packed, (ny * 2,) + packed.shape[1:])], axis=1)
    columns = exchange(columns, ("y", "c"))

    row_x = jnp.where((z == 0) | (z == 3), 1, 0)
    table = pick(jnp.where(x == row_x, table, other_table), z >> 1)
    lengths, offsets = table[0], table[1]
    count = lengths.shape[0]
    starts = jnp.sum(
        jnp.where(jnp.arange(count)[None, :] < jnp.arange(count)[:, None], lengths[None, :], 0), axis=1
    )
    frame_ids = jnp.arange(full_len, dtype=jnp.int32)
    row_starts = jnp.max(jnp.where(starts[:, None] <= frame_ids[None, :], starts[:, None], 0), axis=0)[None, :]
    spot = jnp.arange(2 * ny)
    chunk = jnp.concatenate([(2 * (spot // ny) + i) * ny + spot % ny for i in (c, 1 - c)])
    mine = (chunk[:, None] * size + jnp.arange(size, dtype=jnp.int32)).reshape(-1)
    inside = (mine[:, None] >= starts[None, :]) & (mine[:, None] < (starts + lengths)[None, :])
    position = jnp.sum(jnp.where(inside, offsets[None, :] + mine[:, None] - starts[None, :], 0), axis=1)
    encoding = sin_cos(position, width)

    both, later_outward, columns = after(both, outward_weight, columns)
    fr, ct = both[:, :width], both[:, width:]
    outward = lax.all_gather(later_outward, SEQ, axis=0, tiled=True)
    in_part = columns[:, :, : 3 * hw].reshape(-1, 3 * hw)
    in_parts = [in_part] + [hop(in_part, "z", NZ, k) for k in range(1, NZ)]
    sh_rows = lax.dynamic_slice_in_dim(shrink_weight, x * part, part, 0)
    ff_part = stack_rows([columns[:, :share, 3 * hw :].reshape(-1, units), fold_columns(sh_rows, units)])
    mine, up_mine = assemble_pair(near_parts(both, ny), place.xy)
    ff_part = jnp.broadcast_to(ff_part[None], (NZ,) + ff_part.shape)
    mine, encoding, ff_part, *in_parts = after(mine, encoding, ff_part, *in_parts)
    first_pair = [mine, hop(mine, "c")]
    w_in, small_rows = collect_inward(in_parts, place, share)
    ff_got = exchange(ff_part, ("z",))

    vectors = small_rows.reshape(spread, SMALL_ROWS, 3 * hw)[:, :extra].reshape(spread, kinds, share).astype(F32)
    expand_b = vectors[:, len(small) :].reshape(NZ, ny, 2, 2, part)
    expand_b = pick(pick(pick(expand_b, y, 1), c, 1), x, 1).reshape(1, NZ * part)
    vectors = jnp.swapaxes(vectors[:, : len(small)], 0, 1).reshape(len(small), width)
    gain_one, shift_one, query_b, value_b, outward_b, gain_two, shift_two, shrink_b = (
        vectors[i : i + 1] for i in range(len(small))
    )
    qkv_bias = jnp.concatenate(
        [
            lax.dynamic_slice_in_dim(query_b, me * hw, hw, 1),
            jnp.zeros((1, hw), F32),
            lax.dynamic_slice_in_dim(value_b, me * hw, hw, 1),
        ],
        axis=1,
    )

    first_all, qkv, *context_pair, log_total = attention(
        place.core, first_pair, encoding, vectors[:2], w_in, qkv_bias, row_starts, hd, ny, size
    )
    *context_pair, up_mine = after(*context_pair, up_mine)
    if ny == 2:
        context = by_half(c, context_pair[0][None], hop(context_pair[1], "c")[None], 0)
        context = context.reshape(2, 2, ny, size, hw)
        context = by_half(x, pick(context, x, 1)[:, None], hop(pick(context, 1 - x, 1), "x")[:, None], 1)
        context = by_half(y, pick(context, y, 2)[:, :, None], hop(pick(context, 1 - y, 2), "y")[:, :, None], 2)
    else:
        context = exchange(by_half(c, *context_pair, 0).reshape(layer, size, hw), LAYER)
    context = context.reshape(layer, size, hw)
    up_pair = [up_mine, hop(up_mine, "c")]

    inputs = fr.astype(F32) + lax.dynamic_slice_in_dim(encoding, (x * ny + y) * size, size, 0)
    normal_one, scale_one = normalize(inputs)
    context = jnp.swapaxes(context, 0, 1).reshape(size, width)
    middle = inputs + dot_nn(context, outward) + outward_b

    normal_two, scale_two = normalize(middle)
    second = (normal_two * gain_two + shift_two).astype(BF16)
    ff_got, *second_near = after(ff_got, *near_parts(second, ny))
    second_pair = both_cores(second_near, place)
    w_expand, w_shrink = collect_hidden(ff_got, width)
    active, before_grad, send, keep, out_part = feed_forward_front(
        place.core, second_pair, up_pair, w_expand, w_shrink, expand_b, size
    )
    second_parts = list(fold(keep, hop(send, "c"), place, ny))
    second_parts[0], active, before_grad = after(second_parts[0], active, before_grad)
    second_grad = finish(second_parts, ny)
    expand_b_sum, hidden_part = feed_forward_weights(second_pair, up_pair, active, before_grad)
    out_part = lax.psum_scatter(out_part, LAYER, scatter_dimension=0, tiled=True)
    second_grad, expand_b_sum = after(second_grad, expand_b_sum)
    hidden_got = exchange(hidden_part, ("z",))

    upstream = ct.astype(F32)
    middle_part, gain_two_sum, shift_two_sum = normalize_back(normal_two, scale_two, gain_two, second_grad)
    middle_grad = upstream + middle_part
    low_middle = middle_grad.astype(BF16)
    low_pair = both_cores(near_parts(low_middle, ny), place)
    mixed_grad, send, keep, outward_part = attention_back(
        place, qkv, low_pair, context_pair, outward, w_in, row_starts, log_total, hd, ny, size
    )
    got = hop(send, "c")
    cut = outward_part.reshape(2, -1, width)
    far_cut = hop(pick(cut, 1 - c), "c")
    got, far_cut, out_part = after(got, far_cut, out_part)
    first_parts = list(fold(keep, got, place, ny))
    first_parts[0], mixed_late, far_cut, hidden_got = after(first_parts[0], mixed_grad, far_cut, hidden_got)
    inward_part = dot_tn(first_all, mixed_late).astype(BF16)
    first_grad = finish(first_parts, ny)
    inward_got = exchange(inward_part.reshape(spread, share, 3 * hw), SEQ)
    input_part, gain_one_sum, shift_one_sum = normalize_back(normal_one, scale_one, vectors[:1], first_grad)
    late = (middle_grad + input_part).astype(BF16)
    late, out_part, hidden_got = after(late, out_part, hidden_got)
    hidden_sum = sum_sources(hidden_got, NZ)
    frames_grad = to_origin(late, place)
    inward_got, out_part = after(inward_got, out_part)
    layer_output = to_origin((middle + out_part.astype(F32) + shrink_b).astype(BF16), place)

    split = width // 2
    hidden_sum = sum_groups(hidden_sum.reshape(-1, units)).astype(BF16)
    line = hidden_sum[: width // NZ].reshape(ny, 2, share, units)
    if ny == 2:
        line = by_half(c, pick(line, c, 1)[:, None], hop(pick(line, 1 - c, 1), "c")[:, None], 1)
        line = by_half(y, pick(line, y)[None], hop(pick(line, 1 - y), "y")[None], 0)
    else:
        line = exchange(line.reshape(ny * 2, share, units), ("y", "c"))
    mine = stack_rows([line.reshape(-1, units), hidden_sum[width // NZ :]])
    mine, inward_got = after(mine, inward_got)
    other = hop(mine, "x")

    def full_hidden(other):
        pair = [unfold_columns(v[width // NZ :], width // units) for v in (mine, other)]
        g_shrink = by_half(x, *pair, 0).astype(F32)
        pair = [v[: width // NZ].reshape(ny, 2, 1, share, NZ, part) for v in (mine, other)]
        return g_shrink, jnp.transpose(by_half(x, *pair, 2), (3, 4, 0, 1, 2, 5)).reshape(share, -1).astype(F32)

    if hd == 2 and ny == 2:
        line = by_half(c, pick(cut, c)[None], far_cut[None], 0)
        line = line.reshape(2, 1, share, 2, split)
        line = by_half(x, pick(line, x, 3), hop(pick(line, 1 - x, 3), "x"), 1)
        out_got = lax.psum_scatter(line.reshape(NZ * share, split), "z", scatter_dimension=0, tiled=True)
    else:
        out_got = None
        cut = lax.dynamic_update_slice(jnp.zeros((width, width), BF16), outward_part, (me * hw, 0))
        g_outward = lax.psum_scatter(cut, SEQ, scatter_dimension=0, tiled=True)
        g_outward = lax.psum(g_outward.astype(F32), ("g", "x"))

    mixed_sum = jnp.sum(mixed_grad.astype(F32), axis=0)

    def from_heads(value):
        return lax.dynamic_update_slice(jnp.zeros((width,), F32), value, (me * hw,))

    flat = lax.optimization_barrier(jnp.stack(
        [
            gain_one_sum,
            shift_one_sum,
            from_heads(mixed_sum[:hw]),
            from_heads(mixed_sum[2 * hw :]),
            jnp.sum(low_middle.astype(F32), axis=0),
            gain_two_sum,
            shift_two_sum,
            jnp.sum(upstream, axis=0),
        ]
    ))
    small_len = len(small) * share
    sums = jnp.swapaxes(flat.reshape(len(small), spread, share), 0, 1).reshape(spread, small_len)
    spot = jnp.zeros((NZ, ny, 2, 2, part), F32)
    spot = lax.dynamic_update_slice(spot, expand_b_sum.reshape(NZ, 1, 1, 1, part), (0, y, c, x, 0))
    sums = jnp.concatenate([sums, spot.reshape(spread, hidden)], axis=1)
    inward_got, sums = after(inward_got, sums)
    sums = jnp.broadcast_to(sums[None], (2,) + sums.shape).reshape(2 * spread, -1, 128)
    total = sum_groups(jnp.sum(exchange(sums, ("x",) + SEQ), axis=0)).reshape(-1)
    frames_grad, total, other = after(frames_grad, total, other)
    g_shrink, g_expand = full_hidden(other)
    if out_got is not None:
        total, out_got = after(total, out_got)
        out_sum = sum_groups(out_got.astype(F32)).astype(BF16)
        g_outward = by_half(x, out_sum, hop(out_sum, "x"), 1).astype(F32)
    g_small = total[:small_len].reshape(len(small), share)
    g_expand_b = total[small_len:]
    inward_sum = sum_groups(sum_sources(inward_got, NZ)).astype(BF16)
    g_inward = [v.reshape(ny, 2, 1, share, 3, hw) for v in (inward_sum, hop(inward_sum, "x"))]
    g_inward = jnp.transpose(by_half(x, *g_inward, 2), (3, 4, 1, 2, 0, 5)).reshape(share, -1).astype(F32)

    return (
        layer_output,
        frames_grad.astype(F32),
        g_small[0],
        g_small[1],
        g_inward,
        g_small[2],
        g_small[3],
        g_outward,
        g_small[4],
        g_small[5],
        g_small[6],
        g_expand,
        g_expand_b,
        g_shrink,
        g_small[7],
    )


def solution(mesh):
    batch, seq = mesh.shape["batch"], mesh.shape["seq"]
    groups, ny = batch // 2, seq // (2 * NZ)
    fine = Mesh(mesh.devices.reshape(groups, 2, NZ, ny, 2), ("g", "x", "z", "y", "c"))
    b, s = ("g", "x"), ("z", "y", "c")
    in_specs = (
        P(s, b, None),
        P(s, b, None),
        P(b, None),
        P(b, None),
        P(s),
        P(s),
        P(s, None),
        P(s),
        P(s),
        P(s, None),
        P(s),
        P(s),
        P(s),
        P(s, None),
        P(s),
        P(s, None),
        P(s),
    )
    out_specs = (
        P(s, b, None),
        P(s, b, None),
        P(s),
        P(s),
        P(s, None),
        P(s),
        P(s),
        P(s, None),
        P(s),
        P(s),
        P(s),
        P(s, None),
        P(s),
        P(s, None),
        P(s),
    )
    return jax.shard_map(
        functools.partial(on_device, groups, ny), mesh=fine, in_specs=in_specs, out_specs=out_specs, check_vma=False
    )
```

```python
import functools
import math

import jax
import jax.numpy as jnp
from jax import lax
from jax.experimental import pallas as pl
from jax.experimental.pallas import tpu as pltpu
from jax.sharding import Mesh, PartitionSpec as P


HEADS = 16
NZ = 4
SMALL_ROWS = 16
NORM_EPS = 1e-05
NEG = -1e30
F32 = jnp.float32
BF16 = jnp.bfloat16
LAYER_OF_ROW = (1, 2, 0, 3)
SWAP = [(0, 1), (1, 0)]
LAYER = ("c", "x", "y")
SEQ = ("z", "y", "c")


def xor_perm(count, k):
    return [(i, i ^ k) for i in range(count)]


def hop(value, axis, count=2, k=1):
    return lax.ppermute(value, axis, xor_perm(count, k))


def pick(value, index, axis=0):
    return lax.dynamic_index_in_dim(value, index, axis, keepdims=False)


def stack_rows(parts):
    return jnp.concatenate(parts, axis=0)


def assemble_body(pieces, size, place_ref, *refs):
    out_ref = refs[pieces]
    for r in range(pieces):
        spot = place_ref[0] ^ r
        out_ref[pl.ds(pl.multiple_of(spot * size, size), size), :] = refs[r][...]


def assemble(parts, me):
    size, width = parts[0].shape
    count = len(parts)
    return pl.pallas_call(
        functools.partial(assemble_body, count, size),
        out_shape=jax.ShapeDtypeStruct((count * size, width), parts[0].dtype),
        in_specs=[pl.BlockSpec(memory_space=pltpu.SMEM)] + whole(count),
        out_specs=whole(1)[0],
        compiler_params=pltpu.CompilerParams(vmem_limit_bytes=4 << 20),
        cost_estimate=pl.CostEstimate(flops=0, bytes_accessed=4 * count * size * width, transcendentals=0),
        name="assemble",
    )(me, *parts)


def assemble_pair_body(pieces, size, place_ref, *refs):
    left_ref, right_ref = refs[pieces:]
    width = left_ref.shape[1]
    for r in range(pieces):
        rows = pl.ds(pl.multiple_of((place_ref[0] ^ r) * size, size), size)
        left_ref[rows, :] = refs[r][:, 0:width]
        right_ref[rows, :] = refs[r][:, width : 2 * width]


def assemble_pair(parts, me):
    size, width = parts[0].shape
    count = len(parts)
    return pl.pallas_call(
        functools.partial(assemble_pair_body, count, size),
        out_shape=[jax.ShapeDtypeStruct((count * size, width // 2), parts[0].dtype)] * 2,
        in_specs=[pl.BlockSpec(memory_space=pltpu.SMEM)] + whole(count),
        out_specs=whole(2),
        compiler_params=pltpu.CompilerParams(vmem_limit_bytes=4 << 20),
        cost_estimate=pl.CostEstimate(flops=0, bytes_accessed=4 * count * size * width, transcendentals=0),
        name="assemble_pair",
    )(me, *parts)


def near_parts(block, ny):
    return [block] + [lax.ppermute(block, ("x", "y"), xor_perm(2 * ny, r)) for r in range(1, 2 * ny)]


def both_cores(parts, place):
    mine = assemble(parts, place.xy)
    return mine, hop(mine, "c")


def fold_body(count, size, place_ref, keep_ref, got_ref, own_ref, *out_refs):
    for r in range(count):
        spot = place_ref[0] ^ r
        here = pl.ds(pl.multiple_of(spot * size, size), size)
        value = keep_ref[here, :].astype(F32) + got_ref[here, :].astype(F32)
        if r == 0:
            own_ref[...] = value
        else:
            out_refs[r - 1][...] = value.astype(BF16)


def fold(keep, got, place, ny):
    rows, width = keep.shape
    count = 2 * ny
    size = rows // count
    return pl.pallas_call(
        functools.partial(fold_body, count, size),
        out_shape=[jax.ShapeDtypeStruct((size, width), F32)] + [jax.ShapeDtypeStruct((size, width), BF16)] * (count - 1),
        in_specs=[pl.BlockSpec(memory_space=pltpu.SMEM)] + whole(2),
        out_specs=whole(count),
        compiler_params=pltpu.CompilerParams(vmem_limit_bytes=4 << 20),
        cost_estimate=pl.CostEstimate(flops=count * size * width, bytes_accessed=6 * count * size * width, transcendentals=0),
        name="fold",
    )(place.xy, keep, got)


def finish(parts, ny):
    own = parts[0]
    for r in range(1, 2 * ny):
        own = own + lax.ppermute(parts[r], ("x", "y"), xor_perm(2 * ny, r)).astype(F32)
    return own


def fold_columns(value, units):
    return stack_rows([value[:, i : i + units] for i in range(0, value.shape[1], units)])


def unfold_columns(value, count):
    size = value.shape[0] // count
    return jnp.concatenate([value[i * size : (i + 1) * size] for i in range(count)], axis=1)


def collect_inward_body(share, place_ref, *refs):
    weight_ref, small_ref = refs[NZ:]
    deep = share + SMALL_ROWS
    lines = refs[0].shape[0] // deep
    for r in range(NZ):
        base = (place_ref[0] ^ r) * lines
        for i in range(lines):
            start = i * deep
            rows = pl.ds(pl.multiple_of((base + i) * share, share), share)
            weight_ref[rows, :] = refs[r][start : start + share, :]
            rows = pl.ds(pl.multiple_of((base + i) * SMALL_ROWS, SMALL_ROWS), SMALL_ROWS)
            small_ref[rows, :] = refs[r][start + share : start + deep, :]


def collect_inward(parts, place, share):
    rows, width = parts[0].shape
    lines = NZ * rows // (share + SMALL_ROWS)
    return pl.pallas_call(
        functools.partial(collect_inward_body, share),
        out_shape=[jax.ShapeDtypeStruct((lines * n, width), BF16) for n in (share, SMALL_ROWS)],
        in_specs=[pl.BlockSpec(memory_space=pltpu.SMEM)] + whole(NZ),
        out_specs=whole(2),
        compiler_params=pltpu.CompilerParams(vmem_limit_bytes=4 << 20),
        cost_estimate=pl.CostEstimate(flops=0, bytes_accessed=16 * rows * width, transcendentals=0),
        name="collect_inward",
    )(place.layer, *parts)


def collect_hidden_body(parts_ref, expand_ref, shrink_ref):
    quarter = expand_ref.shape[0] // NZ
    part, units = shrink_ref.shape[0] // NZ, expand_ref.shape[1]
    for r in range(NZ):
        expand_ref[r * quarter : (r + 1) * quarter, :] = parts_ref[r, 0:quarter, :]
        for i in range(shrink_ref.shape[1] // units):
            start = quarter + i * part
            here = slice(r * part, (r + 1) * part)
            shrink_ref[here, i * units : (i + 1) * units] = parts_ref[r, start : start + part, :]


def collect_hidden(parts, width):
    units = parts.shape[2]
    return pl.pallas_call(
        collect_hidden_body,
        out_shape=[jax.ShapeDtypeStruct((width, units), BF16), jax.ShapeDtypeStruct((units, width), BF16)],
        in_specs=whole(1),
        out_specs=whole(2),
        compiler_params=pltpu.CompilerParams(vmem_limit_bytes=4 << 20),
        cost_estimate=pl.CostEstimate(flops=0, bytes_accessed=4 * parts.size, transcendentals=0),
        name="collect_hidden",
    )(parts)


def rehome_flat(x, z, c):
    return (x * NZ + z) * 2 + c


def rehome_perm(k):
    return [
        (rehome_flat(x, z, c), rehome_flat(z >> 1, LAYER_OF_ROW[2 * x + (c ^ k)], z & 1))
        for x in range(2)
        for z in range(NZ)
        for c in range(2)
    ]


def to_home(block, place):
    got = [
        lax.ppermute(jnp.where(place.c == k, block[:, 0], block[:, 1]), ("x", "z", "c"), rehome_perm(k))
        for k in range(2)
    ]
    first = place.z < 2
    return stack_rows([jnp.where(first, got[0], got[1]), jnp.where(first, got[1], got[0])])


def to_origin(block, place):
    half = block.shape[0] // 2
    first = place.z < 2
    low, high = block[:half], block[half:]
    sent = [jnp.where(first, low, high), jnp.where(first, high, low)]
    got = [
        lax.ppermute(sent[k], ("x", "z", "c"), [(b, a) for a, b in rehome_perm(k)]) for k in range(2)
    ]
    return jnp.stack(
        [jnp.where(place.c == 0, got[0], got[1]), jnp.where(place.c == 0, got[1], got[0])], axis=1
    )


def after(first, *values):
    return lax.optimization_barrier((first, *values))


def sum_sources(value, count):
    return jnp.sum(value.reshape((count, -1) + value.shape[1:]).astype(F32), axis=0)


def by_half(x, mine, other, axis):
    return jnp.concatenate([jnp.where(x == 0, mine, other), jnp.where(x == 0, other, mine)], axis=axis)


def sin_cos(position, width):
    feature = jnp.arange(width, dtype=jnp.int32)
    rates = jnp.exp((feature // 2).astype(F32) * (-2.0 * math.log(10000.0) / width))
    angle = position.astype(F32)[:, None] * rates[None, :]
    turn = jnp.round(angle * (2.0 / math.pi))
    rest = angle - turn * 1.5703125
    rest = rest - turn * 0.00048375129699707031
    rest = rest - turn * 7.5497899548918861e-08
    quadrant = turn.astype(jnp.int32) + (feature % 2)[None, :]
    square = rest * rest
    sine = rest + rest * square * (
        -0.16666666641626524 + square * (0.008333329385889463 + square * (-0.00019839334836096632 + square * 2.718311493989822e-06))
    )
    cosine = 1.0 + square * (
        -0.49999999725103100 + square * (0.04166662332373906 + square * (-0.001388676377460993 + square * 2.439044879627741e-05))
    )
    value = jnp.where((quadrant & 1) == 0, sine, cosine)
    return jnp.where((quadrant & 2) == 0, value, -value)


def normalize(values):
    center = values - jnp.mean(values, axis=-1, keepdims=True)
    scale = lax.rsqrt(jnp.mean(center * center, axis=-1, keepdims=True) + NORM_EPS)
    return center * scale, scale


def normalize_back(normal, scale, gain, upstream):
    scaled = upstream * gain
    inner = scaled - jnp.mean(scaled, axis=-1, keepdims=True)
    inner = inner - normal * jnp.mean(scaled * normal, axis=-1, keepdims=True)
    return inner * scale, jnp.sum(upstream * normal, axis=0), jnp.sum(upstream, axis=0)


def dot_nt(a, b):
    return lax.dot_general(a, b, (((1,), (1,)), ((), ())), preferred_element_type=F32)


def dot_tn(a, b):
    return lax.dot_general(a, b, (((0,), (0,)), ((), ())), preferred_element_type=F32)


def dot_nn(a, b):
    return jnp.dot(a, b, preferred_element_type=F32)


BLOCK = 256


def chunk_owner(chunk, ny):
    outer, y = divmod(chunk, ny)
    return ((outer & 1) * 2 + (outer >> 1)) * ny + y


def lane_parts(heads, width):
    if heads == 1:
        return [None]
    lane = lax.broadcasted_iota(jnp.int32, (1, width), 1)
    return [(lane >= h * (width // heads)) & (lane < (h + 1) * (width // heads)) for h in range(heads)]


def only(value, lanes):
    return value if lanes is None else jnp.where(lanes, value, jnp.zeros_like(value))


def allowed_pairs(start_ref, first, total):
    key = lax.broadcasted_iota(jnp.int32, (total, BLOCK), 0)
    frame = first + lax.broadcasted_iota(jnp.int32, (total, BLOCK), 1)
    return (key >= start_ref[:, first : first + BLOCK]) & (key <= frame)


def chunk_rows(chunk, ny, size, core):
    half, spot = divmod(chunk_owner(chunk, ny), 2 * ny)
    return pl.ds(pl.multiple_of(((half ^ core) * (2 * ny) + spot) * size, size), size)


def attend(
    heads,
    ny,
    size,
    core_ref,
    mine_ref,
    other_ref,
    encoding_ref,
    affine_ref,
    weight_ref,
    bias_ref,
    start_ref,
    first_ref,
    qkv_ref,
    near_ref,
    far_ref,
    log_ref,
    q_s,
    k_s,
    vt_s,
):
    count = 4 * ny
    width = q_s.shape[1]
    core = core_ref[0]
    step = 2 * size
    half = mine_ref.shape[0]
    for base, ref in ((0, mine_ref), (half, other_ref)):
        for start in range(0, half, step):
            rows = slice(base + start, base + start + step)
            normal, _ = normalize(ref[start : start + step, :].astype(F32) + encoding_ref[rows, :])
            value = (normal * affine_ref[0:1, :] + affine_ref[1:2, :]).astype(BF16)
            first_ref[rows, :] = value
            qkv_ref[rows, :] = (dot_nn(value, weight_ref[...]) + bias_ref[...]).astype(BF16)
    for chunk in range(count):
        rows = chunk_rows(chunk, ny, size, core)
        here = slice(chunk * size, (chunk + 1) * size)
        q_s[here, :] = qkv_ref[rows, 0:width] * 0.125
        k_s[here, :] = qkv_ref[rows, width : 2 * width]
        vt_s[:, here] = jnp.transpose(qkv_ref[rows, 2 * width : 3 * width].astype(F32)).astype(BF16)
    lanes = lane_parts(heads, width)
    each = width // heads
    for block in range(count * size // BLOCK):
        first = block * BLOCK
        total = first + BLOCK
        allowed = allowed_pairs(start_ref, first, total)
        q_block = q_s[first:total, :]
        contexts = []
        for h in range(heads):
            scores = dot_nt(k_s[0:total, :], only(q_block, lanes[h]))
            scores = jnp.where(allowed, scores, NEG)
            top = jnp.max(scores, axis=0, keepdims=True)
            weight = jnp.exp(scores - top)
            mass = jnp.sum(weight, axis=0, keepdims=True)
            part = dot_nn(vt_s[h * each : (h + 1) * each, 0:total], weight.astype(BF16))
            contexts.append(part / mass)
            log_ref[h : h + 1, first:total] = top + jnp.log(mass)
        context = contexts[0] if heads == 1 else jnp.concatenate(contexts, axis=0)
        context = jnp.transpose(context).astype(BF16)
        for sub in range(BLOCK // size):
            owner = chunk_owner(block * (BLOCK // size) + sub, ny)
            side, spot = divmod(owner, 2 * ny)
            rows, piece = slice(spot * size, (spot + 1) * size), context[sub * size : (sub + 1) * size]

            @pl.when(core == side)
            def _(rows=rows, piece=piece):
                near_ref[rows, :] = piece

            @pl.when(core != side)
            def _(rows=rows, piece=piece):
                far_ref[rows, :] = piece


def attend_back(
    heads,
    ny,
    size,
    place_ref,
    qkv_any,
    mine_ref,
    other_any,
    near_any,
    far_any,
    outward_any,
    weight_any,
    start_ref,
    log_ref,
    out_ref,
    send_ref,
    keep_ref,
    outward_grad_ref,
    q_s,
    k_s,
    v_s,
    g_s,
    kt_s,
    dq_s,
    dk_s,
    dv_s,
    qkv_ref,
    other_ref,
    near_ref,
    far_ref,
    outward_ref,
    weight_ref,
    in_sem,
):
    count = 4 * ny
    width = q_s.shape[1]
    core = place_ref[0]
    half = mine_ref.shape[0]
    step = 2 * size
    rows = pl.ds(pl.multiple_of(place_ref[1] * width, width), width)
    pairs = (
        (outward_any.at[rows], outward_ref),
        (other_any, other_ref),
        (qkv_any, qkv_ref),
        (weight_any, weight_ref),
        (near_any, near_ref),
        (far_any, far_ref),
    )
    copies = [pltpu.make_async_copy(source, target, in_sem.at[i]) for i, (source, target) in enumerate(pairs)]
    for copy in copies:
        copy.start()
    copies[0].wait()
    for base, ref in ((0, mine_ref), (half, other_ref)):
        if base:
            copies[1].wait()
        for start in range(0, half, step):
            rows = slice(start, start + step)
            out_ref[base + start : base + start + step, 0:width] = dot_nt(ref[rows, :], outward_ref[...]).astype(BF16)
    copies[2].wait()
    for chunk in range(count):
        rows = chunk_rows(chunk, ny, size, core)
        here = slice(chunk * size, (chunk + 1) * size)
        q_s[here, :] = qkv_ref[rows, 0:width] * 0.125
        key = qkv_ref[rows, width : 2 * width]
        k_s[here, :] = key
        kt_s[:, here] = jnp.transpose(key.astype(F32)).astype(BF16)
        v_s[here, :] = qkv_ref[rows, 2 * width : 3 * width]
        g_s[here, :] = out_ref[rows, 0:width]
    dk_s[...] = jnp.zeros_like(dk_s)
    dv_s[...] = jnp.zeros_like(dv_s)
    lanes = lane_parts(heads, width)
    each = width // heads
    for block in range(count * size // BLOCK):
        first = block * BLOCK
        total = first + BLOCK
        allowed = allowed_pairs(start_ref, first, total)
        q_block, g_block = q_s[first:total, :], g_s[first:total, :]
        queries = []
        for h in range(heads):
            q_one, g_one = only(q_block, lanes[h]), only(g_block, lanes[h])
            scores = dot_nt(k_s[0:total, :], q_one)
            probs = jnp.where(allowed, jnp.exp(scores - log_ref[h : h + 1, first:total]), 0.0)
            prob_grad = dot_nt(v_s[0:total, :], g_one)
            delta = jnp.sum(probs * prob_grad, axis=0, keepdims=True)
            score_grad = (probs * (prob_grad - delta)).astype(BF16)
            dv_s[0:total, :] += dot_nn(probs.astype(BF16), g_one)
            dk_s[0:total, :] += dot_nn(score_grad, q_one)
            queries.append(dot_nn(kt_s[h * each : (h + 1) * each, 0:total], score_grad))
        query_grad = queries[0] if heads == 1 else jnp.concatenate(queries, axis=0)
        dq_s[first:total, :] = jnp.transpose(query_grad) * 0.125
    for chunk in range(count):
        rows = chunk_rows(chunk, ny, size, core)
        here = slice(chunk * size, (chunk + 1) * size)
        out_ref[rows, 0:width] = dq_s[here, :].astype(BF16)
        out_ref[rows, width : 2 * width] = dk_s[here, :].astype(BF16)
        out_ref[rows, 2 * width : 3 * width] = dv_s[here, :].astype(BF16)
    for copy in copies[3:]:
        copy.wait()
    for ref, base in ((send_ref, half), (keep_ref, 0)):
        for start in range(0, half, step):
            rows = slice(base + start, base + start + step)
            ref[start : start + step, :] = dot_nt(out_ref[rows, :], weight_ref[...]).astype(BF16)
    total = dot_tn(near_ref[...], mine_ref[...]) + dot_tn(far_ref[...], other_ref[...])
    outward_grad_ref[...] = total.astype(BF16)


def feed_forward(
    size,
    core_ref,
    mine_ref,
    other_ref,
    up_mine_ref,
    up_other_ref,
    expand_ref,
    shrink_ref,
    bias_ref,
    active_ref,
    grad_ref,
    send_ref,
    keep_ref,
    result_ref,
):
    half = keep_ref.shape[0]
    step = 2 * size
    rate = math.sqrt(2.0 / math.pi)
    core = core_ref[0]
    sides = ((send_ref, other_ref, up_other_ref, half, 1 - core), (keep_ref, mine_ref, up_mine_ref, 0, core))
    for ref, source_ref, up_ref, base, side in sides:
        for start in range(0, half, step):
            rows = slice(start, start + step)
            pair = slice(base + start, base + start + step)
            place = pl.ds(pl.multiple_of(side * half + start, step), step)
            before = dot_nn(source_ref[rows, :], expand_ref[...]) + bias_ref[...]
            upper = dot_nt(up_ref[rows, :], shrink_ref[...])
            square = before * before
            inner = jnp.tanh(rate * (before + 0.044715 * before * square))
            plus = 0.5 * (1.0 + inner)
            active = (before * plus).astype(BF16)
            active_ref[pair, :] = active
            slope = plus + 0.5 * before * (1.0 - inner * inner) * (rate + rate * 3 * 0.044715 * square)
            lower = (upper * slope).astype(BF16)
            grad_ref[pair, :] = lower
            ref[rows, :] = dot_nt(lower, expand_ref[...]).astype(BF16)
            result_ref[place, :] = dot_nn(active, shrink_ref[...]).astype(BF16)


def weight_parts(part, mine_ref, other_ref, up_mine_ref, up_other_ref, active_ref, grad_ref, bias_ref, out_ref):
    half, width = mine_ref.shape
    quarter, all_units = width // NZ, NZ * part
    for r in range(NZ):
        spot, ref = r, out_ref.at[r]
        here = slice(spot * quarter, (spot + 1) * quarter)
        total = dot_tn(mine_ref[:, here], grad_ref[0:half, :]) + dot_tn(other_ref[:, here], grad_ref[half : 2 * half, :])
        ref[0:quarter, :] = total.astype(BF16)
        units = slice(spot * part, (spot + 1) * part)
        total = dot_tn(active_ref[0:half, units], up_mine_ref[...])
        total = (total + dot_tn(active_ref[half : 2 * half, units], up_other_ref[...])).astype(BF16)
        for i in range(width // all_units):
            start = quarter + i * part
            ref[start : start + part, :] = total[:, i * all_units : (i + 1) * all_units]
    bias_ref[...] = jnp.sum(grad_ref[...].astype(F32), axis=0, keepdims=True)


def feed_forward_weights(second, up, active, before_grad):
    frames, units = active.shape
    width, part = up[0].shape[1], units // NZ
    quarter = width // NZ
    if part % 128:
        shrink = dot_tn(active, stack_rows(up)).astype(BF16).reshape(NZ, part, width)
        expand = dot_tn(stack_rows(second), before_grad).astype(BF16).reshape(NZ, quarter, units)
        bias = jnp.sum(before_grad.astype(F32), axis=0, keepdims=True)
        return bias, jnp.stack([stack_rows([expand[k], fold_columns(shrink[k], units)]) for k in range(NZ)])
    return pl.pallas_call(
        functools.partial(weight_parts, part),
        out_shape=(jax.ShapeDtypeStruct((1, units), F32), jax.ShapeDtypeStruct((NZ, 2 * quarter, units), BF16)),
        in_specs=whole(6),
        out_specs=tuple(whole(2)),
        compiler_params=pltpu.CompilerParams(vmem_limit_bytes=16 << 20),
        cost_estimate=pl.CostEstimate(
            flops=4 * frames * width * units, bytes_accessed=8 * frames * width, transcendentals=0
        ),
        name="feed_forward_weights",
    )(*second, *up, active, before_grad)


def whole(count):
    return [pl.BlockSpec(memory_space=pltpu.VMEM)] * count


def anywhere(count):
    return [pl.BlockSpec(memory_space=pl.ANY)] * count


def attention(core, pair, encoding, affine, w_in, bias, starts, heads, ny, size):
    half, wide = pair[0].shape[0], w_in.shape[1]
    frames, depth, width = 2 * half, pair[0].shape[1], wide // 3
    pairs = frames * frames * heads
    return pl.pallas_call(
        functools.partial(attend, heads, ny, size),
        out_shape=(
            jax.ShapeDtypeStruct((frames, depth), BF16),
            jax.ShapeDtypeStruct((frames, wide), BF16),
            jax.ShapeDtypeStruct((half, width), BF16),
            jax.ShapeDtypeStruct((half, width), BF16),
            jax.ShapeDtypeStruct((heads, frames), F32),
        ),
        in_specs=[pl.BlockSpec(memory_space=pltpu.SMEM)] + whole(7),
        out_specs=tuple(whole(5)),
        scratch_shapes=[
            pltpu.VMEM((frames, width), BF16),
            pltpu.VMEM((frames, width), BF16),
            pltpu.VMEM((width, frames), BF16),
        ],
        compiler_params=pltpu.CompilerParams(vmem_limit_bytes=16 << 20),
        cost_estimate=pl.CostEstimate(
            flops=pairs * 256 + 2 * frames * depth * wide, bytes_accessed=8 * frames * depth, transcendentals=pairs // 2
        ),
        name="attend",
    )(core, *pair, encoding, affine, w_in, bias, starts)


def attention_back(place, qkv, pair, context, outward, w_in, starts, log_total, heads, ny, size):
    frames, wide = qkv.shape
    width = wide // 3
    depth = pair[0].shape[1]
    pairs = frames * frames * heads
    half = jax.ShapeDtypeStruct(pair[0].shape, BF16)
    return pl.pallas_call(
        functools.partial(attend_back, heads, ny, size),
        out_shape=(
            jax.ShapeDtypeStruct((frames, wide), BF16),
            half,
            half,
            jax.ShapeDtypeStruct((width, depth), BF16),
        ),
        in_specs=[pl.BlockSpec(memory_space=pltpu.SMEM)] + anywhere(1) + whole(1) + anywhere(5) + whole(2),
        out_specs=tuple(whole(4)),
        scratch_shapes=[pltpu.VMEM((frames, width), BF16)] * 4
        + [pltpu.VMEM((width, frames), BF16)]
        + [pltpu.VMEM((frames, width), F32)] * 3
        + [pltpu.VMEM((frames, wide), BF16), pltpu.VMEM((frames // 2, depth), BF16)]
        + [pltpu.VMEM((frames // 2, width), BF16)] * 2
        + [pltpu.VMEM((width, depth), BF16), pltpu.VMEM((depth, wide), BF16), pltpu.SemaphoreType.DMA((6,))],
        compiler_params=pltpu.CompilerParams(vmem_limit_bytes=(frames >> 6) * 5 << 18),
        cost_estimate=pl.CostEstimate(
            flops=pairs * 640 + 2 * frames * depth * (wide + 2 * width),
            bytes_accessed=8 * frames * depth,
            transcendentals=pairs // 2,
        ),
        name="attend_back",
    )(jnp.concatenate([place.core, place.me]), qkv, *pair, *context, outward, w_in, starts, log_total)


def feed_forward_front(core, pair, up_pair, w_expand, w_shrink, bias, size):
    frames, width = 2 * pair[0].shape[0], pair[0].shape[1]
    units = w_expand.shape[1]
    half = jax.ShapeDtypeStruct((frames // 2, width), BF16)
    inner = jax.ShapeDtypeStruct((frames, units), BF16)
    return pl.pallas_call(
        functools.partial(feed_forward, size),
        out_shape=(inner, inner, half, half, jax.ShapeDtypeStruct((frames, width), BF16)),
        in_specs=[pl.BlockSpec(memory_space=pltpu.SMEM)] + whole(7),
        out_specs=tuple(whole(5)),
        compiler_params=pltpu.CompilerParams(vmem_limit_bytes=16 << 20),
        cost_estimate=pl.CostEstimate(
            flops=8 * frames * width * units, bytes_accessed=10 * frames * width, transcendentals=frames * units
        ),
        name="feed_forward",
    )(core, *pair, *up_pair, w_expand, w_shrink, bias)


class Place:
    def __init__(self, ny):
        self.x, self.z, self.y, self.c = (lax.axis_index(a) for a in ("x", "z", "y", "c"))
        self.xy = jnp.reshape(self.x * ny + self.y, (1,)).astype(jnp.int32)
        self.core = jnp.reshape(self.c, (1,)).astype(jnp.int32)
        self.layer = jnp.reshape(self.z, (1,)).astype(jnp.int32)
        self.me = (self.core * 2) * ny + self.xy


def on_device(
    groups,
    ny,
    frames,
    cotangent,
    segment_lengths,
    position_offsets,
    first_gain,
    first_shift,
    inward_weight,
    query_bias,
    value_bias,
    outward_weight,
    outward_bias,
    second_gain,
    second_shift,
    expand_weight,
    expand_bias,
    shrink_weight,
    shrink_bias,
):
    place = Place(ny)
    x, z, y, c = place.x, place.z, place.y, place.c
    local_len, rows, width = frames.shape
    share = inward_weight.shape[0]
    layer = 4 * ny
    spread = NZ * ny * 2
    full_len = local_len * spread
    size = 2 * local_len
    hd = HEADS // layer
    hw = hd * (width // HEADS)
    hidden = expand_bias.shape[0]
    part = hidden // 2
    me = (c * 2 + x) * ny + y

    def sum_groups(value):
        return lax.psum(value, "g") if groups > 1 else value

    def exchange(value, axes):
        return lax.all_to_all(value, axes, 0, 0, tiled=True)

    both = to_home(jnp.concatenate([frames, cotangent], axis=2), place)
    table = jnp.stack([segment_lengths, position_offsets], axis=1)
    other_table = hop(table, "x")
    other_table, later_inward = after(other_table, inward_weight)

    small = [first_gain, first_shift, query_bias, value_bias, outward_bias, second_gain, second_shift, shrink_bias]
    kinds = len(small) + hidden // share
    units = NZ * part
    packed = jnp.concatenate([v[None] for v in small] + [expand_bias.reshape(-1, share)], axis=0)
    packed = packed.reshape(-1, 3 * hw)
    extra = packed.shape[0]
    packed = jnp.pad(packed, ((0, SMALL_ROWS - extra), (0, units)))[None]
    in_cols = jnp.transpose(later_inward.reshape(share, 3, 2, 2, ny, hw), (3, 4, 2, 0, 1, 5))
    in_cols = pick(in_cols, x).reshape(ny * 2, share, 3 * hw)
    ex_cols = pick(expand_weight.reshape(share, NZ, ny, 2, 2, part), x, 4)
    ex_cols = jnp.transpose(ex_cols, (2, 3, 0, 1, 4)).reshape(ny * 2, share, units)
    columns = jnp.concatenate([in_cols, ex_cols], axis=2)
    columns = jnp.concatenate([columns, jnp.broadcast_to(packed, (ny * 2,) + packed.shape[1:])], axis=1)
    columns = exchange(columns, ("y", "c"))

    row_x = jnp.where((z == 0) | (z == 3), 1, 0)
    table = pick(jnp.where(x == row_x, table, other_table), z >> 1)
    lengths, offsets = table[0], table[1]
    count = lengths.shape[0]
    starts = jnp.sum(
        jnp.where(jnp.arange(count)[None, :] < jnp.arange(count)[:, None], lengths[None, :], 0), axis=1
    )
    frame_ids = jnp.arange(full_len, dtype=jnp.int32)
    row_starts = jnp.max(jnp.where(starts[:, None] <= frame_ids[None, :], starts[:, None], 0), axis=0)[None, :]
    spot = jnp.arange(2 * ny)
    chunk = jnp.concatenate([(2 * (spot // ny) + i) * ny + spot % ny for i in (c, 1 - c)])
    mine = (chunk[:, None] * size + jnp.arange(size, dtype=jnp.int32)).reshape(-1)
    inside = (mine[:, None] >= starts[None, :]) & (mine[:, None] < (starts + lengths)[None, :])
    position = jnp.sum(jnp.where(inside, offsets[None, :] + mine[:, None] - starts[None, :], 0), axis=1)
    encoding = sin_cos(position, width)

    both, later_outward, columns = after(both, outward_weight, columns)
    fr, ct = both[:, :width], both[:, width:]
    outward = lax.all_gather(later_outward, SEQ, axis=0, tiled=True)
    in_part = columns[:, :, : 3 * hw].reshape(-1, 3 * hw)
    in_parts = [in_part] + [hop(in_part, "z", NZ, k) for k in range(1, NZ)]
    sh_rows = lax.dynamic_slice_in_dim(shrink_weight, x * part, part, 0)
    ff_part = stack_rows([columns[:, :share, 3 * hw :].reshape(-1, units), fold_columns(sh_rows, units)])
    mine, up_mine = assemble_pair(near_parts(both, ny), place.xy)
    ff_part = jnp.broadcast_to(ff_part[None], (NZ,) + ff_part.shape)
    mine, encoding, ff_part, *in_parts = after(mine, encoding, ff_part, *in_parts)
    first_pair = [mine, hop(mine, "c")]
    w_in, small_rows = collect_inward(in_parts, place, share)
    ff_got = exchange(ff_part, ("z",))

    vectors = small_rows.reshape(spread, SMALL_ROWS, 3 * hw)[:, :extra].reshape(spread, kinds, share).astype(F32)
    expand_b = vectors[:, len(small) :].reshape(NZ, ny, 2, 2, part)
    expand_b = pick(pick(pick(expand_b, y, 1), c, 1), x, 1).reshape(1, NZ * part)
    vectors = jnp.swapaxes(vectors[:, : len(small)], 0, 1).reshape(len(small), width)
    gain_one, shift_one, query_b, value_b, outward_b, gain_two, shift_two, shrink_b = (
        vectors[i : i + 1] for i in range(len(small))
    )
    qkv_bias = jnp.concatenate(
        [
            lax.dynamic_slice_in_dim(query_b, me * hw, hw, 1),
            jnp.zeros((1, hw), F32),
            lax.dynamic_slice_in_dim(value_b, me * hw, hw, 1),
        ],
        axis=1,
    )

    first_all, qkv, *context_pair, log_total = attention(
        place.core, first_pair, encoding, vectors[:2], w_in, qkv_bias, row_starts, hd, ny, size
    )
    *context_pair, up_mine = after(*context_pair, up_mine)
    if ny == 2:
        context = by_half(c, context_pair[0][None], hop(context_pair[1], "c")[None], 0)
        context = context.reshape(2, 2, ny, size, hw)
        context = by_half(x, pick(context, x, 1)[:, None], hop(pick(context, 1 - x, 1), "x")[:, None], 1)
        context = by_half(y, pick(context, y, 2)[:, :, None], hop(pick(context, 1 - y, 2), "y")[:, :, None], 2)
    else:
        context = exchange(by_half(c, *context_pair, 0).reshape(layer, size, hw), LAYER)
    context = context.reshape(layer, size, hw)
    up_pair = [up_mine, hop(up_mine, "c")]

    inputs = fr.astype(F32) + lax.dynamic_slice_in_dim(encoding, (x * ny + y) * size, size, 0)
    normal_one, scale_one = normalize(inputs)
    context = jnp.swapaxes(context, 0, 1).reshape(size, width)
    middle = inputs + dot_nn(context, outward) + outward_b

    normal_two, scale_two = normalize(middle)
    second = (normal_two * gain_two + shift_two).astype(BF16)
    ff_got, *second_near = after(ff_got, *near_parts(second, ny))
    second_pair = both_cores(second_near, place)
    w_expand, w_shrink = collect_hidden(ff_got, width)
    active, before_grad, send, keep, out_part = feed_forward_front(
        place.core, second_pair, up_pair, w_expand, w_shrink, expand_b, size
    )
    second_parts = list(fold(keep, hop(send, "c"), place, ny))
    second_parts[0], active, before_grad = after(second_parts[0], active, before_grad)
    second_grad = finish(second_parts, ny)
    expand_b_sum, hidden_part = feed_forward_weights(second_pair, up_pair, active, before_grad)
    out_part = lax.psum_scatter(out_part, LAYER, scatter_dimension=0, tiled=True)
    second_grad, expand_b_sum = after(second_grad, expand_b_sum)
    hidden_got = exchange(hidden_part, ("z",))

    upstream = ct.astype(F32)
    middle_part, gain_two_sum, shift_two_sum = normalize_back(normal_two, scale_two, gain_two, second_grad)
    middle_grad = upstream + middle_part
    low_middle = middle_grad.astype(BF16)
    low_pair = both_cores(near_parts(low_middle, ny), place)
    mixed_grad, send, keep, outward_part = attention_back(
        place, qkv, low_pair, context_pair, outward, w_in, row_starts, log_total, hd, ny, size
    )
    got = hop(send, "c")
    cut = outward_part.reshape(2, -1, width)
    far_cut = hop(pick(cut, 1 - c), "c")
    got, far_cut, out_part = after(got, far_cut, out_part)
    first_parts = list(fold(keep, got, place, ny))
    first_parts[0], mixed_late, far_cut, hidden_got = after(first_parts[0], mixed_grad, far_cut, hidden_got)
    inward_part = dot_tn(first_all, mixed_late).astype(BF16)
    first_grad = finish(first_parts, ny)
    line_out = by_half(c, pick(cut, c)[None], far_cut[None], 0)
    if hd == 2 and ny == 2:
        line_out = line_out.reshape(2, 1, share, 2, width // 2)
        line_out = by_half(x, pick(line_out, x, 3), hop(pick(line_out, 1 - x, 3), "x"), 1)
    inward_got = exchange(inward_part.reshape(spread, share, 3 * hw), SEQ)
    input_part, gain_one_sum, shift_one_sum = normalize_back(normal_one, scale_one, vectors[:1], first_grad)
    late = (middle_grad + input_part).astype(BF16)
    late, out_part, hidden_got, line_out = after(late, out_part, hidden_got, line_out)
    hidden_sum = sum_sources(hidden_got, NZ)
    frames_grad = to_origin(late, place)
    layer_output = to_origin((middle + out_part.astype(F32) + shrink_b).astype(BF16), place)

    split = width // 2
    hidden_sum = sum_groups(hidden_sum.reshape(-1, units)).astype(BF16)
    line = hidden_sum[: width // NZ].reshape(ny, 2, share, units)
    if ny == 2:
        line = by_half(c, pick(line, c, 1)[:, None], hop(pick(line, 1 - c, 1), "c")[:, None], 1)
        line = by_half(y, pick(line, y)[None], hop(pick(line, 1 - y), "y")[None], 0)
    else:
        line = exchange(line.reshape(ny * 2, share, units), ("y", "c"))
    mine = stack_rows([line.reshape(-1, units), hidden_sum[width // NZ :]])
    other = hop(mine, "x")

    def full_hidden(other):
        pair = [unfold_columns(v[width // NZ :], width // units) for v in (mine, other)]
        g_shrink = by_half(x, *pair, 0).astype(F32)
        pair = [v[: width // NZ].reshape(ny, 2, 1, share, NZ, part) for v in (mine, other)]
        return g_shrink, jnp.transpose(by_half(x, *pair, 2), (3, 4, 0, 1, 2, 5)).reshape(share, -1).astype(F32)

    if hd == 2 and ny == 2:
        line = line_out
        out_got = lax.psum_scatter(line.reshape(NZ * share, split), "z", scatter_dimension=0, tiled=True)
        inward_got, out_got = after(inward_got, out_got)
        out_sum = sum_groups(out_got.astype(F32)).astype(BF16)
        g_outward = by_half(x, out_sum, hop(out_sum, "x"), 1).astype(F32)
    else:
        cut = lax.dynamic_update_slice(jnp.zeros((width, width), BF16), outward_part, (me * hw, 0))
        g_outward = lax.psum_scatter(cut, SEQ, scatter_dimension=0, tiled=True)
        g_outward = lax.psum(g_outward.astype(F32), ("g", "x"))

    mixed_sum = jnp.sum(mixed_grad.astype(F32), axis=0)

    def from_heads(value):
        return lax.dynamic_update_slice(jnp.zeros((width,), F32), value, (me * hw,))

    flat = lax.optimization_barrier(jnp.stack(
        [
            gain_one_sum,
            shift_one_sum,
            from_heads(mixed_sum[:hw]),
            from_heads(mixed_sum[2 * hw :]),
            jnp.sum(low_middle.astype(F32), axis=0),
            gain_two_sum,
            shift_two_sum,
            jnp.sum(upstream, axis=0),
        ]
    ))
    small_len = len(small) * share
    sums = jnp.swapaxes(flat.reshape(len(small), spread, share), 0, 1).reshape(spread, small_len)
    spot = jnp.zeros((NZ, ny, 2, 2, part), F32)
    spot = lax.dynamic_update_slice(spot, expand_b_sum.reshape(NZ, 1, 1, 1, part), (0, y, c, x, 0))
    sums = jnp.concatenate([sums, spot.reshape(spread, hidden)], axis=1)
    inward_got, sums = after(inward_got, sums)
    sums = jnp.broadcast_to(sums[None], (2,) + sums.shape).reshape(2 * spread, -1, 128)
    total = sum_groups(jnp.sum(exchange(sums, ("x",) + SEQ), axis=0)).reshape(-1)
    frames_grad, total, other = after(frames_grad, total, other)
    g_shrink, g_expand = full_hidden(other)
    g_small = total[:small_len].reshape(len(small), share)
    g_expand_b = total[small_len:]
    inward_sum = sum_groups(sum_sources(inward_got, NZ)).astype(BF16)
    g_inward = [v.reshape(ny, 2, 1, share, 3, hw) for v in (inward_sum, hop(inward_sum, "x"))]
    g_inward = jnp.transpose(by_half(x, *g_inward, 2), (3, 4, 1, 2, 0, 5)).reshape(share, -1).astype(F32)

    return (
        layer_output,
        frames_grad.astype(F32),
        g_small[0],
        g_small[1],
        g_inward,
        g_small[2],
        g_small[3],
        g_outward,
        g_small[4],
        g_small[5],
        g_small[6],
        g_expand,
        g_expand_b,
        g_shrink,
        g_small[7],
    )


def solution(mesh):
    batch, seq = mesh.shape["batch"], mesh.shape["seq"]
    groups, ny = batch // 2, seq // (2 * NZ)
    fine = Mesh(mesh.devices.reshape(groups, 2, NZ, ny, 2), ("g", "x", "z", "y", "c"))
    b, s = ("g", "x"), ("z", "y", "c")
    in_specs = (
        P(s, b, None),
        P(s, b, None),
        P(b, None),
        P(b, None),
        P(s),
        P(s),
        P(s, None),
        P(s),
        P(s),
        P(s, None),
        P(s),
        P(s),
        P(s),
        P(s, None),
        P(s),
        P(s, None),
        P(s),
    )
    out_specs = (
        P(s, b, None),
        P(s, b, None),
        P(s),
        P(s),
        P(s, None),
        P(s),
        P(s),
        P(s, None),
        P(s),
        P(s),
        P(s),
        P(s, None),
        P(s),
        P(s, None),
        P(s),
    )
    return jax.shard_map(
        functools.partial(on_device, groups, ny), mesh=fine, in_specs=in_specs, out_specs=out_specs, check_vma=False
    )
```

```python
import functools
import math

import jax
import jax.numpy as jnp
from jax import lax
from jax.experimental import pallas as pl
from jax.experimental.pallas import tpu as pltpu
from jax.sharding import Mesh, PartitionSpec as P


HEADS = 16
NZ = 4
SMALL_ROWS = 16
NORM_EPS = 1e-05
NEG = -1e30
F32 = jnp.float32
BF16 = jnp.bfloat16
LAYER_OF_ROW = (1, 2, 0, 3)
SWAP = [(0, 1), (1, 0)]
LAYER = ("c", "x", "y")
SEQ = ("z", "y", "c")


def xor_perm(count, k):
    return [(i, i ^ k) for i in range(count)]


def hop(value, axis, count=2, k=1):
    return lax.ppermute(value, axis, xor_perm(count, k))


def pick(value, index, axis=0):
    return lax.dynamic_index_in_dim(value, index, axis, keepdims=False)


def stack_rows(parts):
    return jnp.concatenate(parts, axis=0)


def assemble_body(pieces, size, place_ref, *refs):
    out_ref = refs[pieces]
    for r in range(pieces):
        spot = place_ref[0] ^ r
        out_ref[pl.ds(pl.multiple_of(spot * size, size), size), :] = refs[r][...]


def assemble(parts, me):
    size, width = parts[0].shape
    count = len(parts)
    return pl.pallas_call(
        functools.partial(assemble_body, count, size),
        out_shape=jax.ShapeDtypeStruct((count * size, width), parts[0].dtype),
        in_specs=[pl.BlockSpec(memory_space=pltpu.SMEM)] + whole(count),
        out_specs=whole(1)[0],
        compiler_params=pltpu.CompilerParams(vmem_limit_bytes=4 << 20),
        cost_estimate=pl.CostEstimate(flops=0, bytes_accessed=4 * count * size * width, transcendentals=0),
        name="assemble",
    )(me, *parts)


def assemble_pair_body(pieces, size, place_ref, *refs):
    left_ref, right_ref = refs[pieces:]
    width = left_ref.shape[1]
    for r in range(pieces):
        rows = pl.ds(pl.multiple_of((place_ref[0] ^ r) * size, size), size)
        left_ref[rows, :] = refs[r][:, 0:width]
        right_ref[rows, :] = refs[r][:, width : 2 * width]


def assemble_pair(parts, me):
    size, width = parts[0].shape
    count = len(parts)
    return pl.pallas_call(
        functools.partial(assemble_pair_body, count, size),
        out_shape=[jax.ShapeDtypeStruct((count * size, width // 2), parts[0].dtype)] * 2,
        in_specs=[pl.BlockSpec(memory_space=pltpu.SMEM)] + whole(count),
        out_specs=whole(2),
        compiler_params=pltpu.CompilerParams(vmem_limit_bytes=4 << 20),
        cost_estimate=pl.CostEstimate(flops=0, bytes_accessed=4 * count * size * width, transcendentals=0),
        name="assemble_pair",
    )(me, *parts)


def near_parts(block, ny):
    return [block] + [lax.ppermute(block, ("x", "y"), xor_perm(2 * ny, r)) for r in range(1, 2 * ny)]


def both_cores(parts, place):
    mine = assemble(parts, place.xy)
    return mine, hop(mine, "c")


def fold_body(count, size, place_ref, keep_ref, got_ref, own_ref, *out_refs):
    for r in range(count):
        spot = place_ref[0] ^ r
        here = pl.ds(pl.multiple_of(spot * size, size), size)
        value = keep_ref[here, :].astype(F32) + got_ref[here, :].astype(F32)
        if r == 0:
            own_ref[...] = value
        else:
            out_refs[r - 1][...] = value.astype(BF16)


def fold(keep, got, place, ny):
    rows, width = keep.shape
    count = 2 * ny
    size = rows // count
    return pl.pallas_call(
        functools.partial(fold_body, count, size),
        out_shape=[jax.ShapeDtypeStruct((size, width), F32)] + [jax.ShapeDtypeStruct((size, width), BF16)] * (count - 1),
        in_specs=[pl.BlockSpec(memory_space=pltpu.SMEM)] + whole(2),
        out_specs=whole(count),
        compiler_params=pltpu.CompilerParams(vmem_limit_bytes=4 << 20),
        cost_estimate=pl.CostEstimate(flops=count * size * width, bytes_accessed=6 * count * size * width, transcendentals=0),
        name="fold",
    )(place.xy, keep, got)


def finish(parts, ny):
    own = parts[0]
    for r in range(1, 2 * ny):
        own = own + lax.ppermute(parts[r], ("x", "y"), xor_perm(2 * ny, r)).astype(F32)
    return own


def fold_columns(value, units):
    return stack_rows([value[:, i : i + units] for i in range(0, value.shape[1], units)])


def unfold_columns(value, count):
    size = value.shape[0] // count
    return jnp.concatenate([value[i * size : (i + 1) * size] for i in range(count)], axis=1)


def collect_inward_body(share, place_ref, *refs):
    weight_ref, small_ref = refs[NZ:]
    deep = share + SMALL_ROWS
    lines = refs[0].shape[0] // deep
    for r in range(NZ):
        base = (place_ref[0] ^ r) * lines
        for i in range(lines):
            start = i * deep
            rows = pl.ds(pl.multiple_of((base + i) * share, share), share)
            weight_ref[rows, :] = refs[r][start : start + share, :]
            rows = pl.ds(pl.multiple_of((base + i) * SMALL_ROWS, SMALL_ROWS), SMALL_ROWS)
            small_ref[rows, :] = refs[r][start + share : start + deep, :]


def collect_inward(parts, place, share):
    rows, width = parts[0].shape
    lines = NZ * rows // (share + SMALL_ROWS)
    return pl.pallas_call(
        functools.partial(collect_inward_body, share),
        out_shape=[jax.ShapeDtypeStruct((lines * n, width), BF16) for n in (share, SMALL_ROWS)],
        in_specs=[pl.BlockSpec(memory_space=pltpu.SMEM)] + whole(NZ),
        out_specs=whole(2),
        compiler_params=pltpu.CompilerParams(vmem_limit_bytes=4 << 20),
        cost_estimate=pl.CostEstimate(flops=0, bytes_accessed=16 * rows * width, transcendentals=0),
        name="collect_inward",
    )(place.layer, *parts)


def collect_hidden_body(parts_ref, expand_ref, shrink_ref):
    quarter = expand_ref.shape[0] // NZ
    part, units = shrink_ref.shape[0] // NZ, expand_ref.shape[1]
    for r in range(NZ):
        expand_ref[r * quarter : (r + 1) * quarter, :] = parts_ref[r, 0:quarter, :]
        for i in range(shrink_ref.shape[1] // units):
            start = quarter + i * part
            here = slice(r * part, (r + 1) * part)
            shrink_ref[here, i * units : (i + 1) * units] = parts_ref[r, start : start + part, :]


def collect_hidden(parts, width):
    units = parts.shape[2]
    return pl.pallas_call(
        collect_hidden_body,
        out_shape=[jax.ShapeDtypeStruct((width, units), BF16), jax.ShapeDtypeStruct((units, width), BF16)],
        in_specs=whole(1),
        out_specs=whole(2),
        compiler_params=pltpu.CompilerParams(vmem_limit_bytes=4 << 20),
        cost_estimate=pl.CostEstimate(flops=0, bytes_accessed=4 * parts.size, transcendentals=0),
        name="collect_hidden",
    )(parts)


def rehome_flat(x, z, c):
    return (x * NZ + z) * 2 + c


def rehome_perm(k):
    return [
        (rehome_flat(x, z, c), rehome_flat(z >> 1, LAYER_OF_ROW[2 * x + (c ^ k)], z & 1))
        for x in range(2)
        for z in range(NZ)
        for c in range(2)
    ]


def to_home(block, place):
    got = [
        lax.ppermute(jnp.where(place.c == k, block[:, 0], block[:, 1]), ("x", "z", "c"), rehome_perm(k))
        for k in range(2)
    ]
    first = place.z < 2
    return stack_rows([jnp.where(first, got[0], got[1]), jnp.where(first, got[1], got[0])])


def to_origin(block, place):
    half = block.shape[0] // 2
    first = place.z < 2
    low, high = block[:half], block[half:]
    sent = [jnp.where(first, low, high), jnp.where(first, high, low)]
    got = [
        lax.ppermute(sent[k], ("x", "z", "c"), [(b, a) for a, b in rehome_perm(k)]) for k in range(2)
    ]
    return jnp.stack(
        [jnp.where(place.c == 0, got[0], got[1]), jnp.where(place.c == 0, got[1], got[0])], axis=1
    )


def after(first, *values):
    return lax.optimization_barrier((first, *values))


def sum_sources(value, count):
    return jnp.sum(value.reshape((count, -1) + value.shape[1:]).astype(F32), axis=0)


def by_half(x, mine, other, axis):
    return jnp.concatenate([jnp.where(x == 0, mine, other), jnp.where(x == 0, other, mine)], axis=axis)


def sin_cos(position, width):
    feature = jnp.arange(width, dtype=jnp.int32)
    rates = jnp.exp((feature // 2).astype(F32) * (-2.0 * math.log(10000.0) / width))
    angle = position.astype(F32)[:, None] * rates[None, :]
    turn = jnp.round(angle * (2.0 / math.pi))
    rest = angle - turn * 1.5703125
    rest = rest - turn * 0.00048375129699707031
    rest = rest - turn * 7.5497899548918861e-08
    quadrant = turn.astype(jnp.int32) + (feature % 2)[None, :]
    square = rest * rest
    sine = rest + rest * square * (
        -0.16666666641626524 + square * (0.008333329385889463 + square * (-0.00019839334836096632 + square * 2.718311493989822e-06))
    )
    cosine = 1.0 + square * (
        -0.49999999725103100 + square * (0.04166662332373906 + square * (-0.001388676377460993 + square * 2.439044879627741e-05))
    )
    value = jnp.where((quadrant & 1) == 0, sine, cosine)
    return jnp.where((quadrant & 2) == 0, value, -value)


def normalize(values):
    center = values - jnp.mean(values, axis=-1, keepdims=True)
    scale = lax.rsqrt(jnp.mean(center * center, axis=-1, keepdims=True) + NORM_EPS)
    return center * scale, scale


def normalize_back(normal, scale, gain, upstream):
    scaled = upstream * gain
    inner = scaled - jnp.mean(scaled, axis=-1, keepdims=True)
    inner = inner - normal * jnp.mean(scaled * normal, axis=-1, keepdims=True)
    return inner * scale, jnp.sum(upstream * normal, axis=0), jnp.sum(upstream, axis=0)


def dot_nt(a, b):
    return lax.dot_general(a, b, (((1,), (1,)), ((), ())), preferred_element_type=F32)


def dot_tn(a, b):
    return lax.dot_general(a, b, (((0,), (0,)), ((), ())), preferred_element_type=F32)


def dot_nn(a, b):
    return jnp.dot(a, b, preferred_element_type=F32)


BLOCK = 256


def chunk_owner(chunk, ny):
    outer, y = divmod(chunk, ny)
    return ((outer & 1) * 2 + (outer >> 1)) * ny + y


def lane_parts(heads, width):
    if heads == 1:
        return [None]
    lane = lax.broadcasted_iota(jnp.int32, (1, width), 1)
    return [(lane >= h * (width // heads)) & (lane < (h + 1) * (width // heads)) for h in range(heads)]


def only(value, lanes):
    return value if lanes is None else jnp.where(lanes, value, jnp.zeros_like(value))


def allowed_pairs(start_ref, first, total):
    key = lax.broadcasted_iota(jnp.int32, (total, BLOCK), 0)
    frame = first + lax.broadcasted_iota(jnp.int32, (total, BLOCK), 1)
    return (key >= start_ref[:, first : first + BLOCK]) & (key <= frame)


def chunk_rows(chunk, ny, size, core):
    half, spot = divmod(chunk_owner(chunk, ny), 2 * ny)
    return pl.ds(pl.multiple_of(((half ^ core) * (2 * ny) + spot) * size, size), size)


def attend(
    heads,
    ny,
    size,
    core_ref,
    mine_ref,
    other_ref,
    encoding_ref,
    affine_ref,
    weight_ref,
    bias_ref,
    start_ref,
    first_ref,
    qkv_ref,
    near_ref,
    far_ref,
    log_ref,
    q_s,
    k_s,
    vt_s,
):
    count = 4 * ny
    width = q_s.shape[1]
    core = core_ref[0]
    step = 2 * size
    half = mine_ref.shape[0]
    for base, ref in ((0, mine_ref), (half, other_ref)):
        for start in range(0, half, step):
            rows = slice(base + start, base + start + step)
            normal, _ = normalize(ref[start : start + step, :].astype(F32) + encoding_ref[rows, :])
            value = (normal * affine_ref[0:1, :] + affine_ref[1:2, :]).astype(BF16)
            first_ref[rows, :] = value
            qkv_ref[rows, :] = (dot_nn(value, weight_ref[...]) + bias_ref[...]).astype(BF16)
    for chunk in range(count):
        rows = chunk_rows(chunk, ny, size, core)
        here = slice(chunk * size, (chunk + 1) * size)
        q_s[here, :] = qkv_ref[rows, 0:width] * 0.125
        k_s[here, :] = qkv_ref[rows, width : 2 * width]
        vt_s[:, here] = jnp.transpose(qkv_ref[rows, 2 * width : 3 * width].astype(F32)).astype(BF16)
    lanes = lane_parts(heads, width)
    each = width // heads
    for block in range(count * size // BLOCK):
        first = block * BLOCK
        total = first + BLOCK
        allowed = allowed_pairs(start_ref, first, total)
        q_block = q_s[first:total, :]
        contexts = []
        for h in range(heads):
            scores = dot_nt(k_s[0:total, :], only(q_block, lanes[h]))
            scores = jnp.where(allowed, scores, NEG)
            top = jnp.max(scores, axis=0, keepdims=True)
            weight = jnp.exp(scores - top)
            mass = jnp.sum(weight, axis=0, keepdims=True)
            part = dot_nn(vt_s[h * each : (h + 1) * each, 0:total], weight.astype(BF16))
            contexts.append(part / mass)
            log_ref[h : h + 1, first:total] = top + jnp.log(mass)
        context = contexts[0] if heads == 1 else jnp.concatenate(contexts, axis=0)
        context = jnp.transpose(context).astype(BF16)
        for sub in range(BLOCK // size):
            owner = chunk_owner(block * (BLOCK // size) + sub, ny)
            side, spot = divmod(owner, 2 * ny)
            rows, piece = slice(spot * size, (spot + 1) * size), context[sub * size : (sub + 1) * size]

            @pl.when(core == side)
            def _(rows=rows, piece=piece):
                near_ref[rows, :] = piece

            @pl.when(core != side)
            def _(rows=rows, piece=piece):
                far_ref[rows, :] = piece


def attend_back(
    heads,
    ny,
    size,
    place_ref,
    qkv_any,
    mine_ref,
    other_any,
    near_any,
    far_any,
    outward_any,
    weight_any,
    start_ref,
    log_ref,
    out_ref,
    send_ref,
    keep_ref,
    outward_grad_ref,
    q_s,
    k_s,
    v_s,
    g_s,
    kt_s,
    dq_s,
    dk_s,
    dv_s,
    qkv_ref,
    other_ref,
    near_ref,
    far_ref,
    outward_ref,
    weight_ref,
    in_sem,
):
    count = 4 * ny
    width = q_s.shape[1]
    core = place_ref[0]
    half = mine_ref.shape[0]
    step = 2 * size
    rows = pl.ds(pl.multiple_of(place_ref[1] * width, width), width)
    pairs = (
        (outward_any.at[rows], outward_ref),
        (other_any, other_ref),
        (qkv_any, qkv_ref),
        (weight_any, weight_ref),
        (near_any, near_ref),
        (far_any, far_ref),
    )
    copies = [pltpu.make_async_copy(source, target, in_sem.at[i]) for i, (source, target) in enumerate(pairs)]
    for copy in copies:
        copy.start()
    copies[0].wait()
    for base, ref in ((0, mine_ref), (half, other_ref)):
        if base:
            copies[1].wait()
        for start in range(0, half, step):
            rows = slice(start, start + step)
            out_ref[base + start : base + start + step, 0:width] = dot_nt(ref[rows, :], outward_ref[...]).astype(BF16)
    copies[2].wait()
    for chunk in range(count):
        rows = chunk_rows(chunk, ny, size, core)
        here = slice(chunk * size, (chunk + 1) * size)
        q_s[here, :] = qkv_ref[rows, 0:width] * 0.125
        key = qkv_ref[rows, width : 2 * width]
        k_s[here, :] = key
        kt_s[:, here] = jnp.transpose(key.astype(F32)).astype(BF16)
        v_s[here, :] = qkv_ref[rows, 2 * width : 3 * width]
        g_s[here, :] = out_ref[rows, 0:width]
    dk_s[...] = jnp.zeros_like(dk_s)
    dv_s[...] = jnp.zeros_like(dv_s)
    lanes = lane_parts(heads, width)
    each = width // heads
    for block in range(count * size // BLOCK):
        first = block * BLOCK
        total = first + BLOCK
        allowed = allowed_pairs(start_ref, first, total)
        q_block, g_block = q_s[first:total, :], g_s[first:total, :]
        queries = []
        for h in range(heads):
            q_one, g_one = only(q_block, lanes[h]), only(g_block, lanes[h])
            scores = dot_nt(k_s[0:total, :], q_one)
            probs = jnp.where(allowed, jnp.exp(scores - log_ref[h : h + 1, first:total]), 0.0)
            prob_grad = dot_nt(v_s[0:total, :], g_one)
            delta = jnp.sum(probs * prob_grad, axis=0, keepdims=True)
            score_grad = (probs * (prob_grad - delta)).astype(BF16)
            dv_s[0:total, :] += dot_nn(probs.astype(BF16), g_one)
            dk_s[0:total, :] += dot_nn(score_grad, q_one)
            queries.append(dot_nn(kt_s[h * each : (h + 1) * each, 0:total], score_grad))
        query_grad = queries[0] if heads == 1 else jnp.concatenate(queries, axis=0)
        dq_s[first:total, :] = jnp.transpose(query_grad) * 0.125
    for chunk in range(count):
        rows = chunk_rows(chunk, ny, size, core)
        here = slice(chunk * size, (chunk + 1) * size)
        out_ref[rows, 0:width] = dq_s[here, :].astype(BF16)
        out_ref[rows, width : 2 * width] = dk_s[here, :].astype(BF16)
        out_ref[rows, 2 * width : 3 * width] = dv_s[here, :].astype(BF16)
    for copy in copies[3:]:
        copy.wait()
    for ref, base in ((send_ref, half), (keep_ref, 0)):
        for start in range(0, half, step):
            rows = slice(base + start, base + start + step)
            ref[start : start + step, :] = dot_nt(out_ref[rows, :], weight_ref[...]).astype(BF16)
    total = dot_tn(near_ref[...], mine_ref[...]) + dot_tn(far_ref[...], other_ref[...])
    outward_grad_ref[...] = total.astype(BF16)


def feed_forward(
    size,
    core_ref,
    mine_ref,
    other_ref,
    up_mine_ref,
    up_other_ref,
    expand_ref,
    shrink_ref,
    bias_ref,
    active_ref,
    grad_ref,
    send_ref,
    keep_ref,
    result_ref,
):
    half = keep_ref.shape[0]
    step = 2 * size
    rate = math.sqrt(2.0 / math.pi)
    core = core_ref[0]
    sides = ((send_ref, other_ref, up_other_ref, half, 1 - core), (keep_ref, mine_ref, up_mine_ref, 0, core))
    for ref, source_ref, up_ref, base, side in sides:
        for start in range(0, half, step):
            rows = slice(start, start + step)
            pair = slice(base + start, base + start + step)
            place = pl.ds(pl.multiple_of(side * half + start, step), step)
            before = dot_nn(source_ref[rows, :], expand_ref[...]) + bias_ref[...]
            upper = dot_nt(up_ref[rows, :], shrink_ref[...])
            square = before * before
            inner = jnp.tanh(rate * (before + 0.044715 * before * square))
            plus = 0.5 * (1.0 + inner)
            active = (before * plus).astype(BF16)
            active_ref[pair, :] = active
            slope = plus + 0.5 * before * (1.0 - inner * inner) * (rate + rate * 3 * 0.044715 * square)
            lower = (upper * slope).astype(BF16)
            grad_ref[pair, :] = lower
            ref[rows, :] = dot_nt(lower, expand_ref[...]).astype(BF16)
            result_ref[place, :] = dot_nn(active, shrink_ref[...]).astype(BF16)


def weight_parts(part, mine_ref, other_ref, up_mine_ref, up_other_ref, active_ref, grad_ref, bias_ref, out_ref):
    half, width = mine_ref.shape
    quarter, all_units = width // NZ, NZ * part
    for r in range(NZ):
        spot, ref = r, out_ref.at[r]
        here = slice(spot * quarter, (spot + 1) * quarter)
        total = dot_tn(mine_ref[:, here], grad_ref[0:half, :]) + dot_tn(other_ref[:, here], grad_ref[half : 2 * half, :])
        ref[0:quarter, :] = total.astype(BF16)
        units = slice(spot * part, (spot + 1) * part)
        total = dot_tn(active_ref[0:half, units], up_mine_ref[...])
        total = (total + dot_tn(active_ref[half : 2 * half, units], up_other_ref[...])).astype(BF16)
        for i in range(width // all_units):
            start = quarter + i * part
            ref[start : start + part, :] = total[:, i * all_units : (i + 1) * all_units]
    bias_ref[...] = jnp.sum(grad_ref[...].astype(F32), axis=0, keepdims=True)


def feed_forward_weights(second, up, active, before_grad):
    frames, units = active.shape
    width, part = up[0].shape[1], units // NZ
    quarter = width // NZ
    if part % 128:
        shrink = dot_tn(active, stack_rows(up)).astype(BF16).reshape(NZ, part, width)
        expand = dot_tn(stack_rows(second), before_grad).astype(BF16).reshape(NZ, quarter, units)
        bias = jnp.sum(before_grad.astype(F32), axis=0, keepdims=True)
        return bias, jnp.stack([stack_rows([expand[k], fold_columns(shrink[k], units)]) for k in range(NZ)])
    return pl.pallas_call(
        functools.partial(weight_parts, part),
        out_shape=(jax.ShapeDtypeStruct((1, units), F32), jax.ShapeDtypeStruct((NZ, 2 * quarter, units), BF16)),
        in_specs=whole(6),
        out_specs=tuple(whole(2)),
        compiler_params=pltpu.CompilerParams(vmem_limit_bytes=16 << 20),
        cost_estimate=pl.CostEstimate(
            flops=4 * frames * width * units, bytes_accessed=8 * frames * width, transcendentals=0
        ),
        name="feed_forward_weights",
    )(*second, *up, active, before_grad)


def whole(count):
    return [pl.BlockSpec(memory_space=pltpu.VMEM)] * count


def anywhere(count):
    return [pl.BlockSpec(memory_space=pl.ANY)] * count


def attention(core, pair, encoding, affine, w_in, bias, starts, heads, ny, size):
    half, wide = pair[0].shape[0], w_in.shape[1]
    frames, depth, width = 2 * half, pair[0].shape[1], wide // 3
    pairs = frames * frames * heads
    return pl.pallas_call(
        functools.partial(attend, heads, ny, size),
        out_shape=(
            jax.ShapeDtypeStruct((frames, depth), BF16),
            jax.ShapeDtypeStruct((frames, wide), BF16),
            jax.ShapeDtypeStruct((half, width), BF16),
            jax.ShapeDtypeStruct((half, width), BF16),
            jax.ShapeDtypeStruct((heads, frames), F32),
        ),
        in_specs=[pl.BlockSpec(memory_space=pltpu.SMEM)] + whole(7),
        out_specs=tuple(whole(5)),
        scratch_shapes=[
            pltpu.VMEM((frames, width), BF16),
            pltpu.VMEM((frames, width), BF16),
            pltpu.VMEM((width, frames), BF16),
        ],
        compiler_params=pltpu.CompilerParams(vmem_limit_bytes=16 << 20),
        cost_estimate=pl.CostEstimate(
            flops=pairs * 256 + 2 * frames * depth * wide, bytes_accessed=8 * frames * depth, transcendentals=pairs // 2
        ),
        name="attend",
    )(core, *pair, encoding, affine, w_in, bias, starts)


def attention_back(place, qkv, pair, context, outward, w_in, starts, log_total, heads, ny, size):
    frames, wide = qkv.shape
    width = wide // 3
    depth = pair[0].shape[1]
    pairs = frames * frames * heads
    half = jax.ShapeDtypeStruct(pair[0].shape, BF16)
    return pl.pallas_call(
        functools.partial(attend_back, heads, ny, size),
        out_shape=(
            jax.ShapeDtypeStruct((frames, wide), BF16),
            half,
            half,
            jax.ShapeDtypeStruct((width, depth), BF16),
        ),
        in_specs=[pl.BlockSpec(memory_space=pltpu.SMEM)] + anywhere(1) + whole(1) + anywhere(5) + whole(2),
        out_specs=tuple(whole(4)),
        scratch_shapes=[pltpu.VMEM((frames, width), BF16)] * 4
        + [pltpu.VMEM((width, frames), BF16)]
        + [pltpu.VMEM((frames, width), F32)] * 3
        + [pltpu.VMEM((frames, wide), BF16), pltpu.VMEM((frames // 2, depth), BF16)]
        + [pltpu.VMEM((frames // 2, width), BF16)] * 2
        + [pltpu.VMEM((width, depth), BF16), pltpu.VMEM((depth, wide), BF16), pltpu.SemaphoreType.DMA((6,))],
        compiler_params=pltpu.CompilerParams(vmem_limit_bytes=(frames >> 6) * 5 << 18),
        cost_estimate=pl.CostEstimate(
            flops=pairs * 640 + 2 * frames * depth * (wide + 2 * width),
            bytes_accessed=8 * frames * depth,
            transcendentals=pairs // 2,
        ),
        name="attend_back",
    )(jnp.concatenate([place.core, place.me]), qkv, *pair, *context, outward, w_in, starts, log_total)


def feed_forward_front(core, pair, up_pair, w_expand, w_shrink, bias, size):
    frames, width = 2 * pair[0].shape[0], pair[0].shape[1]
    units = w_expand.shape[1]
    half = jax.ShapeDtypeStruct((frames // 2, width), BF16)
    inner = jax.ShapeDtypeStruct((frames, units), BF16)
    return pl.pallas_call(
        functools.partial(feed_forward, size),
        out_shape=(inner, inner, half, half, jax.ShapeDtypeStruct((frames, width), BF16)),
        in_specs=[pl.BlockSpec(memory_space=pltpu.SMEM)] + whole(7),
        out_specs=tuple(whole(5)),
        compiler_params=pltpu.CompilerParams(vmem_limit_bytes=16 << 20),
        cost_estimate=pl.CostEstimate(
            flops=8 * frames * width * units, bytes_accessed=10 * frames * width, transcendentals=frames * units
        ),
        name="feed_forward",
    )(core, *pair, *up_pair, w_expand, w_shrink, bias)


class Place:
    def __init__(self, ny):
        self.x, self.z, self.y, self.c = (lax.axis_index(a) for a in ("x", "z", "y", "c"))
        self.xy = jnp.reshape(self.x * ny + self.y, (1,)).astype(jnp.int32)
        self.core = jnp.reshape(self.c, (1,)).astype(jnp.int32)
        self.layer = jnp.reshape(self.z, (1,)).astype(jnp.int32)
        self.me = (self.core * 2) * ny + self.xy


def on_device(
    groups,
    ny,
    frames,
    cotangent,
    segment_lengths,
    position_offsets,
    first_gain,
    first_shift,
    inward_weight,
    query_bias,
    value_bias,
    outward_weight,
    outward_bias,
    second_gain,
    second_shift,
    expand_weight,
    expand_bias,
    shrink_weight,
    shrink_bias,
):
    place = Place(ny)
    x, z, y, c = place.x, place.z, place.y, place.c
    local_len, rows, width = frames.shape
    share = inward_weight.shape[0]
    layer = 4 * ny
    spread = NZ * ny * 2
    full_len = local_len * spread
    size = 2 * local_len
    hd = HEADS // layer
    hw = hd * (width // HEADS)
    hidden = expand_bias.shape[0]
    part = hidden // 2
    me = (c * 2 + x) * ny + y

    def sum_groups(value):
        return lax.psum(value, "g") if groups > 1 else value

    def exchange(value, axes):
        return lax.all_to_all(value, axes, 0, 0, tiled=True)

    both = to_home(jnp.concatenate([frames, cotangent], axis=2), place)
    table = jnp.stack([segment_lengths, position_offsets], axis=1)
    other_table = hop(table, "x")
    other_table, later_inward = after(other_table, inward_weight)

    small = [first_gain, first_shift, query_bias, value_bias, outward_bias, second_gain, second_shift, shrink_bias]
    kinds = len(small) + hidden // share
    units = NZ * part
    packed = jnp.concatenate([v[None] for v in small] + [expand_bias.reshape(-1, share)], axis=0)
    packed = packed.reshape(-1, 3 * hw)
    extra = packed.shape[0]
    packed = jnp.pad(packed, ((0, SMALL_ROWS - extra), (0, units)))[None]
    in_cols = jnp.transpose(later_inward.reshape(share, 3, 2, 2, ny, hw), (3, 4, 2, 0, 1, 5))
    in_cols = pick(in_cols, x).reshape(ny * 2, share, 3 * hw)
    ex_cols = pick(expand_weight.reshape(share, NZ, ny, 2, 2, part), x, 4)
    ex_cols = jnp.transpose(ex_cols, (2, 3, 0, 1, 4)).reshape(ny * 2, share, units)
    columns = jnp.concatenate([in_cols, ex_cols], axis=2)
    columns = jnp.concatenate([columns, jnp.broadcast_to(packed, (ny * 2,) + packed.shape[1:])], axis=1)
    columns = exchange(columns, ("y", "c"))

    row_x = jnp.where((z == 0) | (z == 3), 1, 0)
    table = pick(jnp.where(x == row_x, table, other_table), z >> 1)
    lengths, offsets = table[0], table[1]
    count = lengths.shape[0]
    starts = jnp.sum(
        jnp.where(jnp.arange(count)[None, :] < jnp.arange(count)[:, None], lengths[None, :], 0), axis=1
    )
    frame_ids = jnp.arange(full_len, dtype=jnp.int32)
    row_starts = jnp.max(jnp.where(starts[:, None] <= frame_ids[None, :], starts[:, None], 0), axis=0)[None, :]
    spot = jnp.arange(2 * ny)
    chunk = jnp.concatenate([(2 * (spot // ny) + i) * ny + spot % ny for i in (c, 1 - c)])
    mine = (chunk[:, None] * size + jnp.arange(size, dtype=jnp.int32)).reshape(-1)
    inside = (mine[:, None] >= starts[None, :]) & (mine[:, None] < (starts + lengths)[None, :])
    position = jnp.sum(jnp.where(inside, offsets[None, :] + mine[:, None] - starts[None, :], 0), axis=1)
    encoding = sin_cos(position, width)

    both, later_outward, columns = after(both, outward_weight, columns)
    fr, ct = both[:, :width], both[:, width:]
    outward = lax.all_gather(later_outward, SEQ, axis=0, tiled=True)
    in_part = columns[:, :, : 3 * hw].reshape(-1, 3 * hw)
    in_parts = [in_part] + [hop(in_part, "z", NZ, k) for k in range(1, NZ)]
    sh_rows = lax.dynamic_slice_in_dim(shrink_weight, x * part, part, 0)
    ff_part = stack_rows([columns[:, :share, 3 * hw :].reshape(-1, units), fold_columns(sh_rows, units)])
    mine, up_mine = assemble_pair(near_parts(both, ny), place.xy)
    ff_part = jnp.broadcast_to(ff_part[None], (NZ,) + ff_part.shape)
    mine, encoding, ff_part, *in_parts = after(mine, encoding, ff_part, *in_parts)
    first_pair = [mine, hop(mine, "c")]
    w_in, small_rows = collect_inward(in_parts, place, share)
    ff_got = exchange(ff_part, ("z",))

    vectors = small_rows.reshape(spread, SMALL_ROWS, 3 * hw)[:, :extra].reshape(spread, kinds, share).astype(F32)
    expand_b = vectors[:, len(small) :].reshape(NZ, ny, 2, 2, part)
    expand_b = pick(pick(pick(expand_b, y, 1), c, 1), x, 1).reshape(1, NZ * part)
    vectors = jnp.swapaxes(vectors[:, : len(small)], 0, 1).reshape(len(small), width)
    gain_one, shift_one, query_b, value_b, outward_b, gain_two, shift_two, shrink_b = (
        vectors[i : i + 1] for i in range(len(small))
    )
    qkv_bias = jnp.concatenate(
        [
            lax.dynamic_slice_in_dim(query_b, me * hw, hw, 1),
            jnp.zeros((1, hw), F32),
            lax.dynamic_slice_in_dim(value_b, me * hw, hw, 1),
        ],
        axis=1,
    )

    first_all, qkv, *context_pair, log_total = attention(
        place.core, first_pair, encoding, vectors[:2], w_in, qkv_bias, row_starts, hd, ny, size
    )
    *context_pair, up_mine = after(*context_pair, up_mine)
    if ny == 2:
        context = by_half(c, context_pair[0][None], hop(context_pair[1], "c")[None], 0)
        context = context.reshape(2, 2, ny, size, hw)
        context = by_half(x, pick(context, x, 1)[:, None], hop(pick(context, 1 - x, 1), "x")[:, None], 1)
        context = by_half(y, pick(context, y, 2)[:, :, None], hop(pick(context, 1 - y, 2), "y")[:, :, None], 2)
    else:
        context = exchange(by_half(c, *context_pair, 0).reshape(layer, size, hw), LAYER)
    context = context.reshape(layer, size, hw)
    up_pair = [up_mine, hop(up_mine, "c")]

    inputs = fr.astype(F32) + lax.dynamic_slice_in_dim(encoding, (x * ny + y) * size, size, 0)
    normal_one, scale_one = normalize(inputs)
    context = jnp.swapaxes(context, 0, 1).reshape(size, width)
    middle = inputs + dot_nn(context, outward) + outward_b

    normal_two, scale_two = normalize(middle)
    second = (normal_two * gain_two + shift_two).astype(BF16)
    ff_got, *second_near = after(ff_got, *near_parts(second, ny))
    second_pair = both_cores(second_near, place)
    w_expand, w_shrink = collect_hidden(ff_got, width)
    active, before_grad, send, keep, out_part = feed_forward_front(
        place.core, second_pair, up_pair, w_expand, w_shrink, expand_b, size
    )
    second_parts = list(fold(keep, hop(send, "c"), place, ny))
    second_parts[0], active, before_grad = after(second_parts[0], active, before_grad)
    second_grad = finish(second_parts, ny)
    expand_b_sum, hidden_part = feed_forward_weights(second_pair, up_pair, active, before_grad)
    out_part = lax.psum_scatter(out_part, LAYER, scatter_dimension=0, tiled=True)
    second_grad, expand_b_sum = after(second_grad, expand_b_sum)
    hidden_got = exchange(hidden_part, ("z",))

    upstream = ct.astype(F32)
    middle_part, gain_two_sum, shift_two_sum = normalize_back(normal_two, scale_two, gain_two, second_grad)
    middle_grad = upstream + middle_part
    low_middle = middle_grad.astype(BF16)
    low_pair = both_cores(near_parts(low_middle, ny), place)
    mixed_grad, send, keep, outward_part = attention_back(
        place, qkv, low_pair, context_pair, outward, w_in, row_starts, log_total, hd, ny, size
    )
    got = hop(send, "c")
    cut = outward_part.reshape(2, -1, width)
    far_cut = hop(pick(cut, 1 - c), "c")
    got, far_cut, out_part = after(got, far_cut, out_part)
    first_parts = list(fold(keep, got, place, ny))
    first_parts[0], mixed_late, far_cut, hidden_got = after(first_parts[0], mixed_grad, far_cut, hidden_got)
    inward_part = dot_tn(first_all, mixed_late).astype(BF16)
    first_grad = finish(first_parts, ny)
    line_out = by_half(c, pick(cut, c)[None], far_cut[None], 0)
    if hd == 2 and ny == 2:
        line_out = line_out.reshape(2, 1, share, 2, width // 2)
        line_out = by_half(x, pick(line_out, x, 3), hop(pick(line_out, 1 - x, 3), "x"), 1)
    deep = width // 2
    inward_keep, inward_send = (
        lax.dynamic_slice_in_dim(inward_part, i * deep, deep, 0) for i in (z >> 1, 1 - (z >> 1))
    )
    inward_got = hop(inward_send, "z", NZ, 2)
    input_part, gain_one_sum, shift_one_sum = normalize_back(normal_one, scale_one, vectors[:1], first_grad)
    late = (middle_grad + input_part).astype(BF16)
    late, out_part, hidden_got, line_out, inward_got = after(late, out_part, hidden_got, line_out, inward_got)
    inward_half = inward_keep.astype(F32) + inward_got.astype(F32)
    deep = width // NZ
    inward_keep, inward_send = (
        lax.dynamic_slice_in_dim(inward_half, i * deep, deep, 0) for i in (z & 1, 1 - (z & 1))
    )
    inward_sum = inward_keep + hop(inward_send.astype(BF16), "z", NZ, 1).astype(F32)
    inward_sum, out_part, gain_one_sum = after(inward_sum, out_part, gain_one_sum)
    inward_sum = sum_groups(inward_sum).astype(BF16)
    hidden_sum = sum_sources(hidden_got, NZ)
    frames_grad = to_origin(late, place)
    layer_output = to_origin((middle + out_part.astype(F32) + shrink_b).astype(BF16), place)

    split = width // 2
    hidden_sum = sum_groups(hidden_sum.reshape(-1, units)).astype(BF16)

    def to_rows(value):
        line = value.reshape(ny, 2, share, value.shape[1])
        if ny > 2:
            return exchange(line.reshape(ny * 2, share, -1), ("y", "c")).reshape(line.shape)
        line = by_half(c, pick(line, c, 1)[:, None], hop(pick(line, 1 - c, 1), "c")[:, None], 1)
        return by_half(y, pick(line, y)[None], hop(pick(line, 1 - y), "y")[None], 0)

    line = to_rows(hidden_sum[: width // NZ])
    mine = stack_rows([line.reshape(-1, units), hidden_sum[width // NZ :]])
    other = hop(mine, "x")

    def full_hidden(other):
        pair = [unfold_columns(v[width // NZ :], width // units) for v in (mine, other)]
        g_shrink = by_half(x, *pair, 0).astype(F32)
        pair = [v[: width // NZ].reshape(ny, 2, 1, share, NZ, part) for v in (mine, other)]
        return g_shrink, jnp.transpose(by_half(x, *pair, 2), (3, 4, 0, 1, 2, 5)).reshape(share, -1).astype(F32)

    if hd == 2 and ny == 2:
        line = line_out
        out_got = lax.psum_scatter(line.reshape(NZ * share, split), "z", scatter_dimension=0, tiled=True)
    else:
        out_got = None
        cut = lax.dynamic_update_slice(jnp.zeros((width, width), BF16), outward_part, (me * hw, 0))
        g_outward = lax.psum_scatter(cut, SEQ, scatter_dimension=0, tiled=True)
        g_outward = lax.psum(g_outward.astype(F32), ("g", "x"))

    mixed_sum = jnp.sum(mixed_grad.astype(F32), axis=0)

    def from_heads(value):
        return lax.dynamic_update_slice(jnp.zeros((width,), F32), value, (me * hw,))

    flat = lax.optimization_barrier(jnp.stack(
        [
            gain_one_sum,
            shift_one_sum,
            from_heads(mixed_sum[:hw]),
            from_heads(mixed_sum[2 * hw :]),
            jnp.sum(low_middle.astype(F32), axis=0),
            gain_two_sum,
            shift_two_sum,
            jnp.sum(upstream, axis=0),
        ]
    ))
    small_len = len(small) * share
    sums = jnp.swapaxes(flat.reshape(len(small), spread, share), 0, 1).reshape(spread, small_len)
    spot = jnp.zeros((NZ, ny, 2, 2, part), F32)
    spot = lax.dynamic_update_slice(spot, expand_b_sum.reshape(NZ, 1, 1, 1, part), (0, y, c, x, 0))
    sums = jnp.concatenate([sums, spot.reshape(spread, hidden)], axis=1)
    sums = jnp.broadcast_to(sums[None], (2,) + sums.shape).reshape(2 * spread, -1, 128)
    total = sum_groups(jnp.sum(exchange(sums, ("x",) + SEQ), axis=0)).reshape(-1)
    frames_grad, total, other = after(frames_grad, total, other)
    g_shrink, g_expand = full_hidden(other)
    if out_got is not None:
        total, out_got = after(total, out_got)
        out_sum = sum_groups(out_got.astype(F32)).astype(BF16)
        g_outward = by_half(x, out_sum, hop(out_sum, "x"), 1).astype(F32)
    g_small = total[:small_len].reshape(len(small), share)
    g_expand_b = total[small_len:]
    inward_sum = to_rows(inward_sum)
    g_inward = [v.reshape(ny, 2, 1, share, 3, hw) for v in (inward_sum, hop(inward_sum, "x"))]
    g_inward = jnp.transpose(by_half(x, *g_inward, 2), (3, 4, 1, 2, 0, 5)).reshape(share, -1).astype(F32)

    return (
        layer_output,
        frames_grad.astype(F32),
        g_small[0],
        g_small[1],
        g_inward,
        g_small[2],
        g_small[3],
        g_outward,
        g_small[4],
        g_small[5],
        g_small[6],
        g_expand,
        g_expand_b,
        g_shrink,
        g_small[7],
    )


def solution(mesh):
    batch, seq = mesh.shape["batch"], mesh.shape["seq"]
    groups, ny = batch // 2, seq // (2 * NZ)
    fine = Mesh(mesh.devices.reshape(groups, 2, NZ, ny, 2), ("g", "x", "z", "y", "c"))
    b, s = ("g", "x"), ("z", "y", "c")
    in_specs = (
        P(s, b, None),
        P(s, b, None),
        P(b, None),
        P(b, None),
        P(s),
        P(s),
        P(s, None),
        P(s),
        P(s),
        P(s, None),
        P(s),
        P(s),
        P(s),
        P(s, None),
        P(s),
        P(s, None),
        P(s),
    )
    out_specs = (
        P(s, b, None),
        P(s, b, None),
        P(s),
        P(s),
        P(s, None),
        P(s),
        P(s),
        P(s, None),
        P(s),
        P(s),
        P(s),
        P(s, None),
        P(s),
        P(s, None),
        P(s),
    )
    return jax.shard_map(
        functools.partial(on_device, groups, ny), mesh=fine, in_specs=in_specs, out_specs=out_specs, check_vma=False
    )
```

```python
import functools
import math

import jax
import jax.numpy as jnp
from jax import lax
from jax.experimental import pallas as pl
from jax.experimental.pallas import tpu as pltpu
from jax.sharding import Mesh, PartitionSpec as P


HEADS = 16
NZ = 4
SMALL_ROWS = 16
NORM_EPS = 1e-05
NEG = -1e30
F32 = jnp.float32
BF16 = jnp.bfloat16
LAYER_OF_ROW = (1, 2, 0, 3)
SWAP = [(0, 1), (1, 0)]
LAYER = ("c", "x", "y")
SEQ = ("z", "y", "c")


def xor_perm(count, k):
    return [(i, i ^ k) for i in range(count)]


def hop(value, axis, count=2, k=1):
    return lax.ppermute(value, axis, xor_perm(count, k))


def pick(value, index, axis=0):
    return lax.dynamic_index_in_dim(value, index, axis, keepdims=False)


def stack_rows(parts):
    return jnp.concatenate(parts, axis=0)


def assemble_body(pieces, size, place_ref, *refs):
    out_ref = refs[pieces]
    for r in range(pieces):
        spot = place_ref[0] ^ r
        out_ref[pl.ds(pl.multiple_of(spot * size, size), size), :] = refs[r][...]


def assemble(parts, me):
    size, width = parts[0].shape
    count = len(parts)
    return pl.pallas_call(
        functools.partial(assemble_body, count, size),
        out_shape=jax.ShapeDtypeStruct((count * size, width), parts[0].dtype),
        in_specs=[pl.BlockSpec(memory_space=pltpu.SMEM)] + whole(count),
        out_specs=whole(1)[0],
        compiler_params=pltpu.CompilerParams(vmem_limit_bytes=4 << 20),
        cost_estimate=pl.CostEstimate(flops=0, bytes_accessed=4 * count * size * width, transcendentals=0),
        name="assemble",
    )(me, *parts)


def assemble_pair_body(pieces, size, place_ref, *refs):
    left_ref, right_ref = refs[pieces:]
    width = left_ref.shape[1]
    for r in range(pieces):
        rows = pl.ds(pl.multiple_of((place_ref[0] ^ r) * size, size), size)
        left_ref[rows, :] = refs[r][:, 0:width]
        right_ref[rows, :] = refs[r][:, width : 2 * width]


def assemble_pair(parts, me):
    size, width = parts[0].shape
    count = len(parts)
    return pl.pallas_call(
        functools.partial(assemble_pair_body, count, size),
        out_shape=[jax.ShapeDtypeStruct((count * size, width // 2), parts[0].dtype)] * 2,
        in_specs=[pl.BlockSpec(memory_space=pltpu.SMEM)] + whole(count),
        out_specs=whole(2),
        compiler_params=pltpu.CompilerParams(vmem_limit_bytes=4 << 20),
        cost_estimate=pl.CostEstimate(flops=0, bytes_accessed=4 * count * size * width, transcendentals=0),
        name="assemble_pair",
    )(me, *parts)


def near_parts(block, ny):
    return [block] + [lax.ppermute(block, ("x", "y"), xor_perm(2 * ny, r)) for r in range(1, 2 * ny)]


def both_cores(parts, place):
    mine = assemble(parts, place.xy)
    return mine, hop(mine, "c")


def fold_body(count, size, place_ref, keep_ref, got_ref, own_ref, *out_refs):
    for r in range(count):
        spot = place_ref[0] ^ r
        here = pl.ds(pl.multiple_of(spot * size, size), size)
        value = keep_ref[here, :].astype(F32) + got_ref[here, :].astype(F32)
        if r == 0:
            own_ref[...] = value
        else:
            out_refs[r - 1][...] = value.astype(BF16)


def fold(keep, got, place, ny):
    rows, width = keep.shape
    count = 2 * ny
    size = rows // count
    return pl.pallas_call(
        functools.partial(fold_body, count, size),
        out_shape=[jax.ShapeDtypeStruct((size, width), F32)] + [jax.ShapeDtypeStruct((size, width), BF16)] * (count - 1),
        in_specs=[pl.BlockSpec(memory_space=pltpu.SMEM)] + whole(2),
        out_specs=whole(count),
        compiler_params=pltpu.CompilerParams(vmem_limit_bytes=4 << 20),
        cost_estimate=pl.CostEstimate(flops=count * size * width, bytes_accessed=6 * count * size * width, transcendentals=0),
        name="fold",
    )(place.xy, keep, got)


def finish(parts, ny):
    own = parts[0]
    for r in range(1, 2 * ny):
        own = own + lax.ppermute(parts[r], ("x", "y"), xor_perm(2 * ny, r)).astype(F32)
    return own


def fold_columns(value, units):
    return stack_rows([value[:, i : i + units] for i in range(0, value.shape[1], units)])


def unfold_columns(value, count):
    size = value.shape[0] // count
    return jnp.concatenate([value[i * size : (i + 1) * size] for i in range(count)], axis=1)


def collect_inward_body(share, place_ref, *refs):
    weight_ref, small_ref = refs[NZ:]
    deep = share + SMALL_ROWS
    lines = refs[0].shape[0] // deep
    for r in range(NZ):
        base = (place_ref[0] ^ r) * lines
        for i in range(lines):
            start = i * deep
            rows = pl.ds(pl.multiple_of((base + i) * share, share), share)
            weight_ref[rows, :] = refs[r][start : start + share, :]
            rows = pl.ds(pl.multiple_of((base + i) * SMALL_ROWS, SMALL_ROWS), SMALL_ROWS)
            small_ref[rows, :] = refs[r][start + share : start + deep, :]


def collect_inward(parts, place, share):
    rows, width = parts[0].shape
    lines = NZ * rows // (share + SMALL_ROWS)
    return pl.pallas_call(
        functools.partial(collect_inward_body, share),
        out_shape=[jax.ShapeDtypeStruct((lines * n, width), BF16) for n in (share, SMALL_ROWS)],
        in_specs=[pl.BlockSpec(memory_space=pltpu.SMEM)] + whole(NZ),
        out_specs=whole(2),
        compiler_params=pltpu.CompilerParams(vmem_limit_bytes=4 << 20),
        cost_estimate=pl.CostEstimate(flops=0, bytes_accessed=16 * rows * width, transcendentals=0),
        name="collect_inward",
    )(place.layer, *parts)


def collect_hidden_body(parts_ref, expand_ref, shrink_ref):
    quarter = expand_ref.shape[0] // NZ
    part, units = shrink_ref.shape[0] // NZ, expand_ref.shape[1]
    for r in range(NZ):
        expand_ref[r * quarter : (r + 1) * quarter, :] = parts_ref[r, 0:quarter, :]
        for i in range(shrink_ref.shape[1] // units):
            start = quarter + i * part
            here = slice(r * part, (r + 1) * part)
            shrink_ref[here, i * units : (i + 1) * units] = parts_ref[r, start : start + part, :]


def collect_hidden(parts, width):
    units = parts.shape[2]
    return pl.pallas_call(
        collect_hidden_body,
        out_shape=[jax.ShapeDtypeStruct((width, units), BF16), jax.ShapeDtypeStruct((units, width), BF16)],
        in_specs=whole(1),
        out_specs=whole(2),
        compiler_params=pltpu.CompilerParams(vmem_limit_bytes=4 << 20),
        cost_estimate=pl.CostEstimate(flops=0, bytes_accessed=4 * parts.size, transcendentals=0),
        name="collect_hidden",
    )(parts)


def rehome_flat(x, z, c):
    return (x * NZ + z) * 2 + c


def rehome_perm(k):
    return [
        (rehome_flat(x, z, c), rehome_flat(z >> 1, LAYER_OF_ROW[2 * x + (c ^ k)], z & 1))
        for x in range(2)
        for z in range(NZ)
        for c in range(2)
    ]


def to_home(block, place):
    got = [
        lax.ppermute(jnp.where(place.c == k, block[:, 0], block[:, 1]), ("x", "z", "c"), rehome_perm(k))
        for k in range(2)
    ]
    first = place.z < 2
    return stack_rows([jnp.where(first, got[0], got[1]), jnp.where(first, got[1], got[0])])


def to_origin(block, place):
    half = block.shape[0] // 2
    first = place.z < 2
    low, high = block[:half], block[half:]
    sent = [jnp.where(first, low, high), jnp.where(first, high, low)]
    got = [
        lax.ppermute(sent[k], ("x", "z", "c"), [(b, a) for a, b in rehome_perm(k)]) for k in range(2)
    ]
    return jnp.stack(
        [jnp.where(place.c == 0, got[0], got[1]), jnp.where(place.c == 0, got[1], got[0])], axis=1
    )


def after(first, *values):
    return lax.optimization_barrier((first, *values))


def sum_sources(value, count):
    return jnp.sum(value.reshape((count, -1) + value.shape[1:]).astype(F32), axis=0)


def by_half(x, mine, other, axis):
    return jnp.concatenate([jnp.where(x == 0, mine, other), jnp.where(x == 0, other, mine)], axis=axis)


def sin_cos(position, width):
    feature = jnp.arange(width, dtype=jnp.int32)
    rates = jnp.exp((feature // 2).astype(F32) * (-2.0 * math.log(10000.0) / width))
    angle = position.astype(F32)[:, None] * rates[None, :]
    turn = jnp.round(angle * (2.0 / math.pi))
    rest = angle - turn * 1.5703125
    rest = rest - turn * 0.00048375129699707031
    rest = rest - turn * 7.5497899548918861e-08
    quadrant = turn.astype(jnp.int32) + (feature % 2)[None, :]
    square = rest * rest
    sine = rest + rest * square * (
        -0.16666666641626524 + square * (0.008333329385889463 + square * (-0.00019839334836096632 + square * 2.718311493989822e-06))
    )
    cosine = 1.0 + square * (
        -0.49999999725103100 + square * (0.04166662332373906 + square * (-0.001388676377460993 + square * 2.439044879627741e-05))
    )
    value = jnp.where((quadrant & 1) == 0, sine, cosine)
    return jnp.where((quadrant & 2) == 0, value, -value)


def normalize(values):
    center = values - jnp.mean(values, axis=-1, keepdims=True)
    scale = lax.rsqrt(jnp.mean(center * center, axis=-1, keepdims=True) + NORM_EPS)
    return center * scale, scale


def normalize_back(normal, scale, gain, upstream):
    scaled = upstream * gain
    inner = scaled - jnp.mean(scaled, axis=-1, keepdims=True)
    inner = inner - normal * jnp.mean(scaled * normal, axis=-1, keepdims=True)
    return inner * scale, jnp.sum(upstream * normal, axis=0), jnp.sum(upstream, axis=0)


def dot_nt(a, b):
    return lax.dot_general(a, b, (((1,), (1,)), ((), ())), preferred_element_type=F32)


def dot_tn(a, b):
    return lax.dot_general(a, b, (((0,), (0,)), ((), ())), preferred_element_type=F32)


def dot_nn(a, b):
    return jnp.dot(a, b, preferred_element_type=F32)


BLOCK = 256


def chunk_owner(chunk, ny):
    outer, y = divmod(chunk, ny)
    return ((outer & 1) * 2 + (outer >> 1)) * ny + y


def lane_parts(heads, width):
    if heads == 1:
        return [None]
    lane = lax.broadcasted_iota(jnp.int32, (1, width), 1)
    return [(lane >= h * (width // heads)) & (lane < (h + 1) * (width // heads)) for h in range(heads)]


def only(value, lanes):
    return value if lanes is None else jnp.where(lanes, value, jnp.zeros_like(value))


def allowed_pairs(start_ref, first, total):
    key = lax.broadcasted_iota(jnp.int32, (total, BLOCK), 0)
    frame = first + lax.broadcasted_iota(jnp.int32, (total, BLOCK), 1)
    return (key >= start_ref[:, first : first + BLOCK]) & (key <= frame)


def chunk_rows(chunk, ny, size, core):
    half, spot = divmod(chunk_owner(chunk, ny), 2 * ny)
    return pl.ds(pl.multiple_of(((half ^ core) * (2 * ny) + spot) * size, size), size)


def attend(
    heads,
    ny,
    size,
    core_ref,
    mine_ref,
    other_ref,
    encoding_ref,
    affine_ref,
    weight_ref,
    bias_ref,
    start_ref,
    first_ref,
    qkv_ref,
    near_ref,
    far_ref,
    log_ref,
    q_s,
    k_s,
    vt_s,
):
    count = 4 * ny
    width = q_s.shape[1]
    core = core_ref[0]
    step = 2 * size
    half = mine_ref.shape[0]
    for base, ref in ((0, mine_ref), (half, other_ref)):
        for start in range(0, half, step):
            rows = slice(base + start, base + start + step)
            normal, _ = normalize(ref[start : start + step, :].astype(F32) + encoding_ref[rows, :])
            value = (normal * affine_ref[0:1, :] + affine_ref[1:2, :]).astype(BF16)
            first_ref[rows, :] = value
            qkv_ref[rows, :] = (dot_nn(value, weight_ref[...]) + bias_ref[...]).astype(BF16)
    for chunk in range(count):
        rows = chunk_rows(chunk, ny, size, core)
        here = slice(chunk * size, (chunk + 1) * size)
        q_s[here, :] = qkv_ref[rows, 0:width] * 0.125
        k_s[here, :] = qkv_ref[rows, width : 2 * width]
        vt_s[:, here] = jnp.transpose(qkv_ref[rows, 2 * width : 3 * width].astype(F32)).astype(BF16)
    lanes = lane_parts(heads, width)
    each = width // heads
    for block in range(count * size // BLOCK):
        first = block * BLOCK
        total = first + BLOCK
        allowed = allowed_pairs(start_ref, first, total)
        q_block = q_s[first:total, :]
        contexts = []
        for h in range(heads):
            scores = dot_nt(k_s[0:total, :], only(q_block, lanes[h]))
            scores = jnp.where(allowed, scores, NEG)
            top = jnp.max(scores, axis=0, keepdims=True)
            weight = jnp.exp(scores - top)
            mass = jnp.sum(weight, axis=0, keepdims=True)
            part = dot_nn(vt_s[h * each : (h + 1) * each, 0:total], weight.astype(BF16))
            contexts.append(part / mass)
            log_ref[h : h + 1, first:total] = top + jnp.log(mass)
        context = contexts[0] if heads == 1 else jnp.concatenate(contexts, axis=0)
        context = jnp.transpose(context).astype(BF16)
        for sub in range(BLOCK // size):
            owner = chunk_owner(block * (BLOCK // size) + sub, ny)
            side, spot = divmod(owner, 2 * ny)
            rows, piece = slice(spot * size, (spot + 1) * size), context[sub * size : (sub + 1) * size]

            @pl.when(core == side)
            def _(rows=rows, piece=piece):
                near_ref[rows, :] = piece

            @pl.when(core != side)
            def _(rows=rows, piece=piece):
                far_ref[rows, :] = piece


def attend_back(
    heads,
    ny,
    size,
    core_ref,
    qkv_ref,
    mine_ref,
    other_ref,
    near_ref,
    far_ref,
    outward_ref,
    weight_ref,
    start_ref,
    log_ref,
    out_ref,
    send_ref,
    keep_ref,
    outward_grad_ref,
    q_s,
    k_s,
    v_s,
    g_s,
    kt_s,
    dq_s,
    dk_s,
    dv_s,
):
    count = 4 * ny
    width = q_s.shape[1]
    core = core_ref[0]
    half = mine_ref.shape[0]
    step = 2 * size
    for base, ref in ((0, mine_ref), (half, other_ref)):
        for start in range(0, half, step):
            rows = slice(start, start + step)
            out_ref[base + start : base + start + step, 0:width] = dot_nt(ref[rows, :], outward_ref[...]).astype(BF16)
    for chunk in range(count):
        rows = chunk_rows(chunk, ny, size, core)
        here = slice(chunk * size, (chunk + 1) * size)
        q_s[here, :] = qkv_ref[rows, 0:width] * 0.125
        key = qkv_ref[rows, width : 2 * width]
        k_s[here, :] = key
        kt_s[:, here] = jnp.transpose(key.astype(F32)).astype(BF16)
        v_s[here, :] = qkv_ref[rows, 2 * width : 3 * width]
        g_s[here, :] = out_ref[rows, 0:width]
    dk_s[...] = jnp.zeros_like(dk_s)
    dv_s[...] = jnp.zeros_like(dv_s)
    lanes = lane_parts(heads, width)
    each = width // heads
    for block in range(count * size // BLOCK):
        first = block * BLOCK
        total = first + BLOCK
        allowed = allowed_pairs(start_ref, first, total)
        q_block, g_block = q_s[first:total, :], g_s[first:total, :]
        queries = []
        for h in range(heads):
            q_one, g_one = only(q_block, lanes[h]), only(g_block, lanes[h])
            scores = dot_nt(k_s[0:total, :], q_one)
            probs = jnp.where(allowed, jnp.exp(scores - log_ref[h : h + 1, first:total]), 0.0)
            prob_grad = dot_nt(v_s[0:total, :], g_one)
            delta = jnp.sum(probs * prob_grad, axis=0, keepdims=True)
            score_grad = (probs * (prob_grad - delta)).astype(BF16)
            dv_s[0:total, :] += dot_nn(probs.astype(BF16), g_one)
            dk_s[0:total, :] += dot_nn(score_grad, q_one)
            queries.append(dot_nn(kt_s[h * each : (h + 1) * each, 0:total], score_grad))
        query_grad = queries[0] if heads == 1 else jnp.concatenate(queries, axis=0)
        dq_s[first:total, :] = jnp.transpose(query_grad) * 0.125
    for chunk in range(count):
        rows = chunk_rows(chunk, ny, size, core)
        here = slice(chunk * size, (chunk + 1) * size)
        out_ref[rows, 0:width] = dq_s[here, :].astype(BF16)
        out_ref[rows, width : 2 * width] = dk_s[here, :].astype(BF16)
        out_ref[rows, 2 * width : 3 * width] = dv_s[here, :].astype(BF16)
    for ref, base in ((send_ref, half), (keep_ref, 0)):
        for start in range(0, half, step):
            rows = slice(base + start, base + start + step)
            ref[start : start + step, :] = dot_nt(out_ref[rows, :], weight_ref[...]).astype(BF16)
    total = dot_tn(near_ref[...], mine_ref[...]) + dot_tn(far_ref[...], other_ref[...])
    outward_grad_ref[...] = total.astype(BF16)


def feed_forward(
    size,
    core_ref,
    mine_ref,
    other_ref,
    up_mine_ref,
    up_other_ref,
    expand_ref,
    shrink_ref,
    bias_ref,
    active_ref,
    grad_ref,
    send_ref,
    keep_ref,
    result_ref,
):
    half = keep_ref.shape[0]
    step = 2 * size
    rate = math.sqrt(2.0 / math.pi)
    core = core_ref[0]
    sides = ((send_ref, other_ref, up_other_ref, half, 1 - core), (keep_ref, mine_ref, up_mine_ref, 0, core))
    for ref, source_ref, up_ref, base, side in sides:
        for start in range(0, half, step):
            rows = slice(start, start + step)
            pair = slice(base + start, base + start + step)
            place = pl.ds(pl.multiple_of(side * half + start, step), step)
            before = dot_nn(source_ref[rows, :], expand_ref[...]) + bias_ref[...]
            upper = dot_nt(up_ref[rows, :], shrink_ref[...])
            square = before * before
            inner = jnp.tanh(rate * (before + 0.044715 * before * square))
            plus = 0.5 * (1.0 + inner)
            active = (before * plus).astype(BF16)
            active_ref[pair, :] = active
            slope = plus + 0.5 * before * (1.0 - inner * inner) * (rate + rate * 3 * 0.044715 * square)
            lower = (upper * slope).astype(BF16)
            grad_ref[pair, :] = lower
            ref[rows, :] = dot_nt(lower, expand_ref[...]).astype(BF16)
            result_ref[place, :] = dot_nn(active, shrink_ref[...]).astype(BF16)


def weight_parts(part, mine_ref, other_ref, up_mine_ref, up_other_ref, active_ref, grad_ref, bias_ref, out_ref):
    half, width = mine_ref.shape
    quarter, all_units = width // NZ, NZ * part
    for r in range(NZ):
        spot, ref = r, out_ref.at[r]
        here = slice(spot * quarter, (spot + 1) * quarter)
        total = dot_tn(mine_ref[:, here], grad_ref[0:half, :]) + dot_tn(other_ref[:, here], grad_ref[half : 2 * half, :])
        ref[0:quarter, :] = total.astype(BF16)
        units = slice(spot * part, (spot + 1) * part)
        total = dot_tn(active_ref[0:half, units], up_mine_ref[...])
        total = (total + dot_tn(active_ref[half : 2 * half, units], up_other_ref[...])).astype(BF16)
        for i in range(width // all_units):
            start = quarter + i * part
            ref[start : start + part, :] = total[:, i * all_units : (i + 1) * all_units]
    bias_ref[...] = jnp.sum(grad_ref[...].astype(F32), axis=0, keepdims=True)


def feed_forward_weights(second, up, active, before_grad):
    frames, units = active.shape
    width, part = up[0].shape[1], units // NZ
    quarter = width // NZ
    if part % 128:
        shrink = dot_tn(active, stack_rows(up)).astype(BF16).reshape(NZ, part, width)
        expand = dot_tn(stack_rows(second), before_grad).astype(BF16).reshape(NZ, quarter, units)
        bias = jnp.sum(before_grad.astype(F32), axis=0, keepdims=True)
        return bias, jnp.stack([stack_rows([expand[k], fold_columns(shrink[k], units)]) for k in range(NZ)])
    return pl.pallas_call(
        functools.partial(weight_parts, part),
        out_shape=(jax.ShapeDtypeStruct((1, units), F32), jax.ShapeDtypeStruct((NZ, 2 * quarter, units), BF16)),
        in_specs=whole(6),
        out_specs=tuple(whole(2)),
        compiler_params=pltpu.CompilerParams(vmem_limit_bytes=16 << 20),
        cost_estimate=pl.CostEstimate(
            flops=4 * frames * width * units, bytes_accessed=8 * frames * width, transcendentals=0
        ),
        name="feed_forward_weights",
    )(*second, *up, active, before_grad)


def whole(count):
    return [pl.BlockSpec(memory_space=pltpu.VMEM)] * count


def attention(core, pair, encoding, affine, w_in, bias, starts, heads, ny, size):
    half, wide = pair[0].shape[0], w_in.shape[1]
    frames, depth, width = 2 * half, pair[0].shape[1], wide // 3
    pairs = frames * frames * heads
    return pl.pallas_call(
        functools.partial(attend, heads, ny, size),
        out_shape=(
            jax.ShapeDtypeStruct((frames, depth), BF16),
            jax.ShapeDtypeStruct((frames, wide), BF16),
            jax.ShapeDtypeStruct((half, width), BF16),
            jax.ShapeDtypeStruct((half, width), BF16),
            jax.ShapeDtypeStruct((heads, frames), F32),
        ),
        in_specs=[pl.BlockSpec(memory_space=pltpu.SMEM)] + whole(7),
        out_specs=tuple(whole(5)),
        scratch_shapes=[
            pltpu.VMEM((frames, width), BF16),
            pltpu.VMEM((frames, width), BF16),
            pltpu.VMEM((width, frames), BF16),
        ],
        compiler_params=pltpu.CompilerParams(vmem_limit_bytes=16 << 20),
        cost_estimate=pl.CostEstimate(
            flops=pairs * 256 + 2 * frames * depth * wide, bytes_accessed=8 * frames * depth, transcendentals=pairs // 2
        ),
        name="attend",
    )(core, *pair, encoding, affine, w_in, bias, starts)


def attention_back(place, qkv, pair, context, w_out, w_in, starts, log_total, heads, ny, size):
    frames, wide = qkv.shape
    width = wide // 3
    depth = pair[0].shape[1]
    pairs = frames * frames * heads
    half = jax.ShapeDtypeStruct(pair[0].shape, BF16)
    return pl.pallas_call(
        functools.partial(attend_back, heads, ny, size),
        out_shape=(
            jax.ShapeDtypeStruct((frames, wide), BF16),
            half,
            half,
            jax.ShapeDtypeStruct((width, depth), BF16),
        ),
        in_specs=[pl.BlockSpec(memory_space=pltpu.SMEM)] + whole(9),
        out_specs=tuple(whole(4)),
        scratch_shapes=[pltpu.VMEM((frames, width), BF16)] * 4
        + [pltpu.VMEM((width, frames), BF16)]
        + [pltpu.VMEM((frames, width), F32)] * 3,
        compiler_params=pltpu.CompilerParams(vmem_limit_bytes=20 << 20),
        cost_estimate=pl.CostEstimate(
            flops=pairs * 640 + 2 * frames * depth * (wide + 2 * width),
            bytes_accessed=8 * frames * depth,
            transcendentals=pairs // 2,
        ),
        name="attend_back",
    )(place.core, qkv, *pair, *context, w_out, w_in, starts, log_total)


def feed_forward_front(core, pair, up_pair, w_expand, w_shrink, bias, size):
    frames, width = 2 * pair[0].shape[0], pair[0].shape[1]
    units = w_expand.shape[1]
    half = jax.ShapeDtypeStruct((frames // 2, width), BF16)
    inner = jax.ShapeDtypeStruct((frames, units), BF16)
    return pl.pallas_call(
        functools.partial(feed_forward, size),
        out_shape=(inner, inner, half, half, jax.ShapeDtypeStruct((frames, width), BF16)),
        in_specs=[pl.BlockSpec(memory_space=pltpu.SMEM)] + whole(7),
        out_specs=tuple(whole(5)),
        compiler_params=pltpu.CompilerParams(vmem_limit_bytes=16 << 20),
        cost_estimate=pl.CostEstimate(
            flops=8 * frames * width * units, bytes_accessed=10 * frames * width, transcendentals=frames * units
        ),
        name="feed_forward",
    )(core, *pair, *up_pair, w_expand, w_shrink, bias)


class Place:
    def __init__(self, ny):
        self.x, self.z, self.y, self.c = (lax.axis_index(a) for a in ("x", "z", "y", "c"))
        self.xy = jnp.reshape(self.x * ny + self.y, (1,)).astype(jnp.int32)
        self.core = jnp.reshape(self.c, (1,)).astype(jnp.int32)
        self.layer = jnp.reshape(self.z, (1,)).astype(jnp.int32)


def on_device(
    groups,
    ny,
    frames,
    cotangent,
    segment_lengths,
    position_offsets,
    first_gain,
    first_shift,
    inward_weight,
    query_bias,
    value_bias,
    outward_weight,
    outward_bias,
    second_gain,
    second_shift,
    expand_weight,
    expand_bias,
    shrink_weight,
    shrink_bias,
):
    place = Place(ny)
    x, z, y, c = place.x, place.z, place.y, place.c
    local_len, rows, width = frames.shape
    share = inward_weight.shape[0]
    layer = 4 * ny
    spread = NZ * ny * 2
    full_len = local_len * spread
    size = 2 * local_len
    hd = HEADS // layer
    hw = hd * (width // HEADS)
    hidden = expand_bias.shape[0]
    part = hidden // 2
    me = (c * 2 + x) * ny + y

    def sum_groups(value):
        return lax.psum(value, "g") if groups > 1 else value

    def exchange(value, axes):
        return lax.all_to_all(value, axes, 0, 0, tiled=True)

    both = to_home(jnp.concatenate([frames, cotangent], axis=2), place)
    table = jnp.stack([segment_lengths, position_offsets], axis=1)
    other_table = hop(table, "x")
    other_table, later_inward = after(other_table, inward_weight)

    small = [first_gain, first_shift, query_bias, value_bias, outward_bias, second_gain, second_shift, shrink_bias]
    kinds = len(small) + hidden // share
    units = NZ * part
    packed = jnp.concatenate([v[None] for v in small] + [expand_bias.reshape(-1, share)], axis=0)
    packed = packed.reshape(-1, 3 * hw)
    extra = packed.shape[0]
    packed = jnp.pad(packed, ((0, SMALL_ROWS - extra), (0, units)))[None]
    in_cols = jnp.transpose(later_inward.reshape(share, 3, 2, 2, ny, hw), (3, 4, 2, 0, 1, 5))
    in_cols = pick(in_cols, x).reshape(ny * 2, share, 3 * hw)
    ex_cols = pick(expand_weight.reshape(share, NZ, ny, 2, 2, part), x, 4)
    ex_cols = jnp.transpose(ex_cols, (2, 3, 0, 1, 4)).reshape(ny * 2, share, units)
    columns = jnp.concatenate([in_cols, ex_cols], axis=2)
    columns = jnp.concatenate([columns, jnp.broadcast_to(packed, (ny * 2,) + packed.shape[1:])], axis=1)
    columns = exchange(columns, ("y", "c"))

    row_x = jnp.where((z == 0) | (z == 3), 1, 0)
    table = pick(jnp.where(x == row_x, table, other_table), z >> 1)
    lengths, offsets = table[0], table[1]
    count = lengths.shape[0]
    starts = jnp.sum(
        jnp.where(jnp.arange(count)[None, :] < jnp.arange(count)[:, None], lengths[None, :], 0), axis=1
    )
    frame_ids = jnp.arange(full_len, dtype=jnp.int32)
    row_starts = jnp.max(jnp.where(starts[:, None] <= frame_ids[None, :], starts[:, None], 0), axis=0)[None, :]
    spot = jnp.arange(2 * ny)
    chunk = jnp.concatenate([(2 * (spot // ny) + i) * ny + spot % ny for i in (c, 1 - c)])
    mine = (chunk[:, None] * size + jnp.arange(size, dtype=jnp.int32)).reshape(-1)
    inside = (mine[:, None] >= starts[None, :]) & (mine[:, None] < (starts + lengths)[None, :])
    position = jnp.sum(jnp.where(inside, offsets[None, :] + mine[:, None] - starts[None, :], 0), axis=1)
    encoding = sin_cos(position, width)

    both, later_outward, columns = after(both, outward_weight, columns)
    fr, ct = both[:, :width], both[:, width:]
    outward = lax.all_gather(later_outward, SEQ, axis=0, tiled=True)
    in_part = columns[:, :, : 3 * hw].reshape(-1, 3 * hw)
    in_parts = [in_part] + [hop(in_part, "z", NZ, k) for k in range(1, NZ)]
    sh_rows = lax.dynamic_slice_in_dim(shrink_weight, x * part, part, 0)
    ff_part = stack_rows([columns[:, :share, 3 * hw :].reshape(-1, units), fold_columns(sh_rows, units)])
    mine, up_mine = assemble_pair(near_parts(both, ny), place.xy)
    ff_part = jnp.broadcast_to(ff_part[None], (NZ,) + ff_part.shape)
    mine, encoding, ff_part, *in_parts = after(mine, encoding, ff_part, *in_parts)
    first_pair = [mine, hop(mine, "c")]
    w_in, small_rows = collect_inward(in_parts, place, share)
    ff_got = exchange(ff_part, ("z",))

    vectors = small_rows.reshape(spread, SMALL_ROWS, 3 * hw)[:, :extra].reshape(spread, kinds, share).astype(F32)
    expand_b = vectors[:, len(small) :].reshape(NZ, ny, 2, 2, part)
    expand_b = pick(pick(pick(expand_b, y, 1), c, 1), x, 1).reshape(1, NZ * part)
    vectors = jnp.swapaxes(vectors[:, : len(small)], 0, 1).reshape(len(small), width)
    gain_one, shift_one, query_b, value_b, outward_b, gain_two, shift_two, shrink_b = (
        vectors[i : i + 1] for i in range(len(small))
    )
    qkv_bias = jnp.concatenate(
        [
            lax.dynamic_slice_in_dim(query_b, me * hw, hw, 1),
            jnp.zeros((1, hw), F32),
            lax.dynamic_slice_in_dim(value_b, me * hw, hw, 1),
        ],
        axis=1,
    )

    first_all, qkv, *context_pair, log_total = attention(
        place.core, first_pair, encoding, vectors[:2], w_in, qkv_bias, row_starts, hd, ny, size
    )
    *context_pair, up_mine = after(*context_pair, up_mine)
    if ny == 2:
        context = by_half(c, context_pair[0][None], hop(context_pair[1], "c")[None], 0)
        context = context.reshape(2, 2, ny, size, hw)
        context = by_half(x, pick(context, x, 1)[:, None], hop(pick(context, 1 - x, 1), "x")[:, None], 1)
        context = by_half(y, pick(context, y, 2)[:, :, None], hop(pick(context, 1 - y, 2), "y")[:, :, None], 2)
    else:
        context = exchange(by_half(c, *context_pair, 0).reshape(layer, size, hw), LAYER)
    context = context.reshape(layer, size, hw)
    up_pair = [up_mine, hop(up_mine, "c")]

    inputs = fr.astype(F32) + lax.dynamic_slice_in_dim(encoding, (x * ny + y) * size, size, 0)
    normal_one, scale_one = normalize(inputs)
    context = jnp.swapaxes(context, 0, 1).reshape(size, width)
    middle = inputs + dot_nn(context, outward) + outward_b

    normal_two, scale_two = normalize(middle)
    second = (normal_two * gain_two + shift_two).astype(BF16)
    ff_got, *second_near = after(ff_got, *near_parts(second, ny))
    second_pair = both_cores(second_near, place)
    w_expand, w_shrink = collect_hidden(ff_got, width)
    active, before_grad, send, keep, out_part = feed_forward_front(
        place.core, second_pair, up_pair, w_expand, w_shrink, expand_b, size
    )
    second_parts = list(fold(keep, hop(send, "c"), place, ny))
    second_parts[0], active, before_grad = after(second_parts[0], active, before_grad)
    second_grad = finish(second_parts, ny)
    expand_b_sum, hidden_part = feed_forward_weights(second_pair, up_pair, active, before_grad)
    out_part = lax.psum_scatter(out_part, LAYER, scatter_dimension=0, tiled=True)
    second_grad, expand_b_sum = after(second_grad, expand_b_sum)
    hidden_got = exchange(hidden_part, ("z",))

    upstream = ct.astype(F32)
    middle_part, gain_two_sum, shift_two_sum = normalize_back(normal_two, scale_two, gain_two, second_grad)
    middle_grad = upstream + middle_part
    low_middle = middle_grad.astype(BF16)
    low_pair = both_cores(near_parts(low_middle, ny), place)
    w_out = lax.dynamic_slice_in_dim(outward, me * hw, hw, 0)
    mixed_grad, send, keep, outward_part = attention_back(
        place, qkv, low_pair, context_pair, w_out, w_in, row_starts, log_total, hd, ny, size
    )
    got = hop(send, "c")
    cut = outward_part.reshape(2, -1, width)
    far_cut = hop(pick(cut, 1 - c), "c")
    got, far_cut = after(got, far_cut)
    first_parts = list(fold(keep, got, place, ny))
    first_parts[0], mixed_late, far_cut, hidden_got = after(first_parts[0], mixed_grad, far_cut, hidden_got)
    inward_part = dot_tn(first_all, mixed_late).astype(BF16)
    first_grad = finish(first_parts, ny)
    far_cut, out_part = after(far_cut, out_part)
    line_out = by_half(c, pick(cut, c)[None], far_cut[None], 0)
    if hd == 2 and ny == 2:
        line_out = line_out.reshape(2, 1, share, 2, width // 2)
        line_out = by_half(x, pick(line_out, x, 3), hop(pick(line_out, 1 - x, 3), "x"), 1)
    inward_got = exchange(inward_part.reshape(spread, share, 3 * hw), SEQ)
    input_part, gain_one_sum, shift_one_sum = normalize_back(normal_one, scale_one, vectors[:1], first_grad)
    late = (middle_grad + input_part).astype(BF16)
    late, out_part, hidden_got, line_out = after(late, out_part, hidden_got, line_out)
    hidden_sum = sum_sources(hidden_got, NZ)
    frames_grad = to_origin(late, place)
    inward_got, out_part = after(inward_got, out_part)
    layer_output = to_origin((middle + out_part.astype(F32) + shrink_b).astype(BF16), place)

    split = width // 2
    hidden_sum = sum_groups(hidden_sum.reshape(-1, units)).astype(BF16)
    line = hidden_sum[: width // NZ].reshape(ny, 2, share, units)
    if ny == 2:
        line = by_half(c, pick(line, c, 1)[:, None], hop(pick(line, 1 - c, 1), "c")[:, None], 1)
        line = by_half(y, pick(line, y)[None], hop(pick(line, 1 - y), "y")[None], 0)
    else:
        line = exchange(line.reshape(ny * 2, share, units), ("y", "c"))
    mine = stack_rows([line.reshape(-1, units), hidden_sum[width // NZ :]])
    other = hop(mine, "x")

    def full_hidden(other):
        pair = [unfold_columns(v[width // NZ :], width // units) for v in (mine, other)]
        g_shrink = by_half(x, *pair, 0).astype(F32)
        pair = [v[: width // NZ].reshape(ny, 2, 1, share, NZ, part) for v in (mine, other)]
        return g_shrink, jnp.transpose(by_half(x, *pair, 2), (3, 4, 0, 1, 2, 5)).reshape(share, -1).astype(F32)

    if hd == 2 and ny == 2:
        line = line_out
        out_got = lax.psum_scatter(line.reshape(NZ * share, split), "z", scatter_dimension=0, tiled=True)
        inward_late, out_got = after(inward_got, out_got)
        out_sum = sum_groups(out_got.astype(F32)).astype(BF16)
        g_outward = by_half(x, out_sum, hop(out_sum, "x"), 1).astype(F32)
    else:
        cut = lax.dynamic_update_slice(jnp.zeros((width, width), BF16), outward_part, (me * hw, 0))
        g_outward = lax.psum_scatter(cut, SEQ, scatter_dimension=0, tiled=True)
        g_outward = lax.psum(g_outward.astype(F32), ("g", "x"))

    mixed_sum = jnp.sum(mixed_grad.astype(F32), axis=0)

    def from_heads(value):
        return lax.dynamic_update_slice(jnp.zeros((width,), F32), value, (me * hw,))

    flat = lax.optimization_barrier(jnp.stack(
        [
            gain_one_sum,
            shift_one_sum,
            from_heads(mixed_sum[:hw]),
            from_heads(mixed_sum[2 * hw :]),
            jnp.sum(low_middle.astype(F32), axis=0),
            gain_two_sum,
            shift_two_sum,
            jnp.sum(upstream, axis=0),
        ]
    ))
    small_len = len(small) * share
    sums = jnp.swapaxes(flat.reshape(len(small), spread, share), 0, 1).reshape(spread, small_len)
    spot = jnp.zeros((NZ, ny, 2, 2, part), F32)
    spot = lax.dynamic_update_slice(spot, expand_b_sum.reshape(NZ, 1, 1, 1, part), (0, y, c, x, 0))
    sums = jnp.concatenate([sums, spot.reshape(spread, hidden)], axis=1)
    inward_got, sums = after(inward_got, sums)
    sums = jnp.broadcast_to(sums[None], (2,) + sums.shape).reshape(2 * spread, -1, 128)
    total = sum_groups(jnp.sum(exchange(sums, ("x",) + SEQ), axis=0)).reshape(-1)
    frames_grad, total, other = after(frames_grad, total, other)
    g_shrink, g_expand = full_hidden(other)
    g_small = total[:small_len].reshape(len(small), share)
    g_expand_b = total[small_len:]
    inward_got = inward_late if hd == 2 and ny == 2 else inward_got
    inward_sum = sum_groups(sum_sources(inward_got, NZ)).astype(BF16)
    g_inward = [v.reshape(ny, 2, 1, share, 3, hw) for v in (inward_sum, hop(inward_sum, "x"))]
    g_inward = jnp.transpose(by_half(x, *g_inward, 2), (3, 4, 1, 2, 0, 5)).reshape(share, -1).astype(F32)

    return (
        layer_output,
        frames_grad.astype(F32),
        g_small[0],
        g_small[1],
        g_inward,
        g_small[2],
        g_small[3],
        g_outward,
        g_small[4],
        g_small[5],
        g_small[6],
        g_expand,
        g_expand_b,
        g_shrink,
        g_small[7],
    )


def solution(mesh):
    batch, seq = mesh.shape["batch"], mesh.shape["seq"]
    groups, ny = batch // 2, seq // (2 * NZ)
    fine = Mesh(mesh.devices.reshape(groups, 2, NZ, ny, 2), ("g", "x", "z", "y", "c"))
    b, s = ("g", "x"), ("z", "y", "c")
    in_specs = (
        P(s, b, None),
        P(s, b, None),
        P(b, None),
        P(b, None),
        P(s),
        P(s),
        P(s, None),
        P(s),
        P(s),
        P(s, None),
        P(s),
        P(s),
        P(s),
        P(s, None),
        P(s),
        P(s, None),
        P(s),
    )
    out_specs = (
        P(s, b, None),
        P(s, b, None),
        P(s),
        P(s),
        P(s, None),
        P(s),
        P(s),
        P(s, None),
        P(s),
        P(s),
        P(s),
        P(s, None),
        P(s),
        P(s, None),
        P(s),
    )
    return jax.shard_map(
        functools.partial(on_device, groups, ny), mesh=fine, in_specs=in_specs, out_specs=out_specs, check_vma=False
    )
```

```python
import functools
import math

import jax
import jax.numpy as jnp
from jax import lax
from jax.experimental import pallas as pl
from jax.experimental.pallas import tpu as pltpu
from jax.sharding import Mesh, PartitionSpec as P


HEADS = 16
NZ = 4
SMALL_ROWS = 16
NORM_EPS = 1e-05
NEG = -1e30
F32 = jnp.float32
BF16 = jnp.bfloat16
LAYER_OF_ROW = (1, 2, 0, 3)
SWAP = [(0, 1), (1, 0)]
LAYER = ("c", "x", "y")
SEQ = ("z", "y", "c")


def xor_perm(count, k):
    return [(i, i ^ k) for i in range(count)]


def hop(value, axis, count=2, k=1):
    return lax.ppermute(value, axis, xor_perm(count, k))


def pick(value, index, axis=0):
    return lax.dynamic_index_in_dim(value, index, axis, keepdims=False)


def stack_rows(parts):
    return jnp.concatenate(parts, axis=0)


def assemble_body(pieces, size, place_ref, *refs):
    out_ref = refs[pieces]
    for r in range(pieces):
        spot = place_ref[0] ^ r
        out_ref[pl.ds(pl.multiple_of(spot * size, size), size), :] = refs[r][...]


def assemble(parts, me):
    size, width = parts[0].shape
    count = len(parts)
    return pl.pallas_call(
        functools.partial(assemble_body, count, size),
        out_shape=jax.ShapeDtypeStruct((count * size, width), parts[0].dtype),
        in_specs=[pl.BlockSpec(memory_space=pltpu.SMEM)] + whole(count),
        out_specs=whole(1)[0],
        compiler_params=pltpu.CompilerParams(vmem_limit_bytes=4 << 20),
        cost_estimate=pl.CostEstimate(flops=0, bytes_accessed=4 * count * size * width, transcendentals=0),
        name="assemble",
    )(me, *parts)


def assemble_pair_body(pieces, size, place_ref, *refs):
    left_ref, right_ref = refs[pieces:]
    width = left_ref.shape[1]
    for r in range(pieces):
        rows = pl.ds(pl.multiple_of((place_ref[0] ^ r) * size, size), size)
        left_ref[rows, :] = refs[r][:, 0:width]
        right_ref[rows, :] = refs[r][:, width : 2 * width]


def assemble_pair(parts, me):
    size, width = parts[0].shape
    count = len(parts)
    return pl.pallas_call(
        functools.partial(assemble_pair_body, count, size),
        out_shape=[jax.ShapeDtypeStruct((count * size, width // 2), parts[0].dtype)] * 2,
        in_specs=[pl.BlockSpec(memory_space=pltpu.SMEM)] + whole(count),
        out_specs=whole(2),
        compiler_params=pltpu.CompilerParams(vmem_limit_bytes=4 << 20),
        cost_estimate=pl.CostEstimate(flops=0, bytes_accessed=4 * count * size * width, transcendentals=0),
        name="assemble_pair",
    )(me, *parts)


def near_parts(block, ny):
    return [block] + [lax.ppermute(block, ("x", "y"), xor_perm(2 * ny, r)) for r in range(1, 2 * ny)]


def both_cores(parts, place):
    mine = assemble(parts, place.xy)
    return mine, hop(mine, "c")


def fold_body(count, size, place_ref, keep_ref, got_ref, own_ref, *out_refs):
    for r in range(count):
        spot = place_ref[0] ^ r
        here = pl.ds(pl.multiple_of(spot * size, size), size)
        value = keep_ref[here, :].astype(F32) + got_ref[here, :].astype(F32)
        if r == 0:
            own_ref[...] = value
        else:
            out_refs[r - 1][...] = value.astype(BF16)


def fold(keep, got, place, ny):
    rows, width = keep.shape
    count = 2 * ny
    size = rows // count
    return pl.pallas_call(
        functools.partial(fold_body, count, size),
        out_shape=[jax.ShapeDtypeStruct((size, width), F32)] + [jax.ShapeDtypeStruct((size, width), BF16)] * (count - 1),
        in_specs=[pl.BlockSpec(memory_space=pltpu.SMEM)] + whole(2),
        out_specs=whole(count),
        compiler_params=pltpu.CompilerParams(vmem_limit_bytes=4 << 20),
        cost_estimate=pl.CostEstimate(flops=count * size * width, bytes_accessed=6 * count * size * width, transcendentals=0),
        name="fold",
    )(place.xy, keep, got)


def finish(parts, ny):
    own = parts[0]
    for r in range(1, 2 * ny):
        own = own + lax.ppermute(parts[r], ("x", "y"), xor_perm(2 * ny, r)).astype(F32)
    return own


def fold_columns(value, units):
    return stack_rows([value[:, i : i + units] for i in range(0, value.shape[1], units)])


def unfold_columns(value, count):
    size = value.shape[0] // count
    return jnp.concatenate([value[i * size : (i + 1) * size] for i in range(count)], axis=1)


def collect_inward_body(share, place_ref, *refs):
    weight_ref, small_ref = refs[NZ:]
    deep = share + SMALL_ROWS
    lines = refs[0].shape[0] // deep
    for r in range(NZ):
        base = (place_ref[0] ^ r) * lines
        for i in range(lines):
            start = i * deep
            rows = pl.ds(pl.multiple_of((base + i) * share, share), share)
            weight_ref[rows, :] = refs[r][start : start + share, :]
            rows = pl.ds(pl.multiple_of((base + i) * SMALL_ROWS, SMALL_ROWS), SMALL_ROWS)
            small_ref[rows, :] = refs[r][start + share : start + deep, :]


def collect_inward(parts, place, share):
    rows, width = parts[0].shape
    lines = NZ * rows // (share + SMALL_ROWS)
    return pl.pallas_call(
        functools.partial(collect_inward_body, share),
        out_shape=[jax.ShapeDtypeStruct((lines * n, width), BF16) for n in (share, SMALL_ROWS)],
        in_specs=[pl.BlockSpec(memory_space=pltpu.SMEM)] + whole(NZ),
        out_specs=whole(2),
        compiler_params=pltpu.CompilerParams(vmem_limit_bytes=4 << 20),
        cost_estimate=pl.CostEstimate(flops=0, bytes_accessed=16 * rows * width, transcendentals=0),
        name="collect_inward",
    )(place.layer, *parts)


def collect_hidden_body(parts_ref, expand_ref, shrink_ref):
    quarter = expand_ref.shape[0] // NZ
    part, units = shrink_ref.shape[0] // NZ, expand_ref.shape[1]
    for r in range(NZ):
        expand_ref[r * quarter : (r + 1) * quarter, :] = parts_ref[r, 0:quarter, :]
        for i in range(shrink_ref.shape[1] // units):
            start = quarter + i * part
            here = slice(r * part, (r + 1) * part)
            shrink_ref[here, i * units : (i + 1) * units] = parts_ref[r, start : start + part, :]


def collect_hidden(parts, width):
    units = parts.shape[2]
    return pl.pallas_call(
        collect_hidden_body,
        out_shape=[jax.ShapeDtypeStruct((width, units), BF16), jax.ShapeDtypeStruct((units, width), BF16)],
        in_specs=whole(1),
        out_specs=whole(2),
        compiler_params=pltpu.CompilerParams(vmem_limit_bytes=4 << 20),
        cost_estimate=pl.CostEstimate(flops=0, bytes_accessed=4 * parts.size, transcendentals=0),
        name="collect_hidden",
    )(parts)


def rehome_flat(x, z, c):
    return (x * NZ + z) * 2 + c


def rehome_perm(k):
    return [
        (rehome_flat(x, z, c), rehome_flat(z >> 1, LAYER_OF_ROW[2 * x + (c ^ k)], z & 1))
        for x in range(2)
        for z in range(NZ)
        for c in range(2)
    ]


def to_home(block, place):
    got = [
        lax.ppermute(jnp.where(place.c == k, block[:, 0], block[:, 1]), ("x", "z", "c"), rehome_perm(k))
        for k in range(2)
    ]
    first = place.z < 2
    return stack_rows([jnp.where(first, got[0], got[1]), jnp.where(first, got[1], got[0])])


def to_origin(block, place):
    half = block.shape[0] // 2
    first = place.z < 2
    low, high = block[:half], block[half:]
    sent = [jnp.where(first, low, high), jnp.where(first, high, low)]
    got = [
        lax.ppermute(sent[k], ("x", "z", "c"), [(b, a) for a, b in rehome_perm(k)]) for k in range(2)
    ]
    return jnp.stack(
        [jnp.where(place.c == 0, got[0], got[1]), jnp.where(place.c == 0, got[1], got[0])], axis=1
    )


def after(first, *values):
    return lax.optimization_barrier((first, *values))


def sum_sources(value, count):
    return jnp.sum(value.reshape((count, -1) + value.shape[1:]).astype(F32), axis=0)


def by_half(x, mine, other, axis):
    return jnp.concatenate([jnp.where(x == 0, mine, other), jnp.where(x == 0, other, mine)], axis=axis)


def sin_cos(position, width):
    feature = jnp.arange(width, dtype=jnp.int32)
    rates = jnp.exp((feature // 2).astype(F32) * (-2.0 * math.log(10000.0) / width))
    angle = position.astype(F32)[:, None] * rates[None, :]
    turn = jnp.round(angle * (2.0 / math.pi))
    rest = angle - turn * 1.5703125
    rest = rest - turn * 0.00048375129699707031
    rest = rest - turn * 7.5497899548918861e-08
    quadrant = turn.astype(jnp.int32) + (feature % 2)[None, :]
    square = rest * rest
    sine = rest + rest * square * (
        -0.16666666641626524 + square * (0.008333329385889463 + square * (-0.00019839334836096632 + square * 2.718311493989822e-06))
    )
    cosine = 1.0 + square * (
        -0.49999999725103100 + square * (0.04166662332373906 + square * (-0.001388676377460993 + square * 2.439044879627741e-05))
    )
    value = jnp.where((quadrant & 1) == 0, sine, cosine)
    return jnp.where((quadrant & 2) == 0, value, -value)


def normalize(values):
    center = values - jnp.mean(values, axis=-1, keepdims=True)
    scale = lax.rsqrt(jnp.mean(center * center, axis=-1, keepdims=True) + NORM_EPS)
    return center * scale, scale


def normalize_back(normal, scale, gain, upstream):
    scaled = upstream * gain
    inner = scaled - jnp.mean(scaled, axis=-1, keepdims=True)
    inner = inner - normal * jnp.mean(scaled * normal, axis=-1, keepdims=True)
    return inner * scale, jnp.sum(upstream * normal, axis=0), jnp.sum(upstream, axis=0)


def dot_nt(a, b):
    return lax.dot_general(a, b, (((1,), (1,)), ((), ())), preferred_element_type=F32)


def dot_tn(a, b):
    return lax.dot_general(a, b, (((0,), (0,)), ((), ())), preferred_element_type=F32)


def dot_nn(a, b):
    return jnp.dot(a, b, preferred_element_type=F32)


BLOCK = 256


def chunk_owner(chunk, ny):
    outer, y = divmod(chunk, ny)
    return ((outer & 1) * 2 + (outer >> 1)) * ny + y


def lane_parts(heads, width):
    if heads == 1:
        return [None]
    lane = lax.broadcasted_iota(jnp.int32, (1, width), 1)
    return [(lane >= h * (width // heads)) & (lane < (h + 1) * (width // heads)) for h in range(heads)]


def only(value, lanes):
    return value if lanes is None else jnp.where(lanes, value, jnp.zeros_like(value))


def allowed_pairs(start_ref, first, total):
    key = lax.broadcasted_iota(jnp.int32, (total, BLOCK), 0)
    frame = first + lax.broadcasted_iota(jnp.int32, (total, BLOCK), 1)
    return (key >= start_ref[:, first : first + BLOCK]) & (key <= frame)


def chunk_rows(chunk, ny, size, core):
    half, spot = divmod(chunk_owner(chunk, ny), 2 * ny)
    return pl.ds(pl.multiple_of(((half ^ core) * (2 * ny) + spot) * size, size), size)


def attend(
    heads,
    ny,
    size,
    core_ref,
    mine_ref,
    other_ref,
    encoding_ref,
    affine_ref,
    weight_ref,
    bias_ref,
    start_ref,
    first_ref,
    qkv_ref,
    near_ref,
    far_ref,
    log_ref,
    q_s,
    k_s,
    vt_s,
):
    count = 4 * ny
    width = q_s.shape[1]
    core = core_ref[0]
    step = 2 * size
    half = mine_ref.shape[0]
    for base, ref in ((0, mine_ref), (half, other_ref)):
        for start in range(0, half, step):
            rows = slice(base + start, base + start + step)
            normal, _ = normalize(ref[start : start + step, :].astype(F32) + encoding_ref[rows, :])
            value = (normal * affine_ref[0:1, :] + affine_ref[1:2, :]).astype(BF16)
            first_ref[rows, :] = value
            qkv_ref[rows, :] = (dot_nn(value, weight_ref[...]) + bias_ref[...]).astype(BF16)
    for chunk in range(count):
        rows = chunk_rows(chunk, ny, size, core)
        here = slice(chunk * size, (chunk + 1) * size)
        q_s[here, :] = qkv_ref[rows, 0:width] * 0.125
        k_s[here, :] = qkv_ref[rows, width : 2 * width]
        vt_s[:, here] = jnp.transpose(qkv_ref[rows, 2 * width : 3 * width].astype(F32)).astype(BF16)
    lanes = lane_parts(heads, width)
    each = width // heads
    for block in range(count * size // BLOCK):
        first = block * BLOCK
        total = first + BLOCK
        allowed = allowed_pairs(start_ref, first, total)
        q_block = q_s[first:total, :]
        contexts = []
        for h in range(heads):
            scores = dot_nt(k_s[0:total, :], only(q_block, lanes[h]))
            scores = jnp.where(allowed, scores, NEG)
            top = jnp.max(scores, axis=0, keepdims=True)
            weight = jnp.exp(scores - top)
            mass = jnp.sum(weight, axis=0, keepdims=True)
            part = dot_nn(vt_s[h * each : (h + 1) * each, 0:total], weight.astype(BF16))
            contexts.append(part / mass)
            log_ref[h : h + 1, first:total] = top + jnp.log(mass)
        context = contexts[0] if heads == 1 else jnp.concatenate(contexts, axis=0)
        context = jnp.transpose(context).astype(BF16)
        for sub in range(BLOCK // size):
            owner = chunk_owner(block * (BLOCK // size) + sub, ny)
            side, spot = divmod(owner, 2 * ny)
            rows, piece = slice(spot * size, (spot + 1) * size), context[sub * size : (sub + 1) * size]

            @pl.when(core == side)
            def _(rows=rows, piece=piece):
                near_ref[rows, :] = piece

            @pl.when(core != side)
            def _(rows=rows, piece=piece):
                far_ref[rows, :] = piece


def attend_back(
    heads,
    ny,
    size,
    core_ref,
    qkv_ref,
    mine_ref,
    other_ref,
    near_ref,
    far_ref,
    outward_ref,
    weight_ref,
    start_ref,
    log_ref,
    out_ref,
    send_ref,
    keep_ref,
    outward_grad_ref,
    q_s,
    k_s,
    v_s,
    g_s,
    kt_s,
    dq_s,
    dk_s,
    dv_s,
):
    count = 4 * ny
    width = q_s.shape[1]
    core = core_ref[0]
    half = mine_ref.shape[0]
    step = 2 * size
    for base, ref in ((0, mine_ref), (half, other_ref)):
        for start in range(0, half, step):
            rows = slice(start, start + step)
            out_ref[base + start : base + start + step, 0:width] = dot_nt(ref[rows, :], outward_ref[...]).astype(BF16)
    for chunk in range(count):
        rows = chunk_rows(chunk, ny, size, core)
        here = slice(chunk * size, (chunk + 1) * size)
        q_s[here, :] = qkv_ref[rows, 0:width] * 0.125
        key = qkv_ref[rows, width : 2 * width]
        k_s[here, :] = key
        kt_s[:, here] = jnp.transpose(key.astype(F32)).astype(BF16)
        v_s[here, :] = qkv_ref[rows, 2 * width : 3 * width]
        g_s[here, :] = out_ref[rows, 0:width]
    dk_s[...] = jnp.zeros_like(dk_s)
    dv_s[...] = jnp.zeros_like(dv_s)
    lanes = lane_parts(heads, width)
    each = width // heads
    for block in range(count * size // BLOCK):
        first = block * BLOCK
        total = first + BLOCK
        allowed = allowed_pairs(start_ref, first, total)
        q_block, g_block = q_s[first:total, :], g_s[first:total, :]
        queries = []
        for h in range(heads):
            q_one, g_one = only(q_block, lanes[h]), only(g_block, lanes[h])
            scores = dot_nt(k_s[0:total, :], q_one)
            probs = jnp.where(allowed, jnp.exp(scores - log_ref[h : h + 1, first:total]), 0.0)
            prob_grad = dot_nt(v_s[0:total, :], g_one)
            delta = jnp.sum(probs * prob_grad, axis=0, keepdims=True)
            score_grad = (probs * (prob_grad - delta)).astype(BF16)
            dv_s[0:total, :] += dot_nn(probs.astype(BF16), g_one)
            dk_s[0:total, :] += dot_nn(score_grad, q_one)
            queries.append(dot_nn(kt_s[h * each : (h + 1) * each, 0:total], score_grad))
        query_grad = queries[0] if heads == 1 else jnp.concatenate(queries, axis=0)
        dq_s[first:total, :] = jnp.transpose(query_grad) * 0.125
    for chunk in range(count):
        rows = chunk_rows(chunk, ny, size, core)
        here = slice(chunk * size, (chunk + 1) * size)
        out_ref[rows, 0:width] = dq_s[here, :].astype(BF16)
        out_ref[rows, width : 2 * width] = dk_s[here, :].astype(BF16)
        out_ref[rows, 2 * width : 3 * width] = dv_s[here, :].astype(BF16)
    for ref, base in ((send_ref, half), (keep_ref, 0)):
        for start in range(0, half, step):
            rows = slice(base + start, base + start + step)
            ref[start : start + step, :] = dot_nt(out_ref[rows, :], weight_ref[...]).astype(BF16)
    total = dot_tn(near_ref[...], mine_ref[...]) + dot_tn(far_ref[...], other_ref[...])
    outward_grad_ref[...] = total.astype(BF16)


def feed_forward(
    size,
    core_ref,
    mine_ref,
    other_ref,
    up_mine_ref,
    up_other_ref,
    expand_ref,
    shrink_ref,
    bias_ref,
    active_ref,
    grad_ref,
    send_ref,
    keep_ref,
    result_ref,
):
    half = keep_ref.shape[0]
    step = 2 * size
    rate = math.sqrt(2.0 / math.pi)
    core = core_ref[0]
    sides = ((send_ref, other_ref, up_other_ref, half, 1 - core), (keep_ref, mine_ref, up_mine_ref, 0, core))
    for ref, source_ref, up_ref, base, side in sides:
        for start in range(0, half, step):
            rows = slice(start, start + step)
            pair = slice(base + start, base + start + step)
            place = pl.ds(pl.multiple_of(side * half + start, step), step)
            before = dot_nn(source_ref[rows, :], expand_ref[...]) + bias_ref[...]
            upper = dot_nt(up_ref[rows, :], shrink_ref[...])
            square = before * before
            inner = jnp.tanh(rate * (before + 0.044715 * before * square))
            plus = 0.5 * (1.0 + inner)
            active = (before * plus).astype(BF16)
            active_ref[pair, :] = active
            slope = plus + 0.5 * before * (1.0 - inner * inner) * (rate + rate * 3 * 0.044715 * square)
            lower = (upper * slope).astype(BF16)
            grad_ref[pair, :] = lower
            ref[rows, :] = dot_nt(lower, expand_ref[...]).astype(BF16)
            result_ref[place, :] = dot_nn(active, shrink_ref[...]).astype(BF16)


def weight_parts(part, mine_ref, other_ref, up_mine_ref, up_other_ref, active_ref, grad_ref, bias_ref, out_ref):
    half, width = mine_ref.shape
    quarter, all_units = width // NZ, NZ * part
    for r in range(NZ):
        spot, ref = r, out_ref.at[r]
        here = slice(spot * quarter, (spot + 1) * quarter)
        total = dot_tn(mine_ref[:, here], grad_ref[0:half, :]) + dot_tn(other_ref[:, here], grad_ref[half : 2 * half, :])
        ref[0:quarter, :] = total.astype(BF16)
        units = slice(spot * part, (spot + 1) * part)
        total = dot_tn(active_ref[0:half, units], up_mine_ref[...])
        total = (total + dot_tn(active_ref[half : 2 * half, units], up_other_ref[...])).astype(BF16)
        for i in range(width // all_units):
            start = quarter + i * part
            ref[start : start + part, :] = total[:, i * all_units : (i + 1) * all_units]
    bias_ref[...] = jnp.sum(grad_ref[...].astype(F32), axis=0, keepdims=True)


def feed_forward_weights(second, up, active, before_grad):
    frames, units = active.shape
    width, part = up[0].shape[1], units // NZ
    quarter = width // NZ
    if part % 128:
        shrink = dot_tn(active, stack_rows(up)).astype(BF16).reshape(NZ, part, width)
        expand = dot_tn(stack_rows(second), before_grad).astype(BF16).reshape(NZ, quarter, units)
        bias = jnp.sum(before_grad.astype(F32), axis=0, keepdims=True)
        return bias, jnp.stack([stack_rows([expand[k], fold_columns(shrink[k], units)]) for k in range(NZ)])
    return pl.pallas_call(
        functools.partial(weight_parts, part),
        out_shape=(jax.ShapeDtypeStruct((1, units), F32), jax.ShapeDtypeStruct((NZ, 2 * quarter, units), BF16)),
        in_specs=whole(6),
        out_specs=tuple(whole(2)),
        compiler_params=pltpu.CompilerParams(vmem_limit_bytes=16 << 20),
        cost_estimate=pl.CostEstimate(
            flops=4 * frames * width * units, bytes_accessed=8 * frames * width, transcendentals=0
        ),
        name="feed_forward_weights",
    )(*second, *up, active, before_grad)


def whole(count):
    return [pl.BlockSpec(memory_space=pltpu.VMEM)] * count


def attention(core, pair, encoding, affine, w_in, bias, starts, heads, ny, size):
    half, wide = pair[0].shape[0], w_in.shape[1]
    frames, depth, width = 2 * half, pair[0].shape[1], wide // 3
    pairs = frames * frames * heads
    return pl.pallas_call(
        functools.partial(attend, heads, ny, size),
        out_shape=(
            jax.ShapeDtypeStruct((frames, depth), BF16),
            jax.ShapeDtypeStruct((frames, wide), BF16),
            jax.ShapeDtypeStruct((half, width), BF16),
            jax.ShapeDtypeStruct((half, width), BF16),
            jax.ShapeDtypeStruct((heads, frames), F32),
        ),
        in_specs=[pl.BlockSpec(memory_space=pltpu.SMEM)] + whole(7),
        out_specs=tuple(whole(5)),
        scratch_shapes=[
            pltpu.VMEM((frames, width), BF16),
            pltpu.VMEM((frames, width), BF16),
            pltpu.VMEM((width, frames), BF16),
        ],
        compiler_params=pltpu.CompilerParams(vmem_limit_bytes=16 << 20),
        cost_estimate=pl.CostEstimate(
            flops=pairs * 256 + 2 * frames * depth * wide, bytes_accessed=8 * frames * depth, transcendentals=pairs // 2
        ),
        name="attend",
    )(core, *pair, encoding, affine, w_in, bias, starts)


def attention_back(place, qkv, pair, context, w_out, w_in, starts, log_total, heads, ny, size):
    frames, wide = qkv.shape
    width = wide // 3
    depth = pair[0].shape[1]
    pairs = frames * frames * heads
    half = jax.ShapeDtypeStruct(pair[0].shape, BF16)
    return pl.pallas_call(
        functools.partial(attend_back, heads, ny, size),
        out_shape=(
            jax.ShapeDtypeStruct((frames, wide), BF16),
            half,
            half,
            jax.ShapeDtypeStruct((width, depth), BF16),
        ),
        in_specs=[pl.BlockSpec(memory_space=pltpu.SMEM)] + whole(9),
        out_specs=tuple(whole(4)),
        scratch_shapes=[pltpu.VMEM((frames, width), BF16)] * 4
        + [pltpu.VMEM((width, frames), BF16)]
        + [pltpu.VMEM((frames, width), F32)] * 3,
        compiler_params=pltpu.CompilerParams(vmem_limit_bytes=20 << 20),
        cost_estimate=pl.CostEstimate(
            flops=pairs * 640 + 2 * frames * depth * (wide + 2 * width),
            bytes_accessed=8 * frames * depth,
            transcendentals=pairs // 2,
        ),
        name="attend_back",
    )(place.core, qkv, *pair, *context, w_out, w_in, starts, log_total)


def feed_forward_front(core, pair, up_pair, w_expand, w_shrink, bias, size):
    frames, width = 2 * pair[0].shape[0], pair[0].shape[1]
    units = w_expand.shape[1]
    half = jax.ShapeDtypeStruct((frames // 2, width), BF16)
    inner = jax.ShapeDtypeStruct((frames, units), BF16)
    return pl.pallas_call(
        functools.partial(feed_forward, size),
        out_shape=(inner, inner, half, half, jax.ShapeDtypeStruct((frames, width), BF16)),
        in_specs=[pl.BlockSpec(memory_space=pltpu.SMEM)] + whole(7),
        out_specs=tuple(whole(5)),
        compiler_params=pltpu.CompilerParams(vmem_limit_bytes=16 << 20),
        cost_estimate=pl.CostEstimate(
            flops=8 * frames * width * units, bytes_accessed=10 * frames * width, transcendentals=frames * units
        ),
        name="feed_forward",
    )(core, *pair, *up_pair, w_expand, w_shrink, bias)


class Place:
    def __init__(self, ny):
        self.x, self.z, self.y, self.c = (lax.axis_index(a) for a in ("x", "z", "y", "c"))
        self.xy = jnp.reshape(self.x * ny + self.y, (1,)).astype(jnp.int32)
        self.core = jnp.reshape(self.c, (1,)).astype(jnp.int32)
        self.layer = jnp.reshape(self.z, (1,)).astype(jnp.int32)


def on_device(
    groups,
    ny,
    frames,
    cotangent,
    segment_lengths,
    position_offsets,
    first_gain,
    first_shift,
    inward_weight,
    query_bias,
    value_bias,
    outward_weight,
    outward_bias,
    second_gain,
    second_shift,
    expand_weight,
    expand_bias,
    shrink_weight,
    shrink_bias,
):
    place = Place(ny)
    x, z, y, c = place.x, place.z, place.y, place.c
    local_len, rows, width = frames.shape
    share = inward_weight.shape[0]
    layer = 4 * ny
    spread = NZ * ny * 2
    full_len = local_len * spread
    size = 2 * local_len
    hd = HEADS // layer
    hw = hd * (width // HEADS)
    hidden = expand_bias.shape[0]
    part = hidden // 2
    me = (c * 2 + x) * ny + y

    def sum_groups(value):
        return lax.psum(value, "g") if groups > 1 else value

    def exchange(value, axes):
        return lax.all_to_all(value, axes, 0, 0, tiled=True)

    both = to_home(jnp.concatenate([frames, cotangent], axis=2), place)
    table = jnp.stack([segment_lengths, position_offsets], axis=1)
    other_table = hop(table, "x")
    other_table, later_inward = after(other_table, inward_weight)

    small = [first_gain, first_shift, query_bias, value_bias, outward_bias, second_gain, second_shift, shrink_bias]
    kinds = len(small) + hidden // share
    units = NZ * part
    packed = jnp.concatenate([v[None] for v in small] + [expand_bias.reshape(-1, share)], axis=0)
    packed = packed.reshape(-1, 3 * hw)
    extra = packed.shape[0]
    packed = jnp.pad(packed, ((0, SMALL_ROWS - extra), (0, units)))[None]
    in_cols = jnp.transpose(later_inward.reshape(share, 3, 2, 2, ny, hw), (3, 4, 2, 0, 1, 5))
    in_cols = pick(in_cols, x).reshape(ny * 2, share, 3 * hw)
    ex_cols = pick(expand_weight.reshape(share, NZ, ny, 2, 2, part), x, 4)
    ex_cols = jnp.transpose(ex_cols, (2, 3, 0, 1, 4)).reshape(ny * 2, share, units)
    columns = jnp.concatenate([in_cols, ex_cols], axis=2)
    columns = jnp.concatenate([columns, jnp.broadcast_to(packed, (ny * 2,) + packed.shape[1:])], axis=1)
    columns = exchange(columns, ("y", "c"))

    row_x = jnp.where((z == 0) | (z == 3), 1, 0)
    table = pick(jnp.where(x == row_x, table, other_table), z >> 1)
    lengths, offsets = table[0], table[1]
    count = lengths.shape[0]
    starts = jnp.sum(
        jnp.where(jnp.arange(count)[None, :] < jnp.arange(count)[:, None], lengths[None, :], 0), axis=1
    )
    frame_ids = jnp.arange(full_len, dtype=jnp.int32)
    row_starts = jnp.max(jnp.where(starts[:, None] <= frame_ids[None, :], starts[:, None], 0), axis=0)[None, :]
    spot = jnp.arange(2 * ny)
    chunk = jnp.concatenate([(2 * (spot // ny) + i) * ny + spot % ny for i in (c, 1 - c)])
    mine = (chunk[:, None] * size + jnp.arange(size, dtype=jnp.int32)).reshape(-1)
    inside = (mine[:, None] >= starts[None, :]) & (mine[:, None] < (starts + lengths)[None, :])
    position = jnp.sum(jnp.where(inside, offsets[None, :] + mine[:, None] - starts[None, :], 0), axis=1)
    encoding = sin_cos(position, width)

    both, columns = after(both, columns)
    fr, ct = both[:, :width], both[:, width:]
    outward = lax.all_gather(outward_weight, SEQ, axis=0, tiled=True)
    in_part = columns[:, :, : 3 * hw].reshape(-1, 3 * hw)
    in_parts = [in_part] + [hop(in_part, "z", NZ, k) for k in range(1, NZ)]
    sh_rows = lax.dynamic_slice_in_dim(shrink_weight, x * part, part, 0)
    ff_part = stack_rows([columns[:, :share, 3 * hw :].reshape(-1, units), fold_columns(sh_rows, units)])
    mine, up_mine = assemble_pair(near_parts(both, ny), place.xy)
    ff_part = jnp.broadcast_to(ff_part[None], (NZ,) + ff_part.shape)
    mine, encoding, ff_part, *in_parts = after(mine, encoding, ff_part, *in_parts)
    first_pair = [mine, hop(mine, "c")]
    w_in, small_rows = collect_inward(in_parts, place, share)
    ff_got = exchange(ff_part, ("z",))

    vectors = small_rows.reshape(spread, SMALL_ROWS, 3 * hw)[:, :extra].reshape(spread, kinds, share).astype(F32)
    expand_b = vectors[:, len(small) :].reshape(NZ, ny, 2, 2, part)
    expand_b = pick(pick(pick(expand_b, y, 1), c, 1), x, 1).reshape(1, NZ * part)
    vectors = jnp.swapaxes(vectors[:, : len(small)], 0, 1).reshape(len(small), width)
    gain_one, shift_one, query_b, value_b, outward_b, gain_two, shift_two, shrink_b = (
        vectors[i : i + 1] for i in range(len(small))
    )
    qkv_bias = jnp.concatenate(
        [
            lax.dynamic_slice_in_dim(query_b, me * hw, hw, 1),
            jnp.zeros((1, hw), F32),
            lax.dynamic_slice_in_dim(value_b, me * hw, hw, 1),
        ],
        axis=1,
    )

    first_all, qkv, *context_pair, log_total = attention(
        place.core, first_pair, encoding, vectors[:2], w_in, qkv_bias, row_starts, hd, ny, size
    )
    *context_pair, up_mine = after(*context_pair, up_mine)
    if ny == 2:
        context = by_half(c, context_pair[0][None], hop(context_pair[1], "c")[None], 0)
        context = context.reshape(2, 2, ny, size, hw)
        context = by_half(x, pick(context, x, 1)[:, None], hop(pick(context, 1 - x, 1), "x")[:, None], 1)
        context = by_half(y, pick(context, y, 2)[:, :, None], hop(pick(context, 1 - y, 2), "y")[:, :, None], 2)
    else:
        context = exchange(by_half(c, *context_pair, 0).reshape(layer, size, hw), LAYER)
    context = context.reshape(layer, size, hw)
    up_pair = [up_mine, hop(up_mine, "c")]

    inputs = fr.astype(F32) + lax.dynamic_slice_in_dim(encoding, (x * ny + y) * size, size, 0)
    normal_one, scale_one = normalize(inputs)
    context = jnp.swapaxes(context, 0, 1).reshape(size, width)
    middle = inputs + dot_nn(context, outward) + outward_b

    normal_two, scale_two = normalize(middle)
    second = (normal_two * gain_two + shift_two).astype(BF16)
    ff_got, *second_near = after(ff_got, *near_parts(second, ny))
    second_pair = both_cores(second_near, place)
    w_expand, w_shrink = collect_hidden(ff_got, width)
    active, before_grad, send, keep, out_part = feed_forward_front(
        place.core, second_pair, up_pair, w_expand, w_shrink, expand_b, size
    )
    second_parts = list(fold(keep, hop(send, "c"), place, ny))
    second_parts[0], active, before_grad = after(second_parts[0], active, before_grad)
    second_grad = finish(second_parts, ny)
    expand_b_sum, hidden_part = feed_forward_weights(second_pair, up_pair, active, before_grad)
    out_part = lax.psum_scatter(out_part, LAYER, scatter_dimension=0, tiled=True)
    second_grad, expand_b_sum = after(second_grad, expand_b_sum)
    hidden_got = exchange(hidden_part, ("z",))

    upstream = ct.astype(F32)
    middle_part, gain_two_sum, shift_two_sum = normalize_back(normal_two, scale_two, gain_two, second_grad)
    middle_grad = upstream + middle_part
    low_middle = middle_grad.astype(BF16)
    low_pair = both_cores(near_parts(low_middle, ny), place)
    w_out = lax.dynamic_slice_in_dim(outward, me * hw, hw, 0)
    mixed_grad, send, keep, outward_part = attention_back(
        place, qkv, low_pair, context_pair, w_out, w_in, row_starts, log_total, hd, ny, size
    )
    got = hop(send, "c")
    cut = outward_part.reshape(2, -1, width)
    far_cut = hop(pick(cut, 1 - c), "c")
    got, far_cut = after(got, far_cut)
    first_parts = list(fold(keep, got, place, ny))
    first_parts[0], mixed_late, far_cut, hidden_got = after(first_parts[0], mixed_grad, far_cut, hidden_got)
    inward_part = dot_tn(first_all, mixed_late).astype(BF16)
    first_grad = finish(first_parts, ny)
    far_cut, out_part = after(far_cut, out_part)
    line_out = by_half(c, pick(cut, c)[None], far_cut[None], 0)
    if hd == 2 and ny == 2:
        line_out = line_out.reshape(2, 1, share, 2, width // 2)
        line_out = by_half(x, pick(line_out, x, 3), hop(pick(line_out, 1 - x, 3), "x"), 1)
    inward_got = exchange(inward_part.reshape(spread, share, 3 * hw), SEQ)
    input_part, gain_one_sum, shift_one_sum = normalize_back(normal_one, scale_one, vectors[:1], first_grad)
    late = (middle_grad + input_part).astype(BF16)
    late, out_part, hidden_got, line_out = after(late, out_part, hidden_got, line_out)
    hidden_sum = sum_sources(hidden_got, NZ)
    frames_grad = to_origin(late, place)
    inward_got, out_part = after(inward_got, out_part)
    layer_output = to_origin((middle + out_part.astype(F32) + shrink_b).astype(BF16), place)

    split = width // 2
    hidden_sum = sum_groups(hidden_sum.reshape(-1, units)).astype(BF16)
    line = hidden_sum[: width // NZ].reshape(ny, 2, share, units)
    if ny == 2:
        line = by_half(c, pick(line, c, 1)[:, None], hop(pick(line, 1 - c, 1), "c")[:, None], 1)
        line = by_half(y, pick(line, y)[None], hop(pick(line, 1 - y), "y")[None], 0)
    else:
        line = exchange(line.reshape(ny * 2, share, units), ("y", "c"))
    mine = stack_rows([line.reshape(-1, units), hidden_sum[width // NZ :]])
    other = hop(mine, "x")

    def full_hidden(other):
        pair = [unfold_columns(v[width // NZ :], width // units) for v in (mine, other)]
        g_shrink = by_half(x, *pair, 0).astype(F32)
        pair = [v[: width // NZ].reshape(ny, 2, 1, share, NZ, part) for v in (mine, other)]
        return g_shrink, jnp.transpose(by_half(x, *pair, 2), (3, 4, 0, 1, 2, 5)).reshape(share, -1).astype(F32)

    if hd == 2 and ny == 2:
        line = line_out
        out_got = lax.psum_scatter(line.reshape(NZ * share, split), "z", scatter_dimension=0, tiled=True)
        inward_late, out_got = after(inward_got, out_got)
        out_sum = sum_groups(out_got.astype(F32)).astype(BF16)
        g_outward = by_half(x, out_sum, hop(out_sum, "x"), 1).astype(F32)
    else:
        cut = lax.dynamic_update_slice(jnp.zeros((width, width), BF16), outward_part, (me * hw, 0))
        g_outward = lax.psum_scatter(cut, SEQ, scatter_dimension=0, tiled=True)
        g_outward = lax.psum(g_outward.astype(F32), ("g", "x"))

    mixed_sum = jnp.sum(mixed_grad.astype(F32), axis=0)

    def from_heads(value):
        return lax.dynamic_update_slice(jnp.zeros((width,), F32), value, (me * hw,))

    flat = lax.optimization_barrier(jnp.stack(
        [
            gain_one_sum,
            shift_one_sum,
            from_heads(mixed_sum[:hw]),
            from_heads(mixed_sum[2 * hw :]),
            jnp.sum(low_middle.astype(F32), axis=0),
            gain_two_sum,
            shift_two_sum,
            jnp.sum(upstream, axis=0),
        ]
    ))
    small_len = len(small) * share
    sums = jnp.swapaxes(flat.reshape(len(small), spread, share), 0, 1).reshape(spread, small_len)
    spot = jnp.zeros((NZ, ny, 2, 2, part), F32)
    spot = lax.dynamic_update_slice(spot, expand_b_sum.reshape(NZ, 1, 1, 1, part), (0, y, c, x, 0))
    sums = jnp.concatenate([sums, spot.reshape(spread, hidden)], axis=1)
    inward_got, sums = after(inward_got, sums)
    sums = jnp.broadcast_to(sums[None], (2,) + sums.shape).reshape(2 * spread, -1, 128)
    total = sum_groups(jnp.sum(exchange(sums, ("x",) + SEQ), axis=0)).reshape(-1)
    frames_grad, total, other = after(frames_grad, total, other)
    g_shrink, g_expand = full_hidden(other)
    g_small = total[:small_len].reshape(len(small), share)
    g_expand_b = total[small_len:]
    inward_got = inward_late if hd == 2 and ny == 2 else inward_got
    inward_sum = sum_groups(sum_sources(inward_got, NZ)).astype(BF16)
    g_inward = [v.reshape(ny, 2, 1, share, 3, hw) for v in (inward_sum, hop(inward_sum, "x"))]
    g_inward = jnp.transpose(by_half(x, *g_inward, 2), (3, 4, 1, 2, 0, 5)).reshape(share, -1).astype(F32)

    return (
        layer_output,
        frames_grad.astype(F32),
        g_small[0],
        g_small[1],
        g_inward,
        g_small[2],
        g_small[3],
        g_outward,
        g_small[4],
        g_small[5],
        g_small[6],
        g_expand,
        g_expand_b,
        g_shrink,
        g_small[7],
    )


def solution(mesh):
    batch, seq = mesh.shape["batch"], mesh.shape["seq"]
    groups, ny = batch // 2, seq // (2 * NZ)
    fine = Mesh(mesh.devices.reshape(groups, 2, NZ, ny, 2), ("g", "x", "z", "y", "c"))
    b, s = ("g", "x"), ("z", "y", "c")
    in_specs = (
        P(s, b, None),
        P(s, b, None),
        P(b, None),
        P(b, None),
        P(s),
        P(s),
        P(s, None),
        P(s),
        P(s),
        P(s, None),
        P(s),
        P(s),
        P(s),
        P(s, None),
        P(s),
        P(s, None),
        P(s),
    )
    out_specs = (
        P(s, b, None),
        P(s, b, None),
        P(s),
        P(s),
        P(s, None),
        P(s),
        P(s),
        P(s, None),
        P(s),
        P(s),
        P(s),
        P(s, None),
        P(s),
        P(s, None),
        P(s),
    )
    return jax.shard_map(
        functools.partial(on_device, groups, ny), mesh=fine, in_specs=in_specs, out_specs=out_specs, check_vma=False
    )
```

```python
import functools
import math

import jax
import jax.numpy as jnp
from jax import lax
from jax.experimental import pallas as pl
from jax.experimental.pallas import tpu as pltpu
from jax.sharding import Mesh, PartitionSpec as P


HEADS = 16
NZ = 4
SMALL_ROWS = 16
NORM_EPS = 1e-05
NEG = -1e30
F32 = jnp.float32
BF16 = jnp.bfloat16
LAYER_OF_ROW = (1, 2, 0, 3)
SWAP = [(0, 1), (1, 0)]
LAYER = ("c", "x", "y")
SEQ = ("z", "y", "c")


def xor_perm(count, k):
    return [(i, i ^ k) for i in range(count)]


def hop(value, axis, count=2, k=1):
    return lax.ppermute(value, axis, xor_perm(count, k))


def pick(value, index, axis=0):
    return lax.dynamic_index_in_dim(value, index, axis, keepdims=False)


def stack_rows(parts):
    return jnp.concatenate(parts, axis=0)


def assemble_body(pieces, size, place_ref, *refs):
    out_ref = refs[pieces]
    for r in range(pieces):
        spot = place_ref[0] ^ r
        out_ref[pl.ds(pl.multiple_of(spot * size, size), size), :] = refs[r][...]


def assemble(parts, me):
    size, width = parts[0].shape
    count = len(parts)
    return pl.pallas_call(
        functools.partial(assemble_body, count, size),
        out_shape=jax.ShapeDtypeStruct((count * size, width), parts[0].dtype),
        in_specs=[pl.BlockSpec(memory_space=pltpu.SMEM)] + whole(count),
        out_specs=whole(1)[0],
        compiler_params=pltpu.CompilerParams(vmem_limit_bytes=4 << 20),
        cost_estimate=pl.CostEstimate(flops=0, bytes_accessed=4 * count * size * width, transcendentals=0),
        name="assemble",
    )(me, *parts)


def assemble_pair_body(pieces, size, place_ref, *refs):
    left_ref, right_ref = refs[pieces:]
    width = left_ref.shape[1]
    for r in range(pieces):
        rows = pl.ds(pl.multiple_of((place_ref[0] ^ r) * size, size), size)
        left_ref[rows, :] = refs[r][:, 0:width]
        right_ref[rows, :] = refs[r][:, width : 2 * width]


def assemble_pair(parts, me):
    size, width = parts[0].shape
    count = len(parts)
    return pl.pallas_call(
        functools.partial(assemble_pair_body, count, size),
        out_shape=[jax.ShapeDtypeStruct((count * size, width // 2), parts[0].dtype)] * 2,
        in_specs=[pl.BlockSpec(memory_space=pltpu.SMEM)] + whole(count),
        out_specs=whole(2),
        compiler_params=pltpu.CompilerParams(vmem_limit_bytes=4 << 20),
        cost_estimate=pl.CostEstimate(flops=0, bytes_accessed=4 * count * size * width, transcendentals=0),
        name="assemble_pair",
    )(me, *parts)


def near_parts(block, ny):
    return [block] + [lax.ppermute(block, ("x", "y"), xor_perm(2 * ny, r)) for r in range(1, 2 * ny)]


def both_cores(parts, place):
    mine = assemble(parts, place.xy)
    return mine, hop(mine, "c")


def fold_body(count, size, place_ref, keep_ref, got_ref, own_ref, *out_refs):
    for r in range(count):
        spot = place_ref[0] ^ r
        here = pl.ds(pl.multiple_of(spot * size, size), size)
        value = keep_ref[here, :].astype(F32) + got_ref[here, :].astype(F32)
        if r == 0:
            own_ref[...] = value
        else:
            out_refs[r - 1][...] = value.astype(BF16)


def fold(keep, got, place, ny):
    rows, width = keep.shape
    count = 2 * ny
    size = rows // count
    return pl.pallas_call(
        functools.partial(fold_body, count, size),
        out_shape=[jax.ShapeDtypeStruct((size, width), F32)] + [jax.ShapeDtypeStruct((size, width), BF16)] * (count - 1),
        in_specs=[pl.BlockSpec(memory_space=pltpu.SMEM)] + whole(2),
        out_specs=whole(count),
        compiler_params=pltpu.CompilerParams(vmem_limit_bytes=4 << 20),
        cost_estimate=pl.CostEstimate(flops=count * size * width, bytes_accessed=6 * count * size * width, transcendentals=0),
        name="fold",
    )(place.xy, keep, got)


def finish(parts, ny):
    own = parts[0]
    for r in range(1, 2 * ny):
        own = own + lax.ppermute(parts[r], ("x", "y"), xor_perm(2 * ny, r)).astype(F32)
    return own


def fold_columns(value, units):
    return stack_rows([value[:, i : i + units] for i in range(0, value.shape[1], units)])


def unfold_columns(value, count):
    size = value.shape[0] // count
    return jnp.concatenate([value[i * size : (i + 1) * size] for i in range(count)], axis=1)


def collect_inward_body(place_ref, *refs):
    weight_ref, small_ref = refs[NZ:]
    quarter = weight_ref.shape[0] // NZ
    for r in range(NZ):
        spot = place_ref[0] ^ r
        weight_ref[pl.ds(pl.multiple_of(spot * quarter, quarter), quarter), :] = refs[r][0:quarter, :]
        rows = pl.ds(pl.multiple_of(spot * SMALL_ROWS, SMALL_ROWS), SMALL_ROWS)
        small_ref[rows, :] = refs[r][quarter : quarter + SMALL_ROWS, :]


def collect_inward(parts, place):
    rows, width = parts[0].shape
    return pl.pallas_call(
        collect_inward_body,
        out_shape=[jax.ShapeDtypeStruct((NZ * n, width), BF16) for n in (rows - SMALL_ROWS, SMALL_ROWS)],
        in_specs=[pl.BlockSpec(memory_space=pltpu.SMEM)] + whole(NZ),
        out_specs=whole(2),
        compiler_params=pltpu.CompilerParams(vmem_limit_bytes=4 << 20),
        cost_estimate=pl.CostEstimate(flops=0, bytes_accessed=16 * rows * width, transcendentals=0),
        name="collect_inward",
    )(place.layer, *parts)


def collect_hidden_body(parts_ref, expand_ref, shrink_ref):
    quarter = expand_ref.shape[0] // NZ
    part, units = shrink_ref.shape[0] // NZ, expand_ref.shape[1]
    for r in range(NZ):
        expand_ref[r * quarter : (r + 1) * quarter, :] = parts_ref[r, 0:quarter, :]
        for i in range(shrink_ref.shape[1] // units):
            start = quarter + i * part
            here = slice(r * part, (r + 1) * part)
            shrink_ref[here, i * units : (i + 1) * units] = parts_ref[r, start : start + part, :]


def collect_hidden(parts, width):
    units = parts.shape[2]
    return pl.pallas_call(
        collect_hidden_body,
        out_shape=[jax.ShapeDtypeStruct((width, units), BF16), jax.ShapeDtypeStruct((units, width), BF16)],
        in_specs=whole(1),
        out_specs=whole(2),
        compiler_params=pltpu.CompilerParams(vmem_limit_bytes=4 << 20),
        cost_estimate=pl.CostEstimate(flops=0, bytes_accessed=4 * parts.size, transcendentals=0),
        name="collect_hidden",
    )(parts)


def rehome_flat(x, z, c):
    return (x * NZ + z) * 2 + c


def rehome_perm(k):
    return [
        (rehome_flat(x, z, c), rehome_flat(z >> 1, LAYER_OF_ROW[2 * x + (c ^ k)], z & 1))
        for x in range(2)
        for z in range(NZ)
        for c in range(2)
    ]


def to_home(block, place):
    got = [
        lax.ppermute(jnp.where(place.c == k, block[:, 0], block[:, 1]), ("x", "z", "c"), rehome_perm(k))
        for k in range(2)
    ]
    first = place.z < 2
    return stack_rows([jnp.where(first, got[0], got[1]), jnp.where(first, got[1], got[0])])


def to_origin(block, place):
    half = block.shape[0] // 2
    first = place.z < 2
    low, high = block[:half], block[half:]
    sent = [jnp.where(first, low, high), jnp.where(first, high, low)]
    got = [
        lax.ppermute(sent[k], ("x", "z", "c"), [(b, a) for a, b in rehome_perm(k)]) for k in range(2)
    ]
    return jnp.stack(
        [jnp.where(place.c == 0, got[0], got[1]), jnp.where(place.c == 0, got[1], got[0])], axis=1
    )


def after(first, *values):
    return lax.optimization_barrier((first, *values))


def sum_sources(value, count):
    return jnp.sum(value.reshape((count, -1) + value.shape[1:]).astype(F32), axis=0)


def by_half(x, mine, other, axis):
    return jnp.concatenate([jnp.where(x == 0, mine, other), jnp.where(x == 0, other, mine)], axis=axis)


def sin_cos(position, width):
    feature = jnp.arange(width, dtype=jnp.int32)
    rates = jnp.exp((feature // 2).astype(F32) * (-2.0 * math.log(10000.0) / width))
    angle = position.astype(F32)[:, None] * rates[None, :]
    turn = jnp.round(angle * (2.0 / math.pi))
    rest = angle - turn * 1.5703125
    rest = rest - turn * 0.00048375129699707031
    rest = rest - turn * 7.5497899548918861e-08
    quadrant = turn.astype(jnp.int32) + (feature % 2)[None, :]
    square = rest * rest
    sine = rest + rest * square * (
        -0.16666666641626524 + square * (0.008333329385889463 + square * (-0.00019839334836096632 + square * 2.718311493989822e-06))
    )
    cosine = 1.0 + square * (
        -0.49999999725103100 + square * (0.04166662332373906 + square * (-0.001388676377460993 + square * 2.439044879627741e-05))
    )
    value = jnp.where((quadrant & 1) == 0, sine, cosine)
    return jnp.where((quadrant & 2) == 0, value, -value)


def normalize(values):
    center = values - jnp.mean(values, axis=-1, keepdims=True)
    scale = lax.rsqrt(jnp.mean(center * center, axis=-1, keepdims=True) + NORM_EPS)
    return center * scale, scale


def normalize_back(normal, scale, gain, upstream):
    scaled = upstream * gain
    inner = scaled - jnp.mean(scaled, axis=-1, keepdims=True)
    inner = inner - normal * jnp.mean(scaled * normal, axis=-1, keepdims=True)
    return inner * scale, jnp.sum(upstream * normal, axis=0), jnp.sum(upstream, axis=0)


def dot_nt(a, b):
    return lax.dot_general(a, b, (((1,), (1,)), ((), ())), preferred_element_type=F32)


def dot_tn(a, b):
    return lax.dot_general(a, b, (((0,), (0,)), ((), ())), preferred_element_type=F32)


def dot_nn(a, b):
    return jnp.dot(a, b, preferred_element_type=F32)


BLOCK = 256


def chunk_owner(chunk, ny):
    outer, y = divmod(chunk, ny)
    return ((outer & 1) * 2 + (outer >> 1)) * ny + y


def lane_parts(heads, width):
    if heads == 1:
        return [None]
    lane = lax.broadcasted_iota(jnp.int32, (1, width), 1)
    return [(lane >= h * (width // heads)) & (lane < (h + 1) * (width // heads)) for h in range(heads)]


def only(value, lanes):
    return value if lanes is None else jnp.where(lanes, value, jnp.zeros_like(value))


def allowed_pairs(start_ref, first, total):
    key = lax.broadcasted_iota(jnp.int32, (total, BLOCK), 0)
    frame = first + lax.broadcasted_iota(jnp.int32, (total, BLOCK), 1)
    return (key >= start_ref[:, first : first + BLOCK]) & (key <= frame)


def chunk_rows(chunk, ny, size, core):
    half, spot = divmod(chunk_owner(chunk, ny), 2 * ny)
    return pl.ds(pl.multiple_of(((half ^ core) * (2 * ny) + spot) * size, size), size)


def attend(
    heads,
    ny,
    size,
    core_ref,
    mine_ref,
    other_ref,
    encoding_ref,
    affine_ref,
    weight_ref,
    bias_ref,
    start_ref,
    first_ref,
    qkv_ref,
    near_ref,
    far_ref,
    log_ref,
    q_s,
    k_s,
    vt_s,
):
    count = 4 * ny
    width = q_s.shape[1]
    core = core_ref[0]
    step = 2 * size
    half = mine_ref.shape[0]
    for base, ref in ((0, mine_ref), (half, other_ref)):
        for start in range(0, half, step):
            rows = slice(base + start, base + start + step)
            normal, _ = normalize(ref[start : start + step, :].astype(F32) + encoding_ref[rows, :])
            value = (normal * affine_ref[0:1, :] + affine_ref[1:2, :]).astype(BF16)
            first_ref[rows, :] = value
            qkv_ref[rows, :] = (dot_nn(value, weight_ref[...]) + bias_ref[...]).astype(BF16)
    for chunk in range(count):
        rows = chunk_rows(chunk, ny, size, core)
        here = slice(chunk * size, (chunk + 1) * size)
        q_s[here, :] = qkv_ref[rows, 0:width] * 0.125
        k_s[here, :] = qkv_ref[rows, width : 2 * width]
        vt_s[:, here] = jnp.transpose(qkv_ref[rows, 2 * width : 3 * width].astype(F32)).astype(BF16)
    lanes = lane_parts(heads, width)
    each = width // heads
    for block in range(count * size // BLOCK):
        first = block * BLOCK
        total = first + BLOCK
        allowed = allowed_pairs(start_ref, first, total)
        q_block = q_s[first:total, :]
        contexts = []
        for h in range(heads):
            scores = dot_nt(k_s[0:total, :], only(q_block, lanes[h]))
            scores = jnp.where(allowed, scores, NEG)
            top = jnp.max(scores, axis=0, keepdims=True)
            weight = jnp.exp(scores - top)
            mass = jnp.sum(weight, axis=0, keepdims=True)
            part = dot_nn(vt_s[h * each : (h + 1) * each, 0:total], weight.astype(BF16))
            contexts.append(part / mass)
            log_ref[h : h + 1, first:total] = top + jnp.log(mass)
        context = contexts[0] if heads == 1 else jnp.concatenate(contexts, axis=0)
        context = jnp.transpose(context).astype(BF16)
        for sub in range(BLOCK // size):
            owner = chunk_owner(block * (BLOCK // size) + sub, ny)
            side, spot = divmod(owner, 2 * ny)
            rows, piece = slice(spot * size, (spot + 1) * size), context[sub * size : (sub + 1) * size]

            @pl.when(core == side)
            def _(rows=rows, piece=piece):
                near_ref[rows, :] = piece

            @pl.when(core != side)
            def _(rows=rows, piece=piece):
                far_ref[rows, :] = piece


def attend_back(
    heads,
    ny,
    size,
    core_ref,
    qkv_ref,
    mine_ref,
    other_ref,
    near_ref,
    far_ref,
    outward_ref,
    weight_ref,
    start_ref,
    log_ref,
    out_ref,
    send_ref,
    keep_ref,
    outward_grad_ref,
    q_s,
    k_s,
    v_s,
    g_s,
    kt_s,
    dq_s,
    dk_s,
    dv_s,
):
    count = 4 * ny
    width = q_s.shape[1]
    core = core_ref[0]
    half = mine_ref.shape[0]
    step = 2 * size
    for base, ref in ((0, mine_ref), (half, other_ref)):
        for start in range(0, half, step):
            rows = slice(start, start + step)
            out_ref[base + start : base + start + step, 0:width] = dot_nt(ref[rows, :], outward_ref[...]).astype(BF16)
    for chunk in range(count):
        rows = chunk_rows(chunk, ny, size, core)
        here = slice(chunk * size, (chunk + 1) * size)
        q_s[here, :] = qkv_ref[rows, 0:width] * 0.125
        key = qkv_ref[rows, width : 2 * width]
        k_s[here, :] = key
        kt_s[:, here] = jnp.transpose(key.astype(F32)).astype(BF16)
        v_s[here, :] = qkv_ref[rows, 2 * width : 3 * width]
        g_s[here, :] = out_ref[rows, 0:width]
    dk_s[...] = jnp.zeros_like(dk_s)
    dv_s[...] = jnp.zeros_like(dv_s)
    lanes = lane_parts(heads, width)
    each = width // heads
    for block in range(count * size // BLOCK):
        first = block * BLOCK
        total = first + BLOCK
        allowed = allowed_pairs(start_ref, first, total)
        q_block, g_block = q_s[first:total, :], g_s[first:total, :]
        queries = []
        for h in range(heads):
            q_one, g_one = only(q_block, lanes[h]), only(g_block, lanes[h])
            scores = dot_nt(k_s[0:total, :], q_one)
            probs = jnp.where(allowed, jnp.exp(scores - log_ref[h : h + 1, first:total]), 0.0)
            prob_grad = dot_nt(v_s[0:total, :], g_one)
            delta = jnp.sum(probs * prob_grad, axis=0, keepdims=True)
            score_grad = (probs * (prob_grad - delta)).astype(BF16)
            dv_s[0:total, :] += dot_nn(probs.astype(BF16), g_one)
            dk_s[0:total, :] += dot_nn(score_grad, q_one)
            queries.append(dot_nn(kt_s[h * each : (h + 1) * each, 0:total], score_grad))
        query_grad = queries[0] if heads == 1 else jnp.concatenate(queries, axis=0)
        dq_s[first:total, :] = jnp.transpose(query_grad) * 0.125
    for chunk in range(count):
        rows = chunk_rows(chunk, ny, size, core)
        here = slice(chunk * size, (chunk + 1) * size)
        out_ref[rows, 0:width] = dq_s[here, :].astype(BF16)
        out_ref[rows, width : 2 * width] = dk_s[here, :].astype(BF16)
        out_ref[rows, 2 * width : 3 * width] = dv_s[here, :].astype(BF16)
    for ref, base in ((send_ref, half), (keep_ref, 0)):
        for start in range(0, half, step):
            rows = slice(base + start, base + start + step)
            ref[start : start + step, :] = dot_nt(out_ref[rows, :], weight_ref[...]).astype(BF16)
    total = dot_tn(near_ref[...], mine_ref[...]) + dot_tn(far_ref[...], other_ref[...])
    total = total.astype(BF16)
    if len(outward_grad_ref.shape) == 2:
        outward_grad_ref[...] = total
    else:
        rows, columns = outward_grad_ref.shape[2:]
        for i in range(4):
            start, left = (i >> 1) * rows, (i & 1) * columns
            outward_grad_ref[i >> 1, i & 1] = total[start : start + rows, left : left + columns]


def feed_forward(
    size,
    core_ref,
    mine_ref,
    other_ref,
    up_mine_ref,
    up_other_ref,
    expand_ref,
    shrink_ref,
    bias_ref,
    active_ref,
    grad_ref,
    send_ref,
    keep_ref,
    result_ref,
):
    half = keep_ref.shape[0]
    step = 2 * size
    rate = math.sqrt(2.0 / math.pi)
    core = core_ref[0]
    sides = ((send_ref, other_ref, up_other_ref, half, 1 - core), (keep_ref, mine_ref, up_mine_ref, 0, core))
    for ref, source_ref, up_ref, base, side in sides:
        for start in range(0, half, step):
            rows = slice(start, start + step)
            pair = slice(base + start, base + start + step)
            place = pl.ds(pl.multiple_of(side * half + start, step), step)
            before = dot_nn(source_ref[rows, :], expand_ref[...]) + bias_ref[...]
            upper = dot_nt(up_ref[rows, :], shrink_ref[...])
            square = before * before
            inner = jnp.tanh(rate * (before + 0.044715 * before * square))
            plus = 0.5 * (1.0 + inner)
            active = (before * plus).astype(BF16)
            active_ref[pair, :] = active
            slope = plus + 0.5 * before * (1.0 - inner * inner) * (rate + rate * 3 * 0.044715 * square)
            lower = (upper * slope).astype(BF16)
            grad_ref[pair, :] = lower
            ref[rows, :] = dot_nt(lower, expand_ref[...]).astype(BF16)
            result_ref[place, :] = dot_nn(active, shrink_ref[...]).astype(BF16)


def weight_parts(part, mine_ref, other_ref, up_mine_ref, up_other_ref, active_ref, grad_ref, bias_ref, out_ref):
    half, width = mine_ref.shape
    quarter, all_units = width // NZ, NZ * part
    for r in range(NZ):
        spot, ref = r, out_ref.at[r]
        here = slice(spot * quarter, (spot + 1) * quarter)
        total = dot_tn(mine_ref[:, here], grad_ref[0:half, :]) + dot_tn(other_ref[:, here], grad_ref[half : 2 * half, :])
        ref[0:quarter, :] = total.astype(BF16)
        units = slice(spot * part, (spot + 1) * part)
        total = dot_tn(active_ref[0:half, units], up_mine_ref[...])
        total = (total + dot_tn(active_ref[half : 2 * half, units], up_other_ref[...])).astype(BF16)
        for i in range(width // all_units):
            start = quarter + i * part
            ref[start : start + part, :] = total[:, i * all_units : (i + 1) * all_units]
    bias_ref[...] = jnp.sum(grad_ref[...].astype(F32), axis=0, keepdims=True)


def feed_forward_weights(second, up, active, before_grad):
    frames, units = active.shape
    width, part = up[0].shape[1], units // NZ
    quarter = width // NZ
    if part % 128:
        shrink = dot_tn(active, stack_rows(up)).astype(BF16).reshape(NZ, part, width)
        expand = dot_tn(stack_rows(second), before_grad).astype(BF16).reshape(NZ, quarter, units)
        bias = jnp.sum(before_grad.astype(F32), axis=0, keepdims=True)
        return bias, jnp.stack([stack_rows([expand[k], fold_columns(shrink[k], units)]) for k in range(NZ)])
    return pl.pallas_call(
        functools.partial(weight_parts, part),
        out_shape=(jax.ShapeDtypeStruct((1, units), F32), jax.ShapeDtypeStruct((NZ, 2 * quarter, units), BF16)),
        in_specs=whole(6),
        out_specs=tuple(whole(2)),
        compiler_params=pltpu.CompilerParams(vmem_limit_bytes=16 << 20),
        cost_estimate=pl.CostEstimate(
            flops=4 * frames * width * units, bytes_accessed=8 * frames * width, transcendentals=0
        ),
        name="feed_forward_weights",
    )(*second, *up, active, before_grad)


def whole(count):
    return [pl.BlockSpec(memory_space=pltpu.VMEM)] * count


def attention(core, pair, encoding, affine, w_in, bias, starts, heads, ny, size):
    half, wide = pair[0].shape[0], w_in.shape[1]
    frames, depth, width = 2 * half, pair[0].shape[1], wide // 3
    pairs = frames * frames * heads
    return pl.pallas_call(
        functools.partial(attend, heads, ny, size),
        out_shape=(
            jax.ShapeDtypeStruct((frames, depth), BF16),
            jax.ShapeDtypeStruct((frames, wide), BF16),
            jax.ShapeDtypeStruct((half, width), BF16),
            jax.ShapeDtypeStruct((half, width), BF16),
            jax.ShapeDtypeStruct((heads, frames), F32),
        ),
        in_specs=[pl.BlockSpec(memory_space=pltpu.SMEM)] + whole(7),
        out_specs=tuple(whole(5)),
        scratch_shapes=[
            pltpu.VMEM((frames, width), BF16),
            pltpu.VMEM((frames, width), BF16),
            pltpu.VMEM((width, frames), BF16),
        ],
        compiler_params=pltpu.CompilerParams(vmem_limit_bytes=16 << 20),
        cost_estimate=pl.CostEstimate(
            flops=pairs * 256 + 2 * frames * depth * wide, bytes_accessed=8 * frames * depth, transcendentals=pairs // 2
        ),
        name="attend",
    )(core, *pair, encoding, affine, w_in, bias, starts)


def attention_back(place, qkv, pair, context, w_out, w_in, starts, log_total, heads, ny, size):
    frames, wide = qkv.shape
    width = wide // 3
    depth = pair[0].shape[1]
    cut = heads == 2 and ny == 2
    pairs = frames * frames * heads
    half = jax.ShapeDtypeStruct(pair[0].shape, BF16)
    return pl.pallas_call(
        functools.partial(attend_back, heads, ny, size),
        out_shape=(
            jax.ShapeDtypeStruct((frames, wide), BF16),
            half,
            half,
            jax.ShapeDtypeStruct((2, 2, width // 2, depth // 2) if cut else (width, depth), BF16),
        ),
        in_specs=[pl.BlockSpec(memory_space=pltpu.SMEM)] + whole(9),
        out_specs=tuple(whole(4)),
        scratch_shapes=[pltpu.VMEM((frames, width), BF16)] * 4
        + [pltpu.VMEM((width, frames), BF16)]
        + [pltpu.VMEM((frames, width), F32)] * 3,
        compiler_params=pltpu.CompilerParams(vmem_limit_bytes=20 << 20),
        cost_estimate=pl.CostEstimate(
            flops=pairs * 640 + 2 * frames * depth * (wide + 2 * width),
            bytes_accessed=8 * frames * depth,
            transcendentals=pairs // 2,
        ),
        name="attend_back",
    )(place.core, qkv, *pair, *context, w_out, w_in, starts, log_total)


def feed_forward_front(core, pair, up_pair, w_expand, w_shrink, bias, size):
    frames, width = 2 * pair[0].shape[0], pair[0].shape[1]
    units = w_expand.shape[1]
    half = jax.ShapeDtypeStruct((frames // 2, width), BF16)
    inner = jax.ShapeDtypeStruct((frames, units), BF16)
    return pl.pallas_call(
        functools.partial(feed_forward, size),
        out_shape=(inner, inner, half, half, jax.ShapeDtypeStruct((frames, width), BF16)),
        in_specs=[pl.BlockSpec(memory_space=pltpu.SMEM)] + whole(7),
        out_specs=tuple(whole(5)),
        compiler_params=pltpu.CompilerParams(vmem_limit_bytes=16 << 20),
        cost_estimate=pl.CostEstimate(
            flops=8 * frames * width * units, bytes_accessed=10 * frames * width, transcendentals=frames * units
        ),
        name="feed_forward",
    )(core, *pair, *up_pair, w_expand, w_shrink, bias)


class Place:
    def __init__(self, ny):
        self.x, self.z, self.y, self.c = (lax.axis_index(a) for a in ("x", "z", "y", "c"))
        self.xy = jnp.reshape(self.x * ny + self.y, (1,)).astype(jnp.int32)
        self.core = jnp.reshape(self.c, (1,)).astype(jnp.int32)
        self.layer = jnp.reshape(self.z, (1,)).astype(jnp.int32)


def on_device(
    groups,
    ny,
    frames,
    cotangent,
    segment_lengths,
    position_offsets,
    first_gain,
    first_shift,
    inward_weight,
    query_bias,
    value_bias,
    outward_weight,
    outward_bias,
    second_gain,
    second_shift,
    expand_weight,
    expand_bias,
    shrink_weight,
    shrink_bias,
):
    place = Place(ny)
    x, z, y, c = place.x, place.z, place.y, place.c
    local_len, rows, width = frames.shape
    share = inward_weight.shape[0]
    layer = 4 * ny
    spread = NZ * ny * 2
    full_len = local_len * spread
    size = 2 * local_len
    hd = HEADS // layer
    hw = hd * (width // HEADS)
    hidden = expand_bias.shape[0]
    part = hidden // 2
    me = (c * 2 + x) * ny + y

    def sum_groups(value):
        return lax.psum(value, "g") if groups > 1 else value

    def exchange(value, axes):
        return lax.all_to_all(value, axes, 0, 0, tiled=True)

    both = to_home(jnp.concatenate([frames, cotangent], axis=2), place)
    table = jnp.stack([segment_lengths, position_offsets], axis=1)

    small = [first_gain, first_shift, query_bias, value_bias, outward_bias, second_gain, second_shift, shrink_bias]
    kinds = len(small) + hidden // share
    units = NZ * part
    packed = jnp.concatenate([v[None] for v in small] + [expand_bias.reshape(-1, share)], axis=0)
    packed = packed.reshape(-1, 3 * hw)
    extra = packed.shape[0]
    packed = jnp.pad(packed, ((0, SMALL_ROWS - extra), (0, units)))[None]
    in_cols = jnp.transpose(inward_weight.reshape(share, 3, 2, 2, ny, hw), (3, 4, 2, 0, 1, 5))
    in_cols = pick(in_cols, x).reshape(ny * 2, share, 3 * hw)
    ex_cols = pick(expand_weight.reshape(share, NZ, ny, 2, 2, part), x, 4)
    ex_cols = jnp.transpose(ex_cols, (2, 3, 0, 1, 4)).reshape(ny * 2, share, units)
    columns = jnp.concatenate([in_cols, ex_cols], axis=2)
    columns = jnp.concatenate([columns, jnp.broadcast_to(packed, (ny * 2,) + packed.shape[1:])], axis=1)
    columns, table = after(columns, table)
    columns = exchange(columns, ("y", "c"))
    other_table = hop(table, "x")

    row_x = jnp.where((z == 0) | (z == 3), 1, 0)
    table = pick(jnp.where(x == row_x, table, other_table), z >> 1)
    lengths, offsets = table[0], table[1]
    count = lengths.shape[0]
    starts = jnp.sum(
        jnp.where(jnp.arange(count)[None, :] < jnp.arange(count)[:, None], lengths[None, :], 0), axis=1
    )
    frame_ids = jnp.arange(full_len, dtype=jnp.int32)
    row_starts = jnp.max(jnp.where(starts[:, None] <= frame_ids[None, :], starts[:, None], 0), axis=0)[None, :]
    spot = jnp.arange(2 * ny)
    chunk = jnp.concatenate([(2 * (spot // ny) + i) * ny + spot % ny for i in (c, 1 - c)])
    mine = (chunk[:, None] * size + jnp.arange(size, dtype=jnp.int32)).reshape(-1)
    inside = (mine[:, None] >= starts[None, :]) & (mine[:, None] < (starts + lengths)[None, :])
    position = jnp.sum(jnp.where(inside, offsets[None, :] + mine[:, None] - starts[None, :], 0), axis=1)
    encoding = sin_cos(position, width)

    both, later_outward, columns = after(both, outward_weight, columns)
    fr, ct = both[:, :width], both[:, width:]
    outward = lax.all_gather(later_outward, SEQ, axis=0, tiled=True)
    small_part = columns[:, share : share + extra, : 3 * hw].reshape(-1, 3 * hw)
    small_part = jnp.pad(small_part, ((0, SMALL_ROWS - small_part.shape[0]), (0, 0)))
    in_part = stack_rows([columns[:, :share, : 3 * hw].reshape(-1, 3 * hw), small_part])
    in_parts = [in_part] + [hop(in_part, "z", NZ, k) for k in range(1, NZ)]
    sh_rows = lax.dynamic_slice_in_dim(shrink_weight, x * part, part, 0)
    ff_part = stack_rows([columns[:, :share, 3 * hw :].reshape(-1, units), fold_columns(sh_rows, units)])
    mine, up_mine = assemble_pair(near_parts(both, ny), place.xy)
    ff_part = jnp.broadcast_to(ff_part[None], (NZ,) + ff_part.shape)
    mine, encoding, ff_part, *in_parts = after(mine, encoding, ff_part, *in_parts)
    first_pair = [mine, hop(mine, "c")]
    w_in, small_rows = collect_inward(in_parts, place)
    ff_got = exchange(ff_part, ("z",))

    vectors = small_rows.reshape(NZ, SMALL_ROWS, 3 * hw)[:, : ny * 2 * extra]
    vectors = vectors.reshape(spread, kinds, share).astype(F32)
    expand_b = vectors[:, len(small) :].reshape(NZ, ny, 2, 2, part)
    expand_b = pick(pick(pick(expand_b, y, 1), c, 1), x, 1).reshape(1, NZ * part)
    vectors = jnp.swapaxes(vectors[:, : len(small)], 0, 1).reshape(len(small), width)
    gain_one, shift_one, query_b, value_b, outward_b, gain_two, shift_two, shrink_b = (
        vectors[i : i + 1] for i in range(len(small))
    )
    qkv_bias = jnp.concatenate(
        [
            lax.dynamic_slice_in_dim(query_b, me * hw, hw, 1),
            jnp.zeros((1, hw), F32),
            lax.dynamic_slice_in_dim(value_b, me * hw, hw, 1),
        ],
        axis=1,
    )

    first_all, qkv, *context_pair, log_total = attention(
        place.core, first_pair, encoding, vectors[:2], w_in, qkv_bias, row_starts, hd, ny, size
    )
    *context_pair, up_mine = after(*context_pair, up_mine)
    if ny == 2:
        context = by_half(c, context_pair[0][None], hop(context_pair[1], "c")[None], 0)
        context = context.reshape(2, 2, ny, size, hw)
        context = by_half(x, pick(context, x, 1)[:, None], hop(pick(context, 1 - x, 1), "x")[:, None], 1)
        context = by_half(y, pick(context, y, 2)[:, :, None], hop(pick(context, 1 - y, 2), "y")[:, :, None], 2)
    else:
        context = exchange(by_half(c, *context_pair, 0).reshape(layer, size, hw), LAYER)
    context = context.reshape(layer, size, hw)
    up_pair = [up_mine, hop(up_mine, "c")]

    inputs = fr.astype(F32) + lax.dynamic_slice_in_dim(encoding, (x * ny + y) * size, size, 0)
    normal_one, scale_one = normalize(inputs)
    context = jnp.swapaxes(context, 0, 1).reshape(size, width)
    middle = inputs + dot_nn(context, outward) + outward_b

    normal_two, scale_two = normalize(middle)
    second = (normal_two * gain_two + shift_two).astype(BF16)
    ff_got, *second_near = after(ff_got, *near_parts(second, ny))
    second_pair = both_cores(second_near, place)
    w_expand, w_shrink = collect_hidden(ff_got, width)
    active, before_grad, send, keep, out_part = feed_forward_front(
        place.core, second_pair, up_pair, w_expand, w_shrink, expand_b, size
    )
    second_parts = list(fold(keep, hop(send, "c"), place, ny))
    second_parts[0], active, before_grad = after(second_parts[0], active, before_grad)
    second_grad = finish(second_parts, ny)
    expand_b_sum, hidden_part = feed_forward_weights(second_pair, up_pair, active, before_grad)
    out_part = lax.psum_scatter(out_part, LAYER, scatter_dimension=0, tiled=True)
    second_grad, expand_b_sum = after(second_grad, expand_b_sum)
    hidden_got = exchange(hidden_part, ("z",))

    upstream = ct.astype(F32)
    middle_part, gain_two_sum, shift_two_sum = normalize_back(normal_two, scale_two, gain_two, second_grad)
    middle_grad = upstream + middle_part
    low_middle = middle_grad.astype(BF16)
    low_pair = both_cores(near_parts(low_middle, ny), place)
    w_out = lax.dynamic_slice_in_dim(outward, me * hw, hw, 0)
    mixed_grad, send, keep, outward_part = attention_back(
        place, qkv, low_pair, context_pair, w_out, w_in, row_starts, log_total, hd, ny, size
    )
    got = hop(send, "c")
    cut = outward_part if hd == 2 and ny == 2 else outward_part.reshape(2, 1, -1, width)
    far_cut = hop(pick(cut, 1 - c), "c")
    got, far_cut = after(got, far_cut)
    first_parts = list(fold(keep, got, place, ny))
    first_parts[0], mixed_late, far_cut, hidden_got = after(first_parts[0], mixed_grad, far_cut, hidden_got)
    inward_part = dot_tn(first_all, mixed_late).astype(BF16)
    first_grad = finish(first_parts, ny)
    far_cut, out_part = after(far_cut, out_part)
    line_out = by_half(c, pick(cut, c)[None], far_cut[None], 0)
    if hd == 2 and ny == 2:
        line_out = by_half(x, pick(line_out, x, 1)[:, None], hop(pick(line_out, 1 - x, 1), "x")[:, None], 1)
    inward_got = exchange(inward_part.reshape(spread, share, 3 * hw), SEQ)
    input_part, gain_one_sum, shift_one_sum = normalize_back(normal_one, scale_one, vectors[:1], first_grad)
    late = (middle_grad + input_part).astype(BF16)
    late, out_part, hidden_got, line_out = after(late, out_part, hidden_got, line_out)
    hidden_sum = sum_sources(hidden_got, NZ)
    frames_grad = to_origin(late, place)
    inward_got, out_part = after(inward_got, out_part)
    layer_output = to_origin((middle + out_part.astype(F32) + shrink_b).astype(BF16), place)

    split = width // 2
    hidden_sum = sum_groups(hidden_sum.reshape(-1, units)).astype(BF16)
    line = hidden_sum[: width // NZ].reshape(ny, 2, share, units)
    if ny == 2:
        line = by_half(c, pick(line, c, 1)[:, None], hop(pick(line, 1 - c, 1), "c")[:, None], 1)
        line = by_half(y, pick(line, y)[None], hop(pick(line, 1 - y), "y")[None], 0)
    else:
        line = exchange(line.reshape(ny * 2, share, units), ("y", "c"))
    mine = stack_rows([line.reshape(-1, units), hidden_sum[width // NZ :]])
    other = hop(mine, "x")

    def full_hidden(other):
        pair = [unfold_columns(v[width // NZ :], width // units) for v in (mine, other)]
        g_shrink = by_half(x, *pair, 0).astype(F32)
        pair = [v[: width // NZ].reshape(ny, 2, 1, share, NZ, part) for v in (mine, other)]
        return g_shrink, jnp.transpose(by_half(x, *pair, 2), (3, 4, 0, 1, 2, 5)).reshape(share, -1).astype(F32)

    if hd == 2 and ny == 2:
        line = line_out
        out_got = lax.psum_scatter(line.reshape(NZ * share, split), "z", scatter_dimension=0, tiled=True)
        inward_late, out_got = after(inward_got, out_got)
        out_sum = sum_groups(out_got.astype(F32)).astype(BF16)
        g_outward = by_half(x, out_sum, hop(out_sum, "x"), 1).astype(F32)
    else:
        cut = lax.dynamic_update_slice(jnp.zeros((width, width), BF16), outward_part, (me * hw, 0))
        g_outward = lax.psum_scatter(cut, SEQ, scatter_dimension=0, tiled=True)
        g_outward = lax.psum(g_outward.astype(F32), ("g", "x"))

    mixed_sum = jnp.sum(mixed_grad.astype(F32), axis=0)

    def from_heads(value):
        return lax.dynamic_update_slice(jnp.zeros((width,), F32), value, (me * hw,))

    flat = lax.optimization_barrier(jnp.stack(
        [
            gain_one_sum,
            shift_one_sum,
            from_heads(mixed_sum[:hw]),
            from_heads(mixed_sum[2 * hw :]),
            jnp.sum(low_middle.astype(F32), axis=0),
            gain_two_sum,
            shift_two_sum,
            jnp.sum(upstream, axis=0),
        ]
    ))
    small_len = len(small) * share
    sums = jnp.swapaxes(flat.reshape(len(small), spread, share), 0, 1).reshape(spread, small_len)
    spot = jnp.zeros((NZ, ny, 2, 2, part), F32)
    spot = lax.dynamic_update_slice(spot, expand_b_sum.reshape(NZ, 1, 1, 1, part), (0, y, c, x, 0))
    sums = jnp.concatenate([sums, spot.reshape(spread, hidden)], axis=1)
    inward_got, sums = after(inward_got, sums)
    sums = jnp.broadcast_to(sums[None], (2,) + sums.shape).reshape(2 * spread, -1, 128)
    total = sum_groups(jnp.sum(exchange(sums, ("x",) + SEQ), axis=0)).reshape(-1)
    frames_grad, total, other = after(frames_grad, total, other)
    g_shrink, g_expand = full_hidden(other)
    g_small = total[:small_len].reshape(len(small), share)
    g_expand_b = total[small_len:]
    inward_got = inward_late if hd == 2 and ny == 2 else inward_got
    inward_sum = sum_groups(sum_sources(inward_got, NZ)).astype(BF16)
    g_inward = [v.reshape(ny, 2, 1, share, 3, hw) for v in (inward_sum, hop(inward_sum, "x"))]
    g_inward = jnp.transpose(by_half(x, *g_inward, 2), (3, 4, 1, 2, 0, 5)).reshape(share, -1).astype(F32)

    return (
        layer_output,
        frames_grad.astype(F32),
        g_small[0],
        g_small[1],
        g_inward,
        g_small[2],
        g_small[3],
        g_outward,
        g_small[4],
        g_small[5],
        g_small[6],
        g_expand,
        g_expand_b,
        g_shrink,
        g_small[7],
    )


def solution(mesh):
    batch, seq = mesh.shape["batch"], mesh.shape["seq"]
    groups, ny = batch // 2, seq // (2 * NZ)
    fine = Mesh(mesh.devices.reshape(groups, 2, NZ, ny, 2), ("g", "x", "z", "y", "c"))
    b, s = ("g", "x"), ("z", "y", "c")
    in_specs = (
        P(s, b, None),
        P(s, b, None),
        P(b, None),
        P(b, None),
        P(s),
        P(s),
        P(s, None),
        P(s),
        P(s),
        P(s, None),
        P(s),
        P(s),
        P(s),
        P(s, None),
        P(s),
        P(s, None),
        P(s),
    )
    out_specs = (
        P(s, b, None),
        P(s, b, None),
        P(s),
        P(s),
        P(s, None),
        P(s),
        P(s),
        P(s, None),
        P(s),
        P(s),
        P(s),
        P(s, None),
        P(s),
        P(s, None),
        P(s),
    )
    return jax.shard_map(
        functools.partial(on_device, groups, ny), mesh=fine, in_specs=in_specs, out_specs=out_specs, check_vma=False
    )
```

```python
import functools
import math

import jax
import jax.numpy as jnp
from jax import lax
from jax.experimental import pallas as pl
from jax.experimental.pallas import tpu as pltpu
from jax.sharding import Mesh, PartitionSpec as P


HEADS = 16
NZ = 4
SMALL_ROWS = 16
NORM_EPS = 1e-05
NEG = -1e30
F32 = jnp.float32
BF16 = jnp.bfloat16
LAYER_OF_ROW = (1, 2, 0, 3)
SWAP = [(0, 1), (1, 0)]
LAYER = ("c", "x", "y")
SEQ = ("z", "y", "c")


def xor_perm(count, k):
    return [(i, i ^ k) for i in range(count)]


def hop(value, axis, count=2, k=1):
    return lax.ppermute(value, axis, xor_perm(count, k))


def pick(value, index, axis=0):
    return lax.dynamic_index_in_dim(value, index, axis, keepdims=False)


def stack_rows(parts):
    return jnp.concatenate(parts, axis=0)


def assemble_body(pieces, size, place_ref, *refs):
    out_ref = refs[pieces]
    for r in range(pieces):
        spot = place_ref[0] ^ r
        out_ref[pl.ds(pl.multiple_of(spot * size, size), size), :] = refs[r][...]


def assemble(parts, me):
    size, width = parts[0].shape
    count = len(parts)
    return pl.pallas_call(
        functools.partial(assemble_body, count, size),
        out_shape=jax.ShapeDtypeStruct((count * size, width), parts[0].dtype),
        in_specs=[pl.BlockSpec(memory_space=pltpu.SMEM)] + whole(count),
        out_specs=whole(1)[0],
        compiler_params=pltpu.CompilerParams(vmem_limit_bytes=4 << 20),
        cost_estimate=pl.CostEstimate(flops=0, bytes_accessed=4 * count * size * width, transcendentals=0),
        name="assemble",
    )(me, *parts)


def assemble_pair_body(pieces, size, place_ref, *refs):
    left_ref, right_ref = refs[pieces:]
    width = left_ref.shape[1]
    for r in range(pieces):
        rows = pl.ds(pl.multiple_of((place_ref[0] ^ r) * size, size), size)
        left_ref[rows, :] = refs[r][:, 0:width]
        right_ref[rows, :] = refs[r][:, width : 2 * width]


def assemble_pair(parts, me):
    size, width = parts[0].shape
    count = len(parts)
    return pl.pallas_call(
        functools.partial(assemble_pair_body, count, size),
        out_shape=[jax.ShapeDtypeStruct((count * size, width // 2), parts[0].dtype)] * 2,
        in_specs=[pl.BlockSpec(memory_space=pltpu.SMEM)] + whole(count),
        out_specs=whole(2),
        compiler_params=pltpu.CompilerParams(vmem_limit_bytes=4 << 20),
        cost_estimate=pl.CostEstimate(flops=0, bytes_accessed=4 * count * size * width, transcendentals=0),
        name="assemble_pair",
    )(me, *parts)


def near_parts(block, ny):
    return [block] + [lax.ppermute(block, ("x", "y"), xor_perm(2 * ny, r)) for r in range(1, 2 * ny)]


def both_cores(parts, place):
    mine = assemble(parts, place.xy)
    return mine, hop(mine, "c")


def fold_body(count, size, place_ref, keep_ref, got_ref, own_ref, *out_refs):
    for r in range(count):
        spot = place_ref[0] ^ r
        here = pl.ds(pl.multiple_of(spot * size, size), size)
        value = keep_ref[here, :].astype(F32) + got_ref[here, :].astype(F32)
        if r == 0:
            own_ref[...] = value
        else:
            out_refs[r - 1][...] = value.astype(BF16)


def fold(keep, got, place, ny):
    rows, width = keep.shape
    count = 2 * ny
    size = rows // count
    return pl.pallas_call(
        functools.partial(fold_body, count, size),
        out_shape=[jax.ShapeDtypeStruct((size, width), F32)] + [jax.ShapeDtypeStruct((size, width), BF16)] * (count - 1),
        in_specs=[pl.BlockSpec(memory_space=pltpu.SMEM)] + whole(2),
        out_specs=whole(count),
        compiler_params=pltpu.CompilerParams(vmem_limit_bytes=4 << 20),
        cost_estimate=pl.CostEstimate(flops=count * size * width, bytes_accessed=6 * count * size * width, transcendentals=0),
        name="fold",
    )(place.xy, keep, got)


def finish(parts, ny):
    own = parts[0]
    for r in range(1, 2 * ny):
        own = own + lax.ppermute(parts[r], ("x", "y"), xor_perm(2 * ny, r)).astype(F32)
    return own


def fold_columns(value, units):
    return stack_rows([value[:, i : i + units] for i in range(0, value.shape[1], units)])


def unfold_columns(value, count):
    size = value.shape[0] // count
    return jnp.concatenate([value[i * size : (i + 1) * size] for i in range(count)], axis=1)


def collect_inward_body(place_ref, *refs):
    weight_ref, small_ref = refs[NZ:]
    quarter = weight_ref.shape[0] // NZ
    for r in range(NZ):
        spot = place_ref[0] ^ r
        weight_ref[pl.ds(pl.multiple_of(spot * quarter, quarter), quarter), :] = refs[r][0:quarter, :]
        rows = pl.ds(pl.multiple_of(spot * SMALL_ROWS, SMALL_ROWS), SMALL_ROWS)
        small_ref[rows, :] = refs[r][quarter : quarter + SMALL_ROWS, :]


def collect_inward(parts, place):
    rows, width = parts[0].shape
    return pl.pallas_call(
        collect_inward_body,
        out_shape=[jax.ShapeDtypeStruct((NZ * n, width), BF16) for n in (rows - SMALL_ROWS, SMALL_ROWS)],
        in_specs=[pl.BlockSpec(memory_space=pltpu.SMEM)] + whole(NZ),
        out_specs=whole(2),
        compiler_params=pltpu.CompilerParams(vmem_limit_bytes=4 << 20),
        cost_estimate=pl.CostEstimate(flops=0, bytes_accessed=16 * rows * width, transcendentals=0),
        name="collect_inward",
    )(place.layer, *parts)


def collect_hidden_body(parts_ref, expand_ref, shrink_ref):
    quarter = expand_ref.shape[0] // NZ
    part, units = shrink_ref.shape[0] // NZ, expand_ref.shape[1]
    for r in range(NZ):
        expand_ref[r * quarter : (r + 1) * quarter, :] = parts_ref[r, 0:quarter, :]
        for i in range(shrink_ref.shape[1] // units):
            start = quarter + i * part
            here = slice(r * part, (r + 1) * part)
            shrink_ref[here, i * units : (i + 1) * units] = parts_ref[r, start : start + part, :]


def collect_hidden(parts, width):
    units = parts.shape[2]
    return pl.pallas_call(
        collect_hidden_body,
        out_shape=[jax.ShapeDtypeStruct((width, units), BF16), jax.ShapeDtypeStruct((units, width), BF16)],
        in_specs=whole(1),
        out_specs=whole(2),
        compiler_params=pltpu.CompilerParams(vmem_limit_bytes=4 << 20),
        cost_estimate=pl.CostEstimate(flops=0, bytes_accessed=4 * parts.size, transcendentals=0),
        name="collect_hidden",
    )(parts)


def rehome_flat(x, z, c):
    return (x * NZ + z) * 2 + c


def rehome_perm(k):
    return [
        (rehome_flat(x, z, c), rehome_flat(z >> 1, LAYER_OF_ROW[2 * x + (c ^ k)], z & 1))
        for x in range(2)
        for z in range(NZ)
        for c in range(2)
    ]


def to_home(block, place):
    got = [
        lax.ppermute(jnp.where(place.c == k, block[:, 0], block[:, 1]), ("x", "z", "c"), rehome_perm(k))
        for k in range(2)
    ]
    first = place.z < 2
    return stack_rows([jnp.where(first, got[0], got[1]), jnp.where(first, got[1], got[0])])


def to_origin(block, place):
    half = block.shape[0] // 2
    first = place.z < 2
    low, high = block[:half], block[half:]
    sent = [jnp.where(first, low, high), jnp.where(first, high, low)]
    got = [
        lax.ppermute(sent[k], ("x", "z", "c"), [(b, a) for a, b in rehome_perm(k)]) for k in range(2)
    ]
    return jnp.stack(
        [jnp.where(place.c == 0, got[0], got[1]), jnp.where(place.c == 0, got[1], got[0])], axis=1
    )


def after(first, *values):
    return lax.optimization_barrier((first, *values))


def sum_sources(value, count):
    return jnp.sum(value.reshape((count, -1) + value.shape[1:]).astype(F32), axis=0)


def by_half(x, mine, other, axis):
    return jnp.concatenate([jnp.where(x == 0, mine, other), jnp.where(x == 0, other, mine)], axis=axis)


def sin_cos(position, width):
    feature = jnp.arange(width, dtype=jnp.int32)
    rates = jnp.exp((feature // 2).astype(F32) * (-2.0 * math.log(10000.0) / width))
    angle = position.astype(F32)[:, None] * rates[None, :]
    turn = jnp.round(angle * (2.0 / math.pi))
    rest = angle - turn * 1.5703125
    rest = rest - turn * 0.00048375129699707031
    rest = rest - turn * 7.5497899548918861e-08
    quadrant = turn.astype(jnp.int32) + (feature % 2)[None, :]
    square = rest * rest
    sine = rest + rest * square * (
        -0.16666666641626524 + square * (0.008333329385889463 + square * (-0.00019839334836096632 + square * 2.718311493989822e-06))
    )
    cosine = 1.0 + square * (
        -0.49999999725103100 + square * (0.04166662332373906 + square * (-0.001388676377460993 + square * 2.439044879627741e-05))
    )
    value = jnp.where((quadrant & 1) == 0, sine, cosine)
    return jnp.where((quadrant & 2) == 0, value, -value)


def normalize(values):
    center = values - jnp.mean(values, axis=-1, keepdims=True)
    scale = lax.rsqrt(jnp.mean(center * center, axis=-1, keepdims=True) + NORM_EPS)
    return center * scale, scale


def normalize_back(normal, scale, gain, upstream):
    scaled = upstream * gain
    inner = scaled - jnp.mean(scaled, axis=-1, keepdims=True)
    inner = inner - normal * jnp.mean(scaled * normal, axis=-1, keepdims=True)
    return inner * scale, jnp.sum(upstream * normal, axis=0), jnp.sum(upstream, axis=0)


def dot_nt(a, b):
    return lax.dot_general(a, b, (((1,), (1,)), ((), ())), preferred_element_type=F32)


def dot_tn(a, b):
    return lax.dot_general(a, b, (((0,), (0,)), ((), ())), preferred_element_type=F32)


def dot_nn(a, b):
    return jnp.dot(a, b, preferred_element_type=F32)


BLOCK = 256


def chunk_owner(chunk, ny):
    outer, y = divmod(chunk, ny)
    return ((outer & 1) * 2 + (outer >> 1)) * ny + y


def lane_parts(heads, width):
    if heads == 1:
        return [None]
    lane = lax.broadcasted_iota(jnp.int32, (1, width), 1)
    return [(lane >= h * (width // heads)) & (lane < (h + 1) * (width // heads)) for h in range(heads)]


def only(value, lanes):
    return value if lanes is None else jnp.where(lanes, value, jnp.zeros_like(value))


def allowed_pairs(start_ref, first, total):
    key = lax.broadcasted_iota(jnp.int32, (total, BLOCK), 0)
    frame = first + lax.broadcasted_iota(jnp.int32, (total, BLOCK), 1)
    return (key >= start_ref[:, first : first + BLOCK]) & (key <= frame)


def chunk_rows(chunk, ny, size, core):
    half, spot = divmod(chunk_owner(chunk, ny), 2 * ny)
    return pl.ds(pl.multiple_of(((half ^ core) * (2 * ny) + spot) * size, size), size)


def attend(
    heads,
    ny,
    size,
    core_ref,
    mine_ref,
    other_ref,
    encoding_ref,
    affine_ref,
    weight_ref,
    bias_ref,
    start_ref,
    first_ref,
    qkv_ref,
    near_ref,
    far_ref,
    log_ref,
    q_s,
    k_s,
    vt_s,
):
    count = 4 * ny
    width = q_s.shape[1]
    core = core_ref[0]
    step = 2 * size
    half = mine_ref.shape[0]
    for base, ref in ((0, mine_ref), (half, other_ref)):
        for start in range(0, half, step):
            rows = slice(base + start, base + start + step)
            normal, _ = normalize(ref[start : start + step, :].astype(F32) + encoding_ref[rows, :])
            value = (normal * affine_ref[0:1, :] + affine_ref[1:2, :]).astype(BF16)
            first_ref[rows, :] = value
            qkv_ref[rows, :] = (dot_nn(value, weight_ref[...]) + bias_ref[...]).astype(BF16)
    for chunk in range(count):
        rows = chunk_rows(chunk, ny, size, core)
        here = slice(chunk * size, (chunk + 1) * size)
        q_s[here, :] = qkv_ref[rows, 0:width] * 0.125
        k_s[here, :] = qkv_ref[rows, width : 2 * width]
        vt_s[:, here] = jnp.transpose(qkv_ref[rows, 2 * width : 3 * width].astype(F32)).astype(BF16)
    lanes = lane_parts(heads, width)
    each = width // heads
    for block in range(count * size // BLOCK):
        first = block * BLOCK
        total = first + BLOCK
        allowed = allowed_pairs(start_ref, first, total)
        q_block = q_s[first:total, :]
        contexts = []
        for h in range(heads):
            scores = dot_nt(k_s[0:total, :], only(q_block, lanes[h]))
            scores = jnp.where(allowed, scores, NEG)
            top = jnp.max(scores, axis=0, keepdims=True)
            weight = jnp.exp(scores - top)
            mass = jnp.sum(weight, axis=0, keepdims=True)
            part = dot_nn(vt_s[h * each : (h + 1) * each, 0:total], weight.astype(BF16))
            contexts.append(part / mass)
            log_ref[h : h + 1, first:total] = top + jnp.log(mass)
        context = contexts[0] if heads == 1 else jnp.concatenate(contexts, axis=0)
        context = jnp.transpose(context).astype(BF16)
        for sub in range(BLOCK // size):
            owner = chunk_owner(block * (BLOCK // size) + sub, ny)
            side, spot = divmod(owner, 2 * ny)
            rows, piece = slice(spot * size, (spot + 1) * size), context[sub * size : (sub + 1) * size]

            @pl.when(core == side)
            def _(rows=rows, piece=piece):
                near_ref[rows, :] = piece

            @pl.when(core != side)
            def _(rows=rows, piece=piece):
                far_ref[rows, :] = piece


def attend_back(
    heads,
    ny,
    size,
    core_ref,
    qkv_ref,
    mine_ref,
    other_ref,
    near_ref,
    far_ref,
    outward_ref,
    weight_ref,
    start_ref,
    log_ref,
    out_ref,
    send_ref,
    keep_ref,
    outward_grad_ref,
    q_s,
    k_s,
    v_s,
    g_s,
    kt_s,
    dq_s,
    dk_s,
    dv_s,
):
    count = 4 * ny
    width = q_s.shape[1]
    core = core_ref[0]
    half = mine_ref.shape[0]
    step = 2 * size
    for base, ref in ((0, mine_ref), (half, other_ref)):
        for start in range(0, half, step):
            rows = slice(start, start + step)
            out_ref[base + start : base + start + step, 0:width] = dot_nt(ref[rows, :], outward_ref[...]).astype(BF16)
    for chunk in range(count):
        rows = chunk_rows(chunk, ny, size, core)
        here = slice(chunk * size, (chunk + 1) * size)
        q_s[here, :] = qkv_ref[rows, 0:width] * 0.125
        key = qkv_ref[rows, width : 2 * width]
        k_s[here, :] = key
        kt_s[:, here] = jnp.transpose(key.astype(F32)).astype(BF16)
        v_s[here, :] = qkv_ref[rows, 2 * width : 3 * width]
        g_s[here, :] = out_ref[rows, 0:width]
    dk_s[...] = jnp.zeros_like(dk_s)
    dv_s[...] = jnp.zeros_like(dv_s)
    lanes = lane_parts(heads, width)
    each = width // heads
    for block in range(count * size // BLOCK):
        first = block * BLOCK
        total = first + BLOCK
        allowed = allowed_pairs(start_ref, first, total)
        q_block, g_block = q_s[first:total, :], g_s[first:total, :]
        queries = []
        for h in range(heads):
            q_one, g_one = only(q_block, lanes[h]), only(g_block, lanes[h])
            scores = dot_nt(k_s[0:total, :], q_one)
            probs = jnp.where(allowed, jnp.exp(scores - log_ref[h : h + 1, first:total]), 0.0)
            prob_grad = dot_nt(v_s[0:total, :], g_one)
            delta = jnp.sum(probs * prob_grad, axis=0, keepdims=True)
            score_grad = (probs * (prob_grad - delta)).astype(BF16)
            dv_s[0:total, :] += dot_nn(probs.astype(BF16), g_one)
            dk_s[0:total, :] += dot_nn(score_grad, q_one)
            queries.append(dot_nn(kt_s[h * each : (h + 1) * each, 0:total], score_grad))
        query_grad = queries[0] if heads == 1 else jnp.concatenate(queries, axis=0)
        dq_s[first:total, :] = jnp.transpose(query_grad) * 0.125
    for chunk in range(count):
        rows = chunk_rows(chunk, ny, size, core)
        here = slice(chunk * size, (chunk + 1) * size)
        out_ref[rows, 0:width] = dq_s[here, :].astype(BF16)
        out_ref[rows, width : 2 * width] = dk_s[here, :].astype(BF16)
        out_ref[rows, 2 * width : 3 * width] = dv_s[here, :].astype(BF16)
    for ref, base in ((send_ref, half), (keep_ref, 0)):
        for start in range(0, half, step):
            rows = slice(base + start, base + start + step)
            ref[start : start + step, :] = dot_nt(out_ref[rows, :], weight_ref[...]).astype(BF16)
    total = dot_tn(near_ref[...], mine_ref[...]) + dot_tn(far_ref[...], other_ref[...])
    total = total.astype(BF16)
    if len(outward_grad_ref.shape) == 2:
        outward_grad_ref[...] = total
    else:
        rows, columns = outward_grad_ref.shape[2:]
        for i in range(4):
            start, left = (i >> 1) * rows, (i & 1) * columns
            outward_grad_ref[i >> 1, i & 1] = total[start : start + rows, left : left + columns]


def feed_forward(
    size,
    core_ref,
    mine_ref,
    other_ref,
    up_mine_ref,
    up_other_ref,
    expand_ref,
    shrink_ref,
    bias_ref,
    active_ref,
    grad_ref,
    send_ref,
    keep_ref,
    result_ref,
):
    half = keep_ref.shape[0]
    step = 2 * size
    rate = math.sqrt(2.0 / math.pi)
    core = core_ref[0]
    sides = ((send_ref, other_ref, up_other_ref, half, 1 - core), (keep_ref, mine_ref, up_mine_ref, 0, core))
    for ref, source_ref, up_ref, base, side in sides:
        for start in range(0, half, step):
            rows = slice(start, start + step)
            pair = slice(base + start, base + start + step)
            place = pl.ds(pl.multiple_of(side * half + start, step), step)
            before = dot_nn(source_ref[rows, :], expand_ref[...]) + bias_ref[...]
            upper = dot_nt(up_ref[rows, :], shrink_ref[...])
            square = before * before
            inner = jnp.tanh(rate * (before + 0.044715 * before * square))
            plus = 0.5 * (1.0 + inner)
            active = (before * plus).astype(BF16)
            active_ref[pair, :] = active
            slope = plus + 0.5 * before * (1.0 - inner * inner) * (rate + rate * 3 * 0.044715 * square)
            lower = (upper * slope).astype(BF16)
            grad_ref[pair, :] = lower
            ref[rows, :] = dot_nt(lower, expand_ref[...]).astype(BF16)
            result_ref[place, :] = dot_nn(active, shrink_ref[...]).astype(BF16)


def weight_parts(part, mine_ref, other_ref, up_mine_ref, up_other_ref, active_ref, grad_ref, bias_ref, out_ref):
    half, width = mine_ref.shape
    quarter, all_units = width // NZ, NZ * part
    for r in range(NZ):
        spot, ref = r, out_ref.at[r]
        here = slice(spot * quarter, (spot + 1) * quarter)
        total = dot_tn(mine_ref[:, here], grad_ref[0:half, :]) + dot_tn(other_ref[:, here], grad_ref[half : 2 * half, :])
        ref[0:quarter, :] = total.astype(BF16)
        units = slice(spot * part, (spot + 1) * part)
        total = dot_tn(active_ref[0:half, units], up_mine_ref[...])
        total = (total + dot_tn(active_ref[half : 2 * half, units], up_other_ref[...])).astype(BF16)
        for i in range(width // all_units):
            start = quarter + i * part
            ref[start : start + part, :] = total[:, i * all_units : (i + 1) * all_units]
    bias_ref[...] = jnp.sum(grad_ref[...].astype(F32), axis=0, keepdims=True)


def feed_forward_weights(second, up, active, before_grad):
    frames, units = active.shape
    width, part = up[0].shape[1], units // NZ
    quarter = width // NZ
    if part % 128:
        shrink = dot_tn(active, stack_rows(up)).astype(BF16).reshape(NZ, part, width)
        expand = dot_tn(stack_rows(second), before_grad).astype(BF16).reshape(NZ, quarter, units)
        bias = jnp.sum(before_grad.astype(F32), axis=0, keepdims=True)
        return bias, jnp.stack([stack_rows([expand[k], fold_columns(shrink[k], units)]) for k in range(NZ)])
    return pl.pallas_call(
        functools.partial(weight_parts, part),
        out_shape=(jax.ShapeDtypeStruct((1, units), F32), jax.ShapeDtypeStruct((NZ, 2 * quarter, units), BF16)),
        in_specs=whole(6),
        out_specs=tuple(whole(2)),
        compiler_params=pltpu.CompilerParams(vmem_limit_bytes=16 << 20),
        cost_estimate=pl.CostEstimate(
            flops=4 * frames * width * units, bytes_accessed=8 * frames * width, transcendentals=0
        ),
        name="feed_forward_weights",
    )(*second, *up, active, before_grad)


def whole(count):
    return [pl.BlockSpec(memory_space=pltpu.VMEM)] * count


def attention(core, pair, encoding, affine, w_in, bias, starts, heads, ny, size):
    half, wide = pair[0].shape[0], w_in.shape[1]
    frames, depth, width = 2 * half, pair[0].shape[1], wide // 3
    pairs = frames * frames * heads
    return pl.pallas_call(
        functools.partial(attend, heads, ny, size),
        out_shape=(
            jax.ShapeDtypeStruct((frames, depth), BF16),
            jax.ShapeDtypeStruct((frames, wide), BF16),
            jax.ShapeDtypeStruct((half, width), BF16),
            jax.ShapeDtypeStruct((half, width), BF16),
            jax.ShapeDtypeStruct((heads, frames), F32),
        ),
        in_specs=[pl.BlockSpec(memory_space=pltpu.SMEM)] + whole(7),
        out_specs=tuple(whole(5)),
        scratch_shapes=[
            pltpu.VMEM((frames, width), BF16),
            pltpu.VMEM((frames, width), BF16),
            pltpu.VMEM((width, frames), BF16),
        ],
        compiler_params=pltpu.CompilerParams(vmem_limit_bytes=16 << 20),
        cost_estimate=pl.CostEstimate(
            flops=pairs * 256 + 2 * frames * depth * wide, bytes_accessed=8 * frames * depth, transcendentals=pairs // 2
        ),
        name="attend",
    )(core, *pair, encoding, affine, w_in, bias, starts)


def attention_back(place, qkv, pair, context, w_out, w_in, starts, log_total, heads, ny, size):
    frames, wide = qkv.shape
    width = wide // 3
    depth = pair[0].shape[1]
    cut = heads == 2 and ny == 2
    pairs = frames * frames * heads
    half = jax.ShapeDtypeStruct(pair[0].shape, BF16)
    return pl.pallas_call(
        functools.partial(attend_back, heads, ny, size),
        out_shape=(
            jax.ShapeDtypeStruct((frames, wide), BF16),
            half,
            half,
            jax.ShapeDtypeStruct((2, 2, width // 2, depth // 2) if cut else (width, depth), BF16),
        ),
        in_specs=[pl.BlockSpec(memory_space=pltpu.SMEM)] + whole(9),
        out_specs=tuple(whole(4)),
        scratch_shapes=[pltpu.VMEM((frames, width), BF16)] * 4
        + [pltpu.VMEM((width, frames), BF16)]
        + [pltpu.VMEM((frames, width), F32)] * 3,
        compiler_params=pltpu.CompilerParams(vmem_limit_bytes=20 << 20),
        cost_estimate=pl.CostEstimate(
            flops=pairs * 640 + 2 * frames * depth * (wide + 2 * width),
            bytes_accessed=8 * frames * depth,
            transcendentals=pairs // 2,
        ),
        name="attend_back",
    )(place.core, qkv, *pair, *context, w_out, w_in, starts, log_total)


def feed_forward_front(core, pair, up_pair, w_expand, w_shrink, bias, size):
    frames, width = 2 * pair[0].shape[0], pair[0].shape[1]
    units = w_expand.shape[1]
    half = jax.ShapeDtypeStruct((frames // 2, width), BF16)
    inner = jax.ShapeDtypeStruct((frames, units), BF16)
    return pl.pallas_call(
        functools.partial(feed_forward, size),
        out_shape=(inner, inner, half, half, jax.ShapeDtypeStruct((frames, width), BF16)),
        in_specs=[pl.BlockSpec(memory_space=pltpu.SMEM)] + whole(7),
        out_specs=tuple(whole(5)),
        compiler_params=pltpu.CompilerParams(vmem_limit_bytes=16 << 20),
        cost_estimate=pl.CostEstimate(
            flops=8 * frames * width * units, bytes_accessed=10 * frames * width, transcendentals=frames * units
        ),
        name="feed_forward",
    )(core, *pair, *up_pair, w_expand, w_shrink, bias)


class Place:
    def __init__(self, ny):
        self.x, self.z, self.y, self.c = (lax.axis_index(a) for a in ("x", "z", "y", "c"))
        self.xy = jnp.reshape(self.x * ny + self.y, (1,)).astype(jnp.int32)
        self.core = jnp.reshape(self.c, (1,)).astype(jnp.int32)
        self.layer = jnp.reshape(self.z, (1,)).astype(jnp.int32)


def on_device(
    groups,
    ny,
    frames,
    cotangent,
    segment_lengths,
    position_offsets,
    first_gain,
    first_shift,
    inward_weight,
    query_bias,
    value_bias,
    outward_weight,
    outward_bias,
    second_gain,
    second_shift,
    expand_weight,
    expand_bias,
    shrink_weight,
    shrink_bias,
):
    place = Place(ny)
    x, z, y, c = place.x, place.z, place.y, place.c
    local_len, rows, width = frames.shape
    share = inward_weight.shape[0]
    layer = 4 * ny
    spread = NZ * ny * 2
    full_len = local_len * spread
    size = 2 * local_len
    hd = HEADS // layer
    hw = hd * (width // HEADS)
    hidden = expand_bias.shape[0]
    part = hidden // 2
    me = (c * 2 + x) * ny + y

    def sum_groups(value):
        return lax.psum(value, "g") if groups > 1 else value

    def exchange(value, axes):
        return lax.all_to_all(value, axes, 0, 0, tiled=True)

    both = to_home(jnp.concatenate([frames, cotangent], axis=2), place)
    table = jnp.stack([segment_lengths, position_offsets], axis=1)

    small = [first_gain, first_shift, query_bias, value_bias, outward_bias, second_gain, second_shift, shrink_bias]
    kinds = len(small) + hidden // share
    units = NZ * part
    packed = jnp.concatenate([v[None] for v in small] + [expand_bias.reshape(-1, share)], axis=0)
    packed = packed.reshape(-1, 3 * hw)
    extra = packed.shape[0]
    packed = jnp.pad(packed, ((0, SMALL_ROWS - extra), (0, units)))[None]
    in_cols = jnp.transpose(inward_weight.reshape(share, 3, 2, 2, ny, hw), (3, 4, 2, 0, 1, 5))
    in_cols = pick(in_cols, x).reshape(ny * 2, share, 3 * hw)
    ex_cols = pick(expand_weight.reshape(share, NZ, ny, 2, 2, part), x, 4)
    ex_cols = jnp.transpose(ex_cols, (2, 3, 0, 1, 4)).reshape(ny * 2, share, units)
    columns = jnp.concatenate([in_cols, ex_cols], axis=2)
    columns = jnp.concatenate([columns, jnp.broadcast_to(packed, (ny * 2,) + packed.shape[1:])], axis=1)
    columns, table = after(columns, table)
    columns = exchange(columns, ("y", "c"))
    other_table = hop(table, "x")

    row_x = jnp.where((z == 0) | (z == 3), 1, 0)
    table = pick(jnp.where(x == row_x, table, other_table), z >> 1)
    lengths, offsets = table[0], table[1]
    count = lengths.shape[0]
    starts = jnp.sum(
        jnp.where(jnp.arange(count)[None, :] < jnp.arange(count)[:, None], lengths[None, :], 0), axis=1
    )
    frame_ids = jnp.arange(full_len, dtype=jnp.int32)
    row_starts = jnp.max(jnp.where(starts[:, None] <= frame_ids[None, :], starts[:, None], 0), axis=0)[None, :]
    spot = jnp.arange(2 * ny)
    chunk = jnp.concatenate([(2 * (spot // ny) + i) * ny + spot % ny for i in (c, 1 - c)])
    mine = (chunk[:, None] * size + jnp.arange(size, dtype=jnp.int32)).reshape(-1)
    inside = (mine[:, None] >= starts[None, :]) & (mine[:, None] < (starts + lengths)[None, :])
    position = jnp.sum(jnp.where(inside, offsets[None, :] + mine[:, None] - starts[None, :], 0), axis=1)
    encoding = sin_cos(position, width)

    both, later_outward, columns = after(both, outward_weight, columns)
    fr, ct = both[:, :width], both[:, width:]
    outward = lax.all_gather(later_outward, SEQ, axis=0, tiled=True)
    small_part = columns[:, share : share + extra, : 3 * hw].reshape(-1, 3 * hw)
    small_part = jnp.pad(small_part, ((0, SMALL_ROWS - small_part.shape[0]), (0, 0)))
    in_part = stack_rows([columns[:, :share, : 3 * hw].reshape(-1, 3 * hw), small_part])
    in_parts = [in_part] + [hop(in_part, "z", NZ, k) for k in range(1, NZ)]
    sh_rows = lax.dynamic_slice_in_dim(shrink_weight, x * part, part, 0)
    ff_part = stack_rows([columns[:, :share, 3 * hw :].reshape(-1, units), fold_columns(sh_rows, units)])
    mine, up_mine = assemble_pair(near_parts(both, ny), place.xy)
    ff_part = jnp.broadcast_to(ff_part[None], (NZ,) + ff_part.shape)
    mine, encoding, ff_part, *in_parts = after(mine, encoding, ff_part, *in_parts)
    first_pair = [mine, hop(mine, "c")]
    w_in, small_rows = collect_inward(in_parts, place)
    ff_got = exchange(ff_part, ("z",))

    vectors = small_rows.reshape(NZ, SMALL_ROWS, 3 * hw)[:, : ny * 2 * extra]
    vectors = vectors.reshape(spread, kinds, share).astype(F32)
    expand_b = vectors[:, len(small) :].reshape(NZ, ny, 2, 2, part)
    expand_b = pick(pick(pick(expand_b, y, 1), c, 1), x, 1).reshape(1, NZ * part)
    vectors = jnp.swapaxes(vectors[:, : len(small)], 0, 1).reshape(len(small), width)
    gain_one, shift_one, query_b, value_b, outward_b, gain_two, shift_two, shrink_b = (
        vectors[i : i + 1] for i in range(len(small))
    )
    qkv_bias = jnp.concatenate(
        [
            lax.dynamic_slice_in_dim(query_b, me * hw, hw, 1),
            jnp.zeros((1, hw), F32),
            lax.dynamic_slice_in_dim(value_b, me * hw, hw, 1),
        ],
        axis=1,
    )

    first_all, qkv, *context_pair, log_total = attention(
        place.core, first_pair, encoding, vectors[:2], w_in, qkv_bias, row_starts, hd, ny, size
    )
    *context_pair, up_mine = after(*context_pair, up_mine)
    if ny == 2:
        context = by_half(c, context_pair[0][None], hop(context_pair[1], "c")[None], 0)
        context = context.reshape(2, 2, ny, size, hw)
        context = by_half(x, pick(context, x, 1)[:, None], hop(pick(context, 1 - x, 1), "x")[:, None], 1)
        context = by_half(y, pick(context, y, 2)[:, :, None], hop(pick(context, 1 - y, 2), "y")[:, :, None], 2)
    else:
        context = exchange(by_half(c, *context_pair, 0).reshape(layer, size, hw), LAYER)
    context = context.reshape(layer, size, hw)
    up_pair = [up_mine, hop(up_mine, "c")]

    inputs = fr.astype(F32) + lax.dynamic_slice_in_dim(encoding, (x * ny + y) * size, size, 0)
    normal_one, scale_one = normalize(inputs)
    context = jnp.swapaxes(context, 0, 1).reshape(size, width)
    middle = inputs + dot_nn(context, outward) + outward_b

    normal_two, scale_two = normalize(middle)
    second = (normal_two * gain_two + shift_two).astype(BF16)
    ff_got, *second_near = after(ff_got, *near_parts(second, ny))
    second_pair = both_cores(second_near, place)
    w_expand, w_shrink = collect_hidden(ff_got, width)
    active, before_grad, send, keep, out_part = feed_forward_front(
        place.core, second_pair, up_pair, w_expand, w_shrink, expand_b, size
    )
    second_parts = list(fold(keep, hop(send, "c"), place, ny))
    second_parts[0], active, before_grad = after(second_parts[0], active, before_grad)
    second_grad = finish(second_parts, ny)
    expand_b_sum, hidden_part = feed_forward_weights(second_pair, up_pair, active, before_grad)
    out_part = lax.psum_scatter(out_part, LAYER, scatter_dimension=0, tiled=True)
    second_grad, expand_b_sum = after(second_grad, expand_b_sum)
    hidden_got = exchange(hidden_part, ("z",))

    upstream = ct.astype(F32)
    middle_part, gain_two_sum, shift_two_sum = normalize_back(normal_two, scale_two, gain_two, second_grad)
    middle_grad = upstream + middle_part
    low_middle = middle_grad.astype(BF16)
    low_pair = both_cores(near_parts(low_middle, ny), place)
    w_out = lax.dynamic_slice_in_dim(outward, me * hw, hw, 0)
    mixed_grad, send, keep, outward_part = attention_back(
        place, qkv, low_pair, context_pair, w_out, w_in, row_starts, log_total, hd, ny, size
    )
    got = hop(send, "c")
    cut = outward_part if hd == 2 and ny == 2 else outward_part.reshape(2, 1, -1, width)
    far_cut = hop(pick(cut, 1 - c), "c")
    got, far_cut = after(got, far_cut)
    first_parts = list(fold(keep, got, place, ny))
    first_parts[0], mixed_late, far_cut, hidden_got = after(first_parts[0], mixed_grad, far_cut, hidden_got)
    inward_part = dot_tn(first_all, mixed_late).astype(BF16)
    first_grad = finish(first_parts, ny)
    far_cut, out_part = after(far_cut, out_part)
    line_out = by_half(c, pick(cut, c)[None], far_cut[None], 0)
    if hd == 2 and ny == 2:
        line_out = by_half(x, pick(line_out, x, 1)[:, None], hop(pick(line_out, 1 - x, 1), "x")[:, None], 1)
    inward_got = exchange(inward_part.reshape(spread, share, 3 * hw), SEQ)
    input_part, gain_one_sum, shift_one_sum = normalize_back(normal_one, scale_one, vectors[:1], first_grad)
    late = (middle_grad + input_part).astype(BF16)
    late, out_part, hidden_got, line_out = after(late, out_part, hidden_got, line_out)
    hidden_sum = sum_sources(hidden_got, NZ)
    frames_grad = to_origin(late, place)
    inward_got, out_part = after(inward_got, out_part)
    layer_output = to_origin((middle + out_part.astype(F32) + shrink_b).astype(BF16), place)

    split = width // 2
    hidden_sum = sum_groups(hidden_sum.reshape(-1, units)).astype(BF16)
    line = hidden_sum[: width // NZ].reshape(ny, 2, share, units)
    if ny == 2:
        line = by_half(c, pick(line, c, 1)[:, None], hop(pick(line, 1 - c, 1), "c")[:, None], 1)
        line = by_half(y, pick(line, y)[None], hop(pick(line, 1 - y), "y")[None], 0)
    else:
        line = exchange(line.reshape(ny * 2, share, units), ("y", "c"))
    mine = stack_rows([line.reshape(-1, units), hidden_sum[width // NZ :]])
    other = hop(mine, "x")

    def full_hidden(other):
        pair = [unfold_columns(v[width // NZ :], width // units) for v in (mine, other)]
        g_shrink = by_half(x, *pair, 0).astype(F32)
        pair = [v[: width // NZ].reshape(ny, 2, 1, share, NZ, part) for v in (mine, other)]
        return g_shrink, jnp.transpose(by_half(x, *pair, 2), (3, 4, 0, 1, 2, 5)).reshape(share, -1).astype(F32)

    if hd == 2 and ny == 2:
        line = line_out.reshape(2, 2, share, split)
        keep, send = pick(line, z >> 1), pick(line, 1 - (z >> 1))
        line = keep.astype(F32) + hop(send, "z", NZ, 2).astype(F32)
        keep, send = pick(line, z & 1), pick(line, 1 - (z & 1))
        out_got = keep + hop(send.astype(BF16), "z", NZ, 1).astype(F32)
        inward_late, out_got = after(inward_got, out_got)
        out_sum = sum_groups(out_got.astype(F32)).astype(BF16)
        g_outward = by_half(x, out_sum, hop(out_sum, "x"), 1).astype(F32)
    else:
        cut = lax.dynamic_update_slice(jnp.zeros((width, width), BF16), outward_part, (me * hw, 0))
        g_outward = lax.psum_scatter(cut, SEQ, scatter_dimension=0, tiled=True)
        g_outward = lax.psum(g_outward.astype(F32), ("g", "x"))

    mixed_sum = jnp.sum(mixed_grad.astype(F32), axis=0)

    def from_heads(value):
        return lax.dynamic_update_slice(jnp.zeros((width,), F32), value, (me * hw,))

    flat = lax.optimization_barrier(jnp.stack(
        [
            gain_one_sum,
            shift_one_sum,
            from_heads(mixed_sum[:hw]),
            from_heads(mixed_sum[2 * hw :]),
            jnp.sum(low_middle.astype(F32), axis=0),
            gain_two_sum,
            shift_two_sum,
            jnp.sum(upstream, axis=0),
        ]
    ))
    small_len = len(small) * share
    sums = jnp.swapaxes(flat.reshape(len(small), spread, share), 0, 1).reshape(spread, small_len)
    spot = jnp.zeros((NZ, ny, 2, 2, part), F32)
    spot = lax.dynamic_update_slice(spot, expand_b_sum.reshape(NZ, 1, 1, 1, part), (0, y, c, x, 0))
    sums = jnp.concatenate([sums, spot.reshape(spread, hidden)], axis=1)
    inward_got, sums = after(inward_got, sums)
    sums = jnp.broadcast_to(sums[None], (2,) + sums.shape).reshape(2 * spread, -1, 128)
    total = sum_groups(jnp.sum(exchange(sums, ("x",) + SEQ), axis=0)).reshape(-1)
    frames_grad, total, other = after(frames_grad, total, other)
    g_shrink, g_expand = full_hidden(other)
    g_small = total[:small_len].reshape(len(small), share)
    g_expand_b = total[small_len:]
    inward_got = inward_late if hd == 2 and ny == 2 else inward_got
    inward_sum = sum_groups(sum_sources(inward_got, NZ)).astype(BF16)
    g_inward = [v.reshape(ny, 2, 1, share, 3, hw) for v in (inward_sum, hop(inward_sum, "x"))]
    g_inward = jnp.transpose(by_half(x, *g_inward, 2), (3, 4, 1, 2, 0, 5)).reshape(share, -1).astype(F32)

    return (
        layer_output,
        frames_grad.astype(F32),
        g_small[0],
        g_small[1],
        g_inward,
        g_small[2],
        g_small[3],
        g_outward,
        g_small[4],
        g_small[5],
        g_small[6],
        g_expand,
        g_expand_b,
        g_shrink,
        g_small[7],
    )


def solution(mesh):
    batch, seq = mesh.shape["batch"], mesh.shape["seq"]
    groups, ny = batch // 2, seq // (2 * NZ)
    fine = Mesh(mesh.devices.reshape(groups, 2, NZ, ny, 2), ("g", "x", "z", "y", "c"))
    b, s = ("g", "x"), ("z", "y", "c")
    in_specs = (
        P(s, b, None),
        P(s, b, None),
        P(b, None),
        P(b, None),
        P(s),
        P(s),
        P(s, None),
        P(s),
        P(s),
        P(s, None),
        P(s),
        P(s),
        P(s),
        P(s, None),
        P(s),
        P(s, None),
        P(s),
    )
    out_specs = (
        P(s, b, None),
        P(s, b, None),
        P(s),
        P(s),
        P(s, None),
        P(s),
        P(s),
        P(s, None),
        P(s),
        P(s),
        P(s),
        P(s, None),
        P(s),
        P(s, None),
        P(s),
    )
    return jax.shard_map(
        functools.partial(on_device, groups, ny), mesh=fine, in_specs=in_specs, out_specs=out_specs, check_vma=False
    )
```

```python
import functools
import math

import jax
import jax.numpy as jnp
from jax import lax
from jax.experimental import pallas as pl
from jax.experimental.pallas import tpu as pltpu
from jax.sharding import Mesh, PartitionSpec as P


HEADS = 16
NZ = 4
SMALL_ROWS = 16
NORM_EPS = 1e-05
NEG = -1e30
F32 = jnp.float32
BF16 = jnp.bfloat16
LAYER_OF_ROW = (1, 2, 0, 3)
SWAP = [(0, 1), (1, 0)]
LAYER = ("c", "x", "y")
SEQ = ("z", "y", "c")


def xor_perm(count, k):
    return [(i, i ^ k) for i in range(count)]


def hop(value, axis, count=2, k=1):
    return lax.ppermute(value, axis, xor_perm(count, k))


def pick(value, index, axis=0):
    return lax.dynamic_index_in_dim(value, index, axis, keepdims=False)


def stack_rows(parts):
    return jnp.concatenate(parts, axis=0)


def assemble_body(pieces, size, place_ref, *refs):
    out_ref = refs[pieces]
    for r in range(pieces):
        spot = place_ref[0] ^ r
        out_ref[pl.ds(pl.multiple_of(spot * size, size), size), :] = refs[r][...]


def assemble(parts, me):
    size, width = parts[0].shape
    count = len(parts)
    return pl.pallas_call(
        functools.partial(assemble_body, count, size),
        out_shape=jax.ShapeDtypeStruct((count * size, width), parts[0].dtype),
        in_specs=[pl.BlockSpec(memory_space=pltpu.SMEM)] + whole(count),
        out_specs=whole(1)[0],
        compiler_params=pltpu.CompilerParams(vmem_limit_bytes=4 << 20),
        cost_estimate=pl.CostEstimate(flops=0, bytes_accessed=4 * count * size * width, transcendentals=0),
        name="assemble",
    )(me, *parts)


def assemble_pair_body(pieces, size, place_ref, *refs):
    left_ref, right_ref = refs[pieces:]
    width = left_ref.shape[1]
    for r in range(pieces):
        rows = pl.ds(pl.multiple_of((place_ref[0] ^ r) * size, size), size)
        left_ref[rows, :] = refs[r][:, 0:width]
        right_ref[rows, :] = refs[r][:, width : 2 * width]


def assemble_pair(parts, me):
    size, width = parts[0].shape
    count = len(parts)
    return pl.pallas_call(
        functools.partial(assemble_pair_body, count, size),
        out_shape=[jax.ShapeDtypeStruct((count * size, width // 2), parts[0].dtype)] * 2,
        in_specs=[pl.BlockSpec(memory_space=pltpu.SMEM)] + whole(count),
        out_specs=whole(2),
        compiler_params=pltpu.CompilerParams(vmem_limit_bytes=4 << 20),
        cost_estimate=pl.CostEstimate(flops=0, bytes_accessed=4 * count * size * width, transcendentals=0),
        name="assemble_pair",
    )(me, *parts)


def near_parts(block, ny):
    return [block] + [lax.ppermute(block, ("x", "y"), xor_perm(2 * ny, r)) for r in range(1, 2 * ny)]


def both_cores(parts, place):
    mine = assemble(parts, place.xy)
    return mine, hop(mine, "c")


def fold_body(count, size, place_ref, keep_ref, got_ref, own_ref, *out_refs):
    for r in range(count):
        spot = place_ref[0] ^ r
        here = pl.ds(pl.multiple_of(spot * size, size), size)
        value = keep_ref[here, :].astype(F32) + got_ref[here, :].astype(F32)
        if r == 0:
            own_ref[...] = value
        else:
            out_refs[r - 1][...] = value.astype(BF16)


def fold(keep, got, place, ny):
    rows, width = keep.shape
    count = 2 * ny
    size = rows // count
    return pl.pallas_call(
        functools.partial(fold_body, count, size),
        out_shape=[jax.ShapeDtypeStruct((size, width), F32)] + [jax.ShapeDtypeStruct((size, width), BF16)] * (count - 1),
        in_specs=[pl.BlockSpec(memory_space=pltpu.SMEM)] + whole(2),
        out_specs=whole(count),
        compiler_params=pltpu.CompilerParams(vmem_limit_bytes=4 << 20),
        cost_estimate=pl.CostEstimate(flops=count * size * width, bytes_accessed=6 * count * size * width, transcendentals=0),
        name="fold",
    )(place.xy, keep, got)


def finish(parts, ny):
    own = parts[0]
    for r in range(1, 2 * ny):
        own = own + lax.ppermute(parts[r], ("x", "y"), xor_perm(2 * ny, r)).astype(F32)
    return own


def fold_columns(value, units):
    return stack_rows([value[:, i : i + units] for i in range(0, value.shape[1], units)])


def unfold_columns(value, count):
    size = value.shape[0] // count
    return jnp.concatenate([value[i * size : (i + 1) * size] for i in range(count)], axis=1)


def collect_inward_body(place_ref, *refs):
    weight_ref, small_ref = refs[NZ:]
    quarter = weight_ref.shape[0] // NZ
    for r in range(NZ):
        spot = place_ref[0] ^ r
        weight_ref[pl.ds(pl.multiple_of(spot * quarter, quarter), quarter), :] = refs[r][0:quarter, :]
        rows = pl.ds(pl.multiple_of(spot * SMALL_ROWS, SMALL_ROWS), SMALL_ROWS)
        small_ref[rows, :] = refs[r][quarter : quarter + SMALL_ROWS, :]


def collect_inward(parts, place):
    rows, width = parts[0].shape
    return pl.pallas_call(
        collect_inward_body,
        out_shape=[jax.ShapeDtypeStruct((NZ * n, width), BF16) for n in (rows - SMALL_ROWS, SMALL_ROWS)],
        in_specs=[pl.BlockSpec(memory_space=pltpu.SMEM)] + whole(NZ),
        out_specs=whole(2),
        compiler_params=pltpu.CompilerParams(vmem_limit_bytes=4 << 20),
        cost_estimate=pl.CostEstimate(flops=0, bytes_accessed=16 * rows * width, transcendentals=0),
        name="collect_inward",
    )(place.layer, *parts)


def collect_hidden_body(parts_ref, expand_ref, shrink_ref):
    quarter = expand_ref.shape[0] // NZ
    part, units = shrink_ref.shape[0] // NZ, expand_ref.shape[1]
    for r in range(NZ):
        expand_ref[r * quarter : (r + 1) * quarter, :] = parts_ref[r, 0:quarter, :]
        for i in range(shrink_ref.shape[1] // units):
            start = quarter + i * part
            here = slice(r * part, (r + 1) * part)
            shrink_ref[here, i * units : (i + 1) * units] = parts_ref[r, start : start + part, :]


def collect_hidden(parts, width):
    units = parts.shape[2]
    return pl.pallas_call(
        collect_hidden_body,
        out_shape=[jax.ShapeDtypeStruct((width, units), BF16), jax.ShapeDtypeStruct((units, width), BF16)],
        in_specs=whole(1),
        out_specs=whole(2),
        compiler_params=pltpu.CompilerParams(vmem_limit_bytes=4 << 20),
        cost_estimate=pl.CostEstimate(flops=0, bytes_accessed=4 * parts.size, transcendentals=0),
        name="collect_hidden",
    )(parts)


def unpack_hidden_body(lines, place_ref, mine_ref, other_ref, expand_ref, shrink_ref):
    share = expand_ref.shape[0]
    part = shrink_ref.shape[0] // 2
    units, deep = mine_ref.shape[1], lines * share
    for ref, slot in ((mine_ref, place_ref[0]), (other_ref, 1 - place_ref[0])):
        for line in range(lines):
            for k in range(NZ):
                spot = ((k * lines + line) * 2 + slot) * part
                value = ref[line * share : (line + 1) * share, k * part : (k + 1) * part].astype(F32)
                expand_ref[:, pl.ds(pl.multiple_of(spot, part), part)] = value
        rows = pl.ds(pl.multiple_of(slot * part, part), part)
        for i in range(shrink_ref.shape[1] // units):
            start = deep + i * part
            shrink_ref[rows, i * units : (i + 1) * units] = ref[start : start + part, :].astype(F32)


def unpack_hidden(place, mine, other, lines, share, part, width):
    return pl.pallas_call(
        functools.partial(unpack_hidden_body, lines),
        out_shape=[
            jax.ShapeDtypeStruct((share, 2 * NZ * lines * part), F32),
            jax.ShapeDtypeStruct((2 * part, width), F32),
        ],
        in_specs=[pl.BlockSpec(memory_space=pltpu.SMEM)] + whole(2),
        out_specs=whole(2),
        compiler_params=pltpu.CompilerParams(vmem_limit_bytes=4 << 20),
        cost_estimate=pl.CostEstimate(flops=0, bytes_accessed=12 * mine.size, transcendentals=0),
        name="unpack_hidden",
    )(jnp.reshape(place.x, (1,)).astype(jnp.int32), mine, other)


def rehome_flat(x, z, c):
    return (x * NZ + z) * 2 + c


def rehome_perm(k):
    return [
        (rehome_flat(x, z, c), rehome_flat(z >> 1, LAYER_OF_ROW[2 * x + (c ^ k)], z & 1))
        for x in range(2)
        for z in range(NZ)
        for c in range(2)
    ]


def to_home(block, place):
    got = [
        lax.ppermute(jnp.where(place.c == k, block[:, 0], block[:, 1]), ("x", "z", "c"), rehome_perm(k))
        for k in range(2)
    ]
    first = place.z < 2
    return stack_rows([jnp.where(first, got[0], got[1]), jnp.where(first, got[1], got[0])])


def to_origin(block, place):
    half = block.shape[0] // 2
    first = place.z < 2
    low, high = block[:half], block[half:]
    sent = [jnp.where(first, low, high), jnp.where(first, high, low)]
    got = [
        lax.ppermute(sent[k], ("x", "z", "c"), [(b, a) for a, b in rehome_perm(k)]) for k in range(2)
    ]
    return jnp.stack(
        [jnp.where(place.c == 0, got[0], got[1]), jnp.where(place.c == 0, got[1], got[0])], axis=1
    )


def after(first, *values):
    return lax.optimization_barrier((first, *values))


def sum_sources(value, count):
    return jnp.sum(value.reshape((count, -1) + value.shape[1:]).astype(F32), axis=0)


def by_half(x, mine, other, axis):
    return jnp.concatenate([jnp.where(x == 0, mine, other), jnp.where(x == 0, other, mine)], axis=axis)


def sin_cos(position, width):
    feature = jnp.arange(width, dtype=jnp.int32)
    rates = jnp.exp((feature // 2).astype(F32) * (-2.0 * math.log(10000.0) / width))
    angle = position.astype(F32)[:, None] * rates[None, :]
    turn = jnp.round(angle * (2.0 / math.pi))
    rest = angle - turn * 1.5703125
    rest = rest - turn * 0.00048375129699707031
    rest = rest - turn * 7.5497899548918861e-08
    quadrant = turn.astype(jnp.int32) + (feature % 2)[None, :]
    square = rest * rest
    sine = rest + rest * square * (
        -0.16666666641626524 + square * (0.008333329385889463 + square * (-0.00019839334836096632 + square * 2.718311493989822e-06))
    )
    cosine = 1.0 + square * (
        -0.49999999725103100 + square * (0.04166662332373906 + square * (-0.001388676377460993 + square * 2.439044879627741e-05))
    )
    value = jnp.where((quadrant & 1) == 0, sine, cosine)
    return jnp.where((quadrant & 2) == 0, value, -value)


def normalize(values):
    center = values - jnp.mean(values, axis=-1, keepdims=True)
    scale = lax.rsqrt(jnp.mean(center * center, axis=-1, keepdims=True) + NORM_EPS)
    return center * scale, scale


def normalize_back(normal, scale, gain, upstream):
    scaled = upstream * gain
    inner = scaled - jnp.mean(scaled, axis=-1, keepdims=True)
    inner = inner - normal * jnp.mean(scaled * normal, axis=-1, keepdims=True)
    return inner * scale, jnp.sum(upstream * normal, axis=0), jnp.sum(upstream, axis=0)


def dot_nt(a, b):
    return lax.dot_general(a, b, (((1,), (1,)), ((), ())), preferred_element_type=F32)


def dot_tn(a, b):
    return lax.dot_general(a, b, (((0,), (0,)), ((), ())), preferred_element_type=F32)


def dot_nn(a, b):
    return jnp.dot(a, b, preferred_element_type=F32)


BLOCK = 256


def chunk_owner(chunk, ny):
    outer, y = divmod(chunk, ny)
    return ((outer & 1) * 2 + (outer >> 1)) * ny + y


def lane_parts(heads, width):
    if heads == 1:
        return [None]
    lane = lax.broadcasted_iota(jnp.int32, (1, width), 1)
    return [(lane >= h * (width // heads)) & (lane < (h + 1) * (width // heads)) for h in range(heads)]


def only(value, lanes):
    return value if lanes is None else jnp.where(lanes, value, jnp.zeros_like(value))


def allowed_pairs(start_ref, first, total):
    key = lax.broadcasted_iota(jnp.int32, (total, BLOCK), 0)
    frame = first + lax.broadcasted_iota(jnp.int32, (total, BLOCK), 1)
    return (key >= start_ref[:, first : first + BLOCK]) & (key <= frame)


def chunk_rows(chunk, ny, size, core):
    half, spot = divmod(chunk_owner(chunk, ny), 2 * ny)
    return pl.ds(pl.multiple_of(((half ^ core) * (2 * ny) + spot) * size, size), size)


def attend(
    heads,
    ny,
    size,
    core_ref,
    mine_ref,
    other_ref,
    encoding_ref,
    affine_ref,
    weight_ref,
    bias_ref,
    start_ref,
    first_ref,
    qkv_ref,
    near_ref,
    far_ref,
    log_ref,
    q_s,
    k_s,
    vt_s,
):
    count = 4 * ny
    width = q_s.shape[1]
    core = core_ref[0]
    step = 2 * size
    half = mine_ref.shape[0]
    for base, ref in ((0, mine_ref), (half, other_ref)):
        for start in range(0, half, step):
            rows = slice(base + start, base + start + step)
            normal, _ = normalize(ref[start : start + step, :].astype(F32) + encoding_ref[rows, :])
            value = (normal * affine_ref[0:1, :] + affine_ref[1:2, :]).astype(BF16)
            first_ref[rows, :] = value
            qkv_ref[rows, :] = (dot_nn(value, weight_ref[...]) + bias_ref[...]).astype(BF16)
    for chunk in range(count):
        rows = chunk_rows(chunk, ny, size, core)
        here = slice(chunk * size, (chunk + 1) * size)
        q_s[here, :] = qkv_ref[rows, 0:width] * 0.125
        k_s[here, :] = qkv_ref[rows, width : 2 * width]
        vt_s[:, here] = jnp.transpose(qkv_ref[rows, 2 * width : 3 * width].astype(F32)).astype(BF16)
    lanes = lane_parts(heads, width)
    each = width // heads
    for block in range(count * size // BLOCK):
        first = block * BLOCK
        total = first + BLOCK
        allowed = allowed_pairs(start_ref, first, total)
        q_block = q_s[first:total, :]
        contexts = []
        for h in range(heads):
            scores = dot_nt(k_s[0:total, :], only(q_block, lanes[h]))
            scores = jnp.where(allowed, scores, NEG)
            top = jnp.max(scores, axis=0, keepdims=True)
            weight = jnp.exp(scores - top)
            mass = jnp.sum(weight, axis=0, keepdims=True)
            part = dot_nn(vt_s[h * each : (h + 1) * each, 0:total], weight.astype(BF16))
            contexts.append(part / mass)
            log_ref[h : h + 1, first:total] = top + jnp.log(mass)
        context = contexts[0] if heads == 1 else jnp.concatenate(contexts, axis=0)
        context = jnp.transpose(context).astype(BF16)
        for sub in range(BLOCK // size):
            owner = chunk_owner(block * (BLOCK // size) + sub, ny)
            side, spot = divmod(owner, 2 * ny)
            rows, piece = slice(spot * size, (spot + 1) * size), context[sub * size : (sub + 1) * size]

            @pl.when(core == side)
            def _(rows=rows, piece=piece):
                near_ref[rows, :] = piece

            @pl.when(core != side)
            def _(rows=rows, piece=piece):
                far_ref[rows, :] = piece


def attend_back(
    heads,
    ny,
    size,
    core_ref,
    qkv_ref,
    mine_ref,
    other_ref,
    near_ref,
    far_ref,
    outward_ref,
    weight_ref,
    start_ref,
    log_ref,
    out_ref,
    send_ref,
    keep_ref,
    outward_grad_ref,
    q_s,
    k_s,
    v_s,
    g_s,
    kt_s,
    dq_s,
    dk_s,
    dv_s,
):
    count = 4 * ny
    width = q_s.shape[1]
    core = core_ref[0]
    half = mine_ref.shape[0]
    step = 2 * size
    for base, ref in ((0, mine_ref), (half, other_ref)):
        for start in range(0, half, step):
            rows = slice(start, start + step)
            out_ref[base + start : base + start + step, 0:width] = dot_nt(ref[rows, :], outward_ref[...]).astype(BF16)
    for chunk in range(count):
        rows = chunk_rows(chunk, ny, size, core)
        here = slice(chunk * size, (chunk + 1) * size)
        q_s[here, :] = qkv_ref[rows, 0:width] * 0.125
        key = qkv_ref[rows, width : 2 * width]
        k_s[here, :] = key
        kt_s[:, here] = jnp.transpose(key.astype(F32)).astype(BF16)
        v_s[here, :] = qkv_ref[rows, 2 * width : 3 * width]
        g_s[here, :] = out_ref[rows, 0:width]
    dk_s[...] = jnp.zeros_like(dk_s)
    dv_s[...] = jnp.zeros_like(dv_s)
    lanes = lane_parts(heads, width)
    each = width // heads
    for block in range(count * size // BLOCK):
        first = block * BLOCK
        total = first + BLOCK
        allowed = allowed_pairs(start_ref, first, total)
        q_block, g_block = q_s[first:total, :], g_s[first:total, :]
        queries = []
        for h in range(heads):
            q_one, g_one = only(q_block, lanes[h]), only(g_block, lanes[h])
            scores = dot_nt(k_s[0:total, :], q_one)
            probs = jnp.where(allowed, jnp.exp(scores - log_ref[h : h + 1, first:total]), 0.0)
            prob_grad = dot_nt(v_s[0:total, :], g_one)
            delta = jnp.sum(probs * prob_grad, axis=0, keepdims=True)
            score_grad = (probs * (prob_grad - delta)).astype(BF16)
            dv_s[0:total, :] += dot_nn(probs.astype(BF16), g_one)
            dk_s[0:total, :] += dot_nn(score_grad, q_one)
            queries.append(dot_nn(kt_s[h * each : (h + 1) * each, 0:total], score_grad))
        query_grad = queries[0] if heads == 1 else jnp.concatenate(queries, axis=0)
        dq_s[first:total, :] = jnp.transpose(query_grad) * 0.125
    for chunk in range(count):
        rows = chunk_rows(chunk, ny, size, core)
        here = slice(chunk * size, (chunk + 1) * size)
        out_ref[rows, 0:width] = dq_s[here, :].astype(BF16)
        out_ref[rows, width : 2 * width] = dk_s[here, :].astype(BF16)
        out_ref[rows, 2 * width : 3 * width] = dv_s[here, :].astype(BF16)
    for ref, base in ((send_ref, half), (keep_ref, 0)):
        for start in range(0, half, step):
            rows = slice(base + start, base + start + step)
            ref[start : start + step, :] = dot_nt(out_ref[rows, :], weight_ref[...]).astype(BF16)
    total = dot_tn(near_ref[...], mine_ref[...]) + dot_tn(far_ref[...], other_ref[...])
    total = total.astype(BF16)
    if len(outward_grad_ref.shape) == 2:
        outward_grad_ref[...] = total
    else:
        rows, columns = outward_grad_ref.shape[2:]
        for i in range(4):
            start, left = (i >> 1) * rows, (i & 1) * columns
            outward_grad_ref[i >> 1, i & 1] = total[start : start + rows, left : left + columns]


def feed_forward(
    size,
    core_ref,
    mine_ref,
    other_ref,
    up_mine_ref,
    up_other_ref,
    expand_ref,
    shrink_ref,
    bias_ref,
    active_ref,
    grad_ref,
    send_ref,
    keep_ref,
    result_ref,
):
    half = keep_ref.shape[0]
    step = 2 * size
    rate = math.sqrt(2.0 / math.pi)
    core = core_ref[0]
    sides = ((send_ref, other_ref, up_other_ref, half, 1 - core), (keep_ref, mine_ref, up_mine_ref, 0, core))
    for ref, source_ref, up_ref, base, side in sides:
        for start in range(0, half, step):
            rows = slice(start, start + step)
            pair = slice(base + start, base + start + step)
            place = pl.ds(pl.multiple_of(side * half + start, step), step)
            before = dot_nn(source_ref[rows, :], expand_ref[...]) + bias_ref[...]
            upper = dot_nt(up_ref[rows, :], shrink_ref[...])
            square = before * before
            inner = jnp.tanh(rate * (before + 0.044715 * before * square))
            plus = 0.5 * (1.0 + inner)
            active = (before * plus).astype(BF16)
            active_ref[pair, :] = active
            slope = plus + 0.5 * before * (1.0 - inner * inner) * (rate + rate * 3 * 0.044715 * square)
            lower = (upper * slope).astype(BF16)
            grad_ref[pair, :] = lower
            ref[rows, :] = dot_nt(lower, expand_ref[...]).astype(BF16)
            result_ref[place, :] = dot_nn(active, shrink_ref[...]).astype(BF16)


def weight_parts(part, mine_ref, other_ref, up_mine_ref, up_other_ref, active_ref, grad_ref, bias_ref, out_ref):
    half, width = mine_ref.shape
    quarter, all_units = width // NZ, NZ * part
    for r in range(NZ):
        spot, ref = r, out_ref.at[r]
        here = slice(spot * quarter, (spot + 1) * quarter)
        total = dot_tn(mine_ref[:, here], grad_ref[0:half, :]) + dot_tn(other_ref[:, here], grad_ref[half : 2 * half, :])
        ref[0:quarter, :] = total.astype(BF16)
        units = slice(spot * part, (spot + 1) * part)
        total = dot_tn(active_ref[0:half, units], up_mine_ref[...])
        total = (total + dot_tn(active_ref[half : 2 * half, units], up_other_ref[...])).astype(BF16)
        for i in range(width // all_units):
            start = quarter + i * part
            ref[start : start + part, :] = total[:, i * all_units : (i + 1) * all_units]
    bias_ref[...] = jnp.sum(grad_ref[...].astype(F32), axis=0, keepdims=True)


def feed_forward_weights(second, up, active, before_grad):
    frames, units = active.shape
    width, part = up[0].shape[1], units // NZ
    quarter = width // NZ
    if part % 128:
        shrink = dot_tn(active, stack_rows(up)).astype(BF16).reshape(NZ, part, width)
        expand = dot_tn(stack_rows(second), before_grad).astype(BF16).reshape(NZ, quarter, units)
        bias = jnp.sum(before_grad.astype(F32), axis=0, keepdims=True)
        return bias, jnp.stack([stack_rows([expand[k], fold_columns(shrink[k], units)]) for k in range(NZ)])
    return pl.pallas_call(
        functools.partial(weight_parts, part),
        out_shape=(jax.ShapeDtypeStruct((1, units), F32), jax.ShapeDtypeStruct((NZ, 2 * quarter, units), BF16)),
        in_specs=whole(6),
        out_specs=tuple(whole(2)),
        compiler_params=pltpu.CompilerParams(vmem_limit_bytes=16 << 20),
        cost_estimate=pl.CostEstimate(
            flops=4 * frames * width * units, bytes_accessed=8 * frames * width, transcendentals=0
        ),
        name="feed_forward_weights",
    )(*second, *up, active, before_grad)


def whole(count):
    return [pl.BlockSpec(memory_space=pltpu.VMEM)] * count


def attention(core, pair, encoding, affine, w_in, bias, starts, heads, ny, size):
    half, wide = pair[0].shape[0], w_in.shape[1]
    frames, depth, width = 2 * half, pair[0].shape[1], wide // 3
    pairs = frames * frames * heads
    return pl.pallas_call(
        functools.partial(attend, heads, ny, size),
        out_shape=(
            jax.ShapeDtypeStruct((frames, depth), BF16),
            jax.ShapeDtypeStruct((frames, wide), BF16),
            jax.ShapeDtypeStruct((half, width), BF16),
            jax.ShapeDtypeStruct((half, width), BF16),
            jax.ShapeDtypeStruct((heads, frames), F32),
        ),
        in_specs=[pl.BlockSpec(memory_space=pltpu.SMEM)] + whole(7),
        out_specs=tuple(whole(5)),
        scratch_shapes=[
            pltpu.VMEM((frames, width), BF16),
            pltpu.VMEM((frames, width), BF16),
            pltpu.VMEM((width, frames), BF16),
        ],
        compiler_params=pltpu.CompilerParams(vmem_limit_bytes=16 << 20),
        cost_estimate=pl.CostEstimate(
            flops=pairs * 256 + 2 * frames * depth * wide, bytes_accessed=8 * frames * depth, transcendentals=pairs // 2
        ),
        name="attend",
    )(core, *pair, encoding, affine, w_in, bias, starts)


def attention_back(place, qkv, pair, context, w_out, w_in, starts, log_total, heads, ny, size):
    frames, wide = qkv.shape
    width = wide // 3
    depth = pair[0].shape[1]
    cut = heads == 2 and ny == 2
    pairs = frames * frames * heads
    half = jax.ShapeDtypeStruct(pair[0].shape, BF16)
    return pl.pallas_call(
        functools.partial(attend_back, heads, ny, size),
        out_shape=(
            jax.ShapeDtypeStruct((frames, wide), BF16),
            half,
            half,
            jax.ShapeDtypeStruct((2, 2, width // 2, depth // 2) if cut else (width, depth), BF16),
        ),
        in_specs=[pl.BlockSpec(memory_space=pltpu.SMEM)] + whole(9),
        out_specs=tuple(whole(4)),
        scratch_shapes=[pltpu.VMEM((frames, width), BF16)] * 4
        + [pltpu.VMEM((width, frames), BF16)]
        + [pltpu.VMEM((frames, width), F32)] * 3,
        compiler_params=pltpu.CompilerParams(vmem_limit_bytes=20 << 20),
        cost_estimate=pl.CostEstimate(
            flops=pairs * 640 + 2 * frames * depth * (wide + 2 * width),
            bytes_accessed=8 * frames * depth,
            transcendentals=pairs // 2,
        ),
        name="attend_back",
    )(place.core, qkv, *pair, *context, w_out, w_in, starts, log_total)


def feed_forward_front(core, pair, up_pair, w_expand, w_shrink, bias, size):
    frames, width = 2 * pair[0].shape[0], pair[0].shape[1]
    units = w_expand.shape[1]
    half = jax.ShapeDtypeStruct((frames // 2, width), BF16)
    inner = jax.ShapeDtypeStruct((frames, units), BF16)
    return pl.pallas_call(
        functools.partial(feed_forward, size),
        out_shape=(inner, inner, half, half, jax.ShapeDtypeStruct((frames, width), BF16)),
        in_specs=[pl.BlockSpec(memory_space=pltpu.SMEM)] + whole(7),
        out_specs=tuple(whole(5)),
        compiler_params=pltpu.CompilerParams(vmem_limit_bytes=16 << 20),
        cost_estimate=pl.CostEstimate(
            flops=8 * frames * width * units, bytes_accessed=10 * frames * width, transcendentals=frames * units
        ),
        name="feed_forward",
    )(core, *pair, *up_pair, w_expand, w_shrink, bias)


class Place:
    def __init__(self, ny):
        self.x, self.z, self.y, self.c = (lax.axis_index(a) for a in ("x", "z", "y", "c"))
        self.xy = jnp.reshape(self.x * ny + self.y, (1,)).astype(jnp.int32)
        self.core = jnp.reshape(self.c, (1,)).astype(jnp.int32)
        self.layer = jnp.reshape(self.z, (1,)).astype(jnp.int32)


def on_device(
    groups,
    ny,
    frames,
    cotangent,
    segment_lengths,
    position_offsets,
    first_gain,
    first_shift,
    inward_weight,
    query_bias,
    value_bias,
    outward_weight,
    outward_bias,
    second_gain,
    second_shift,
    expand_weight,
    expand_bias,
    shrink_weight,
    shrink_bias,
):
    place = Place(ny)
    x, z, y, c = place.x, place.z, place.y, place.c
    local_len, rows, width = frames.shape
    share = inward_weight.shape[0]
    layer = 4 * ny
    spread = NZ * ny * 2
    full_len = local_len * spread
    size = 2 * local_len
    hd = HEADS // layer
    hw = hd * (width // HEADS)
    hidden = expand_bias.shape[0]
    part = hidden // 2
    me = (c * 2 + x) * ny + y

    def sum_groups(value):
        return lax.psum(value, "g") if groups > 1 else value

    def exchange(value, axes):
        return lax.all_to_all(value, axes, 0, 0, tiled=True)

    both = to_home(jnp.concatenate([frames, cotangent], axis=2), place)
    table = jnp.stack([segment_lengths, position_offsets], axis=1)

    small = [first_gain, first_shift, query_bias, value_bias, outward_bias, second_gain, second_shift, shrink_bias]
    kinds = len(small) + hidden // share
    units = NZ * part
    packed = jnp.concatenate([v[None] for v in small] + [expand_bias.reshape(-1, share)], axis=0)
    packed = packed.reshape(-1, 3 * hw)
    extra = packed.shape[0]
    packed = jnp.pad(packed, ((0, SMALL_ROWS - extra), (0, units)))[None]
    in_cols = jnp.transpose(inward_weight.reshape(share, 3, 2, 2, ny, hw), (3, 4, 2, 0, 1, 5))
    in_cols = pick(in_cols, x).reshape(ny * 2, share, 3 * hw)
    ex_cols = pick(expand_weight.reshape(share, NZ, ny, 2, 2, part), x, 4)
    ex_cols = jnp.transpose(ex_cols, (2, 3, 0, 1, 4)).reshape(ny * 2, share, units)
    columns = jnp.concatenate([in_cols, ex_cols], axis=2)
    columns = jnp.concatenate([columns, jnp.broadcast_to(packed, (ny * 2,) + packed.shape[1:])], axis=1)
    columns, table = after(columns, table)
    columns = exchange(columns, ("y", "c"))
    other_table = hop(table, "x")

    row_x = jnp.where((z == 0) | (z == 3), 1, 0)
    table = pick(jnp.where(x == row_x, table, other_table), z >> 1)
    lengths, offsets = table[0], table[1]
    count = lengths.shape[0]
    starts = jnp.sum(
        jnp.where(jnp.arange(count)[None, :] < jnp.arange(count)[:, None], lengths[None, :], 0), axis=1
    )
    frame_ids = jnp.arange(full_len, dtype=jnp.int32)
    row_starts = jnp.max(jnp.where(starts[:, None] <= frame_ids[None, :], starts[:, None], 0), axis=0)[None, :]
    spot = jnp.arange(2 * ny)
    chunk = jnp.concatenate([(2 * (spot // ny) + i) * ny + spot % ny for i in (c, 1 - c)])
    mine = (chunk[:, None] * size + jnp.arange(size, dtype=jnp.int32)).reshape(-1)
    inside = (mine[:, None] >= starts[None, :]) & (mine[:, None] < (starts + lengths)[None, :])
    position = jnp.sum(jnp.where(inside, offsets[None, :] + mine[:, None] - starts[None, :], 0), axis=1)
    encoding = sin_cos(position, width)

    both, later_outward, columns = after(both, outward_weight, columns)
    fr, ct = both[:, :width], both[:, width:]
    outward = lax.all_gather(later_outward, SEQ, axis=0, tiled=True)
    small_part = columns[:, share : share + extra, : 3 * hw].reshape(-1, 3 * hw)
    small_part = jnp.pad(small_part, ((0, SMALL_ROWS - small_part.shape[0]), (0, 0)))
    in_part = stack_rows([columns[:, :share, : 3 * hw].reshape(-1, 3 * hw), small_part])
    in_parts = [in_part] + [hop(in_part, "z", NZ, k) for k in range(1, NZ)]
    sh_rows = lax.dynamic_slice_in_dim(shrink_weight, x * part, part, 0)
    ff_part = stack_rows([columns[:, :share, 3 * hw :].reshape(-1, units), fold_columns(sh_rows, units)])
    mine, up_mine = assemble_pair(near_parts(both, ny), place.xy)
    ff_part = jnp.broadcast_to(ff_part[None], (NZ,) + ff_part.shape)
    mine, encoding, ff_part, *in_parts = after(mine, encoding, ff_part, *in_parts)
    first_pair = [mine, hop(mine, "c")]
    w_in, small_rows = collect_inward(in_parts, place)
    ff_got = exchange(ff_part, ("z",))

    vectors = small_rows.reshape(NZ, SMALL_ROWS, 3 * hw)[:, : ny * 2 * extra]
    vectors = vectors.reshape(spread, kinds, share).astype(F32)
    expand_b = vectors[:, len(small) :].reshape(NZ, ny, 2, 2, part)
    expand_b = pick(pick(pick(expand_b, y, 1), c, 1), x, 1).reshape(1, NZ * part)
    vectors = jnp.swapaxes(vectors[:, : len(small)], 0, 1).reshape(len(small), width)
    gain_one, shift_one, query_b, value_b, outward_b, gain_two, shift_two, shrink_b = (
        vectors[i : i + 1] for i in range(len(small))
    )
    qkv_bias = jnp.concatenate(
        [
            lax.dynamic_slice_in_dim(query_b, me * hw, hw, 1),
            jnp.zeros((1, hw), F32),
            lax.dynamic_slice_in_dim(value_b, me * hw, hw, 1),
        ],
        axis=1,
    )

    first_all, qkv, *context_pair, log_total = attention(
        place.core, first_pair, encoding, vectors[:2], w_in, qkv_bias, row_starts, hd, ny, size
    )
    *context_pair, up_mine = after(*context_pair, up_mine)
    if ny == 2:
        context = by_half(c, context_pair[0][None], hop(context_pair[1], "c")[None], 0)
        context = context.reshape(2, 2, ny, size, hw)
        context = by_half(x, pick(context, x, 1)[:, None], hop(pick(context, 1 - x, 1), "x")[:, None], 1)
        context = by_half(y, pick(context, y, 2)[:, :, None], hop(pick(context, 1 - y, 2), "y")[:, :, None], 2)
    else:
        context = exchange(by_half(c, *context_pair, 0).reshape(layer, size, hw), LAYER)
    context = context.reshape(layer, size, hw)
    up_pair = [up_mine, hop(up_mine, "c")]

    inputs = fr.astype(F32) + lax.dynamic_slice_in_dim(encoding, (x * ny + y) * size, size, 0)
    normal_one, scale_one = normalize(inputs)
    context = jnp.swapaxes(context, 0, 1).reshape(size, width)
    middle = inputs + dot_nn(context, outward) + outward_b

    normal_two, scale_two = normalize(middle)
    second = (normal_two * gain_two + shift_two).astype(BF16)
    ff_got, *second_near = after(ff_got, *near_parts(second, ny))
    second_pair = both_cores(second_near, place)
    w_expand, w_shrink = collect_hidden(ff_got, width)
    active, before_grad, send, keep, out_part = feed_forward_front(
        place.core, second_pair, up_pair, w_expand, w_shrink, expand_b, size
    )
    second_parts = list(fold(keep, hop(send, "c"), place, ny))
    second_parts[0], active, before_grad = after(second_parts[0], active, before_grad)
    second_grad = finish(second_parts, ny)
    expand_b_sum, hidden_part = feed_forward_weights(second_pair, up_pair, active, before_grad)
    out_part = lax.psum_scatter(out_part, LAYER, scatter_dimension=0, tiled=True)
    second_grad, expand_b_sum = after(second_grad, expand_b_sum)
    hidden_got = exchange(hidden_part, ("z",))

    upstream = ct.astype(F32)
    middle_part, gain_two_sum, shift_two_sum = normalize_back(normal_two, scale_two, gain_two, second_grad)
    middle_grad = upstream + middle_part
    low_middle = middle_grad.astype(BF16)
    low_pair = both_cores(near_parts(low_middle, ny), place)
    w_out = lax.dynamic_slice_in_dim(outward, me * hw, hw, 0)
    mixed_grad, send, keep, outward_part = attention_back(
        place, qkv, low_pair, context_pair, w_out, w_in, row_starts, log_total, hd, ny, size
    )
    got = hop(send, "c")
    cut = outward_part if hd == 2 and ny == 2 else outward_part.reshape(2, 1, -1, width)
    far_cut = hop(pick(cut, 1 - c), "c")
    got, far_cut = after(got, far_cut)
    first_parts = list(fold(keep, got, place, ny))
    first_parts[0], mixed_late, far_cut, hidden_got = after(first_parts[0], mixed_grad, far_cut, hidden_got)
    inward_part = dot_tn(first_all, mixed_late).astype(BF16)
    first_grad = finish(first_parts, ny)
    far_cut, out_part = after(far_cut, out_part)
    line_out = by_half(c, pick(cut, c)[None], far_cut[None], 0)
    if hd == 2 and ny == 2:
        line_out = by_half(x, pick(line_out, x, 1)[:, None], hop(pick(line_out, 1 - x, 1), "x")[:, None], 1)
    inward_got = exchange(inward_part.reshape(spread, share, 3 * hw), SEQ)
    input_part, gain_one_sum, shift_one_sum = normalize_back(normal_one, scale_one, vectors[:1], first_grad)
    late = (middle_grad + input_part).astype(BF16)
    late, out_part, hidden_got, line_out = after(late, out_part, hidden_got, line_out)
    hidden_sum = sum_sources(hidden_got, NZ)
    frames_grad = to_origin(late, place)
    inward_got, out_part = after(inward_got, out_part)
    layer_output = to_origin((middle + out_part.astype(F32) + shrink_b).astype(BF16), place)

    split = width // 2
    hidden_sum = sum_groups(hidden_sum.reshape(-1, units)).astype(BF16)
    line = hidden_sum[: width // NZ].reshape(ny, 2, share, units)
    if ny == 2:
        line = by_half(c, pick(line, c, 1)[:, None], hop(pick(line, 1 - c, 1), "c")[:, None], 1)
        line = by_half(y, pick(line, y)[None], hop(pick(line, 1 - y), "y")[None], 0)
    else:
        line = exchange(line.reshape(ny * 2, share, units), ("y", "c"))
    mine = stack_rows([line.reshape(-1, units), hidden_sum[width // NZ :]])
    other = hop(mine, "x")

    def full_hidden(other):
        if part % 128 == 0:
            g_expand, g_shrink = unpack_hidden(place, mine, other, ny * 2, share, part, width)
            return g_shrink, g_expand
        pair = [unfold_columns(v[width // NZ :], width // units) for v in (mine, other)]
        g_shrink = by_half(x, *pair, 0).astype(F32)
        pair = [v[: width // NZ].reshape(ny, 2, 1, share, NZ, part) for v in (mine, other)]
        return g_shrink, jnp.transpose(by_half(x, *pair, 2), (3, 4, 0, 1, 2, 5)).reshape(share, -1).astype(F32)

    if hd == 2 and ny == 2:
        line = line_out
        out_got = lax.psum_scatter(line.reshape(NZ * share, split), "z", scatter_dimension=0, tiled=True)
        inward_late, out_got = after(inward_got, out_got)
        out_sum = sum_groups(out_got.astype(F32)).astype(BF16)
        g_outward = by_half(x, out_sum, hop(out_sum, "x"), 1).astype(F32)
    else:
        cut = lax.dynamic_update_slice(jnp.zeros((width, width), BF16), outward_part, (me * hw, 0))
        g_outward = lax.psum_scatter(cut, SEQ, scatter_dimension=0, tiled=True)
        g_outward = lax.psum(g_outward.astype(F32), ("g", "x"))

    mixed_sum = jnp.sum(mixed_grad.astype(F32), axis=0)

    def from_heads(value):
        return lax.dynamic_update_slice(jnp.zeros((width,), F32), value, (me * hw,))

    flat = lax.optimization_barrier(jnp.stack(
        [
            gain_one_sum,
            shift_one_sum,
            from_heads(mixed_sum[:hw]),
            from_heads(mixed_sum[2 * hw :]),
            jnp.sum(low_middle.astype(F32), axis=0),
            gain_two_sum,
            shift_two_sum,
            jnp.sum(upstream, axis=0),
        ]
    ))
    small_len = len(small) * share
    sums = jnp.swapaxes(flat.reshape(len(small), spread, share), 0, 1).reshape(spread, small_len)
    spot = jnp.zeros((NZ, ny, 2, 2, part), F32)
    spot = lax.dynamic_update_slice(spot, expand_b_sum.reshape(NZ, 1, 1, 1, part), (0, y, c, x, 0))
    sums = jnp.concatenate([sums, spot.reshape(spread, hidden)], axis=1)
    inward_got, sums = after(inward_got, sums)
    sums = jnp.broadcast_to(sums[None], (2,) + sums.shape).reshape(2 * spread, -1, 128)
    total = sum_groups(jnp.sum(exchange(sums, ("x",) + SEQ), axis=0)).reshape(-1)
    frames_grad, total, other = after(frames_grad, total, other)
    g_shrink, g_expand = full_hidden(other)
    g_small = total[:small_len].reshape(len(small), share)
    g_expand_b = total[small_len:]
    inward_got = inward_late if hd == 2 and ny == 2 else inward_got
    inward_sum = sum_groups(sum_sources(inward_got, NZ)).astype(BF16)
    g_inward = [v.reshape(ny, 2, 1, share, 3, hw) for v in (inward_sum, hop(inward_sum, "x"))]
    g_inward = jnp.transpose(by_half(x, *g_inward, 2), (3, 4, 1, 2, 0, 5)).reshape(share, -1).astype(F32)

    return (
        layer_output,
        frames_grad.astype(F32),
        g_small[0],
        g_small[1],
        g_inward,
        g_small[2],
        g_small[3],
        g_outward,
        g_small[4],
        g_small[5],
        g_small[6],
        g_expand,
        g_expand_b,
        g_shrink,
        g_small[7],
    )


def solution(mesh):
    batch, seq = mesh.shape["batch"], mesh.shape["seq"]
    groups, ny = batch // 2, seq // (2 * NZ)
    fine = Mesh(mesh.devices.reshape(groups, 2, NZ, ny, 2), ("g", "x", "z", "y", "c"))
    b, s = ("g", "x"), ("z", "y", "c")
    in_specs = (
        P(s, b, None),
        P(s, b, None),
        P(b, None),
        P(b, None),
        P(s),
        P(s),
        P(s, None),
        P(s),
        P(s),
        P(s, None),
        P(s),
        P(s),
        P(s),
        P(s, None),
        P(s),
        P(s, None),
        P(s),
    )
    out_specs = (
        P(s, b, None),
        P(s, b, None),
        P(s),
        P(s),
        P(s, None),
        P(s),
        P(s),
        P(s, None),
        P(s),
        P(s),
        P(s),
        P(s, None),
        P(s),
        P(s, None),
        P(s),
    )
    return jax.shard_map(
        functools.partial(on_device, groups, ny), mesh=fine, in_specs=in_specs, out_specs=out_specs, check_vma=False
    )
```

```python
import functools
import math

import jax
import jax.numpy as jnp
from jax import lax
from jax.experimental import pallas as pl
from jax.experimental.pallas import tpu as pltpu
from jax.sharding import Mesh, PartitionSpec as P


HEADS = 16
NZ = 4
SMALL_ROWS = 16
NORM_EPS = 1e-05
NEG = -1e30
F32 = jnp.float32
BF16 = jnp.bfloat16
LAYER_OF_ROW = (1, 2, 0, 3)
SWAP = [(0, 1), (1, 0)]
LAYER = ("c", "x", "y")
SEQ = ("z", "y", "c")


def xor_perm(count, k):
    return [(i, i ^ k) for i in range(count)]


def hop(value, axis, count=2, k=1):
    return lax.ppermute(value, axis, xor_perm(count, k))


def pick(value, index, axis=0):
    return lax.dynamic_index_in_dim(value, index, axis, keepdims=False)


def stack_rows(parts):
    return jnp.concatenate(parts, axis=0)


def assemble_body(pieces, size, place_ref, *refs):
    out_ref = refs[pieces]
    for r in range(pieces):
        spot = place_ref[0] ^ r
        out_ref[pl.ds(pl.multiple_of(spot * size, size), size), :] = refs[r][...]


def assemble(parts, me):
    size, width = parts[0].shape
    count = len(parts)
    return pl.pallas_call(
        functools.partial(assemble_body, count, size),
        out_shape=jax.ShapeDtypeStruct((count * size, width), parts[0].dtype),
        in_specs=[pl.BlockSpec(memory_space=pltpu.SMEM)] + whole(count),
        out_specs=whole(1)[0],
        compiler_params=pltpu.CompilerParams(vmem_limit_bytes=4 << 20),
        cost_estimate=pl.CostEstimate(flops=0, bytes_accessed=4 * count * size * width, transcendentals=0),
        name="assemble",
    )(me, *parts)


def assemble_pair_body(pieces, size, place_ref, *refs):
    left_ref, right_ref = refs[pieces:]
    width = left_ref.shape[1]
    for r in range(pieces):
        rows = pl.ds(pl.multiple_of((place_ref[0] ^ r) * size, size), size)
        left_ref[rows, :] = refs[r][:, 0:width]
        right_ref[rows, :] = refs[r][:, width : 2 * width]


def assemble_pair(parts, me):
    size, width = parts[0].shape
    count = len(parts)
    return pl.pallas_call(
        functools.partial(assemble_pair_body, count, size),
        out_shape=[jax.ShapeDtypeStruct((count * size, width // 2), parts[0].dtype)] * 2,
        in_specs=[pl.BlockSpec(memory_space=pltpu.SMEM)] + whole(count),
        out_specs=whole(2),
        compiler_params=pltpu.CompilerParams(vmem_limit_bytes=4 << 20),
        cost_estimate=pl.CostEstimate(flops=0, bytes_accessed=4 * count * size * width, transcendentals=0),
        name="assemble_pair",
    )(me, *parts)


def near_parts(block, ny):
    return [block] + [lax.ppermute(block, ("x", "y"), xor_perm(2 * ny, r)) for r in range(1, 2 * ny)]


def both_cores(parts, place):
    mine = assemble(parts, place.xy)
    return mine, hop(mine, "c")


def fold_body(count, size, place_ref, keep_ref, got_ref, own_ref, *out_refs):
    for r in range(count):
        spot = place_ref[0] ^ r
        here = pl.ds(pl.multiple_of(spot * size, size), size)
        value = keep_ref[here, :].astype(F32) + got_ref[here, :].astype(F32)
        if r == 0:
            own_ref[...] = value
        else:
            out_refs[r - 1][...] = value.astype(BF16)


def fold(keep, got, place, ny):
    rows, width = keep.shape
    count = 2 * ny
    size = rows // count
    return pl.pallas_call(
        functools.partial(fold_body, count, size),
        out_shape=[jax.ShapeDtypeStruct((size, width), F32)] + [jax.ShapeDtypeStruct((size, width), BF16)] * (count - 1),
        in_specs=[pl.BlockSpec(memory_space=pltpu.SMEM)] + whole(2),
        out_specs=whole(count),
        compiler_params=pltpu.CompilerParams(vmem_limit_bytes=4 << 20),
        cost_estimate=pl.CostEstimate(flops=count * size * width, bytes_accessed=6 * count * size * width, transcendentals=0),
        name="fold",
    )(place.xy, keep, got)


def finish(parts, ny):
    own = parts[0]
    for r in range(1, 2 * ny):
        own = own + lax.ppermute(parts[r], ("x", "y"), xor_perm(2 * ny, r)).astype(F32)
    return own


def fold_columns(value, units):
    return stack_rows([value[:, i : i + units] for i in range(0, value.shape[1], units)])


def unfold_columns(value, count):
    size = value.shape[0] // count
    return jnp.concatenate([value[i * size : (i + 1) * size] for i in range(count)], axis=1)


def collect_inward_body(place_ref, *refs):
    weight_ref, small_ref = refs[NZ:]
    quarter = weight_ref.shape[0] // NZ
    for r in range(NZ):
        spot = place_ref[0] ^ r
        weight_ref[pl.ds(pl.multiple_of(spot * quarter, quarter), quarter), :] = refs[r][0:quarter, :]
        rows = pl.ds(pl.multiple_of(spot * SMALL_ROWS, SMALL_ROWS), SMALL_ROWS)
        small_ref[rows, :] = refs[r][quarter : quarter + SMALL_ROWS, :]


def collect_inward(parts, place):
    rows, width = parts[0].shape
    return pl.pallas_call(
        collect_inward_body,
        out_shape=[jax.ShapeDtypeStruct((NZ * n, width), BF16) for n in (rows - SMALL_ROWS, SMALL_ROWS)],
        in_specs=[pl.BlockSpec(memory_space=pltpu.SMEM)] + whole(NZ),
        out_specs=whole(2),
        compiler_params=pltpu.CompilerParams(vmem_limit_bytes=4 << 20),
        cost_estimate=pl.CostEstimate(flops=0, bytes_accessed=16 * rows * width, transcendentals=0),
        name="collect_inward",
    )(place.layer, *parts)


def collect_hidden_body(parts_ref, expand_ref, shrink_ref):
    quarter = expand_ref.shape[0] // NZ
    part, units = shrink_ref.shape[0] // NZ, expand_ref.shape[1]
    for r in range(NZ):
        expand_ref[r * quarter : (r + 1) * quarter, :] = parts_ref[r, 0:quarter, :]
        for i in range(shrink_ref.shape[1] // units):
            start = quarter + i * part
            here = slice(r * part, (r + 1) * part)
            shrink_ref[here, i * units : (i + 1) * units] = parts_ref[r, start : start + part, :]


def collect_hidden(parts, width):
    units = parts.shape[2]
    return pl.pallas_call(
        collect_hidden_body,
        out_shape=[jax.ShapeDtypeStruct((width, units), BF16), jax.ShapeDtypeStruct((units, width), BF16)],
        in_specs=whole(1),
        out_specs=whole(2),
        compiler_params=pltpu.CompilerParams(vmem_limit_bytes=4 << 20),
        cost_estimate=pl.CostEstimate(flops=0, bytes_accessed=4 * parts.size, transcendentals=0),
        name="collect_hidden",
    )(parts)


def unpack_hidden_body(lines, place_ref, mine_ref, other_ref, expand_ref, shrink_ref):
    share = expand_ref.shape[0]
    part = shrink_ref.shape[0] // 2
    units, deep = mine_ref.shape[1], lines * share
    for ref, slot in ((mine_ref, place_ref[0]), (other_ref, 1 - place_ref[0])):
        for line in range(lines):
            for k in range(NZ):
                spot = ((k * lines + line) * 2 + slot) * part
                value = ref[line * share : (line + 1) * share, k * part : (k + 1) * part].astype(F32)
                expand_ref[:, pl.ds(pl.multiple_of(spot, part), part)] = value
        rows = pl.ds(pl.multiple_of(slot * part, part), part)
        for i in range(shrink_ref.shape[1] // units):
            start = deep + i * part
            shrink_ref[rows, i * units : (i + 1) * units] = ref[start : start + part, :].astype(F32)


def unpack_hidden(place, mine, other, lines, share, part, width):
    return pl.pallas_call(
        functools.partial(unpack_hidden_body, lines),
        out_shape=[
            jax.ShapeDtypeStruct((share, 2 * NZ * lines * part), F32),
            jax.ShapeDtypeStruct((2 * part, width), F32),
        ],
        in_specs=[pl.BlockSpec(memory_space=pltpu.SMEM)] + whole(2),
        out_specs=whole(2),
        compiler_params=pltpu.CompilerParams(vmem_limit_bytes=4 << 20),
        cost_estimate=pl.CostEstimate(flops=0, bytes_accessed=12 * mine.size, transcendentals=0),
        name="unpack_hidden",
    )(jnp.reshape(place.x, (1,)).astype(jnp.int32), mine, other)


def rehome_flat(x, z, c):
    return (x * NZ + z) * 2 + c


def rehome_perm(k):
    return [
        (rehome_flat(x, z, c), rehome_flat(z >> 1, LAYER_OF_ROW[2 * x + (c ^ k)], z & 1))
        for x in range(2)
        for z in range(NZ)
        for c in range(2)
    ]


def to_home(block, place):
    got = [
        lax.ppermute(jnp.where(place.c == k, block[:, 0], block[:, 1]), ("x", "z", "c"), rehome_perm(k))
        for k in range(2)
    ]
    first = place.z < 2
    return stack_rows([jnp.where(first, got[0], got[1]), jnp.where(first, got[1], got[0])])


def to_origin(block, place):
    half = block.shape[0] // 2
    first = place.z < 2
    low, high = block[:half], block[half:]
    sent = [jnp.where(first, low, high), jnp.where(first, high, low)]
    got = [
        lax.ppermute(sent[k], ("x", "z", "c"), [(b, a) for a, b in rehome_perm(k)]) for k in range(2)
    ]
    return jnp.stack(
        [jnp.where(place.c == 0, got[0], got[1]), jnp.where(place.c == 0, got[1], got[0])], axis=1
    )


def after(first, *values):
    return lax.optimization_barrier((first, *values))


def sum_sources(value, count):
    return jnp.sum(value.reshape((count, -1) + value.shape[1:]).astype(F32), axis=0)


def by_half(x, mine, other, axis):
    return jnp.concatenate([jnp.where(x == 0, mine, other), jnp.where(x == 0, other, mine)], axis=axis)


def sin_cos(position, width):
    feature = jnp.arange(width, dtype=jnp.int32)
    rates = jnp.exp((feature // 2).astype(F32) * (-2.0 * math.log(10000.0) / width))
    angle = position.astype(F32)[:, None] * rates[None, :]
    turn = jnp.round(angle * (2.0 / math.pi))
    rest = angle - turn * 1.5703125
    rest = rest - turn * 0.00048375129699707031
    rest = rest - turn * 7.5497899548918861e-08
    quadrant = turn.astype(jnp.int32) + (feature % 2)[None, :]
    square = rest * rest
    sine = rest + rest * square * (
        -0.16666666641626524 + square * (0.008333329385889463 + square * (-0.00019839334836096632 + square * 2.718311493989822e-06))
    )
    cosine = 1.0 + square * (
        -0.49999999725103100 + square * (0.04166662332373906 + square * (-0.001388676377460993 + square * 2.439044879627741e-05))
    )
    value = jnp.where((quadrant & 1) == 0, sine, cosine)
    return jnp.where((quadrant & 2) == 0, value, -value)


def normalize(values):
    center = values - jnp.mean(values, axis=-1, keepdims=True)
    scale = lax.rsqrt(jnp.mean(center * center, axis=-1, keepdims=True) + NORM_EPS)
    return center * scale, scale


def normalize_back(normal, scale, gain, upstream):
    scaled = upstream * gain
    inner = scaled - jnp.mean(scaled, axis=-1, keepdims=True)
    inner = inner - normal * jnp.mean(scaled * normal, axis=-1, keepdims=True)
    return inner * scale, jnp.sum(upstream * normal, axis=0), jnp.sum(upstream, axis=0)


def dot_nt(a, b):
    return lax.dot_general(a, b, (((1,), (1,)), ((), ())), preferred_element_type=F32)


def dot_tn(a, b):
    return lax.dot_general(a, b, (((0,), (0,)), ((), ())), preferred_element_type=F32)


def dot_nn(a, b):
    return jnp.dot(a, b, preferred_element_type=F32)


BLOCK = 256


def chunk_owner(chunk, ny):
    outer, y = divmod(chunk, ny)
    return ((outer & 1) * 2 + (outer >> 1)) * ny + y


def lane_parts(heads, width):
    if heads == 1:
        return [None]
    lane = lax.broadcasted_iota(jnp.int32, (1, width), 1)
    return [(lane >= h * (width // heads)) & (lane < (h + 1) * (width // heads)) for h in range(heads)]


def only(value, lanes):
    return value if lanes is None else jnp.where(lanes, value, jnp.zeros_like(value))


def allowed_pairs(start_ref, first, total):
    key = lax.broadcasted_iota(jnp.int32, (total, BLOCK), 0)
    frame = first + lax.broadcasted_iota(jnp.int32, (total, BLOCK), 1)
    return (key >= start_ref[:, first : first + BLOCK]) & (key <= frame)


def chunk_rows(chunk, ny, size, core):
    half, spot = divmod(chunk_owner(chunk, ny), 2 * ny)
    return pl.ds(pl.multiple_of(((half ^ core) * (2 * ny) + spot) * size, size), size)


def attend(
    heads,
    ny,
    size,
    core_ref,
    mine_ref,
    other_ref,
    encoding_ref,
    affine_ref,
    weight_ref,
    bias_ref,
    start_ref,
    first_ref,
    qkv_ref,
    near_ref,
    far_ref,
    log_ref,
    q_s,
    k_s,
    vt_s,
):
    count = 4 * ny
    width = q_s.shape[1]
    core = core_ref[0]
    step = 2 * size
    half = mine_ref.shape[0]
    for base, ref in ((0, mine_ref), (half, other_ref)):
        for start in range(0, half, step):
            rows = slice(base + start, base + start + step)
            normal, _ = normalize(ref[start : start + step, :].astype(F32) + encoding_ref[rows, :])
            value = (normal * affine_ref[0:1, :] + affine_ref[1:2, :]).astype(BF16)
            first_ref[rows, :] = value
            qkv_ref[rows, :] = (dot_nn(value, weight_ref[...]) + bias_ref[...]).astype(BF16)
    for chunk in range(count):
        rows = chunk_rows(chunk, ny, size, core)
        here = slice(chunk * size, (chunk + 1) * size)
        q_s[here, :] = qkv_ref[rows, 0:width] * 0.125
        k_s[here, :] = qkv_ref[rows, width : 2 * width]
        vt_s[:, here] = jnp.transpose(qkv_ref[rows, 2 * width : 3 * width].astype(F32)).astype(BF16)
    lanes = lane_parts(heads, width)
    each = width // heads
    for block in range(count * size // BLOCK):
        first = block * BLOCK
        total = first + BLOCK
        allowed = allowed_pairs(start_ref, first, total)
        q_block = q_s[first:total, :]
        contexts = []
        for h in range(heads):
            scores = dot_nt(k_s[0:total, :], only(q_block, lanes[h]))
            scores = jnp.where(allowed, scores, NEG)
            top = jnp.max(scores, axis=0, keepdims=True)
            weight = jnp.exp(scores - top)
            mass = jnp.sum(weight, axis=0, keepdims=True)
            part = dot_nn(vt_s[h * each : (h + 1) * each, 0:total], weight.astype(BF16))
            contexts.append(part / mass)
            log_ref[h : h + 1, first:total] = top + jnp.log(mass)
        context = contexts[0] if heads == 1 else jnp.concatenate(contexts, axis=0)
        context = jnp.transpose(context).astype(BF16)
        for sub in range(BLOCK // size):
            owner = chunk_owner(block * (BLOCK // size) + sub, ny)
            side, spot = divmod(owner, 2 * ny)
            rows, piece = slice(spot * size, (spot + 1) * size), context[sub * size : (sub + 1) * size]

            @pl.when(core == side)
            def _(rows=rows, piece=piece):
                near_ref[rows, :] = piece

            @pl.when(core != side)
            def _(rows=rows, piece=piece):
                far_ref[rows, :] = piece


def attend_back(
    heads,
    ny,
    size,
    core_ref,
    qkv_ref,
    mine_ref,
    other_ref,
    near_ref,
    far_ref,
    outward_ref,
    weight_ref,
    start_ref,
    log_ref,
    out_ref,
    send_ref,
    keep_ref,
    outward_grad_ref,
    q_s,
    k_s,
    v_s,
    g_s,
    kt_s,
    dq_s,
    dk_s,
    dv_s,
):
    count = 4 * ny
    width = q_s.shape[1]
    core = core_ref[0]
    half = mine_ref.shape[0]
    step = 2 * size
    for base, ref in ((0, mine_ref), (half, other_ref)):
        for start in range(0, half, step):
            rows = slice(start, start + step)
            out_ref[base + start : base + start + step, 0:width] = dot_nt(ref[rows, :], outward_ref[...]).astype(BF16)
    for chunk in range(count):
        rows = chunk_rows(chunk, ny, size, core)
        here = slice(chunk * size, (chunk + 1) * size)
        q_s[here, :] = qkv_ref[rows, 0:width] * 0.125
        key = qkv_ref[rows, width : 2 * width]
        k_s[here, :] = key
        kt_s[:, here] = jnp.transpose(key.astype(F32)).astype(BF16)
        v_s[here, :] = qkv_ref[rows, 2 * width : 3 * width]
        g_s[here, :] = out_ref[rows, 0:width]
    dk_s[...] = jnp.zeros_like(dk_s)
    dv_s[...] = jnp.zeros_like(dv_s)
    lanes = lane_parts(heads, width)
    each = width // heads
    for block in range(count * size // BLOCK):
        first = block * BLOCK
        total = first + BLOCK
        allowed = allowed_pairs(start_ref, first, total)
        q_block, g_block = q_s[first:total, :], g_s[first:total, :]
        queries = []
        for h in range(heads):
            q_one, g_one = only(q_block, lanes[h]), only(g_block, lanes[h])
            scores = dot_nt(k_s[0:total, :], q_one)
            probs = jnp.where(allowed, jnp.exp(scores - log_ref[h : h + 1, first:total]), 0.0)
            prob_grad = dot_nt(v_s[0:total, :], g_one)
            delta = jnp.sum(probs * prob_grad, axis=0, keepdims=True)
            score_grad = (probs * (prob_grad - delta)).astype(BF16)
            dv_s[0:total, :] += dot_nn(probs.astype(BF16), g_one)
            dk_s[0:total, :] += dot_nn(score_grad, q_one)
            queries.append(dot_nn(kt_s[h * each : (h + 1) * each, 0:total], score_grad))
        query_grad = queries[0] if heads == 1 else jnp.concatenate(queries, axis=0)
        dq_s[first:total, :] = jnp.transpose(query_grad) * 0.125
    for chunk in range(count):
        rows = chunk_rows(chunk, ny, size, core)
        here = slice(chunk * size, (chunk + 1) * size)
        out_ref[rows, 0:width] = dq_s[here, :].astype(BF16)
        out_ref[rows, width : 2 * width] = dk_s[here, :].astype(BF16)
        out_ref[rows, 2 * width : 3 * width] = dv_s[here, :].astype(BF16)
    for ref, base in ((send_ref, half), (keep_ref, 0)):
        for start in range(0, half, step):
            rows = slice(base + start, base + start + step)
            ref[start : start + step, :] = dot_nt(out_ref[rows, :], weight_ref[...]).astype(BF16)
    total = dot_tn(near_ref[...], mine_ref[...]) + dot_tn(far_ref[...], other_ref[...])
    total = total.astype(BF16)
    if len(outward_grad_ref.shape) == 2:
        outward_grad_ref[...] = total
    else:
        rows, columns = outward_grad_ref.shape[2:]
        for i in range(4):
            start, left = (i >> 1) * rows, (i & 1) * columns
            outward_grad_ref[i >> 1, i & 1] = total[start : start + rows, left : left + columns]


def feed_forward(
    size,
    core_ref,
    mine_ref,
    other_ref,
    up_mine_ref,
    up_other_ref,
    expand_ref,
    shrink_ref,
    bias_ref,
    active_ref,
    grad_ref,
    send_ref,
    keep_ref,
    result_ref,
):
    half = keep_ref.shape[0]
    step = 2 * size
    rate = math.sqrt(2.0 / math.pi)
    core = core_ref[0]
    sides = ((send_ref, other_ref, up_other_ref, half, 1 - core), (keep_ref, mine_ref, up_mine_ref, 0, core))
    for ref, source_ref, up_ref, base, side in sides:
        for start in range(0, half, step):
            rows = slice(start, start + step)
            pair = slice(base + start, base + start + step)
            place = pl.ds(pl.multiple_of(side * half + start, step), step)
            before = dot_nn(source_ref[rows, :], expand_ref[...]) + bias_ref[...]
            upper = dot_nt(up_ref[rows, :], shrink_ref[...])
            square = before * before
            inner = jnp.tanh(rate * (before + 0.044715 * before * square))
            plus = 0.5 * (1.0 + inner)
            active = (before * plus).astype(BF16)
            active_ref[pair, :] = active
            slope = plus + 0.5 * before * (1.0 - inner * inner) * (rate + rate * 3 * 0.044715 * square)
            lower = (upper * slope).astype(BF16)
            grad_ref[pair, :] = lower
            ref[rows, :] = dot_nt(lower, expand_ref[...]).astype(BF16)
            result_ref[place, :] = dot_nn(active, shrink_ref[...]).astype(BF16)


def weight_parts(part, mine_ref, other_ref, up_mine_ref, up_other_ref, active_ref, grad_ref, bias_ref, out_ref):
    half, width = mine_ref.shape
    quarter, all_units = width // NZ, NZ * part
    for r in range(NZ):
        spot, ref = r, out_ref.at[r]
        here = slice(spot * quarter, (spot + 1) * quarter)
        total = dot_tn(mine_ref[:, here], grad_ref[0:half, :]) + dot_tn(other_ref[:, here], grad_ref[half : 2 * half, :])
        ref[0:quarter, :] = total.astype(BF16)
        units = slice(spot * part, (spot + 1) * part)
        total = dot_tn(active_ref[0:half, units], up_mine_ref[...])
        total = (total + dot_tn(active_ref[half : 2 * half, units], up_other_ref[...])).astype(BF16)
        for i in range(width // all_units):
            start = quarter + i * part
            ref[start : start + part, :] = total[:, i * all_units : (i + 1) * all_units]
    bias_ref[...] = jnp.sum(grad_ref[...].astype(F32), axis=0, keepdims=True)


def feed_forward_weights(second, up, active, before_grad):
    frames, units = active.shape
    width, part = up[0].shape[1], units // NZ
    quarter = width // NZ
    if part % 128:
        shrink = dot_tn(active, stack_rows(up)).astype(BF16).reshape(NZ, part, width)
        expand = dot_tn(stack_rows(second), before_grad).astype(BF16).reshape(NZ, quarter, units)
        bias = jnp.sum(before_grad.astype(F32), axis=0, keepdims=True)
        return bias, jnp.stack([stack_rows([expand[k], fold_columns(shrink[k], units)]) for k in range(NZ)])
    return pl.pallas_call(
        functools.partial(weight_parts, part),
        out_shape=(jax.ShapeDtypeStruct((1, units), F32), jax.ShapeDtypeStruct((NZ, 2 * quarter, units), BF16)),
        in_specs=whole(6),
        out_specs=tuple(whole(2)),
        compiler_params=pltpu.CompilerParams(vmem_limit_bytes=16 << 20),
        cost_estimate=pl.CostEstimate(
            flops=4 * frames * width * units, bytes_accessed=8 * frames * width, transcendentals=0
        ),
        name="feed_forward_weights",
    )(*second, *up, active, before_grad)


def whole(count):
    return [pl.BlockSpec(memory_space=pltpu.VMEM)] * count


def attention(core, pair, encoding, affine, w_in, bias, starts, heads, ny, size):
    half, wide = pair[0].shape[0], w_in.shape[1]
    frames, depth, width = 2 * half, pair[0].shape[1], wide // 3
    pairs = frames * frames * heads
    return pl.pallas_call(
        functools.partial(attend, heads, ny, size),
        out_shape=(
            jax.ShapeDtypeStruct((frames, depth), BF16),
            jax.ShapeDtypeStruct((frames, wide), BF16),
            jax.ShapeDtypeStruct((half, width), BF16),
            jax.ShapeDtypeStruct((half, width), BF16),
            jax.ShapeDtypeStruct((heads, frames), F32),
        ),
        in_specs=[pl.BlockSpec(memory_space=pltpu.SMEM)] + whole(7),
        out_specs=tuple(whole(5)),
        scratch_shapes=[
            pltpu.VMEM((frames, width), BF16),
            pltpu.VMEM((frames, width), BF16),
            pltpu.VMEM((width, frames), BF16),
        ],
        compiler_params=pltpu.CompilerParams(vmem_limit_bytes=16 << 20),
        cost_estimate=pl.CostEstimate(
            flops=pairs * 256 + 2 * frames * depth * wide, bytes_accessed=8 * frames * depth, transcendentals=pairs // 2
        ),
        name="attend",
    )(core, *pair, encoding, affine, w_in, bias, starts)


def attention_back(place, qkv, pair, context, w_out, w_in, starts, log_total, heads, ny, size):
    frames, wide = qkv.shape
    width = wide // 3
    depth = pair[0].shape[1]
    cut = heads == 2 and ny == 2
    pairs = frames * frames * heads
    half = jax.ShapeDtypeStruct(pair[0].shape, BF16)
    return pl.pallas_call(
        functools.partial(attend_back, heads, ny, size),
        out_shape=(
            jax.ShapeDtypeStruct((frames, wide), BF16),
            half,
            half,
            jax.ShapeDtypeStruct((2, 2, width // 2, depth // 2) if cut else (width, depth), BF16),
        ),
        in_specs=[pl.BlockSpec(memory_space=pltpu.SMEM)] + whole(9),
        out_specs=tuple(whole(4)),
        scratch_shapes=[pltpu.VMEM((frames, width), BF16)] * 4
        + [pltpu.VMEM((width, frames), BF16)]
        + [pltpu.VMEM((frames, width), F32)] * 3,
        compiler_params=pltpu.CompilerParams(vmem_limit_bytes=20 << 20),
        cost_estimate=pl.CostEstimate(
            flops=pairs * 640 + 2 * frames * depth * (wide + 2 * width),
            bytes_accessed=8 * frames * depth,
            transcendentals=pairs // 2,
        ),
        name="attend_back",
    )(place.core, qkv, *pair, *context, w_out, w_in, starts, log_total)


def feed_forward_front(core, pair, up_pair, w_expand, w_shrink, bias, size):
    frames, width = 2 * pair[0].shape[0], pair[0].shape[1]
    units = w_expand.shape[1]
    half = jax.ShapeDtypeStruct((frames // 2, width), BF16)
    inner = jax.ShapeDtypeStruct((frames, units), BF16)
    return pl.pallas_call(
        functools.partial(feed_forward, size),
        out_shape=(inner, inner, half, half, jax.ShapeDtypeStruct((frames, width), BF16)),
        in_specs=[pl.BlockSpec(memory_space=pltpu.SMEM)] + whole(7),
        out_specs=tuple(whole(5)),
        compiler_params=pltpu.CompilerParams(vmem_limit_bytes=16 << 20),
        cost_estimate=pl.CostEstimate(
            flops=8 * frames * width * units, bytes_accessed=10 * frames * width, transcendentals=frames * units
        ),
        name="feed_forward",
    )(core, *pair, *up_pair, w_expand, w_shrink, bias)


class Place:
    def __init__(self, ny):
        self.x, self.z, self.y, self.c = (lax.axis_index(a) for a in ("x", "z", "y", "c"))
        self.xy = jnp.reshape(self.x * ny + self.y, (1,)).astype(jnp.int32)
        self.core = jnp.reshape(self.c, (1,)).astype(jnp.int32)
        self.layer = jnp.reshape(self.z, (1,)).astype(jnp.int32)


def on_device(
    groups,
    ny,
    frames,
    cotangent,
    segment_lengths,
    position_offsets,
    first_gain,
    first_shift,
    inward_weight,
    query_bias,
    value_bias,
    outward_weight,
    outward_bias,
    second_gain,
    second_shift,
    expand_weight,
    expand_bias,
    shrink_weight,
    shrink_bias,
):
    place = Place(ny)
    x, z, y, c = place.x, place.z, place.y, place.c
    local_len, rows, width = frames.shape
    share = inward_weight.shape[0]
    layer = 4 * ny
    spread = NZ * ny * 2
    full_len = local_len * spread
    size = 2 * local_len
    hd = HEADS // layer
    hw = hd * (width // HEADS)
    hidden = expand_bias.shape[0]
    part = hidden // 2
    me = (c * 2 + x) * ny + y

    def sum_groups(value):
        return lax.psum(value, "g") if groups > 1 else value

    def exchange(value, axes):
        return lax.all_to_all(value, axes, 0, 0, tiled=True)

    both = to_home(jnp.concatenate([frames, cotangent], axis=2), place)
    table = jnp.stack([segment_lengths, position_offsets], axis=1)

    small = [first_gain, first_shift, query_bias, value_bias, outward_bias, second_gain, second_shift, shrink_bias]
    kinds = len(small) + hidden // share
    units = NZ * part
    packed = jnp.concatenate([v[None] for v in small] + [expand_bias.reshape(-1, share)], axis=0)
    packed = packed.reshape(-1, 3 * hw)
    extra = packed.shape[0]
    packed = jnp.pad(packed, ((0, SMALL_ROWS - extra), (0, units)))[None]
    in_cols = jnp.transpose(inward_weight.reshape(share, 3, 2, 2, ny, hw), (3, 4, 2, 0, 1, 5))
    in_cols = pick(in_cols, x).reshape(ny * 2, share, 3 * hw)
    ex_cols = pick(expand_weight.reshape(share, NZ, ny, 2, 2, part), x, 4)
    ex_cols = jnp.transpose(ex_cols, (2, 3, 0, 1, 4)).reshape(ny * 2, share, units)
    columns = jnp.concatenate([in_cols, ex_cols], axis=2)
    columns = jnp.concatenate([columns, jnp.broadcast_to(packed, (ny * 2,) + packed.shape[1:])], axis=1)
    columns, table = after(columns, table)
    columns = exchange(columns, ("y", "c"))
    other_table = hop(table, "x")

    row_x = jnp.where((z == 0) | (z == 3), 1, 0)
    table = pick(jnp.where(x == row_x, table, other_table), z >> 1)
    lengths, offsets = table[0], table[1]
    count = lengths.shape[0]
    starts = jnp.sum(
        jnp.where(jnp.arange(count)[None, :] < jnp.arange(count)[:, None], lengths[None, :], 0), axis=1
    )
    frame_ids = jnp.arange(full_len, dtype=jnp.int32)
    row_starts = jnp.max(jnp.where(starts[:, None] <= frame_ids[None, :], starts[:, None], 0), axis=0)[None, :]
    spot = jnp.arange(2 * ny)
    chunk = jnp.concatenate([(2 * (spot // ny) + i) * ny + spot % ny for i in (c, 1 - c)])
    mine = (chunk[:, None] * size + jnp.arange(size, dtype=jnp.int32)).reshape(-1)
    inside = (mine[:, None] >= starts[None, :]) & (mine[:, None] < (starts + lengths)[None, :])
    position = jnp.sum(jnp.where(inside, offsets[None, :] + mine[:, None] - starts[None, :], 0), axis=1)
    encoding = sin_cos(position, width)

    both, later_outward, columns = after(both, outward_weight, columns)
    fr, ct = both[:, :width], both[:, width:]
    outward = lax.all_gather(later_outward, SEQ, axis=0, tiled=True)
    small_part = columns[:, share : share + extra, : 3 * hw].reshape(-1, 3 * hw)
    small_part = jnp.pad(small_part, ((0, SMALL_ROWS - small_part.shape[0]), (0, 0)))
    in_part = stack_rows([columns[:, :share, : 3 * hw].reshape(-1, 3 * hw), small_part])
    in_parts = [in_part] + [hop(in_part, "z", NZ, k) for k in range(1, NZ)]
    sh_rows = lax.dynamic_slice_in_dim(shrink_weight, x * part, part, 0)
    ff_part = stack_rows([columns[:, :share, 3 * hw :].reshape(-1, units), fold_columns(sh_rows, units)])
    mine, up_mine = assemble_pair(near_parts(both, ny), place.xy)
    ff_part = jnp.broadcast_to(ff_part[None], (NZ,) + ff_part.shape)
    mine, encoding, ff_part, *in_parts = after(mine, encoding, ff_part, *in_parts)
    first_pair = [mine, hop(mine, "c")]
    w_in, small_rows = collect_inward(in_parts, place)
    ff_got = exchange(ff_part, ("z",))

    vectors = small_rows.reshape(NZ, SMALL_ROWS, 3 * hw)[:, : ny * 2 * extra]
    vectors = vectors.reshape(spread, kinds, share).astype(F32)
    expand_b = vectors[:, len(small) :].reshape(NZ, ny, 2, 2, part)
    expand_b = pick(pick(pick(expand_b, y, 1), c, 1), x, 1).reshape(1, NZ * part)
    vectors = jnp.swapaxes(vectors[:, : len(small)], 0, 1).reshape(len(small), width)
    gain_one, shift_one, query_b, value_b, outward_b, gain_two, shift_two, shrink_b = (
        vectors[i : i + 1] for i in range(len(small))
    )
    qkv_bias = jnp.concatenate(
        [
            lax.dynamic_slice_in_dim(query_b, me * hw, hw, 1),
            jnp.zeros((1, hw), F32),
            lax.dynamic_slice_in_dim(value_b, me * hw, hw, 1),
        ],
        axis=1,
    )

    first_all, qkv, *context_pair, log_total = attention(
        place.core, first_pair, encoding, vectors[:2], w_in, qkv_bias, row_starts, hd, ny, size
    )
    *context_pair, up_mine = after(*context_pair, up_mine)
    if ny == 2:
        context = by_half(c, context_pair[0][None], hop(context_pair[1], "c")[None], 0)
        context = context.reshape(2, 2, ny, size, hw)
        context = by_half(x, pick(context, x, 1)[:, None], hop(pick(context, 1 - x, 1), "x")[:, None], 1)
        context = by_half(y, pick(context, y, 2)[:, :, None], hop(pick(context, 1 - y, 2), "y")[:, :, None], 2)
    else:
        context = exchange(by_half(c, *context_pair, 0).reshape(layer, size, hw), LAYER)
    context = context.reshape(layer, size, hw)
    up_pair = [up_mine, hop(up_mine, "c")]

    inputs = fr.astype(F32) + lax.dynamic_slice_in_dim(encoding, (x * ny + y) * size, size, 0)
    normal_one, scale_one = normalize(inputs)
    context = jnp.swapaxes(context, 0, 1).reshape(size, width)
    middle = inputs + dot_nn(context, outward) + outward_b

    normal_two, scale_two = normalize(middle)
    second = (normal_two * gain_two + shift_two).astype(BF16)
    ff_got, *second_near = after(ff_got, *near_parts(second, ny))
    second_pair = both_cores(second_near, place)
    w_expand, w_shrink = collect_hidden(ff_got, width)
    active, before_grad, send, keep, out_part = feed_forward_front(
        place.core, second_pair, up_pair, w_expand, w_shrink, expand_b, size
    )
    second_parts = list(fold(keep, hop(send, "c"), place, ny))
    second_parts[0], active, before_grad = after(second_parts[0], active, before_grad)
    second_grad = finish(second_parts, ny)
    expand_b_sum, hidden_part = feed_forward_weights(second_pair, up_pair, active, before_grad)
    out_part = lax.psum_scatter(out_part, LAYER, scatter_dimension=0, tiled=True)
    second_grad, expand_b_sum = after(second_grad, expand_b_sum)
    hidden_got = exchange(hidden_part, ("z",))

    upstream = ct.astype(F32)
    middle_part, gain_two_sum, shift_two_sum = normalize_back(normal_two, scale_two, gain_two, second_grad)
    middle_grad = upstream + middle_part
    low_middle = middle_grad.astype(BF16)
    low_pair = both_cores(near_parts(low_middle, ny), place)
    w_out = lax.dynamic_slice_in_dim(outward, me * hw, hw, 0)
    mixed_grad, send, keep, outward_part = attention_back(
        place, qkv, low_pair, context_pair, w_out, w_in, row_starts, log_total, hd, ny, size
    )
    got = hop(send, "c")
    cut = outward_part if hd == 2 and ny == 2 else outward_part.reshape(2, 1, -1, width)
    far_cut = hop(pick(cut, 1 - c), "c")
    got, far_cut = after(got, far_cut)
    first_parts = list(fold(keep, got, place, ny))
    first_parts[0], mixed_late, far_cut, hidden_got = after(first_parts[0], mixed_grad, far_cut, hidden_got)
    inward_part = dot_tn(first_all, mixed_late).astype(BF16)
    first_grad = finish(first_parts, ny)
    far_cut, out_part = after(far_cut, out_part)
    line_out = by_half(c, pick(cut, c)[None], far_cut[None], 0)
    if hd == 2 and ny == 2:
        line_out = by_half(x, pick(line_out, x, 1)[:, None], hop(pick(line_out, 1 - x, 1), "x")[:, None], 1)
    first_grad, line_out = after(first_grad, line_out)
    inward_got = exchange(inward_part.reshape(spread, share, 3 * hw), SEQ)
    input_part, gain_one_sum, shift_one_sum = normalize_back(normal_one, scale_one, vectors[:1], first_grad)
    late = (middle_grad + input_part).astype(BF16)
    late, out_part, hidden_got = after(late, out_part, hidden_got)
    hidden_sum = sum_sources(hidden_got, NZ)
    frames_grad = to_origin(late, place)
    inward_got, out_part = after(inward_got, out_part)
    layer_output = to_origin((middle + out_part.astype(F32) + shrink_b).astype(BF16), place)

    split = width // 2
    hidden_sum = sum_groups(hidden_sum.reshape(-1, units)).astype(BF16)
    line = hidden_sum[: width // NZ].reshape(ny, 2, share, units)
    if ny == 2:
        line = by_half(c, pick(line, c, 1)[:, None], hop(pick(line, 1 - c, 1), "c")[:, None], 1)
        line = by_half(y, pick(line, y)[None], hop(pick(line, 1 - y), "y")[None], 0)
    else:
        line = exchange(line.reshape(ny * 2, share, units), ("y", "c"))
    mine = stack_rows([line.reshape(-1, units), hidden_sum[width // NZ :]])
    other = hop(mine, "x")

    def full_hidden(other):
        if part % 128 == 0:
            g_expand, g_shrink = unpack_hidden(place, mine, other, ny * 2, share, part, width)
            return g_shrink, g_expand
        pair = [unfold_columns(v[width // NZ :], width // units) for v in (mine, other)]
        g_shrink = by_half(x, *pair, 0).astype(F32)
        pair = [v[: width // NZ].reshape(ny, 2, 1, share, NZ, part) for v in (mine, other)]
        return g_shrink, jnp.transpose(by_half(x, *pair, 2), (3, 4, 0, 1, 2, 5)).reshape(share, -1).astype(F32)

    if hd == 2 and ny == 2:
        line = line_out
        out_got = lax.psum_scatter(line.reshape(NZ * share, split), "z", scatter_dimension=0, tiled=True)
        inward_late, out_got = after(inward_got, out_got)
        out_sum = sum_groups(out_got.astype(F32)).astype(BF16)
        g_outward = by_half(x, out_sum, hop(out_sum, "x"), 1).astype(F32)
    else:
        cut = lax.dynamic_update_slice(jnp.zeros((width, width), BF16), outward_part, (me * hw, 0))
        g_outward = lax.psum_scatter(cut, SEQ, scatter_dimension=0, tiled=True)
        g_outward = lax.psum(g_outward.astype(F32), ("g", "x"))

    mixed_sum = jnp.sum(mixed_grad.astype(F32), axis=0)

    def from_heads(value):
        return lax.dynamic_update_slice(jnp.zeros((width,), F32), value, (me * hw,))

    flat = lax.optimization_barrier(jnp.stack(
        [
            gain_one_sum,
            shift_one_sum,
            from_heads(mixed_sum[:hw]),
            from_heads(mixed_sum[2 * hw :]),
            jnp.sum(low_middle.astype(F32), axis=0),
            gain_two_sum,
            shift_two_sum,
            jnp.sum(upstream, axis=0),
        ]
    ))
    small_len = len(small) * share
    sums = jnp.swapaxes(flat.reshape(len(small), spread, share), 0, 1).reshape(spread, small_len)
    spot = jnp.zeros((NZ, ny, 2, 2, part), F32)
    spot = lax.dynamic_update_slice(spot, expand_b_sum.reshape(NZ, 1, 1, 1, part), (0, y, c, x, 0))
    sums = jnp.concatenate([sums, spot.reshape(spread, hidden)], axis=1)
    inward_got, sums = after(inward_got, sums)
    sums = jnp.broadcast_to(sums[None], (2,) + sums.shape).reshape(2 * spread, -1, 128)
    total = sum_groups(jnp.sum(exchange(sums, ("x",) + SEQ), axis=0)).reshape(-1)
    frames_grad, total, other = after(frames_grad, total, other)
    g_shrink, g_expand = full_hidden(other)
    g_small = total[:small_len].reshape(len(small), share)
    g_expand_b = total[small_len:]
    inward_got = inward_late if hd == 2 and ny == 2 else inward_got
    inward_sum = sum_groups(sum_sources(inward_got, NZ)).astype(BF16)
    g_inward = [v.reshape(ny, 2, 1, share, 3, hw) for v in (inward_sum, hop(inward_sum, "x"))]
    g_inward = jnp.transpose(by_half(x, *g_inward, 2), (3, 4, 1, 2, 0, 5)).reshape(share, -1).astype(F32)

    return (
        layer_output,
        frames_grad.astype(F32),
        g_small[0],
        g_small[1],
        g_inward,
        g_small[2],
        g_small[3],
        g_outward,
        g_small[4],
        g_small[5],
        g_small[6],
        g_expand,
        g_expand_b,
        g_shrink,
        g_small[7],
    )


def solution(mesh):
    batch, seq = mesh.shape["batch"], mesh.shape["seq"]
    groups, ny = batch // 2, seq // (2 * NZ)
    fine = Mesh(mesh.devices.reshape(groups, 2, NZ, ny, 2), ("g", "x", "z", "y", "c"))
    b, s = ("g", "x"), ("z", "y", "c")
    in_specs = (
        P(s, b, None),
        P(s, b, None),
        P(b, None),
        P(b, None),
        P(s),
        P(s),
        P(s, None),
        P(s),
        P(s),
        P(s, None),
        P(s),
        P(s),
        P(s),
        P(s, None),
        P(s),
        P(s, None),
        P(s),
    )
    out_specs = (
        P(s, b, None),
        P(s, b, None),
        P(s),
        P(s),
        P(s, None),
        P(s),
        P(s),
        P(s, None),
        P(s),
        P(s),
        P(s),
        P(s, None),
        P(s),
        P(s, None),
        P(s),
    )
    return jax.shard_map(
        functools.partial(on_device, groups, ny), mesh=fine, in_specs=in_specs, out_specs=out_specs, check_vma=False
    )
```
